32 devices in a mesh: row: 8 (over y, x, core), batch: 4 (over z).
Axes of the slice: x: 2, y: 2, z: 4, core: 2. Of those that a mesh axis runs over, the one named last changes fastest.
Arguments:
- field_in: bfloat16 [384, 16, 64, 128], P('batch', 'row'), may hold values from -6 to 6
- refine_step: int32 [384], P('batch'), may hold values from 0 to 3, as said below
- cotangent: bfloat16 [384, 8, 32, 256], P(('batch', 'row')), may hold values from -6 to 6
- conv_weight: float32 [2, 1152, 128], P(None, 'batch', 'row'), may hold values from -0.1875 to 0.1875
- down_weight: float32 [1152, 256], P('batch', 'row'), may hold values from -0.1875 to 0.1875
- embed_in_weight: float32 [128, 512], P('batch', 'row'), may hold values from -0.5 to 0.5
- embed_out_weight: float32 [512, 256], P('batch', 'row'), may hold values from -0.25 to 0.25
- small_params: float32 [1792], P(('batch', 'row')), may hold values from -0.6 to 1.5, as said below
- conv_first: float32 [2, 1152, 128], P(None, 'batch', 'row'), may hold values from -0.0007433941 to 0.0007433941
- down_first: float32 [1152, 256], P('batch', 'row'), may hold values from -0.0007433941 to 0.0007433941
- embed_in_first: float32 [128, 512], P('batch', 'row'), may hold values from -0.0007433941 to 0.0007433941
- embed_out_first: float32 [512, 256], P('batch', 'row'), may hold values from -0.0007433941 to 0.0007433941
- small_first: float32 [1792], P(('batch', 'row')), may hold values from -0.0007433941 to 0.0007433941
- conv_second: float32 [2, 1152, 128], P(None, 'batch', 'row'), may hold values from 6.3433747e-10 to 5.0746998e-09
- down_second: float32 [1152, 256], P('batch', 'row'), may hold values from 6.3433747e-10 to 5.0746998e-09
- embed_in_second: float32 [128, 512], P('batch', 'row'), may hold values from 6.3433747e-10 to 5.0746998e-09
- embed_out_second: float32 [512, 256], P('batch', 'row'), may hold values from 6.3433747e-10 to 5.0746998e-09
- small_second: float32 [1792], P(('batch', 'row')), may hold values from 6.3433747e-10 to 5.0746998e-09
Outputs:
- block_out: bfloat16 [384, 8, 32, 256], P(('batch', 'row'))
- field_grad: bfloat16 [384, 16, 64, 128], P('batch', 'row')
- grad_norm: float32 [], replicated
- conv_weight_new: float32 [2, 1152, 128], P(None, 'batch', 'row')
- down_weight_new: float32 [1152, 256], P('batch', 'row')
- embed_in_new: float32 [128, 512], P('batch', 'row')
- embed_out_new: float32 [512, 256], P('batch', 'row')
- small_new: float32 [1792], P(('batch', 'row'))
- conv_first_new: float32 [2, 1152, 128], P(None, 'batch', 'row')
- down_first_new: float32 [1152, 256], P('batch', 'row')
- embed_in_first_new: float32 [128, 512], P('batch', 'row')
- embed_out_first_new: float32 [512, 256], P('batch', 'row')
- small_first_new: float32 [1792], P(('batch', 'row'))
- conv_second_new: float32 [2, 1152, 128], P(None, 'batch', 'row')
- down_second_new: float32 [1152, 256], P('batch', 'row')
- embed_in_second_new: float32 [128, 512], P('batch', 'row')
- embed_out_second_new: float32 [512, 256], P('batch', 'row')
- small_second_new: float32 [1792], P(('batch', 'row'))
The draws below stay inside these ranges and needn't reach their ends.
Inputs may be any that keep to these rules, and one draw needn't show every extreme that they name: `refine_step`: most samples have index 0. `small_params`: the first 256 entries are the two norms' gains.
All inputs are finite; a program needn't handle non-finite values.
Results may differ from the reference program's by a relative error of at most 0.008.
Values may be sent and summed in bfloat16 or wider, within the bound.
A program may use at most 256 MiB of HBM per device.

```python
import math
import jax
import jax.numpy as jnp
from jax import lax

C = 128
C2 = 256
EMB = 128
HID = 512
GROUPS = 8
REFINE = 4
W = 64
SAMPLES = 384
H = 16
SMALLP = 1792
NPARAM = 788224


def draw_refine_step(key, part):
    first_key, second_key = jax.random.split(key)
    selector = jax.random.randint(first_key, (SAMPLES,), 0, 8)
    levels = jax.random.randint(second_key, (SAMPLES,), 1, REFINE)
    chosen = jnp.where(selector < 5, 0, levels)
    return chosen.at[0].set(REFINE - 1).at[1].set(0).astype(jnp.int32)


def draw_small_params(key, part):
    gain_key, bias_key = jax.random.split(key)
    gain_values = jax.random.uniform(gain_key, (2 * C,), jnp.float32, 0.6, 1.4)
    biases = jnp.clip(0.3 * jax.random.normal(bias_key, (SMALLP - 2 * C,), jnp.float32), -0.6, 0.6)
    return jnp.concatenate([gain_values, biases])


def shard_levels(stream_key, extent, shards, smallest, high):
    level = 1.0
    for dim, parts in shards:
        steps = jax.random.uniform(jax.random.fold_in(jax.random.fold_in(stream_key, 6), dim), (parts,), jnp.float32, smallest / len(shards), high / len(shards))
        level = level * jnp.repeat(jnp.exp(steps), extent[dim] // parts).reshape((-1,) + (1,) * (len(extent) - 1 - dim))
    return level


def normal_values(stream_key, extent, width, reach, shards=(), held_as=jnp.bfloat16):
    values = width * jax.random.normal(stream_key, extent, jnp.float32)
    if shards:
        values = values * shard_levels(stream_key, extent, shards, -0.22, 0.18)
    return jnp.clip(values, -reach, reach).astype(held_as)


def setup_inputs(seed: int = 0) -> dict:
    streams_of = jax.random.split(jax.random.key(seed), 19)
    field_in = normal_values(streams_of[0], (SAMPLES, H, W, C), 1.0, 6.0, ((0, 4), (1, 8)))
    refine_step = draw_refine_step(jax.random.fold_in(streams_of[18], 71), 0)
    cotangent = normal_values(streams_of[2], (SAMPLES, H // 2, W // 2, C2), 1.0, 6.0, ((0, 32),))
    conv_weight = normal_values(streams_of[3], (2, 9 * C, C), (9 * C) ** -0.5, 0.1875, ((1, 4), (2, 8)), jnp.float32)
    down_weight = normal_values(streams_of[4], (9 * C, C2), (9 * C) ** -0.5, 0.1875, ((0, 4), (1, 8)), jnp.float32)
    embed_in_weight = normal_values(streams_of[5], (EMB, HID), EMB ** -0.5, 0.5, ((0, 4), (1, 8)), jnp.float32)
    embed_out_weight = normal_values(streams_of[6], (HID, 2 * C), HID ** -0.5, 0.25, ((0, 4), (1, 8)), jnp.float32)
    small_params = draw_small_params(jax.random.fold_in(streams_of[18], 71), 0)
    conv_first = normal_values(streams_of[8], (2, 9 * C, C), (0.11 / NPARAM ** 0.5), 0.0007433941, ((1, 4), (2, 8)), jnp.float32)
    down_first = normal_values(streams_of[9], (9 * C, C2), (0.11 / NPARAM ** 0.5), 0.0007433941, ((0, 4), (1, 8)), jnp.float32)
    embed_in_first = normal_values(streams_of[10], (EMB, HID), (0.11 / NPARAM ** 0.5), 0.0007433941, ((0, 4), (1, 8)), jnp.float32)
    embed_out_first = normal_values(streams_of[11], (HID, 2 * C), (0.11 / NPARAM ** 0.5), 0.0007433941, ((0, 4), (1, 8)), jnp.float32)
    small_first = normal_values(streams_of[12], (SMALLP,), (0.11 / NPARAM ** 0.5), 0.0007433941, ((0, 32),), jnp.float32)
    conv_second = jnp.clip(jnp.exp(math.log(5.074699771512314e-09) - 2.0794415 * jax.random.uniform(streams_of[13], (2, 9 * C, C), jnp.float32) ** shard_levels(streams_of[13], (2, 9 * C, C), ((1, 4), (2, 8)), -0.2, 0.2)), 6.343374714390393e-10, 5.074699771512314e-09)
    down_second = jnp.clip(jnp.exp(math.log(5.074699771512314e-09) - 2.0794415 * jax.random.uniform(streams_of[14], (9 * C, C2), jnp.float32) ** shard_levels(streams_of[14], (9 * C, C2), ((0, 4), (1, 8)), -0.2, 0.2)), 6.343374714390393e-10, 5.074699771512314e-09)
    embed_in_second = jnp.clip(jnp.exp(math.log(5.074699771512314e-09) - 2.0794415 * jax.random.uniform(streams_of[15], (EMB, HID), jnp.float32) ** shard_levels(streams_of[15], (EMB, HID), ((0, 4), (1, 8)), -0.2, 0.2)), 6.343374714390393e-10, 5.074699771512314e-09)
    embed_out_second = jnp.clip(jnp.exp(math.log(5.074699771512314e-09) - 2.0794415 * jax.random.uniform(streams_of[16], (HID, 2 * C), jnp.float32) ** shard_levels(streams_of[16], (HID, 2 * C), ((0, 4), (1, 8)), -0.2, 0.2)), 6.343374714390393e-10, 5.074699771512314e-09)
    small_second = jnp.clip(jnp.exp(math.log(5.074699771512314e-09) - 2.0794415 * jax.random.uniform(streams_of[17], (SMALLP,), jnp.float32) ** shard_levels(streams_of[17], (SMALLP,), ((0, 32),), -0.2, 0.2)), 6.343374714390393e-10, 5.074699771512314e-09)
    return {"field_in": field_in, "refine_step": refine_step, "cotangent": cotangent, "conv_weight": conv_weight, "down_weight": down_weight, "embed_in_weight": embed_in_weight, "embed_out_weight": embed_out_weight, "small_params": small_params, "conv_first": conv_first, "down_first": down_first, "embed_in_first": embed_in_first, "embed_out_first": embed_out_first, "small_first": small_first, "conv_second": conv_second, "down_second": down_second, "embed_in_second": embed_in_second, "embed_out_second": embed_out_second, "small_second": small_second}


@jax.custom_vjp
def low(v):
    return lax.optimization_barrier(v.astype(jnp.bfloat16)).astype(jnp.float32)

@jax.custom_vjp
def low_back(v):
    return v

def low_keep(v):
    return (low(v), None)

def low_pass(kept, grad):
    return (grad,)

def back_keep(v):
    return (v, None)

def back_low(kept, grad):
    return (low(grad),)
low.defvjp(low_keep, low_pass)
low_back.defvjp(back_keep, back_low)
NORM_EPS = 1e-05
BETA_ONE = 0.9
BETA_TWO = 0.999
ADAM_EPS = 1e-08
DECAY = 0.01
RATE_MATRIX = 0.05
RATE_SMALL = 0.5
CLIP_NORM = 1.0
STEP_COUNT = 10
HIGHEST = lax.Precision.HIGHEST

def embed_steps(refine_step):
    halfway = EMB // 2
    frequency = jnp.exp(-math.log(10000.0) * jnp.arange(halfway).astype(jnp.float32) / halfway)
    angles = (refine_step.astype(jnp.float32) * (1000.0 / REFINE))[:, None] * frequency[None, :]
    return jnp.concatenate([jnp.sin(angles), jnp.cos(angles)], axis=1)

def split_small(small_values):
    boundaries = [0, C, 2 * C, 3 * C, 4 * C, 5 * C, 6 * C, 6 * C + C2, 6 * C + C2 + HID, 8 * C + C2 + HID]
    return [small_values[boundaries[position]:boundaries[position + 1]] for position in range(9)]

def norm_unit(values):
    samples, height, columns, channels = values.shape
    grouped = values.reshape(samples, height, columns, GROUPS, channels // GROUPS)
    entries = height * columns * (channels // GROUPS)
    average = lax.optimization_barrier(jnp.sum(grouped, axis=(1, 2, 4))) / entries
    squares = lax.optimization_barrier(jnp.sum(grouped * grouped, axis=(1, 2, 4))) / entries
    inverse_dev = lax.rsqrt(squares - average * average + NORM_EPS)
    normalized = (grouped - average[:, None, None, :, None]) * inverse_dev[:, None, None, :, None]
    return normalized.reshape(values.shape)

def conv_same(values, weight):
    channels = values.shape[3]
    running = jnp.zeros(values.shape[:3] + (weight.shape[1],), jnp.float32)
    for row_tap in range(3):
        for col_tap in range(3):
            window = jnp.roll(values, (1 - row_tap, 1 - col_tap), axis=(1, 2))
            tap_start = (3 * row_tap + col_tap) * channels
            running = running + jnp.einsum('bhwc,cd->bhwd', window, weight[tap_start:tap_start + channels], precision=HIGHEST)
    return running

def conv_down(values, weight):
    samples, height, columns, channels = values.shape
    running = jnp.zeros((samples, height // 2, columns // 2, weight.shape[1]), jnp.float32)
    for row_tap in range(3):
        for col_tap in range(3):
            window = jnp.roll(values, (1 - row_tap, 1 - col_tap), axis=(1, 2))[:, ::2, ::2]
            tap_start = (3 * row_tap + col_tap) * channels
            running = running + jnp.einsum('bhwc,cd->bhwd', window, weight[tap_start:tap_start + channels], precision=HIGHEST)
    return running

def forward(field_value, embedded, conv_weight, down_weight, embed_in_weight, embed_out_weight, small_params):
    gain_one, gain_two, shift_one, shift_two, bias_one, bias_two, bias_down, bias_hidden, bias_mod = split_small(low(small_params))
    conv_low = low(conv_weight)
    hidden = jax.nn.gelu(jnp.dot(embedded, low(embed_in_weight), precision=HIGHEST) + bias_hidden)
    modulate = jnp.dot(hidden, low(embed_out_weight), precision=HIGHEST) + bias_mod
    scale_plus = 1.0 + modulate[:, :C][:, None, None, :]
    offset = modulate[:, C:][:, None, None, :]
    act_one = low(jax.nn.gelu(norm_unit(field_value) * gain_one + shift_one))
    conv_one = low_back(conv_same(act_one, conv_low[0]) + bias_one)
    middle = (norm_unit(conv_one) * gain_two + shift_two) * scale_plus + offset
    act_two = low(jax.nn.gelu(middle))
    conv_two = low_back(conv_same(act_two, conv_low[1]) + bias_two)
    summed = low(field_value + conv_two)
    return conv_down(summed, low(down_weight)) + bias_down

def adam_update(weight, gradient, first_old, second_old, step_rate, clip_factor):
    scaled = gradient * clip_factor
    first_new = BETA_ONE * first_old + (1.0 - BETA_ONE) * scaled
    second_new = BETA_TWO * second_old + (1.0 - BETA_TWO) * scaled * scaled
    corrected = first_new / (1.0 - BETA_ONE ** STEP_COUNT) / (jnp.sqrt(second_new / (1.0 - BETA_TWO ** STEP_COUNT)) + ADAM_EPS)
    return (weight - step_rate * (corrected + DECAY * weight), first_new, second_new)

def reference(field_in, refine_step, cotangent, conv_weight, down_weight, embed_in_weight, embed_out_weight, small_params, conv_first, down_first, embed_in_first, embed_out_first, small_first, conv_second, down_second, embed_in_second, embed_out_second, small_second):
    block_size = 16
    groups = field_in.shape[0] // block_size
    field_blocks = field_in.astype(jnp.float32).reshape((groups, block_size) + field_in.shape[1:])
    step_blocks = refine_step.reshape(groups, block_size)
    cot_blocks = cotangent.astype(jnp.float32).reshape((groups, block_size) + cotangent.shape[1:])

    def one_block(carry, pieces):
        field_part, step_part, cot_part = pieces
        embedded = embed_steps(step_part)

        def apply(field_value, conv_value, down_value, embed_in_value, embed_out_value, small_value):
            return forward(field_value, embedded, conv_value, down_value, embed_in_value, embed_out_value, small_value)
        output, pullback = jax.vjp(apply, field_part, conv_weight, down_weight, embed_in_weight, embed_out_weight, small_params)
        grads = pullback(cot_part)
        carry = (carry[0] + grads[1], carry[1] + grads[2], carry[2] + grads[3], carry[3] + grads[4], carry[4] + grads[5])
        return (carry, (output.astype(jnp.bfloat16), grads[0].astype(jnp.bfloat16)))
    start_carry = (jnp.zeros(conv_weight.shape, jnp.float32), jnp.zeros(down_weight.shape, jnp.float32), jnp.zeros(embed_in_weight.shape, jnp.float32), jnp.zeros(embed_out_weight.shape, jnp.float32), jnp.zeros(small_params.shape, jnp.float32))
    totals, (outputs, field_grads) = lax.scan(one_block, start_carry, (field_blocks, step_blocks, cot_blocks))
    block_out = outputs.reshape(cotangent.shape)
    field_grad = field_grads.reshape(field_in.shape)
    squares = jnp.sum(totals[0] * totals[0]) + jnp.sum(totals[1] * totals[1]) + jnp.sum(totals[2] * totals[2]) + jnp.sum(totals[3] * totals[3]) + jnp.sum(totals[4] * totals[4])
    grad_norm = jnp.sqrt(squares)
    clip_factor = jnp.minimum(1.0, CLIP_NORM / (grad_norm + 1e-06))
    conv_new = adam_update(conv_weight, totals[0], conv_first, conv_second, RATE_MATRIX, clip_factor)
    down_new = adam_update(down_weight, totals[1], down_first, down_second, RATE_MATRIX, clip_factor)
    embed_in_new = adam_update(embed_in_weight, totals[2], embed_in_first, embed_in_second, RATE_MATRIX, clip_factor)
    embed_out_new = adam_update(embed_out_weight, totals[3], embed_out_first, embed_out_second, RATE_MATRIX, clip_factor)
    small_new = adam_update(small_params, totals[4], small_first, small_second, RATE_SMALL, clip_factor)
    return (block_out, field_grad, grad_norm, conv_new[0], down_new[0], embed_in_new[0], embed_out_new[0], small_new[0], conv_new[1], down_new[1], embed_in_new[1], embed_out_new[1], small_new[1], conv_new[2], down_new[2], embed_in_new[2], embed_out_new[2], small_new[2])
```

```python
import math

import jax
import jax.numpy as jnp
from jax import lax
from jax.sharding import PartitionSpec as P

C = 128
C2 = 256
EMB = 128
HID = 512
GROUPS = 8
REFINE = 4


NORM_EPS = 1e-05
BETA_ONE = 0.9
BETA_TWO = 0.999
ADAM_EPS = 1e-08
DECAY = 0.01
RATE_MATRIX = 0.05
RATE_SMALL = 0.5
CLIP_NORM = 1.0
STEP_COUNT = 10
HIGHEST = lax.Precision.HIGHEST


def embed_steps(refine_step):
    halfway = EMB // 2
    frequency = jnp.exp(-math.log(10000.0) * jnp.arange(halfway).astype(jnp.float32) / halfway)
    angles = (refine_step.astype(jnp.float32) * (1000.0 / REFINE))[:, None] * frequency[None, :]
    return jnp.concatenate([jnp.sin(angles), jnp.cos(angles)], axis=1)


def split_small(small_values):
    boundaries = [
        0,
        C,
        2 * C,
        3 * C,
        4 * C,
        5 * C,
        6 * C,
        6 * C + C2,
        6 * C + C2 + HID,
        8 * C + C2 + HID,
    ]
    return [small_values[boundaries[position] : boundaries[position + 1]] for position in range(9)]


def grouped_view(values):
    samples, height, columns, channels = values.shape
    return values.reshape(samples, height, columns, GROUPS, channels // GROUPS)


def norm_forward(values):
    grouped = grouped_view(values)
    entries = values.shape[1] * values.shape[2] * grouped.shape[4]
    first_sum = jnp.sum(grouped, axis=(1, 2, 4))
    second_sum = jnp.sum(grouped * grouped, axis=(1, 2, 4))
    average = first_sum / entries
    inverse_dev = lax.rsqrt(second_sum / entries - average * average + NORM_EPS)
    normalized = (grouped - average[:, None, None, :, None]) * inverse_dev[:, None, None, :, None]
    return (normalized.reshape(values.shape), inverse_dev)


def norm_backward(grad_unit, normalized, inverse_dev):
    grouped_grad = grouped_view(grad_unit)
    grouped_unit = grouped_view(normalized)
    entries = grad_unit.shape[1] * grad_unit.shape[2] * grouped_grad.shape[4]
    first_sum = jnp.sum(grouped_grad, axis=(1, 2, 4))
    second_sum = jnp.sum(grouped_grad * grouped_unit, axis=(1, 2, 4))
    mean_grad = (first_sum / entries)[:, None, None, :, None]
    mean_cross = (second_sum / entries)[:, None, None, :, None]
    result = (grouped_grad - mean_grad - grouped_unit * mean_cross) * inverse_dev[
        :, None, None, :, None
    ]
    return result.reshape(grad_unit.shape)


def wrapped(values):
    values = jnp.concatenate([values[:, -1:], values, values[:, :1]], axis=1)
    return jnp.concatenate([values[:, :, -1:], values, values[:, :, :1]], axis=2)


def convolve(lhs, rhs, strides, numbers, lhs_dilation=(1, 1), rhs_dilation=(1, 1), padding="VALID"):
    return lax.conv_general_dilated(
        lhs,
        rhs,
        strides,
        padding,
        lhs_dilation=lhs_dilation,
        rhs_dilation=rhs_dilation,
        dimension_numbers=numbers,
        preferred_element_type=jnp.float32,
    )


def kernel_of(weight):
    return weight.reshape(3, 3, weight.shape[0] // 9, weight.shape[1])


def conv_padded(padded, weight):
    return convolve(padded, kernel_of(weight), (1, 1), ("NHWC", "HWIO", "NHWC"))


def conv_adjoint(padded, weight):
    return convolve(padded, kernel_of(weight)[::-1, ::-1], (1, 1), ("NHWC", "HWOI", "NHWC"))


def conv_weight_grad(padded, grad_rounded):
    out = convolve(padded, grad_rounded, (1, 1), ("CHWN", "IHWO", "CHWN"))
    return jnp.transpose(out, (1, 2, 3, 0)).reshape(9 * padded.shape[3], grad_rounded.shape[3])


def down_forward(padded, weight):
    return convolve(padded[:, :-1, :-1], kernel_of(weight), (2, 2), ("NHWC", "HWIO", "NHWC"))


def down_weight_grad(padded, grad_out):
    out = convolve(
        padded[:, :-1, :-1], grad_out, (1, 1), ("CHWN", "IHWO", "CHWN"), rhs_dilation=(2, 2)
    )
    return jnp.transpose(out, (1, 2, 3, 0)).reshape(9 * padded.shape[3], grad_out.shape[3])


def down_adjoint(grad_out, weight):
    spread = convolve(
        grad_out,
        kernel_of(weight)[::-1, ::-1],
        (1, 1),
        ("NHWC", "HWOI", "NHWC"),
        lhs_dilation=(2, 2),
        padding=((2, 2), (2, 2)),
    )
    first_row = spread[:, 0:1]
    rows = spread[:, 1:]
    rows = jnp.concatenate([rows[:, :-1], rows[:, -1:] + first_row], axis=1)
    first_col = rows[:, :, 0:1]
    cols = rows[:, :, 1:]
    return jnp.concatenate([cols[:, :, :-1], cols[:, :, -1:] + first_col], axis=2)


def to_samples(values):
    return lax.all_to_all(values, "row", split_axis=0, concat_axis=1, tiled=True)


def to_rows(values):
    return lax.all_to_all(values, "row", split_axis=1, concat_axis=0, tiled=True)


def gelu_grad(values, upstream):
    return jax.vjp(jax.nn.gelu, values)[1](upstream)[0]


def pack_shards(conv, down, embed_in, embed_out, small):
    return jnp.concatenate(
        [
            conv.reshape(-1),
            down.reshape(-1),
            embed_in.reshape(-1),
            embed_out.reshape(-1),
            small.reshape(-1),
        ]
    )


def unpack_rows(flat, shards):
    pieces = []
    position = 0
    for shard in shards:
        pieces.append(flat[..., position : position + shard.size])
        position += shard.size
    return pieces


def assemble(piece, shape, first_dim):
    batch_count, row_count = (lax.axis_size("batch"), lax.axis_size("row"))
    block = piece.reshape((batch_count, row_count) + shape)
    lead = tuple(range(2, 2 + first_dim))
    order = lead + (0, 2 + first_dim, 1, 3 + first_dim)
    block = jnp.transpose(block, order)
    return block.reshape(
        shape[:first_dim] + (batch_count * shape[first_dim], row_count * shape[first_dim + 1])
    )


def split_to_shards(complete, shape, first_dim):
    batch_count, row_count = (lax.axis_size("batch"), lax.axis_size("row"))
    block = complete.reshape(
        shape[:first_dim] + (batch_count, shape[first_dim], row_count, shape[first_dim + 1])
    )
    order = (first_dim, first_dim + 2) + tuple(range(first_dim)) + (first_dim + 1, first_dim + 3)
    return jnp.transpose(block, order).reshape(batch_count * row_count, -1)


def adam_update(weight, gradient, first_old, second_old, step_rate, clip_factor):
    scaled = gradient * clip_factor
    first_new = BETA_ONE * first_old + (1.0 - BETA_ONE) * scaled
    second_new = BETA_TWO * second_old + (1.0 - BETA_TWO) * scaled * scaled
    corrected = (
        first_new
        / (1.0 - BETA_ONE**STEP_COUNT)
        / (jnp.sqrt(second_new / (1.0 - BETA_TWO**STEP_COUNT)) + ADAM_EPS)
    )
    return (weight - step_rate * (corrected + DECAY * weight), first_new, second_new)


def body(
    field_in,
    refine_step,
    cotangent,
    conv_weight,
    down_weight,
    embed_in_weight,
    embed_out_weight,
    small_params,
    conv_first,
    down_first,
    embed_in_first,
    embed_out_first,
    small_first,
    conv_second,
    down_second,
    embed_in_second,
    embed_out_second,
    small_second,
):
    shards = (conv_weight, down_weight, embed_in_weight, embed_out_weight, small_params)
    start_field = to_samples(field_in).astype(jnp.float32)
    packed = pack_shards(*[shard.astype(jnp.bfloat16) for shard in shards])
    everything = lax.all_gather(packed, ("batch", "row"), axis=0)
    pieces = unpack_rows(everything, shards)
    conv_low = assemble(pieces[0], conv_weight.shape, 1)
    down_low = assemble(pieces[1], down_weight.shape, 0)
    embed_in_low = assemble(pieces[2], embed_in_weight.shape, 0)
    embed_out_low = assemble(pieces[3], embed_out_weight.shape, 0)
    small_low = pieces[4].reshape(-1)
    (
        gain_one,
        gain_two,
        shift_one,
        shift_two,
        bias_one,
        bias_two,
        bias_down,
        bias_hidden,
        bias_mod,
    ) = split_small(small_low.astype(jnp.float32))
    embed_in_values = embed_in_low.astype(jnp.float32)
    embed_out_values = embed_out_low.astype(jnp.float32)
    owned = refine_step.shape[0] // lax.axis_size("row")
    own_steps = lax.dynamic_slice_in_dim(refine_step, lax.axis_index("row") * owned, owned, 0)
    embedded = embed_steps(own_steps)
    hidden_pre = jnp.dot(embedded, embed_in_values, precision=HIGHEST) + bias_hidden
    hidden = jax.nn.gelu(hidden_pre)
    modulate = jnp.dot(hidden, embed_out_values, precision=HIGHEST) + bias_mod
    scale_plus = 1.0 + modulate[:, :C][:, None, None, :]
    offset = modulate[:, C:][:, None, None, :]
    unit_one, inverse_one = norm_forward(start_field)
    pre_one = unit_one * gain_one + shift_one
    act_one = jax.nn.gelu(pre_one).astype(jnp.bfloat16)
    padded_one = wrapped(act_one)
    conv_one = conv_padded(padded_one, conv_low[0]) + bias_one
    unit_two, inverse_two = norm_forward(conv_one)
    normed_two = unit_two * gain_two + shift_two
    middle = normed_two * scale_plus + offset
    act_two = jax.nn.gelu(middle).astype(jnp.bfloat16)
    padded_two = wrapped(act_two)
    conv_two = conv_padded(padded_two, conv_low[1]) + bias_two
    summed = (start_field + conv_two).astype(jnp.bfloat16)
    leading = wrapped(summed)
    block_out = (down_forward(leading, down_low) + bias_down).astype(jnp.bfloat16)
    grad_down = down_weight_grad(leading, cotangent)
    grad_summed = down_adjoint(cotangent, down_low)
    grad_conv_two = grad_summed.astype(jnp.bfloat16)
    grad_conv_w2 = conv_weight_grad(padded_two, grad_conv_two)
    grad_act_two = conv_adjoint(wrapped(grad_conv_two), conv_low[1])
    grad_middle = gelu_grad(middle, grad_act_two)
    grad_scale = jnp.sum(grad_middle * normed_two, axis=(1, 2))
    grad_offset = jnp.sum(grad_middle, axis=(1, 2))
    grad_normed = grad_middle * scale_plus
    grad_gain_two = jnp.sum(grad_normed * unit_two, axis=(0, 1, 2))
    grad_shift_two = jnp.sum(grad_normed, axis=(0, 1, 2))
    grad_conv_one = norm_backward(grad_normed * gain_two, unit_two, inverse_two).astype(
        jnp.bfloat16
    )
    grad_conv_w1 = conv_weight_grad(padded_one, grad_conv_one)
    grad_act_one = conv_adjoint(wrapped(grad_conv_one), conv_low[0])
    grad_pre_one = gelu_grad(pre_one, grad_act_one)
    grad_gain_one = jnp.sum(grad_pre_one * unit_one, axis=(0, 1, 2))
    grad_shift_one = jnp.sum(grad_pre_one, axis=(0, 1, 2))
    grad_start = (
        grad_summed + norm_backward(grad_pre_one * gain_one, unit_one, inverse_one)
    ).astype(jnp.bfloat16)
    grad_start = to_rows(grad_start)
    grad_mod = jnp.concatenate([grad_scale, grad_offset], axis=1)
    grad_embed_out = jnp.dot(hidden.T, grad_mod, precision=HIGHEST)
    grad_hidden_pre = gelu_grad(
        hidden_pre, jnp.dot(grad_mod, embed_out_values.T, precision=HIGHEST)
    )
    grad_embed_in = jnp.dot(embedded.T, grad_hidden_pre, precision=HIGHEST)
    grad_small = jnp.concatenate(
        [
            grad_gain_one,
            grad_gain_two,
            grad_shift_one,
            grad_shift_two,
            jnp.sum(grad_conv_one.astype(jnp.float32), axis=(0, 1, 2)),
            jnp.sum(grad_conv_two.astype(jnp.float32), axis=(0, 1, 2)),
            jnp.sum(cotangent.astype(jnp.float32), axis=(0, 1, 2)),
            jnp.sum(grad_hidden_pre, axis=0),
            jnp.sum(grad_mod, axis=0),
        ]
    )
    grad_conv = jnp.stack([grad_conv_w1, grad_conv_w2])
    laid_out = jnp.concatenate(
        [
            split_to_shards(grad_conv, conv_weight.shape, 1),
            split_to_shards(grad_down, down_weight.shape, 0),
            split_to_shards(grad_embed_in, embed_in_weight.shape, 0),
            split_to_shards(grad_embed_out, embed_out_weight.shape, 0),
            grad_small.reshape(lax.axis_size("batch") * lax.axis_size("row"), -1),
        ],
        axis=1,
    )
    owned_flat = lax.psum_scatter(
        laid_out, ("batch", "row"), scatter_dimension=0, tiled=True
    ).reshape(-1)
    owned_shards = [
        piece.reshape(shard.shape) for piece, shard in zip(unpack_rows(owned_flat, shards), shards)
    ]
    grad_norm = jnp.sqrt(lax.psum(jnp.sum(owned_flat * owned_flat), ("batch", "row")))
    clip_factor = jnp.minimum(1.0, CLIP_NORM / (grad_norm + 1e-06))
    conv_new = adam_update(
        conv_weight, owned_shards[0], conv_first, conv_second, RATE_MATRIX, clip_factor
    )
    down_new = adam_update(
        down_weight, owned_shards[1], down_first, down_second, RATE_MATRIX, clip_factor
    )
    embed_in_new = adam_update(
        embed_in_weight, owned_shards[2], embed_in_first, embed_in_second, RATE_MATRIX, clip_factor
    )
    embed_out_new = adam_update(
        embed_out_weight,
        owned_shards[3],
        embed_out_first,
        embed_out_second,
        RATE_MATRIX,
        clip_factor,
    )
    small_new = adam_update(
        small_params, owned_shards[4], small_first, small_second, RATE_SMALL, clip_factor
    )
    return (
        block_out,
        grad_start,
        grad_norm,
        conv_new[0],
        down_new[0],
        embed_in_new[0],
        embed_out_new[0],
        small_new[0],
        conv_new[1],
        down_new[1],
        embed_in_new[1],
        embed_out_new[1],
        small_new[1],
        conv_new[2],
        down_new[2],
        embed_in_new[2],
        embed_out_new[2],
        small_new[2],
    )


def solution(mesh):
    placed = (
        P("batch", "row", None, None),
        P("batch"),
        P(("batch", "row"), None, None, None),
        P(None, "batch", "row"),
        P("batch", "row"),
        P("batch", "row"),
        P("batch", "row"),
        P(("batch", "row")),
        P(None, "batch", "row"),
        P("batch", "row"),
        P("batch", "row"),
        P("batch", "row"),
        P(("batch", "row")),
        P(None, "batch", "row"),
        P("batch", "row"),
        P("batch", "row"),
        P("batch", "row"),
        P(("batch", "row")),
    )
    return jax.shard_map(
        body,
        mesh=mesh,
        in_specs=placed,
        out_specs=(
            P(("batch", "row"), None, None, None),
            P("batch", "row", None, None),
            P(),
            P(None, "batch", "row"),
            P("batch", "row"),
            P("batch", "row"),
            P("batch", "row"),
            P(("batch", "row")),
            P(None, "batch", "row"),
            P("batch", "row"),
            P("batch", "row"),
            P("batch", "row"),
            P(("batch", "row")),
            P(None, "batch", "row"),
            P("batch", "row"),
            P("batch", "row"),
            P("batch", "row"),
            P(("batch", "row")),
        ),
        check_vma=False,
    )
```

```python
import functools
import math

import jax
import jax.numpy as jnp
import numpy as np
from jax import lax
from jax.experimental import pallas as pl
from jax.experimental.pallas import tpu as pltpu
from jax.sharding import PartitionSpec as P

C = 128
C2 = 256
EMB = 128
HID = 512
GROUPS = 8
REFINE = 4


NORM_EPS = 1e-05
BETA_ONE = 0.9
BETA_TWO = 0.999
ADAM_EPS = 1e-08
DECAY = 0.01
RATE_MATRIX = 0.05
RATE_SMALL = 0.5
CLIP_NORM = 1.0
STEP_COUNT = 10
HIGHEST = lax.Precision.HIGHEST


def embed_steps(refine_step):
    halfway = EMB // 2
    frequency = jnp.exp(-math.log(10000.0) * jnp.arange(halfway).astype(jnp.float32) / halfway)
    angles = (refine_step.astype(jnp.float32) * (1000.0 / REFINE))[:, None] * frequency[None, :]
    return jnp.concatenate([jnp.sin(angles), jnp.cos(angles)], axis=1)


def split_small(small_values):
    boundaries = [
        0,
        C,
        2 * C,
        3 * C,
        4 * C,
        5 * C,
        6 * C,
        6 * C + C2,
        6 * C + C2 + HID,
        8 * C + C2 + HID,
    ]
    return [small_values[boundaries[position] : boundaries[position + 1]] for position in range(9)]


def to_samples(values):
    return lax.all_to_all(values, "row", split_axis=0, concat_axis=1, tiled=True)


def to_rows(values):
    return lax.all_to_all(values, "row", split_axis=1, concat_axis=0, tiled=True)


def gelu_grad(values, upstream):
    return jax.vjp(jax.nn.gelu, values)[1](upstream)[0]


FIELD_COLS = 64
HALF_COLS = 32
ROOT = math.sqrt(2.0 / math.pi)
CUBIC = ROOT * 0.044715


def chunk_of(total, most):
    size = min(total, most)
    while total % size:
        size -= 1
    return size


def over(total, most, body, init):
    size = chunk_of(total, most)

    def several(step, carry):
        for inner in range(size):
            carry = body(step * size + inner, carry)
        return carry

    if size == total:
        return several(0, init)
    return lax.fori_loop(0, total // size, several, init)


def folded(values):
    return jnp.sum(values.reshape(values.shape[0] // 8, 8, values.shape[1]), axis=0)


def twice(row):
    return jnp.concatenate([row, row], axis=1)


def channel_sum(partial):
    both = partial[:, :C] + partial[:, C:]
    return jnp.sum(both, axis=0, keepdims=True)


def group_means(first, second, same_group, entries):
    stacked = jnp.concatenate([first, second, jnp.zeros((6, C), jnp.float32)], axis=0)
    totals = jnp.dot(stacked, same_group, precision=HIGHEST, preferred_element_type=jnp.float32)
    return totals[0:1] / entries, totals[1:2] / entries


def gelu_pair(values):
    square = values * values
    bend = jnp.tanh(values * (ROOT + CUBIC * square))
    half = 0.5 * values
    slope = (0.5 + 0.5 * bend) + half * (1.0 - bend * bend) * (ROOT + (3.0 * CUBIC) * square)
    return half + half * bend, slope


def put_shifted(ref, pair, values):
    for tap, shift in ((0, 1), (1, 0), (2, FIELD_COLS - 1)):
        moved = pltpu.roll(values, shift, 0) if shift else values
        ref[tap, pair + 1] = moved.astype(jnp.bfloat16)


def close_ring(ref, pairs):
    ref[:, 0, :, C:] = ref[:, pairs, :, C:]
    ref[:, pairs + 1, :, :C] = ref[:, 1, :, :C]


def windows(ref, start, count):
    rows = count * FIELD_COLS
    pieces = []
    for tap in range(3):
        pieces.append(ref[tap, pl.ds(start + 1, count)].reshape(rows, 2 * C))
        pieces.append(ref[tap, pl.ds(start, count), :, C:].reshape(rows, C))
        pieces.append(ref[tap, pl.ds(start + 2, count), :, :C].reshape(rows, C))
    return jnp.concatenate(pieces, axis=1)


def add_conv_grad(out_ref, act_ref, grad_ref, pairs):
    size = chunk_of(pairs, 8)
    rows = size * FIELD_COLS

    def body(step, carry):
        start = step * size
        grad = grad_ref[1, pl.ds(start + 1, size)].reshape(rows, 2 * C)
        product = jnp.dot(
            grad.T, windows(act_ref, start, size), preferred_element_type=jnp.float32
        )
        for tap in range(3):
            base = tap * 4 * C
            own_low = product[:C, base : base + C] + product[C:, base + C : base + 2 * C]
            up = product[C:, base : base + C] + product[:C, base + 2 * C : base + 3 * C]
            down = product[:C, base + C : base + 2 * C] + product[C:, base + 3 * C : base + 4 * C]
            for row_tap, value in ((0, up), (1, own_low), (2, down)):
                lanes = pl.ds((3 * row_tap + tap) * C, C)
                out_ref[:, lanes] = out_ref[:, lanes] + value
        return carry

    over_steps(pairs // size, body)


def over_steps(steps, body):
    if steps == 1:
        body(0, 0)
    else:
        lax.fori_loop(0, steps, body, 0)


def sample_kernel(
    pairs,
    x_ref,
    cot_ref,
    mod_ref,
    fwd_one,
    back_one,
    fwd_two,
    back_two,
    down_fwd,
    down_even,
    down_odd,
    vec_ref,
    group_ref,
    out_ref,
    grad_ref,
    conv_grad_one,
    conv_grad_two,
    down_grad,
    sums_ref,
    act_one,
    act_two,
    grad_one,
    grad_two,
    slope_one,
    slope_two,
    unit_two,
    grad_mid,
    sum_even,
    sum_odd,
    grad_even,
    grad_odd,
    down_win,
    cot_win,
):
    entries = 2.0 * pairs * FIELD_COLS * (C // GROUPS)
    size = chunk_of(pairs, 8)
    rows = size * FIELD_COLS
    same_group = group_ref[...]
    gain_one, gain_two = vec_ref[0:1, :C], vec_ref[1:2, :C]
    shift_one, shift_two = vec_ref[2:3, :C], vec_ref[3:4, :C]
    bias_one, bias_two = twice(vec_ref[4:5, :C]), twice(vec_ref[5:6, :C])
    bias_down = vec_ref[6:7, :]
    scale_plus, offset = mod_ref[0, 0:1, :], mod_ref[0, 1:2, :]
    nothing = jnp.zeros((8, 2 * C), jnp.float32)

    @pl.when(pl.program_id(0) == 0)
    def _():
        conv_grad_one[...] = jnp.zeros_like(conv_grad_one)
        conv_grad_two[...] = jnp.zeros_like(conv_grad_two)
        down_grad[...] = jnp.zeros_like(down_grad)

    def field(pair):
        return jnp.concatenate(
            [x_ref[0, pair, 0].astype(jnp.float32), x_ref[0, pair, 1].astype(jnp.float32)], axis=1
        )

    def first_stats(pair, carry):
        value = field(pair)
        return carry[0] + folded(value), carry[1] + folded(value * value)

    total, squares = over(pairs, 8, first_stats, (nothing, nothing))
    mean_one, square_one = group_means(channel_sum(total), channel_sum(squares), same_group, entries)
    inverse_one = lax.rsqrt(square_one - mean_one * mean_one + NORM_EPS)
    center_one = twice(-mean_one * inverse_one)
    inverse_one = twice(inverse_one)
    gain_wide, shift_wide = twice(gain_one), twice(shift_one)

    def first_act(pair, carry):
        unit = field(pair) * inverse_one + center_one
        value, slope = gelu_pair(unit * gain_wide + shift_wide)
        put_shifted(act_one, pair, value)
        slope_one[pair] = slope
        return carry

    over(pairs, 8, first_act, 0)
    close_ring(act_one, pairs)

    def conv_one_chunk(step, carry):
        start = step * size
        value = jnp.dot(
            windows(act_one, start, size), fwd_one[...], preferred_element_type=jnp.float32
        ) + bias_one
        unit_two[pl.ds(start, size)] = value.reshape(size, FIELD_COLS, 2 * C)
        return carry[0] + folded(value), carry[1] + folded(value * value)

    total, squares = lax.fori_loop(0, pairs // size, conv_one_chunk, (nothing, nothing))
    mean_two, square_two = group_means(channel_sum(total), channel_sum(squares), same_group, entries)
    inverse_two = lax.rsqrt(square_two - mean_two * mean_two + NORM_EPS)
    center_two = twice(-mean_two * inverse_two)
    mid_gain = twice(gain_two * scale_plus)
    mid_shift = twice(shift_two * scale_plus + offset)
    inverse_two_wide = twice(inverse_two)

    def second_act(pair, carry):
        unit = unit_two[pair] * inverse_two_wide + center_two
        value, slope = gelu_pair(unit * mid_gain + mid_shift)
        put_shifted(act_two, pair, value)
        slope_two[pair] = slope
        unit_two[pair] = unit
        return carry

    over(pairs, 8, second_act, 0)
    close_ring(act_two, pairs)

    def conv_two_chunk(step, carry):
        start = step * size
        value = jnp.dot(
            windows(act_two, start, size), fwd_two[...], preferred_element_type=jnp.float32
        ) + bias_two
        value = value.reshape(size, FIELD_COLS, 2 * C)
        for half, ref in ((0, sum_even), (1, sum_odd)):
            base = x_ref[0, pl.ds(start, size), half].astype(jnp.float32)
            ref[pl.ds(start, size)] = base + value[:, :, half * C : half * C + C]
        return carry

    over_steps(pairs // size, conv_two_chunk)

    def split_columns(pair, carry):
        even = []
        odd = []
        for ref in (sum_even, sum_odd):
            even.append(ref[pair, pl.ds(0, HALF_COLS, stride=2), :])
            odd.append(ref[pair, pl.ds(1, HALF_COLS, stride=2), :])
        even = jnp.concatenate(even, axis=1)
        odd = jnp.concatenate(odd, axis=1)
        down_win[0, pair + 1] = pltpu.roll(odd, 1, 0).astype(jnp.bfloat16)
        down_win[1, pair + 1] = even.astype(jnp.bfloat16)
        down_win[2, pair + 1] = odd.astype(jnp.bfloat16)
        cot = cot_ref[0, pair]
        wide = cot.astype(jnp.float32)
        cot_win[0, pair] = cot
        cot_win[1, pair] = pltpu.roll(wide, HALF_COLS - 1, 0).astype(jnp.bfloat16)
        return carry + folded(wide)

    cot_total = over(pairs, 8, split_columns, nothing)
    down_win[:, 0, :, C:] = down_win[:, pairs, :, C:]
    cot_win[:, pairs] = cot_win[:, 0]
    small = size * HALF_COLS

    def down_windows(start):
        pieces = [down_win[tap, pl.ds(start + 1, size)].reshape(small, 2 * C) for tap in range(3)]
        pieces += [
            down_win[tap, pl.ds(start, size), :, C:].reshape(small, C) for tap in range(3)
        ]
        return jnp.concatenate(pieces, axis=1)

    def down_chunk(step, carry):
        start = step * size
        lhs = down_windows(start)
        value = jnp.dot(lhs, down_fwd[...], preferred_element_type=jnp.float32) + bias_down
        out_ref[0, pl.ds(start, size)] = value.reshape(size, HALF_COLS, 2 * C).astype(jnp.bfloat16)
        here = cot_win[0, pl.ds(start, size)].reshape(small, 2 * C)
        product = jnp.dot(here.T, lhs, preferred_element_type=jnp.float32)
        for position in range(9):
            row_tap, tap = DOWN_ORDER[position]
            lanes = pl.ds((3 * row_tap + tap) * C, C)
            down_grad[:, lanes] = down_grad[:, lanes] + product[:, position * C : position * C + C]
        pieces = [
            cot_win[shift, pl.ds(start + below, size)].reshape(small, 2 * C)
            for below in range(2)
            for shift in range(2)
        ]
        even = jnp.dot(
            jnp.concatenate([pieces[0], pieces[2]], axis=1),
            down_even[...],
            preferred_element_type=jnp.float32,
        ).reshape(size, HALF_COLS, 2 * C)
        odd = jnp.dot(
            jnp.concatenate(pieces, axis=1), down_odd[...], preferred_element_type=jnp.float32
        ).reshape(size, HALF_COLS, 2 * C)
        for half, ref in ((0, grad_even), (1, grad_odd)):
            lanes = slice(half * C, half * C + C)
            for inner in range(size):
                ref[start + inner, pl.ds(0, HALF_COLS, stride=2), :] = even[inner, :, lanes]
                ref[start + inner, pl.ds(1, HALF_COLS, stride=2), :] = odd[inner, :, lanes]
        return carry

    over_steps(pairs // size, down_chunk)

    def second_grad(pair, carry):
        value = jnp.concatenate([grad_even[pair], grad_odd[pair]], axis=1)
        put_shifted(grad_two, pair, value)
        return carry + folded(value.astype(jnp.bfloat16).astype(jnp.float32))

    bias_two_total = over(pairs, 8, second_grad, nothing)
    close_ring(grad_two, pairs)
    add_conv_grad(conv_grad_two, act_two, grad_two, pairs)

    def back_two_chunk(step, carry):
        start = step * size
        value = jnp.dot(
            windows(grad_two, start, size), back_two[...], preferred_element_type=jnp.float32
        )
        value = value * slope_two[pl.ds(start, size)].reshape(rows, 2 * C)
        grad_mid[pl.ds(start, size)] = value.reshape(size, FIELD_COLS, 2 * C)
        unit = unit_two[pl.ds(start, size)].reshape(rows, 2 * C)
        return carry[0] + folded(value), carry[1] + folded(value * unit)

    total, cross = lax.fori_loop(0, pairs // size, back_two_chunk, (nothing, nothing))
    mid_total, mid_cross = channel_sum(total), channel_sum(cross)
    factor = scale_plus * gain_two
    mean_grad, mean_cross = group_means(
        mid_total * factor, mid_cross * factor, same_group, entries
    )
    from_mid = twice(inverse_two * factor)
    from_unit = twice(inverse_two * mean_cross)
    from_mean = twice(inverse_two * mean_grad)

    def first_grad(pair, carry):
        value = grad_mid[pair] * from_mid - from_mean - unit_two[pair] * from_unit
        put_shifted(grad_one, pair, value)
        return carry + folded(value.astype(jnp.bfloat16).astype(jnp.float32))

    bias_one_total = over(pairs, 8, first_grad, nothing)
    close_ring(grad_one, pairs)
    add_conv_grad(conv_grad_one, act_one, grad_one, pairs)

    def back_one_chunk(step, carry):
        start = step * size
        value = jnp.dot(
            windows(grad_one, start, size), back_one[...], preferred_element_type=jnp.float32
        )
        value = value * slope_one[pl.ds(start, size)].reshape(rows, 2 * C)
        grad_mid[pl.ds(start, size)] = value.reshape(size, FIELD_COLS, 2 * C)
        base = jnp.concatenate(
            [
                x_ref[0, pl.ds(start, size), half].astype(jnp.float32).reshape(rows, C)
                for half in range(2)
            ],
            axis=1,
        )
        unit = base * inverse_one + center_one
        return carry[0] + folded(value), carry[1] + folded(value * unit)

    total, cross = lax.fori_loop(0, pairs // size, back_one_chunk, (nothing, nothing))
    pre_total, pre_cross = channel_sum(total), channel_sum(cross)
    mean_grad, mean_cross = group_means(
        pre_total * gain_one, pre_cross * gain_one, same_group, entries
    )
    from_pre = inverse_one * gain_wide
    from_unit_one = inverse_one * twice(mean_cross)
    from_mean_one = inverse_one * twice(mean_grad)

    def last(pair, carry):
        unit = field(pair) * inverse_one + center_one
        summed = jnp.concatenate([grad_even[pair], grad_odd[pair]], axis=1)
        value = (summed + (grad_mid[pair] * from_pre - from_mean_one - unit * from_unit_one)).astype(
            jnp.bfloat16
        )
        grad_ref[0, pair, 0] = value[:, :C]
        grad_ref[0, pair, 1] = value[:, C:]
        return carry

    over(pairs, 8, last, 0)
    cot_sums = jnp.sum(cot_total, axis=0, keepdims=True)
    sums_ref[0] = jnp.concatenate(
        [
            mid_cross,
            mid_total,
            pre_cross,
            pre_total,
            channel_sum(bias_one_total),
            channel_sum(bias_two_total),
            cot_sums[:, :C],
            cot_sums[:, C:],
        ],
        axis=0,
    )


DOWN_ORDER = ((1, 0), (2, 0), (1, 1), (2, 1), (1, 2), (2, 2), (0, 0), (0, 1), (0, 2))


def forward_blocks(weight):
    zero = jnp.zeros((C, C), weight.dtype)
    taps = weight.reshape(3, 3, C, C)
    rows = []
    for tap in range(3):
        rows.append(jnp.concatenate([taps[1, tap], taps[0, tap]], axis=1))
        rows.append(jnp.concatenate([taps[2, tap], taps[1, tap]], axis=1))
        rows.append(jnp.concatenate([taps[0, tap], zero], axis=1))
        rows.append(jnp.concatenate([zero, taps[2, tap]], axis=1))
    return jnp.concatenate(rows, axis=0)


def adjoint_weight(weight):
    taps = weight.reshape(3, 3, C, C)[::-1, ::-1]
    return jnp.transpose(taps, (0, 1, 3, 2)).reshape(9 * C, C)


def down_blocks(weight):
    taps = weight.reshape(3, 3, C, C2)
    forward = jnp.concatenate([taps[a, b] for a, b in DOWN_ORDER], axis=0)
    back = jnp.transpose(taps, (0, 1, 3, 2))
    zero = jnp.zeros((C2, C), weight.dtype)
    even = [(back[1, 1], back[2, 1]), (zero, back[0, 1])]
    odd = [
        (back[1, 2], back[2, 2]),
        (back[1, 0], back[2, 0]),
        (zero, back[0, 2]),
        (zero, back[0, 0]),
    ]
    even = jnp.concatenate([jnp.concatenate(pair, axis=1) for pair in even], axis=0)
    odd = jnp.concatenate([jnp.concatenate(pair, axis=1) for pair in odd], axis=0)
    return forward, even, odd


def run_samples(field, cotangent, modulation, conv_low, down_low, vectors):
    samples, height = field.shape[:2]
    pairs = height // 2
    halves = field.reshape(samples, pairs, 2, FIELD_COLS, C)
    down_fwd, down_even, down_odd = down_blocks(down_low)
    same_group = jnp.asarray(
        np.kron(np.eye(GROUPS), np.ones((C // GROUPS, C // GROUPS))), jnp.float32
    )

    def whole(array):
        return pl.BlockSpec(array.shape, lambda i: (0,) * array.ndim, pipeline_mode=pl.Buffered(1))

    def per_sample(array):
        rank = len(array.shape)
        return pl.BlockSpec((1,) + array.shape[1:], lambda i: (i,) + (0,) * (rank - 1))

    constants = (
        forward_blocks(conv_low[0]),
        forward_blocks(adjoint_weight(conv_low[0])),
        forward_blocks(conv_low[1]),
        forward_blocks(adjoint_weight(conv_low[1])),
        down_fwd,
        down_even,
        down_odd,
        vectors,
        same_group,
    )
    outs = (
        jax.ShapeDtypeStruct((samples, pairs, HALF_COLS, C2), jnp.bfloat16),
        jax.ShapeDtypeStruct(halves.shape, jnp.bfloat16),
        jax.ShapeDtypeStruct((C, 9 * C), jnp.float32),
        jax.ShapeDtypeStruct((C, 9 * C), jnp.float32),
        jax.ShapeDtypeStruct((C2, 9 * C), jnp.float32),
        jax.ShapeDtypeStruct((samples, 8, C), jnp.float32),
    )
    ring = pltpu.VMEM((3, pairs + 2, FIELD_COLS, 2 * C), jnp.bfloat16)
    wide = pltpu.VMEM((pairs, FIELD_COLS, 2 * C), jnp.float32)
    half = pltpu.VMEM((pairs, FIELD_COLS, C), jnp.float32)
    result = pl.pallas_call(
        functools.partial(sample_kernel, pairs),
        grid=(samples,),
        in_specs=[per_sample(halves), per_sample(cotangent), per_sample(modulation)]
        + [whole(array) for array in constants],
        out_specs=[per_sample(outs[0]), per_sample(outs[1])]
        + [pl.BlockSpec(out.shape, lambda i: (0, 0)) for out in outs[2:5]]
        + [per_sample(outs[5])],
        out_shape=outs,
        scratch_shapes=[ring] * 4
        + [wide] * 4
        + [half] * 4
        + [
            pltpu.VMEM((3, pairs + 1, HALF_COLS, 2 * C), jnp.bfloat16),
            pltpu.VMEM((2, pairs + 1, HALF_COLS, C2), jnp.bfloat16),
        ],
        compiler_params=pltpu.CompilerParams(
            dimension_semantics=("arbitrary",), vmem_limit_bytes=60 << 20
        ),
        name="samples",
    )(halves, cotangent, modulation, *constants)
    return (result[0], result[1].reshape(field.shape)) + tuple(result[2:])


def pack_shards(conv, down, embed_in, embed_out, small):
    return jnp.concatenate(
        [
            conv.reshape(-1),
            down.reshape(-1),
            embed_in.reshape(-1),
            embed_out.reshape(-1),
            small.reshape(-1),
        ]
    )


def unpack_rows(flat, shards):
    pieces = []
    position = 0
    for shard in shards:
        pieces.append(flat[..., position : position + shard.size])
        position += shard.size
    return pieces


def assemble(piece, shape, first_dim):
    batch_count, row_count = (lax.axis_size("batch"), lax.axis_size("row"))
    block = piece.reshape((batch_count, row_count) + shape)
    lead = tuple(range(2, 2 + first_dim))
    order = lead + (0, 2 + first_dim, 1, 3 + first_dim)
    block = jnp.transpose(block, order)
    return block.reshape(
        shape[:first_dim] + (batch_count * shape[first_dim], row_count * shape[first_dim + 1])
    )


def split_to_shards(complete, shape, first_dim):
    batch_count, row_count = (lax.axis_size("batch"), lax.axis_size("row"))
    block = complete.reshape(
        shape[:first_dim] + (batch_count, shape[first_dim], row_count, shape[first_dim + 1])
    )
    order = (first_dim, first_dim + 2) + tuple(range(first_dim)) + (first_dim + 1, first_dim + 3)
    return jnp.transpose(block, order).reshape(batch_count * row_count, -1)


def adam_update(weight, gradient, first_old, second_old, step_rate, clip_factor):
    scaled = gradient * clip_factor
    first_new = BETA_ONE * first_old + (1.0 - BETA_ONE) * scaled
    second_new = BETA_TWO * second_old + (1.0 - BETA_TWO) * scaled * scaled
    corrected = (
        first_new
        / (1.0 - BETA_ONE**STEP_COUNT)
        / (jnp.sqrt(second_new / (1.0 - BETA_TWO**STEP_COUNT)) + ADAM_EPS)
    )
    return (weight - step_rate * (corrected + DECAY * weight), first_new, second_new)


def body(
    field_in,
    refine_step,
    cotangent,
    conv_weight,
    down_weight,
    embed_in_weight,
    embed_out_weight,
    small_params,
    conv_first,
    down_first,
    embed_in_first,
    embed_out_first,
    small_first,
    conv_second,
    down_second,
    embed_in_second,
    embed_out_second,
    small_second,
):
    shards = (conv_weight, down_weight, embed_in_weight, embed_out_weight, small_params)
    field = to_samples(field_in)
    packed = pack_shards(*[shard.astype(jnp.bfloat16) for shard in shards])
    everything = lax.all_gather(packed, ("batch", "row"), axis=0)
    pieces = unpack_rows(everything, shards)
    conv_low = assemble(pieces[0], conv_weight.shape, 1)
    down_low = assemble(pieces[1], down_weight.shape, 0)
    embed_in_low = assemble(pieces[2], embed_in_weight.shape, 0)
    embed_out_low = assemble(pieces[3], embed_out_weight.shape, 0)
    small_low = pieces[4].reshape(-1)
    (
        gain_one,
        gain_two,
        shift_one,
        shift_two,
        bias_one,
        bias_two,
        bias_down,
        bias_hidden,
        bias_mod,
    ) = split_small(small_low.astype(jnp.float32))
    embed_in_values = embed_in_low.astype(jnp.float32)
    embed_out_values = embed_out_low.astype(jnp.float32)
    owned = refine_step.shape[0] // lax.axis_size("row")
    own_steps = lax.dynamic_slice_in_dim(refine_step, lax.axis_index("row") * owned, owned, 0)
    embedded = embed_steps(own_steps)
    hidden_pre = jnp.dot(embedded, embed_in_values, precision=HIGHEST) + bias_hidden
    hidden = jax.nn.gelu(hidden_pre)
    modulate = jnp.dot(hidden, embed_out_values, precision=HIGHEST) + bias_mod
    modulation = jnp.stack([1.0 + modulate[:, :C], modulate[:, C:]], axis=1)
    lanes = jnp.concatenate([small_low[: 6 * C].reshape(6, C), jnp.zeros((6, C), jnp.bfloat16)], axis=1)
    vectors = jnp.concatenate(
        [lanes.astype(jnp.float32), bias_down[None, :], jnp.zeros((1, C2), jnp.float32)], axis=0
    )
    block_out, grad_field, grad_w1, grad_w2, grad_wd, sums = run_samples(
        field, cotangent, modulation, conv_low, down_low, vectors
    )
    grad_start = to_rows(grad_field)
    mid_cross, mid_total, pre_cross, pre_total = [sums[:, position] for position in range(4)]
    scale_plus = modulation[:, 0]
    grad_scale = gain_two * mid_cross + shift_two * mid_total
    grad_mod = jnp.concatenate([grad_scale, mid_total], axis=1)
    grad_embed_out = jnp.dot(hidden.T, grad_mod, precision=HIGHEST)
    grad_hidden_pre = gelu_grad(
        hidden_pre, jnp.dot(grad_mod, embed_out_values.T, precision=HIGHEST)
    )
    grad_embed_in = jnp.dot(embedded.T, grad_hidden_pre, precision=HIGHEST)
    grad_small = jnp.concatenate(
        [
            jnp.sum(pre_cross, axis=0),
            jnp.sum(mid_cross * scale_plus, axis=0),
            jnp.sum(pre_total, axis=0),
            jnp.sum(mid_total * scale_plus, axis=0),
            jnp.sum(sums[:, 4], axis=0),
            jnp.sum(sums[:, 5], axis=0),
            jnp.sum(sums[:, 6:8], axis=0).reshape(-1),
            jnp.sum(grad_hidden_pre, axis=0),
            jnp.sum(grad_mod, axis=0),
        ]
    )
    grad_conv = jnp.stack([grad_w1.T, grad_w2.T])
    grad_down = grad_wd.T
    laid_out = jnp.concatenate(
        [
            split_to_shards(grad_conv, conv_weight.shape, 1),
            split_to_shards(grad_down, down_weight.shape, 0),
            split_to_shards(grad_embed_in, embed_in_weight.shape, 0),
            split_to_shards(grad_embed_out, embed_out_weight.shape, 0),
            grad_small.reshape(lax.axis_size("batch") * lax.axis_size("row"), -1),
        ],
        axis=1,
    )
    owned_flat = lax.psum_scatter(
        laid_out, ("batch", "row"), scatter_dimension=0, tiled=True
    ).reshape(-1)
    owned_shards = [
        piece.reshape(shard.shape) for piece, shard in zip(unpack_rows(owned_flat, shards), shards)
    ]
    grad_norm = jnp.sqrt(lax.psum(jnp.sum(owned_flat * owned_flat), ("batch", "row")))
    clip_factor = jnp.minimum(1.0, CLIP_NORM / (grad_norm + 1e-06))
    conv_new = adam_update(
        conv_weight, owned_shards[0], conv_first, conv_second, RATE_MATRIX, clip_factor
    )
    down_new = adam_update(
        down_weight, owned_shards[1], down_first, down_second, RATE_MATRIX, clip_factor
    )
    embed_in_new = adam_update(
        embed_in_weight, owned_shards[2], embed_in_first, embed_in_second, RATE_MATRIX, clip_factor
    )
    embed_out_new = adam_update(
        embed_out_weight,
        owned_shards[3],
        embed_out_first,
        embed_out_second,
        RATE_MATRIX,
        clip_factor,
    )
    small_new = adam_update(
        small_params, owned_shards[4], small_first, small_second, RATE_SMALL, clip_factor
    )
    return (
        block_out,
        grad_start,
        grad_norm,
        conv_new[0],
        down_new[0],
        embed_in_new[0],
        embed_out_new[0],
        small_new[0],
        conv_new[1],
        down_new[1],
        embed_in_new[1],
        embed_out_new[1],
        small_new[1],
        conv_new[2],
        down_new[2],
        embed_in_new[2],
        embed_out_new[2],
        small_new[2],
    )


def solution(mesh):
    placed = (
        P("batch", "row", None, None),
        P("batch"),
        P(("batch", "row"), None, None, None),
        P(None, "batch", "row"),
        P("batch", "row"),
        P("batch", "row"),
        P("batch", "row"),
        P(("batch", "row")),
        P(None, "batch", "row"),
        P("batch", "row"),
        P("batch", "row"),
        P("batch", "row"),
        P(("batch", "row")),
        P(None, "batch", "row"),
        P("batch", "row"),
        P("batch", "row"),
        P("batch", "row"),
        P(("batch", "row")),
    )
    return jax.shard_map(
        body,
        mesh=mesh,
        in_specs=placed,
        out_specs=(
            P(("batch", "row"), None, None, None),
            P("batch", "row", None, None),
            P(),
            P(None, "batch", "row"),
            P("batch", "row"),
            P("batch", "row"),
            P("batch", "row"),
            P(("batch", "row")),
            P(None, "batch", "row"),
            P("batch", "row"),
            P("batch", "row"),
            P("batch", "row"),
            P(("batch", "row")),
            P(None, "batch", "row"),
            P("batch", "row"),
            P("batch", "row"),
            P("batch", "row"),
            P(("batch", "row")),
        ),
        check_vma=False,
    )
```

```python
import functools
import math

import jax
import jax.numpy as jnp
import numpy as np
from jax import lax
from jax.experimental import pallas as pl
from jax.experimental.pallas import tpu as pltpu
from jax.sharding import PartitionSpec as P

C = 128
C2 = 256
EMB = 128
HID = 512
GROUPS = 8
REFINE = 4


NORM_EPS = 1e-05
BETA_ONE = 0.9
BETA_TWO = 0.999
ADAM_EPS = 1e-08
DECAY = 0.01
RATE_MATRIX = 0.05
RATE_SMALL = 0.5
CLIP_NORM = 1.0
STEP_COUNT = 10
HIGHEST = lax.Precision.HIGHEST


def embed_steps(refine_step):
    halfway = EMB // 2
    frequency = jnp.exp(-math.log(10000.0) * jnp.arange(halfway).astype(jnp.float32) / halfway)
    angles = (refine_step.astype(jnp.float32) * (1000.0 / REFINE))[:, None] * frequency[None, :]
    return jnp.concatenate([jnp.sin(angles), jnp.cos(angles)], axis=1)


def to_samples(values):
    return lax.all_to_all(values, "row", split_axis=0, concat_axis=1, tiled=True)


def to_rows(values):
    return lax.all_to_all(values, "row", split_axis=1, concat_axis=0, tiled=True)


FIELD_COLS = 64
HALF_COLS = 32
ROOT = math.sqrt(2.0 / math.pi)
CUBIC = ROOT * 0.044715


def chunk_of(total, most):
    size = min(total, most)
    while total % size:
        size -= 1
    return size


def over(total, most, body, init):
    size = chunk_of(total, most)

    def several(step, carry):
        for inner in range(size):
            carry = body(step * size + inner, carry)
        return carry

    if size == total:
        return several(0, init)
    return lax.fori_loop(0, total // size, several, init)


def folded(values):
    return jnp.sum(values.reshape(values.shape[0] // 8, 8, values.shape[1]), axis=0)


def twice(row):
    return jnp.concatenate([row, row], axis=1)


def channel_sum(partial):
    both = partial[:, :C] + partial[:, C:]
    return jnp.sum(both, axis=0, keepdims=True)


def group_means(first, second, same_group, entries):
    stacked = jnp.concatenate([first, second, jnp.zeros((6, C), jnp.float32)], axis=0)
    totals = jnp.dot(stacked, same_group, precision=HIGHEST, preferred_element_type=jnp.float32)
    return totals[0:1] / entries, totals[1:2] / entries


def gelu_pair(values):
    square = values * values
    bend = jnp.tanh(values * (ROOT + CUBIC * square))
    half = 0.5 * values
    slope = (0.5 + 0.5 * bend) + half * (1.0 - bend * bend) * (ROOT + (3.0 * CUBIC) * square)
    return half + half * bend, slope


def put_shifted(ref, pair, values):
    for tap, shift in ((0, 1), (1, 0), (2, FIELD_COLS - 1)):
        moved = pltpu.roll(values, shift, 0) if shift else values
        ref[tap, pair + 1] = moved.astype(jnp.bfloat16)


def close_ring(ref, pairs):
    ref[:, 0, :, C:] = ref[:, pairs, :, C:]
    ref[:, pairs + 1, :, :C] = ref[:, 1, :, :C]


def windows(ref, start, count):
    rows = count * FIELD_COLS
    pieces = []
    for tap in range(3):
        pieces.append(ref[tap, pl.ds(start + 1, count)].reshape(rows, 2 * C))
        pieces.append(ref[tap, pl.ds(start, count), :, C:].reshape(rows, C))
        pieces.append(ref[tap, pl.ds(start + 2, count), :, :C].reshape(rows, C))
    return jnp.concatenate(pieces, axis=1)


def add_conv_grad(out_ref, act_ref, grad_ref, pairs):
    size = chunk_of(pairs, 8)
    rows = size * FIELD_COLS

    def body(step, carry):
        start = step * size
        grad = grad_ref[1, pl.ds(start + 1, size)].reshape(rows, 2 * C)
        product = jnp.dot(
            grad.T, windows(act_ref, start, size), preferred_element_type=jnp.float32
        )
        for tap in range(3):
            base = tap * 4 * C
            own_low = product[:C, base : base + C] + product[C:, base + C : base + 2 * C]
            up = product[C:, base : base + C] + product[:C, base + 2 * C : base + 3 * C]
            down = product[:C, base + C : base + 2 * C] + product[C:, base + 3 * C : base + 4 * C]
            for row_tap, value in ((0, up), (1, own_low), (2, down)):
                lanes = pl.ds((3 * row_tap + tap) * C, C)
                out_ref[:, lanes] = out_ref[:, lanes] + value
        return carry

    over_steps(pairs // size, body)


def over_steps(steps, body):
    if steps == 1:
        body(0, 0)
    else:
        lax.fori_loop(0, steps, body, 0)


def sample_kernel(
    pairs,
    x_ref,
    cot_ref,
    mod_ref,
    fwd_one,
    back_one,
    fwd_two,
    back_two,
    down_fwd,
    down_even,
    down_odd,
    vec_ref,
    group_ref,
    out_ref,
    grad_ref,
    conv_grad_one,
    conv_grad_two,
    down_grad,
    sums_ref,
    act_one,
    act_two,
    grad_one,
    grad_two,
    slope_one,
    slope_two,
    unit_two,
    grad_mid,
    sum_even,
    sum_odd,
    grad_even,
    grad_odd,
    down_win,
    cot_win,
):
    entries = 2.0 * pairs * FIELD_COLS * (C // GROUPS)
    size = chunk_of(pairs, 8)
    rows = size * FIELD_COLS
    same_group = group_ref[...]
    gain_one, gain_two = vec_ref[0:1, :C], vec_ref[1:2, :C]
    shift_one, shift_two = vec_ref[2:3, :C], vec_ref[3:4, :C]
    bias_one, bias_two = twice(vec_ref[4:5, :C]), twice(vec_ref[5:6, :C])
    bias_down = vec_ref[6:7, :]
    scale_plus, offset = mod_ref[0, 0:1, :], mod_ref[0, 1:2, :]
    nothing = jnp.zeros((8, 2 * C), jnp.float32)

    @pl.when(pl.program_id(0) == 0)
    def _():
        conv_grad_one[...] = jnp.zeros_like(conv_grad_one)
        conv_grad_two[...] = jnp.zeros_like(conv_grad_two)
        down_grad[...] = jnp.zeros_like(down_grad)

    def field(pair):
        return jnp.concatenate(
            [x_ref[0, pair, 0].astype(jnp.float32), x_ref[0, pair, 1].astype(jnp.float32)], axis=1
        )

    def first_stats(pair, carry):
        value = field(pair)
        return carry[0] + folded(value), carry[1] + folded(value * value)

    total, squares = over(pairs, 8, first_stats, (nothing, nothing))
    mean_one, square_one = group_means(channel_sum(total), channel_sum(squares), same_group, entries)
    inverse_one = lax.rsqrt(square_one - mean_one * mean_one + NORM_EPS)
    center_one = twice(-mean_one * inverse_one)
    inverse_one = twice(inverse_one)
    gain_wide, shift_wide = twice(gain_one), twice(shift_one)

    def first_act(pair, carry):
        unit = field(pair) * inverse_one + center_one
        value, slope = gelu_pair(unit * gain_wide + shift_wide)
        put_shifted(act_one, pair, value)
        slope_one[pair] = slope
        return carry

    over(pairs, 8, first_act, 0)
    close_ring(act_one, pairs)

    def conv_one_chunk(step, carry):
        start = step * size
        value = jnp.dot(
            windows(act_one, start, size), fwd_one[...], preferred_element_type=jnp.float32
        ) + bias_one
        unit_two[pl.ds(start, size)] = value.reshape(size, FIELD_COLS, 2 * C)
        return carry[0] + folded(value), carry[1] + folded(value * value)

    total, squares = lax.fori_loop(0, pairs // size, conv_one_chunk, (nothing, nothing))
    mean_two, square_two = group_means(channel_sum(total), channel_sum(squares), same_group, entries)
    inverse_two = lax.rsqrt(square_two - mean_two * mean_two + NORM_EPS)
    center_two = twice(-mean_two * inverse_two)
    mid_gain = twice(gain_two * scale_plus)
    mid_shift = twice(shift_two * scale_plus + offset)
    inverse_two_wide = twice(inverse_two)

    def second_act(pair, carry):
        unit = unit_two[pair] * inverse_two_wide + center_two
        value, slope = gelu_pair(unit * mid_gain + mid_shift)
        put_shifted(act_two, pair, value)
        slope_two[pair] = slope
        unit_two[pair] = unit
        return carry

    over(pairs, 8, second_act, 0)
    close_ring(act_two, pairs)

    def conv_two_chunk(step, carry):
        start = step * size
        value = jnp.dot(
            windows(act_two, start, size), fwd_two[...], preferred_element_type=jnp.float32
        ) + bias_two
        value = value.reshape(size, FIELD_COLS, 2 * C)
        for half, ref in ((0, sum_even), (1, sum_odd)):
            base = x_ref[0, pl.ds(start, size), half].astype(jnp.float32)
            ref[pl.ds(start, size)] = base + value[:, :, half * C : half * C + C]
        return carry

    over_steps(pairs // size, conv_two_chunk)

    def split_columns(pair, carry):
        even = []
        odd = []
        for ref in (sum_even, sum_odd):
            even.append(ref[pair, pl.ds(0, HALF_COLS, stride=2), :])
            odd.append(ref[pair, pl.ds(1, HALF_COLS, stride=2), :])
        even = jnp.concatenate(even, axis=1)
        odd = jnp.concatenate(odd, axis=1)
        down_win[0, pair + 1] = pltpu.roll(odd, 1, 0).astype(jnp.bfloat16)
        down_win[1, pair + 1] = even.astype(jnp.bfloat16)
        down_win[2, pair + 1] = odd.astype(jnp.bfloat16)
        cot = cot_ref[0, pair]
        wide = cot.astype(jnp.float32)
        cot_win[0, pair] = cot
        cot_win[1, pair] = pltpu.roll(wide, HALF_COLS - 1, 0).astype(jnp.bfloat16)
        return carry + folded(wide)

    cot_total = over(pairs, 8, split_columns, nothing)
    down_win[:, 0, :, C:] = down_win[:, pairs, :, C:]
    cot_win[:, pairs] = cot_win[:, 0]
    small = size * HALF_COLS

    def down_windows(start):
        pieces = [down_win[tap, pl.ds(start + 1, size)].reshape(small, 2 * C) for tap in range(3)]
        pieces += [
            down_win[tap, pl.ds(start, size), :, C:].reshape(small, C) for tap in range(3)
        ]
        return jnp.concatenate(pieces, axis=1)

    def down_chunk(step, carry):
        start = step * size
        lhs = down_windows(start)
        value = jnp.dot(lhs, down_fwd[...], preferred_element_type=jnp.float32) + bias_down
        out_ref[0, pl.ds(start, size)] = value.reshape(size, HALF_COLS, 2 * C).astype(jnp.bfloat16)
        here = cot_win[0, pl.ds(start, size)].reshape(small, 2 * C)
        product = jnp.dot(here.T, lhs, preferred_element_type=jnp.float32)
        for position in range(9):
            row_tap, tap = DOWN_ORDER[position]
            lanes = pl.ds((3 * row_tap + tap) * C, C)
            down_grad[:, lanes] = down_grad[:, lanes] + product[:, position * C : position * C + C]
        pieces = [
            cot_win[shift, pl.ds(start + below, size)].reshape(small, 2 * C)
            for below in range(2)
            for shift in range(2)
        ]
        even = jnp.dot(
            jnp.concatenate([pieces[0], pieces[2]], axis=1),
            down_even[...],
            preferred_element_type=jnp.float32,
        ).reshape(size, HALF_COLS, 2 * C)
        odd = jnp.dot(
            jnp.concatenate(pieces, axis=1), down_odd[...], preferred_element_type=jnp.float32
        ).reshape(size, HALF_COLS, 2 * C)
        for half, ref in ((0, grad_even), (1, grad_odd)):
            lanes = slice(half * C, half * C + C)
            for inner in range(size):
                ref[start + inner, pl.ds(0, HALF_COLS, stride=2), :] = even[inner, :, lanes]
                ref[start + inner, pl.ds(1, HALF_COLS, stride=2), :] = odd[inner, :, lanes]
        return carry

    over_steps(pairs // size, down_chunk)

    def second_grad(pair, carry):
        value = jnp.concatenate([grad_even[pair], grad_odd[pair]], axis=1)
        put_shifted(grad_two, pair, value)
        return carry + folded(value.astype(jnp.bfloat16).astype(jnp.float32))

    bias_two_total = over(pairs, 8, second_grad, nothing)
    close_ring(grad_two, pairs)
    add_conv_grad(conv_grad_two, act_two, grad_two, pairs)

    def back_two_chunk(step, carry):
        start = step * size
        value = jnp.dot(
            windows(grad_two, start, size), back_two[...], preferred_element_type=jnp.float32
        )
        value = value * slope_two[pl.ds(start, size)].reshape(rows, 2 * C)
        grad_mid[pl.ds(start, size)] = value.reshape(size, FIELD_COLS, 2 * C)
        unit = unit_two[pl.ds(start, size)].reshape(rows, 2 * C)
        return carry[0] + folded(value), carry[1] + folded(value * unit)

    total, cross = lax.fori_loop(0, pairs // size, back_two_chunk, (nothing, nothing))
    mid_total, mid_cross = channel_sum(total), channel_sum(cross)
    factor = scale_plus * gain_two
    mean_grad, mean_cross = group_means(
        mid_total * factor, mid_cross * factor, same_group, entries
    )
    from_mid = twice(inverse_two * factor)
    from_unit = twice(inverse_two * mean_cross)
    from_mean = twice(inverse_two * mean_grad)

    def first_grad(pair, carry):
        value = grad_mid[pair] * from_mid - from_mean - unit_two[pair] * from_unit
        put_shifted(grad_one, pair, value)
        return carry + folded(value.astype(jnp.bfloat16).astype(jnp.float32))

    bias_one_total = over(pairs, 8, first_grad, nothing)
    close_ring(grad_one, pairs)
    add_conv_grad(conv_grad_one, act_one, grad_one, pairs)

    def back_one_chunk(step, carry):
        start = step * size
        value = jnp.dot(
            windows(grad_one, start, size), back_one[...], preferred_element_type=jnp.float32
        )
        value = value * slope_one[pl.ds(start, size)].reshape(rows, 2 * C)
        grad_mid[pl.ds(start, size)] = value.reshape(size, FIELD_COLS, 2 * C)
        base = jnp.concatenate(
            [
                x_ref[0, pl.ds(start, size), half].astype(jnp.float32).reshape(rows, C)
                for half in range(2)
            ],
            axis=1,
        )
        unit = base * inverse_one + center_one
        return carry[0] + folded(value), carry[1] + folded(value * unit)

    total, cross = lax.fori_loop(0, pairs // size, back_one_chunk, (nothing, nothing))
    pre_total, pre_cross = channel_sum(total), channel_sum(cross)
    mean_grad, mean_cross = group_means(
        pre_total * gain_one, pre_cross * gain_one, same_group, entries
    )
    from_pre = inverse_one * gain_wide
    from_unit_one = inverse_one * twice(mean_cross)
    from_mean_one = inverse_one * twice(mean_grad)

    def last(pair, carry):
        unit = field(pair) * inverse_one + center_one
        summed = jnp.concatenate([grad_even[pair], grad_odd[pair]], axis=1)
        value = (summed + (grad_mid[pair] * from_pre - from_mean_one - unit * from_unit_one)).astype(
            jnp.bfloat16
        )
        grad_ref[0, pair, 0] = value[:, :C]
        grad_ref[0, pair, 1] = value[:, C:]
        return carry

    over(pairs, 8, last, 0)
    cot_sums = jnp.sum(cot_total, axis=0, keepdims=True)
    sums_ref[0] = jnp.concatenate(
        [
            mid_cross,
            mid_total,
            pre_cross,
            pre_total,
            channel_sum(bias_one_total),
            channel_sum(bias_two_total),
            cot_sums[:, :C],
            cot_sums[:, C:],
        ],
        axis=0,
    )


DOWN_ORDER = ((1, 0), (2, 0), (1, 1), (2, 1), (1, 2), (2, 2), (0, 0), (0, 1), (0, 2))


def run_samples(field, cotangent, modulation, weights, vectors):
    samples, height = field.shape[:2]
    pairs = height // 2
    halves = field.reshape(samples, pairs, 2, FIELD_COLS, C)
    same_group = jnp.asarray(
        np.kron(np.eye(GROUPS), np.ones((C // GROUPS, C // GROUPS))), jnp.float32
    )

    def whole(array):
        return pl.BlockSpec(array.shape, lambda i: (0,) * array.ndim, pipeline_mode=pl.Buffered(1))

    def per_sample(array):
        rank = len(array.shape)
        return pl.BlockSpec((1,) + array.shape[1:], lambda i: (i,) + (0,) * (rank - 1))

    constants = tuple(weights) + (vectors, same_group)
    outs = (
        jax.ShapeDtypeStruct((samples, pairs, HALF_COLS, C2), jnp.bfloat16),
        jax.ShapeDtypeStruct(halves.shape, jnp.bfloat16),
        jax.ShapeDtypeStruct((C, 9 * C), jnp.float32),
        jax.ShapeDtypeStruct((C, 9 * C), jnp.float32),
        jax.ShapeDtypeStruct((C2, 9 * C), jnp.float32),
        jax.ShapeDtypeStruct((samples, 8, C), jnp.float32),
    )
    ring = pltpu.VMEM((3, pairs + 2, FIELD_COLS, 2 * C), jnp.bfloat16)
    wide = pltpu.VMEM((pairs, FIELD_COLS, 2 * C), jnp.float32)
    half = pltpu.VMEM((pairs, FIELD_COLS, C), jnp.float32)
    result = pl.pallas_call(
        functools.partial(sample_kernel, pairs),
        grid=(samples,),
        in_specs=[per_sample(halves), per_sample(cotangent), per_sample(modulation)]
        + [whole(array) for array in constants],
        out_specs=[per_sample(outs[0]), per_sample(outs[1])]
        + [pl.BlockSpec(out.shape, lambda i: (0, 0)) for out in outs[2:5]]
        + [per_sample(outs[5])],
        out_shape=outs,
        scratch_shapes=[ring] * 4
        + [wide] * 4
        + [half] * 4
        + [
            pltpu.VMEM((3, pairs + 1, HALF_COLS, 2 * C), jnp.bfloat16),
            pltpu.VMEM((2, pairs + 1, HALF_COLS, C2), jnp.bfloat16),
        ],
        compiler_params=pltpu.CompilerParams(
            dimension_semantics=("arbitrary",), vmem_limit_bytes=60 << 20
        ),
        name="samples",
    )(halves, cotangent, modulation, *constants)
    return (result[0], result[1].reshape(field.shape)) + tuple(result[2:])


MESH = pl.DeviceIdType.MESH


def greet(row_count, batch_count):
    row, batch = lax.axis_index("row"), lax.axis_index("batch")
    barrier = pltpu.get_barrier_semaphore()
    for step in range(1, row_count):
        pl.semaphore_signal(
            barrier,
            inc=1,
            device_id={"row": lax.rem(row + step, row_count), "batch": batch},
            device_id_type=MESH,
        )
    for step in range(1, batch_count):
        pl.semaphore_signal(
            barrier,
            inc=1,
            device_id={"row": row, "batch": lax.rem(batch + step, batch_count)},
            device_id_type=MESH,
        )
    pl.semaphore_wait(barrier, row_count + batch_count - 2)


def to_peer(axis, step, count, source, target, send_sem, recv_sem):
    row, batch = lax.axis_index("row"), lax.axis_index("batch")
    if axis == "row":
        device = {"row": lax.rem(row + step, count), "batch": batch}
    else:
        device = {"row": row, "batch": lax.rem(batch + step, count)}
    return pltpu.make_async_remote_copy(
        src_ref=source,
        dst_ref=target,
        send_sem=send_sem,
        recv_sem=recv_sem,
        device_id=device,
        device_id_type=MESH,
    )


def finish(copies):
    for copy in copies:
        copy.wait()


def gather_kernel(
    row_count,
    batch_count,
    shard_ref,
    small_ref,
    fwd_one,
    back_one,
    fwd_two,
    back_two,
    down_fwd,
    down_even,
    down_odd,
    small_out,
    embed_in_t,
    embed_out_ref,
    shards,
    smalls,
    conv_t,
    down_t,
    send_main,
    recv_main,
    send_small,
    recv_small,
    local_sem,
):
    row, batch = lax.axis_index("row"), lax.axis_index("batch")
    greet(row_count, batch_count)
    own_main = pltpu.make_async_copy(shard_ref, shards.at[row, batch], local_sem.at[0])
    own_small = pltpu.make_async_copy(small_ref, smalls.at[row, batch], local_sem.at[1])
    own_main.start()
    own_small.start()
    copies = []
    for step in range(1, batch_count):
        copies.append(
            to_peer(
                "batch",
                step,
                batch_count,
                shard_ref,
                shards.at[row, batch],
                send_main.at[step],
                recv_main.at[step],
            )
        )
        copies.append(
            to_peer(
                "batch",
                step,
                batch_count,
                small_ref,
                smalls.at[row, batch],
                send_small.at[step],
                recv_small.at[step],
            )
        )
    for copy in copies:
        copy.start()
    own_main.wait()
    own_small.wait()
    finish(copies)
    copies = []
    for step in range(1, row_count):
        slot = batch_count + step
        copies.append(
            to_peer(
                "row",
                step,
                row_count,
                shards.at[row],
                shards.at[row],
                send_main.at[slot],
                recv_main.at[slot],
            )
        )
        copies.append(
            to_peer(
                "row",
                step,
                row_count,
                smalls.at[row],
                smalls.at[row],
                send_small.at[slot],
                recv_small.at[slot],
            )
        )
    for copy in copies:
        copy.start()
    finish(copies)
    depth, share, wide_share = 9 * C // batch_count, C // row_count, C2 // row_count
    height = 2 * share + wide_share
    embed_share, hidden_share = EMB // batch_count, HID // batch_count
    for place in range(row_count):
        parts = [shards[place, part].astype(jnp.float32) for part in range(batch_count)]
        main = jnp.concatenate([part[:, :depth] for part in parts], axis=1)
        for which in range(2):
            conv_t[which, place * share : place * share + share, :] = main[
                which * share : which * share + share
            ]
        down_t[place * wide_share : place * wide_share + wide_share, :] = main[2 * share :]
        embed_in_t[place * height : place * height + height, :] = jnp.concatenate(
            [part[:, depth : depth + embed_share] for part in parts], axis=1
        )
        tail = depth + embed_share
        half_rows, half_lanes = height // 2, hidden_share // 2
        lanes = []
        for part in parts:
            lanes.append(part[:half_rows, tail : tail + half_lanes])
            lanes.append(part[half_rows:, tail : tail + half_lanes])
        embed_out_ref[place * half_rows : place * half_rows + half_rows, :] = jnp.concatenate(
            lanes, axis=1
        )
        for part in range(batch_count):
            small_out[part * row_count + place : part * row_count + place + 1, :] = smalls[
                place, part, 0:1, :
            ]
    for which, forward, back in ((0, fwd_one, back_one), (1, fwd_two, back_two)):
        zero = jnp.zeros((C, C), jnp.bfloat16)
        for tap in range(3):
            direct = [
                conv_t[which, :, (3 * row_tap + tap) * C : (3 * row_tap + tap) * C + C]
                for row_tap in range(3)
            ]
            fill_blocks(forward, tap, [block.T.astype(jnp.bfloat16) for block in direct], zero)
            fill_blocks(
                back, 2 - tap, [block.astype(jnp.bfloat16) for block in direct[::-1]], zero
            )
    zero = jnp.zeros((C2, C), jnp.bfloat16)
    back = {}
    for position in range(9):
        row_tap, tap = DOWN_ORDER[position]
        block = down_t[:, (3 * row_tap + tap) * C : (3 * row_tap + tap) * C + C]
        down_fwd[position * C : position * C + C, :] = block.T.astype(jnp.bfloat16)
        back[row_tap, tap] = block.astype(jnp.bfloat16)
    even = ((back[1, 1], back[2, 1]), (zero, back[0, 1]))
    odd = (
        (back[1, 2], back[2, 2]),
        (back[1, 0], back[2, 0]),
        (zero, back[0, 2]),
        (zero, back[0, 0]),
    )
    for ref, table in ((down_even, even), (down_odd, odd)):
        for position, (left, right) in enumerate(table):
            ref[position * C2 : position * C2 + C2, :C] = left
            ref[position * C2 : position * C2 + C2, C:] = right


def fill_blocks(ref, tap, blocks, zero):
    table = (
        (blocks[1], blocks[0]),
        (blocks[2], blocks[1]),
        (blocks[0], zero),
        (zero, blocks[2]),
    )
    for position, (left, right) in enumerate(table):
        base = (4 * tap + position) * C
        ref[base : base + C, :C] = left
        ref[base : base + C, C:] = right


def dot_last(lhs, rhs):
    return lax.dot_general(
        lhs,
        rhs,
        (((1,), (1,)), ((), ())),
        precision=HIGHEST,
        preferred_element_type=jnp.float32,
    )


def dot_first(lhs, rhs):
    return lax.dot_general(
        lhs,
        rhs,
        (((0,), (0,)), ((), ())),
        precision=HIGHEST,
        preferred_element_type=jnp.float32,
    )


def reduce_kernel(
    row_count,
    batch_count,
    samples,
    grad_one,
    grad_two,
    grad_down,
    sums_ref,
    scale_ref,
    gate_ref,
    hidden_ref,
    slope_ref,
    embedded_ref,
    embed_out_ref,
    owned_ref,
    small_ref,
    norm_ref,
    row_send,
    row_take,
    batch_send,
    batch_take,
    small_send,
    small_take,
    small_next,
    small_last,
    square_send,
    square_take,
    square_next,
    square_last,
    send_sem,
    recv_sem,
):
    row, batch = lax.axis_index("row"), lax.axis_index("batch")
    depth, share, wide_share = 9 * C // batch_count, C // row_count, C2 // row_count
    height = 2 * share + wide_share
    embed_share, hidden_share = EMB // batch_count, HID // batch_count
    mid_cross, mid_total = sums_ref[0], sums_ref[1]
    gain_two, shift_two = gate_ref[0:1, :], gate_ref[1:2, :]
    scale_plus = scale_ref[...]
    grad_mod = jnp.concatenate([gain_two * mid_cross + shift_two * mid_total, mid_total], axis=1)
    grad_embed_out = dot_first(grad_mod, hidden_ref[...])
    grad_hidden = (
        jnp.dot(
            grad_mod, embed_out_ref[...], precision=HIGHEST, preferred_element_type=jnp.float32
        )
        * slope_ref[...]
    )
    grad_embed_in = dot_first(grad_hidden, embedded_ref[...])

    def down_sum(value):
        return jnp.sum(value, axis=0, keepdims=True)

    small_rows = [
        down_sum(sums_ref[2]),
        down_sum(mid_cross * scale_plus),
        down_sum(sums_ref[3]),
        down_sum(mid_total * scale_plus),
    ] + [down_sum(sums_ref[place]) for place in range(4, 8)]
    hidden_total, mod_total = down_sum(grad_hidden), down_sum(grad_mod)
    small_rows += [hidden_total[:, lane : lane + C] for lane in range(0, HID, C)]
    small_rows += [mod_total[:, lane : lane + C] for lane in range(0, 2 * C, C)]
    small_rows.append(jnp.zeros((2, C), jnp.float32))
    small_send[...] = jnp.concatenate(small_rows, axis=0)
    half_rows = height // 2
    for place in range(row_count):
        low, high = place * share, place * share + share
        row_send[place, :, : 9 * C] = jnp.concatenate(
            [
                grad_one[low:high],
                grad_two[low:high],
                grad_down[place * wide_share : place * wide_share + wide_share],
            ],
            axis=0,
        ).astype(jnp.bfloat16)
        row_send[place, :, 9 * C : 10 * C] = grad_embed_in[
            place * height : place * height + height
        ].astype(jnp.bfloat16)
        piece = grad_embed_out[place * half_rows : place * half_rows + half_rows]
        row_send[place, :, 10 * C :] = jnp.concatenate(
            [piece[:, : HID // 2], piece[:, HID // 2 :]], axis=0
        ).astype(jnp.bfloat16)
    greet(row_count, batch_count)
    copies = []
    for step in range(1, row_count):
        copies.append(
            to_peer(
                "row",
                step,
                row_count,
                row_send.at[lax.rem(row + step, row_count)],
                row_take.at[step],
                send_sem.at[0, step],
                recv_sem.at[0, step],
            )
        )
        copies.append(
            to_peer(
                "row",
                step,
                row_count,
                small_send,
                small_take.at[step],
                send_sem.at[1, step],
                recv_sem.at[1, step],
            )
        )
    for copy in copies:
        copy.start()
    total = row_send[row].astype(jnp.float32)
    finish(copies)
    small_total = small_send[...]
    for step in range(1, row_count):
        total = total + row_take[step].astype(jnp.float32)
        small_total = small_total + small_take[step]
    small_next[...] = small_total
    for part in range(batch_count):
        per_half = batch_count // 2
        rows = slice(0, half_rows) if part < per_half else slice(half_rows, height)
        base = 10 * C + hidden_share * (part % per_half)
        piece = total[rows, base : base + hidden_share]
        batch_send[part] = jnp.concatenate(
            [
                total[:, part * depth : part * depth + depth],
                total[:, 9 * C + part * embed_share : 9 * C + part * embed_share + embed_share],
                jnp.concatenate([piece[:, : hidden_share // 2], piece[:, hidden_share // 2 :]], axis=0),
            ],
            axis=1,
        ).astype(jnp.bfloat16)
    copies = []
    for step in range(1, batch_count):
        copies.append(
            to_peer(
                "batch",
                step,
                batch_count,
                batch_send.at[lax.rem(batch + step, batch_count)],
                batch_take.at[step],
                send_sem.at[2, step],
                recv_sem.at[2, step],
            )
        )
        copies.append(
            to_peer(
                "batch",
                step,
                batch_count,
                small_next,
                small_last.at[step],
                send_sem.at[3, step],
                recv_sem.at[3, step],
            )
        )
    for copy in copies:
        copy.start()
    owned = batch_send[batch].astype(jnp.float32)
    finish(copies)
    small_total = small_next[...]
    for step in range(1, batch_count):
        owned = owned + batch_take[step].astype(jnp.float32)
        small_total = small_total + small_last[step]
    squares = jnp.sum(jnp.sum(owned * owned, axis=0, keepdims=True), axis=1, keepdims=True)
    square_send[...] = jnp.broadcast_to(squares, (8, C))
    copies = [
        to_peer(
            "row",
            step,
            row_count,
            square_send,
            square_take.at[step],
            send_sem.at[4, step],
            recv_sem.at[4, step],
        )
        for step in range(1, row_count)
    ]
    for copy in copies:
        copy.start()
    finish(copies)
    squares = square_send[...]
    for step in range(1, row_count):
        squares = squares + square_take[step]
    square_next[...] = squares
    copies = [
        to_peer(
            "batch",
            step,
            batch_count,
            square_next,
            square_last.at[step],
            send_sem.at[5, step],
            recv_sem.at[5, step],
        )
        for step in range(1, batch_count)
    ]
    for copy in copies:
        copy.start()
    finish(copies)
    squares = square_next[...]
    for step in range(1, batch_count):
        squares = squares + square_last[step]
    small_squares = jnp.sum(
        jnp.sum(small_total * small_total, axis=0, keepdims=True), axis=1, keepdims=True
    )
    norm = jnp.sqrt(squares + small_squares)
    clip = jnp.minimum(1.0, CLIP_NORM / (norm + 1e-06))[0:1, 0:1]
    norm_ref[...] = norm
    owned_ref[...] = owned * clip
    small_ref[...] = small_total * clip


def pack_pieces(conv, down, embed_in, embed_out):
    half = embed_out.shape[0] // 2
    tall = jnp.concatenate([embed_out[:half].T, embed_out[half:].T], axis=0)
    return jnp.concatenate(
        [jnp.concatenate([conv[0].T, conv[1].T, down.T], axis=0), embed_in.T, tall], axis=1
    )


def unpack_pieces(owned, depth, share, embed_share):
    height, half = owned.shape[0], owned.shape[0] // 2
    conv = jnp.stack([owned[:share, :depth].T, owned[share : 2 * share, :depth].T])
    down = owned[2 * share :, :depth].T
    embed_in = owned[:, depth : depth + embed_share].T
    tall = owned[:, depth + embed_share :]
    embed_out = jnp.concatenate([tall[:half].T, tall[half:].T], axis=0)
    return conv, down, embed_in, embed_out


def in_vmem(count):
    return [pl.BlockSpec(memory_space=pltpu.VMEM)] * count


def gather_weights(packed, small):
    row_count, batch_count = (lax.axis_size("row"), lax.axis_size("batch"))
    small_tile = jnp.pad(small[None, :], ((0, 7), (0, C - small.shape[0])))
    outs = (
        [jax.ShapeDtypeStruct((12 * C, 2 * C), jnp.bfloat16)] * 4
        + [
            jax.ShapeDtypeStruct((9 * C, C2), jnp.bfloat16),
            jax.ShapeDtypeStruct((2 * C2, 2 * C), jnp.bfloat16),
            jax.ShapeDtypeStruct((4 * C2, 2 * C), jnp.bfloat16),
        ]
        + [
            jax.ShapeDtypeStruct((row_count * batch_count, C), jnp.float32),
            jax.ShapeDtypeStruct((HID, EMB), jnp.float32),
            jax.ShapeDtypeStruct((2 * C, HID), jnp.float32),
        ]
    )
    slots = row_count + batch_count
    return pl.pallas_call(
        functools.partial(gather_kernel, row_count, batch_count),
        out_shape=outs,
        in_specs=in_vmem(2),
        out_specs=in_vmem(len(outs)),
        scratch_shapes=[
            pltpu.VMEM((row_count, batch_count) + packed.shape, jnp.bfloat16),
            pltpu.VMEM((row_count, batch_count, 8, C), jnp.float32),
            pltpu.VMEM((2, C, 9 * C), jnp.float32),
            pltpu.VMEM((C2, 9 * C), jnp.float32),
            pltpu.SemaphoreType.DMA((slots,)),
            pltpu.SemaphoreType.DMA((slots,)),
            pltpu.SemaphoreType.DMA((slots,)),
            pltpu.SemaphoreType.DMA((slots,)),
            pltpu.SemaphoreType.DMA((2,)),
        ],
        compiler_params=pltpu.CompilerParams(
            collective_id=0, has_side_effects=True, vmem_limit_bytes=60 << 20
        ),
        name="gather",
    )(packed, small_tile)


def reduce_grads(grads, sums, scale_plus, gates, hidden, slope, embedded, embed_out_t):
    row_count, batch_count = (lax.axis_size("row"), lax.axis_size("batch"))
    height = 4 * C // row_count
    width = 12 * C // batch_count
    samples = hidden.shape[0]
    outs = [
        jax.ShapeDtypeStruct((height, width), jnp.float32),
        jax.ShapeDtypeStruct((16, C), jnp.float32),
        jax.ShapeDtypeStruct((8, C), jnp.float32),
    ]
    tile = (16, C)
    most = max(row_count, batch_count)
    return pl.pallas_call(
        functools.partial(reduce_kernel, row_count, batch_count, samples),
        out_shape=outs,
        in_specs=in_vmem(10),
        out_specs=in_vmem(len(outs)),
        scratch_shapes=[
            pltpu.VMEM((row_count, height, 12 * C), jnp.bfloat16),
            pltpu.VMEM((row_count, height, 12 * C), jnp.bfloat16),
            pltpu.VMEM((batch_count, height, width), jnp.bfloat16),
            pltpu.VMEM((batch_count, height, width), jnp.bfloat16),
            pltpu.VMEM(tile, jnp.float32),
            pltpu.VMEM((row_count,) + tile, jnp.float32),
            pltpu.VMEM(tile, jnp.float32),
            pltpu.VMEM((batch_count,) + tile, jnp.float32),
            pltpu.VMEM((8, C), jnp.float32),
            pltpu.VMEM((row_count, 8, C), jnp.float32),
            pltpu.VMEM((8, C), jnp.float32),
            pltpu.VMEM((batch_count, 8, C), jnp.float32),
            pltpu.SemaphoreType.DMA((6, most)),
            pltpu.SemaphoreType.DMA((6, most)),
        ],
        compiler_params=pltpu.CompilerParams(
            collective_id=1, has_side_effects=True, vmem_limit_bytes=60 << 20
        ),
        name="reduce",
    )(*grads, sums, scale_plus, gates, hidden, slope, embedded, embed_out_t)


def adam_update(weight, gradient, first_old, second_old, step_rate, clip_factor):
    scaled = gradient * clip_factor
    first_new = BETA_ONE * first_old + (1.0 - BETA_ONE) * scaled
    second_new = BETA_TWO * second_old + (1.0 - BETA_TWO) * scaled * scaled
    corrected = (
        first_new
        / (1.0 - BETA_ONE**STEP_COUNT)
        / (jnp.sqrt(second_new / (1.0 - BETA_TWO**STEP_COUNT)) + ADAM_EPS)
    )
    return (weight - step_rate * (corrected + DECAY * weight), first_new, second_new)


def body(
    field_in,
    refine_step,
    cotangent,
    conv_weight,
    down_weight,
    embed_in_weight,
    embed_out_weight,
    small_params,
    conv_first,
    down_first,
    embed_in_first,
    embed_out_first,
    small_first,
    conv_second,
    down_second,
    embed_in_second,
    embed_out_second,
    small_second,
):
    field = to_samples(field_in)
    packed = pack_pieces(
        conv_weight.astype(jnp.bfloat16),
        down_weight.astype(jnp.bfloat16),
        embed_in_weight.astype(jnp.bfloat16),
        embed_out_weight.astype(jnp.bfloat16),
    )
    small_rounded = small_params.astype(jnp.bfloat16).astype(jnp.float32)
    gathered = gather_weights(packed, small_rounded)
    weights, small_rows = gathered[:7], gathered[7]
    embed_in_t, embed_out_t = gathered[8], gathered[9]
    small_low = small_rows[:, : small_params.shape[0]].reshape(-1)
    owned = refine_step.shape[0] // lax.axis_size("row")
    padded = -(-owned // 8) * 8
    own_steps = lax.dynamic_slice_in_dim(refine_step, lax.axis_index("row") * owned, owned, 0)
    embedded = embed_steps(own_steps)
    lanes = small_low[: 6 * C].reshape(6, C)
    bias_down = small_low[6 * C : 6 * C + C2]
    bias_hidden = small_low[6 * C + C2 : 6 * C + C2 + HID]
    bias_mod = small_low[6 * C + C2 + HID :]
    hidden_pre = jnp.dot(embedded, embed_in_t.T, precision=HIGHEST) + bias_hidden
    hidden, pull_hidden = jax.vjp(jax.nn.gelu, hidden_pre)
    slope = pull_hidden(jnp.ones_like(hidden_pre))[0]
    modulate = jnp.dot(hidden, embed_out_t.T, precision=HIGHEST) + bias_mod
    modulation = jnp.stack([1.0 + modulate[:, :C], modulate[:, C:]], axis=1)
    vectors = jnp.concatenate(
        [
            jnp.concatenate([lanes, jnp.zeros_like(lanes)], axis=1),
            bias_down[None, :],
            jnp.zeros((1, C2), jnp.float32),
        ],
        axis=0,
    )
    block_out, grad_field, grad_w1, grad_w2, grad_wd, sums = run_samples(
        field, cotangent, modulation, weights, vectors
    )
    grad_start = to_rows(grad_field)

    def lengthened(value):
        return jnp.pad(value, ((0, padded - owned), (0, 0)))

    gates = jnp.concatenate([lanes[1:2], lanes[3:4], jnp.zeros((6, C), jnp.float32)], axis=0)
    sums = jnp.pad(jnp.transpose(sums, (1, 0, 2)), ((0, 0), (0, padded - owned), (0, 0)))
    owned_grads, small_grads, norm_tile = reduce_grads(
        (grad_w1, grad_w2, grad_wd),
        sums,
        lengthened(modulation[:, 0]),
        gates,
        lengthened(hidden),
        lengthened(slope),
        lengthened(embedded),
        embed_out_t,
    )
    grad_norm = norm_tile[0, 0]
    small_len = small_params.shape[0]
    place = (lax.axis_index("batch") * lax.axis_size("row") + lax.axis_index("row")) * small_len
    owned_shards = unpack_pieces(
        owned_grads, conv_weight.shape[1], conv_weight.shape[2], embed_in_weight.shape[0]
    ) + (lax.dynamic_slice_in_dim(small_grads.reshape(-1), place, small_len, 0),)
    clip_factor = 1.0
    conv_new = adam_update(
        conv_weight, owned_shards[0], conv_first, conv_second, RATE_MATRIX, clip_factor
    )
    down_new = adam_update(
        down_weight, owned_shards[1], down_first, down_second, RATE_MATRIX, clip_factor
    )
    embed_in_new = adam_update(
        embed_in_weight, owned_shards[2], embed_in_first, embed_in_second, RATE_MATRIX, clip_factor
    )
    embed_out_new = adam_update(
        embed_out_weight,
        owned_shards[3],
        embed_out_first,
        embed_out_second,
        RATE_MATRIX,
        clip_factor,
    )
    small_new = adam_update(
        small_params, owned_shards[4], small_first, small_second, RATE_SMALL, clip_factor
    )
    return (
        block_out,
        grad_start,
        grad_norm,
        conv_new[0],
        down_new[0],
        embed_in_new[0],
        embed_out_new[0],
        small_new[0],
        conv_new[1],
        down_new[1],
        embed_in_new[1],
        embed_out_new[1],
        small_new[1],
        conv_new[2],
        down_new[2],
        embed_in_new[2],
        embed_out_new[2],
        small_new[2],
    )


def solution(mesh):
    placed = (
        P("batch", "row", None, None),
        P("batch"),
        P(("batch", "row"), None, None, None),
        P(None, "batch", "row"),
        P("batch", "row"),
        P("batch", "row"),
        P("batch", "row"),
        P(("batch", "row")),
        P(None, "batch", "row"),
        P("batch", "row"),
        P("batch", "row"),
        P("batch", "row"),
        P(("batch", "row")),
        P(None, "batch", "row"),
        P("batch", "row"),
        P("batch", "row"),
        P("batch", "row"),
        P(("batch", "row")),
    )
    return jax.shard_map(
        body,
        mesh=mesh,
        in_specs=placed,
        out_specs=(
            P(("batch", "row"), None, None, None),
            P("batch", "row", None, None),
            P(),
            P(None, "batch", "row"),
            P("batch", "row"),
            P("batch", "row"),
            P("batch", "row"),
            P(("batch", "row")),
            P(None, "batch", "row"),
            P("batch", "row"),
            P("batch", "row"),
            P("batch", "row"),
            P(("batch", "row")),
            P(None, "batch", "row"),
            P("batch", "row"),
            P("batch", "row"),
            P("batch", "row"),
            P(("batch", "row")),
        ),
        check_vma=False,
    )
```

```python
import functools
import math

import jax
import jax.numpy as jnp
import numpy as np
from jax import lax
from jax.experimental import pallas as pl
from jax.experimental.pallas import tpu as pltpu
from jax.sharding import PartitionSpec as P

C = 128
C2 = 256
EMB = 128
HID = 512
GROUPS = 8
REFINE = 4


NORM_EPS = 1e-05
BETA_ONE = 0.9
BETA_TWO = 0.999
ADAM_EPS = 1e-08
DECAY = 0.01
RATE_MATRIX = 0.05
RATE_SMALL = 0.5
CLIP_NORM = 1.0
STEP_COUNT = 10
HIGHEST = lax.Precision.HIGHEST


def embed_steps(refine_step):
    halfway = EMB // 2
    frequency = jnp.exp(-math.log(10000.0) * jnp.arange(halfway).astype(jnp.float32) / halfway)
    angles = (refine_step.astype(jnp.float32) * (1000.0 / REFINE))[:, None] * frequency[None, :]
    return jnp.concatenate([jnp.sin(angles), jnp.cos(angles)], axis=1)


MESH = pl.DeviceIdType.MESH


def greet(row_count, batch_count=1):
    row, batch = lax.axis_index("row"), lax.axis_index("batch")
    barrier = pltpu.get_barrier_semaphore()
    for step in range(1, row_count):
        pl.semaphore_signal(
            barrier,
            inc=1,
            device_id={"row": lax.rem(row + step, row_count), "batch": batch},
            device_id_type=MESH,
        )
    for step in range(1, batch_count):
        pl.semaphore_signal(
            barrier,
            inc=1,
            device_id={"row": row, "batch": lax.rem(batch + step, batch_count)},
            device_id_type=MESH,
        )
    pl.semaphore_wait(barrier, row_count + batch_count - 2)


def to_peer(axis, step, count, source, target, send_sem, recv_sem):
    row, batch = lax.axis_index("row"), lax.axis_index("batch")
    if axis == "row":
        device = {"row": lax.rem(row + step, count), "batch": batch}
    else:
        device = {"row": row, "batch": lax.rem(batch + step, count)}
    return pltpu.make_async_remote_copy(
        src_ref=source,
        dst_ref=target,
        send_sem=send_sem,
        recv_sem=recv_sem,
        device_id=device,
        device_id_type=MESH,
    )


def finish(copies):
    for copy in copies:
        copy.wait()


FIELD_COLS = 64
HALF_COLS = 32
ROOT = math.sqrt(2.0 / math.pi)
CUBIC = ROOT * 0.044715


def chunk_of(total, most):
    size = min(total, most)
    while total % size:
        size -= 1
    return size


def over(total, most, body, init):
    size = chunk_of(total, most)

    def several(step, carry):
        for inner in range(size):
            carry = body(step * size + inner, carry)
        return carry

    if size == total:
        return several(0, init)
    return lax.fori_loop(0, total // size, several, init)


def folded(values):
    return jnp.sum(values.reshape(values.shape[0] // 8, 8, values.shape[1]), axis=0)


def twice(row):
    return jnp.concatenate([row, row], axis=1)


def channel_sum(partial):
    both = partial[:, :C] + partial[:, C:]
    return jnp.sum(both, axis=0, keepdims=True)


def group_means(first, second, same_group, entries):
    stacked = jnp.concatenate([first, second, jnp.zeros((6, C), jnp.float32)], axis=0)
    totals = jnp.dot(stacked, same_group, precision=HIGHEST, preferred_element_type=jnp.float32)
    return totals[0:1] / entries, totals[1:2] / entries


def gelu_pair(values):
    square = values * values
    bend = jnp.tanh(values * (ROOT + CUBIC * square))
    half = 0.5 * values
    slope = (0.5 + 0.5 * bend) + half * (1.0 - bend * bend) * (ROOT + (3.0 * CUBIC) * square)
    return half + half * bend, slope


def put_shifted(ref, pair, values):
    for tap, shift in ((0, 1), (1, 0), (2, FIELD_COLS - 1)):
        moved = pltpu.roll(values, shift, 0) if shift else values
        ref[tap, pair + 1] = moved.astype(jnp.bfloat16)


def close_ring(ref, pairs):
    ref[:, 0, :, C:] = ref[:, pairs, :, C:]
    ref[:, pairs + 1, :, :C] = ref[:, 1, :, :C]


def windows(ref, start, count):
    rows = count * FIELD_COLS
    pieces = []
    for tap in range(3):
        pieces.append(ref[tap, pl.ds(start + 1, count)].reshape(rows, 2 * C))
        pieces.append(ref[tap, pl.ds(start, count), :, C:].reshape(rows, C))
        pieces.append(ref[tap, pl.ds(start + 2, count), :, :C].reshape(rows, C))
    return jnp.concatenate(pieces, axis=1)


def add_conv_grad(out_ref, act_ref, grad_ref, pairs):
    size = chunk_of(pairs, 8)
    rows = size * FIELD_COLS

    def body(step, carry):
        start = step * size
        grad = grad_ref[1, pl.ds(start + 1, size)].reshape(rows, 2 * C)
        product = jnp.dot(
            grad.T, windows(act_ref, start, size), preferred_element_type=jnp.float32
        )
        for tap in range(3):
            base = tap * 4 * C
            own_low = product[:C, base : base + C] + product[C:, base + C : base + 2 * C]
            up = product[C:, base : base + C] + product[:C, base + 2 * C : base + 3 * C]
            down = product[:C, base + C : base + 2 * C] + product[C:, base + 3 * C : base + 4 * C]
            for row_tap, value in ((0, up), (1, own_low), (2, down)):
                lanes = pl.ds((3 * row_tap + tap) * C, C)
                out_ref[:, lanes] = out_ref[:, lanes] + value
        return carry

    over_steps(pairs // size, body)


def over_steps(steps, body):
    if steps == 1:
        body(0, 0)
    else:
        lax.fori_loop(0, steps, body, 0)


def sample_kernel(
    pairs,
    samples,
    row_count,
    field_ref,
    cot_ref,
    mod_ref,
    fwd_one,
    back_one,
    fwd_two,
    back_two,
    down_fwd,
    down_even,
    down_odd,
    vec_ref,
    group_ref,
    out_ref,
    grad_ref,
    conv_grad_one,
    conv_grad_two,
    down_grad,
    sums_ref,
    act_one,
    act_two,
    grad_one,
    grad_two,
    slope_one,
    slope_two,
    unit_two,
    grad_mid,
    sum_even,
    sum_odd,
    grad_even,
    grad_odd,
    down_win,
    cot_win,
    x_ref,
    grad_rows,
    field_sem,
    field_sent,
    grad_sem,
    grad_sent,
):
    sample = pl.program_id(0)
    row = lax.axis_index("row")
    share = pairs // row_count

    @pl.when(sample == 0)
    def _():
        greet(row_count)

        def send_field(index, carry):
            mine = x_ref.at[index, pl.ds(row * share, share)]
            for step in range(1, row_count):
                place = lax.rem(row + step, row_count) * samples + index
                to_peer(
                    "row",
                    step,
                    row_count,
                    field_ref.at[place],
                    mine,
                    field_sent,
                    field_sem.at[index],
                ).start()
            pltpu.make_async_copy(
                field_ref.at[row * samples + index], mine, field_sem.at[index]
            ).start()
            return carry

        lax.fori_loop(0, samples, send_field, 0)

    def send_grad(index):
        target = grad_ref.at[row * samples + index]
        for step in range(1, row_count):
            place = lax.rem(row + step, row_count) * share
            to_peer(
                "row",
                step,
                row_count,
                grad_rows.at[index, pl.ds(place, share)],
                target,
                grad_sent,
                grad_sem,
            ).start()
        pltpu.make_async_copy(
            grad_rows.at[index, pl.ds(row * share, share)], target, grad_sem
        ).start()

    @pl.when(sample > 0)
    def _():
        send_grad(sample - 1)

    pltpu.make_async_copy(x_ref.at[sample], x_ref.at[sample], field_sem.at[sample]).wait()
    entries = 2.0 * pairs * FIELD_COLS * (C // GROUPS)
    size = chunk_of(pairs, 8)
    rows = size * FIELD_COLS
    same_group = group_ref[...]
    gain_one, gain_two = vec_ref[0:1, :C], vec_ref[1:2, :C]
    shift_one, shift_two = vec_ref[2:3, :C], vec_ref[3:4, :C]
    bias_one, bias_two = twice(vec_ref[4:5, :C]), twice(vec_ref[5:6, :C])
    bias_down = vec_ref[6:7, :]
    scale_plus, offset = mod_ref[0, 0:1, :], mod_ref[0, 1:2, :]
    nothing = jnp.zeros((8, 2 * C), jnp.float32)

    @pl.when(pl.program_id(0) == 0)
    def _():
        conv_grad_one[...] = jnp.zeros_like(conv_grad_one)
        conv_grad_two[...] = jnp.zeros_like(conv_grad_two)
        down_grad[...] = jnp.zeros_like(down_grad)

    def field(pair):
        return jnp.concatenate(
            [x_ref[sample, pair, 0].astype(jnp.float32), x_ref[sample, pair, 1].astype(jnp.float32)], axis=1
        )

    def first_stats(pair, carry):
        value = field(pair)
        return carry[0] + folded(value), carry[1] + folded(value * value)

    total, squares = over(pairs, 8, first_stats, (nothing, nothing))
    mean_one, square_one = group_means(channel_sum(total), channel_sum(squares), same_group, entries)
    inverse_one = lax.rsqrt(square_one - mean_one * mean_one + NORM_EPS)
    center_one = twice(-mean_one * inverse_one)
    inverse_one = twice(inverse_one)
    gain_wide, shift_wide = twice(gain_one), twice(shift_one)

    def first_act(pair, carry):
        unit = field(pair) * inverse_one + center_one
        value, slope = gelu_pair(unit * gain_wide + shift_wide)
        put_shifted(act_one, pair, value)
        slope_one[pair] = slope
        return carry

    over(pairs, 8, first_act, 0)
    close_ring(act_one, pairs)

    def conv_one_chunk(step, carry):
        start = step * size
        value = jnp.dot(
            windows(act_one, start, size), fwd_one[...], preferred_element_type=jnp.float32
        ) + bias_one
        unit_two[pl.ds(start, size)] = value.reshape(size, FIELD_COLS, 2 * C)
        return carry[0] + folded(value), carry[1] + folded(value * value)

    total, squares = lax.fori_loop(0, pairs // size, conv_one_chunk, (nothing, nothing))
    mean_two, square_two = group_means(channel_sum(total), channel_sum(squares), same_group, entries)
    inverse_two = lax.rsqrt(square_two - mean_two * mean_two + NORM_EPS)
    center_two = twice(-mean_two * inverse_two)
    mid_gain = twice(gain_two * scale_plus)
    mid_shift = twice(shift_two * scale_plus + offset)
    inverse_two_wide = twice(inverse_two)

    def second_act(pair, carry):
        unit = unit_two[pair] * inverse_two_wide + center_two
        value, slope = gelu_pair(unit * mid_gain + mid_shift)
        put_shifted(act_two, pair, value)
        slope_two[pair] = slope
        unit_two[pair] = unit
        return carry

    over(pairs, 8, second_act, 0)
    close_ring(act_two, pairs)

    def conv_two_chunk(step, carry):
        start = step * size
        value = jnp.dot(
            windows(act_two, start, size), fwd_two[...], preferred_element_type=jnp.float32
        ) + bias_two
        value = value.reshape(size, FIELD_COLS, 2 * C)
        for half, ref in ((0, sum_even), (1, sum_odd)):
            base = x_ref[sample, pl.ds(start, size), half].astype(jnp.float32)
            ref[pl.ds(start, size)] = base + value[:, :, half * C : half * C + C]
        return carry

    over_steps(pairs // size, conv_two_chunk)

    def split_columns(pair, carry):
        even = []
        odd = []
        for ref in (sum_even, sum_odd):
            even.append(ref[pair, pl.ds(0, HALF_COLS, stride=2), :])
            odd.append(ref[pair, pl.ds(1, HALF_COLS, stride=2), :])
        even = jnp.concatenate(even, axis=1)
        odd = jnp.concatenate(odd, axis=1)
        down_win[0, pair + 1] = pltpu.roll(odd, 1, 0).astype(jnp.bfloat16)
        down_win[1, pair + 1] = even.astype(jnp.bfloat16)
        down_win[2, pair + 1] = odd.astype(jnp.bfloat16)
        cot = cot_ref[0, pair]
        wide = cot.astype(jnp.float32)
        cot_win[0, pair] = cot
        cot_win[1, pair] = pltpu.roll(wide, HALF_COLS - 1, 0).astype(jnp.bfloat16)
        return carry + folded(wide)

    cot_total = over(pairs, 8, split_columns, nothing)
    down_win[:, 0, :, C:] = down_win[:, pairs, :, C:]
    cot_win[:, pairs] = cot_win[:, 0]
    small = size * HALF_COLS

    def down_windows(start):
        pieces = [down_win[tap, pl.ds(start + 1, size)].reshape(small, 2 * C) for tap in range(3)]
        pieces += [
            down_win[tap, pl.ds(start, size), :, C:].reshape(small, C) for tap in range(3)
        ]
        return jnp.concatenate(pieces, axis=1)

    def down_chunk(step, carry):
        start = step * size
        lhs = down_windows(start)
        value = jnp.dot(lhs, down_fwd[...], preferred_element_type=jnp.float32) + bias_down
        out_ref[0, pl.ds(start, size)] = value.reshape(size, HALF_COLS, 2 * C).astype(jnp.bfloat16)
        here = cot_win[0, pl.ds(start, size)].reshape(small, 2 * C)
        product = jnp.dot(here.T, lhs, preferred_element_type=jnp.float32)
        for position in range(9):
            row_tap, tap = DOWN_ORDER[position]
            lanes = pl.ds((3 * row_tap + tap) * C, C)
            down_grad[:, lanes] = down_grad[:, lanes] + product[:, position * C : position * C + C]
        pieces = [
            cot_win[shift, pl.ds(start + below, size)].reshape(small, 2 * C)
            for below in range(2)
            for shift in range(2)
        ]
        even = jnp.dot(
            jnp.concatenate([pieces[0], pieces[2]], axis=1),
            down_even[...],
            preferred_element_type=jnp.float32,
        ).reshape(size, HALF_COLS, 2 * C)
        odd = jnp.dot(
            jnp.concatenate(pieces, axis=1), down_odd[...], preferred_element_type=jnp.float32
        ).reshape(size, HALF_COLS, 2 * C)
        for half, ref in ((0, grad_even), (1, grad_odd)):
            lanes = slice(half * C, half * C + C)
            for inner in range(size):
                ref[start + inner, pl.ds(0, HALF_COLS, stride=2), :] = even[inner, :, lanes]
                ref[start + inner, pl.ds(1, HALF_COLS, stride=2), :] = odd[inner, :, lanes]
        return carry

    over_steps(pairs // size, down_chunk)

    def second_grad(pair, carry):
        value = jnp.concatenate([grad_even[pair], grad_odd[pair]], axis=1)
        put_shifted(grad_two, pair, value)
        return carry + folded(value.astype(jnp.bfloat16).astype(jnp.float32))

    bias_two_total = over(pairs, 8, second_grad, nothing)
    close_ring(grad_two, pairs)
    add_conv_grad(conv_grad_two, act_two, grad_two, pairs)

    def back_two_chunk(step, carry):
        start = step * size
        value = jnp.dot(
            windows(grad_two, start, size), back_two[...], preferred_element_type=jnp.float32
        )
        value = value * slope_two[pl.ds(start, size)].reshape(rows, 2 * C)
        grad_mid[pl.ds(start, size)] = value.reshape(size, FIELD_COLS, 2 * C)
        unit = unit_two[pl.ds(start, size)].reshape(rows, 2 * C)
        return carry[0] + folded(value), carry[1] + folded(value * unit)

    total, cross = lax.fori_loop(0, pairs // size, back_two_chunk, (nothing, nothing))
    mid_total, mid_cross = channel_sum(total), channel_sum(cross)
    factor = scale_plus * gain_two
    mean_grad, mean_cross = group_means(
        mid_total * factor, mid_cross * factor, same_group, entries
    )
    from_mid = twice(inverse_two * factor)
    from_unit = twice(inverse_two * mean_cross)
    from_mean = twice(inverse_two * mean_grad)

    def first_grad(pair, carry):
        value = grad_mid[pair] * from_mid - from_mean - unit_two[pair] * from_unit
        put_shifted(grad_one, pair, value)
        return carry + folded(value.astype(jnp.bfloat16).astype(jnp.float32))

    bias_one_total = over(pairs, 8, first_grad, nothing)
    close_ring(grad_one, pairs)
    add_conv_grad(conv_grad_one, act_one, grad_one, pairs)

    def back_one_chunk(step, carry):
        start = step * size
        value = jnp.dot(
            windows(grad_one, start, size), back_one[...], preferred_element_type=jnp.float32
        )
        value = value * slope_one[pl.ds(start, size)].reshape(rows, 2 * C)
        grad_mid[pl.ds(start, size)] = value.reshape(size, FIELD_COLS, 2 * C)
        base = jnp.concatenate(
            [
                x_ref[sample, pl.ds(start, size), half].astype(jnp.float32).reshape(rows, C)
                for half in range(2)
            ],
            axis=1,
        )
        unit = base * inverse_one + center_one
        return carry[0] + folded(value), carry[1] + folded(value * unit)

    total, cross = lax.fori_loop(0, pairs // size, back_one_chunk, (nothing, nothing))
    pre_total, pre_cross = channel_sum(total), channel_sum(cross)
    mean_grad, mean_cross = group_means(
        pre_total * gain_one, pre_cross * gain_one, same_group, entries
    )
    from_pre = inverse_one * gain_wide
    from_unit_one = inverse_one * twice(mean_cross)
    from_mean_one = inverse_one * twice(mean_grad)

    def last(pair, carry):
        unit = field(pair) * inverse_one + center_one
        summed = jnp.concatenate([grad_even[pair], grad_odd[pair]], axis=1)
        value = (summed + (grad_mid[pair] * from_pre - from_mean_one - unit * from_unit_one)).astype(
            jnp.bfloat16
        )
        grad_rows[sample, pair, 0] = value[:, :C]
        grad_rows[sample, pair, 1] = value[:, C:]
        return carry

    over(pairs, 8, last, 0)
    cot_sums = jnp.sum(cot_total, axis=0, keepdims=True)
    sums_ref[0] = jnp.concatenate(
        [
            mid_cross,
            mid_total,
            pre_cross,
            pre_total,
            channel_sum(bias_one_total),
            channel_sum(bias_two_total),
            cot_sums[:, :C],
            cot_sums[:, C:],
        ],
        axis=0,
    )

    @pl.when(sample == samples - 1)
    def _():
        send_grad(sample)
        pltpu.make_async_copy(grad_ref, grad_ref, grad_sem).wait()
        others = pl.ds(0, pairs - share)
        for ref, sem in ((x_ref, field_sent), (grad_rows, grad_sent)):
            pltpu.make_async_copy(ref.at[:, others], ref.at[:, others], sem).wait()


DOWN_ORDER = ((1, 0), (2, 0), (1, 1), (2, 1), (1, 2), (2, 2), (0, 0), (0, 1), (0, 2))


def run_samples(field_in, cotangent, modulation, weights, vectors):
    row_count = lax.axis_size("row")
    samples = cotangent.shape[0]
    pairs = field_in.shape[1] // 2 * row_count
    share = pairs // row_count
    halves = field_in.reshape(field_in.shape[0], share, 2, FIELD_COLS, C)
    same_group = jnp.asarray(
        np.kron(np.eye(GROUPS), np.ones((C // GROUPS, C // GROUPS))), jnp.float32
    )

    def whole(array):
        return pl.BlockSpec(array.shape, lambda i: (0,) * array.ndim, pipeline_mode=pl.Buffered(1))

    def per_sample(array):
        rank = len(array.shape)
        return pl.BlockSpec((1,) + array.shape[1:], lambda i: (i,) + (0,) * (rank - 1))

    constants = tuple(weights) + (vectors, same_group)
    outs = (
        jax.ShapeDtypeStruct((samples, pairs, HALF_COLS, C2), jnp.bfloat16),
        jax.ShapeDtypeStruct(halves.shape, jnp.bfloat16),
        jax.ShapeDtypeStruct((C, 9 * C), jnp.float32),
        jax.ShapeDtypeStruct((C, 9 * C), jnp.float32),
        jax.ShapeDtypeStruct((C2, 9 * C), jnp.float32),
        jax.ShapeDtypeStruct((samples, 8, C), jnp.float32),
    )
    anywhere = pl.BlockSpec(memory_space=pl.ANY)
    ring = pltpu.VMEM((3, pairs + 2, FIELD_COLS, 2 * C), jnp.bfloat16)
    wide = pltpu.VMEM((pairs, FIELD_COLS, 2 * C), jnp.float32)
    half = pltpu.VMEM((pairs, FIELD_COLS, C), jnp.float32)
    result = pl.pallas_call(
        functools.partial(sample_kernel, pairs, samples, row_count),
        grid=(samples,),
        in_specs=[anywhere, per_sample(cotangent), per_sample(modulation)]
        + [whole(array) for array in constants],
        out_specs=[per_sample(outs[0]), anywhere]
        + [pl.BlockSpec(out.shape, lambda i: (0, 0)) for out in outs[2:5]]
        + [per_sample(outs[5])],
        out_shape=outs,
        scratch_shapes=[ring] * 4
        + [wide] * 4
        + [half] * 4
        + [
            pltpu.VMEM((3, pairs + 1, HALF_COLS, 2 * C), jnp.bfloat16),
            pltpu.VMEM((2, pairs + 1, HALF_COLS, C2), jnp.bfloat16),
            pltpu.VMEM((samples, pairs, 2, FIELD_COLS, C), jnp.bfloat16),
            pltpu.VMEM((samples, pairs, 2, FIELD_COLS, C), jnp.bfloat16),
            pltpu.SemaphoreType.DMA((samples,)),
            pltpu.SemaphoreType.DMA,
            pltpu.SemaphoreType.DMA,
            pltpu.SemaphoreType.DMA,
        ],
        compiler_params=pltpu.CompilerParams(
            dimension_semantics=("arbitrary",),
            vmem_limit_bytes=60 << 20,
            collective_id=2,
            has_side_effects=True,
        ),
        name="samples",
    )(halves, cotangent, modulation, *constants)
    return (result[0], result[1].reshape(field_in.shape)) + tuple(result[2:])


def gather_kernel(
    row_count,
    batch_count,
    shard_ref,
    small_ref,
    fwd_one,
    back_one,
    fwd_two,
    back_two,
    down_fwd,
    down_even,
    down_odd,
    small_out,
    embed_in_t,
    embed_out_ref,
    shards,
    smalls,
    conv_t,
    down_t,
    send_main,
    recv_main,
    send_small,
    recv_small,
    local_sem,
):
    row, batch = lax.axis_index("row"), lax.axis_index("batch")
    greet(row_count, batch_count)
    own_main = pltpu.make_async_copy(shard_ref, shards.at[row, batch], local_sem.at[0])
    own_small = pltpu.make_async_copy(small_ref, smalls.at[row, batch], local_sem.at[1])
    own_main.start()
    own_small.start()
    copies = []
    for step in range(1, batch_count):
        copies.append(
            to_peer(
                "batch",
                step,
                batch_count,
                shard_ref,
                shards.at[row, batch],
                send_main.at[step],
                recv_main.at[step],
            )
        )
        copies.append(
            to_peer(
                "batch",
                step,
                batch_count,
                small_ref,
                smalls.at[row, batch],
                send_small.at[step],
                recv_small.at[step],
            )
        )
    for copy in copies:
        copy.start()
    own_main.wait()
    own_small.wait()
    finish(copies)
    copies = []
    for step in range(1, row_count):
        slot = batch_count + step
        copies.append(
            to_peer(
                "row",
                step,
                row_count,
                shards.at[row],
                shards.at[row],
                send_main.at[slot],
                recv_main.at[slot],
            )
        )
        copies.append(
            to_peer(
                "row",
                step,
                row_count,
                smalls.at[row],
                smalls.at[row],
                send_small.at[slot],
                recv_small.at[slot],
            )
        )
    for copy in copies:
        copy.start()
    finish(copies)
    depth, share, wide_share = 9 * C // batch_count, C // row_count, C2 // row_count
    height = 2 * share + wide_share
    embed_share, hidden_share = EMB // batch_count, HID // batch_count
    for place in range(row_count):
        parts = [shards[place, part].astype(jnp.float32) for part in range(batch_count)]
        main = jnp.concatenate([part[:, :depth] for part in parts], axis=1)
        for which in range(2):
            conv_t[which, place * share : place * share + share, :] = main[
                which * share : which * share + share
            ]
        down_t[place * wide_share : place * wide_share + wide_share, :] = main[2 * share :]
        embed_in_t[place * height : place * height + height, :] = jnp.concatenate(
            [part[:, depth : depth + embed_share] for part in parts], axis=1
        )
        tail = depth + embed_share
        half_rows, half_lanes = height // 2, hidden_share // 2
        lanes = []
        for part in parts:
            lanes.append(part[:half_rows, tail : tail + half_lanes])
            lanes.append(part[half_rows:, tail : tail + half_lanes])
        embed_out_ref[place * half_rows : place * half_rows + half_rows, :] = jnp.concatenate(
            lanes, axis=1
        )
        for part in range(batch_count):
            small_out[part * row_count + place : part * row_count + place + 1, :] = smalls[
                place, part, 0:1, :
            ]
    for which, forward, back in ((0, fwd_one, back_one), (1, fwd_two, back_two)):
        zero = jnp.zeros((C, C), jnp.bfloat16)
        for tap in range(3):
            direct = [
                conv_t[which, :, (3 * row_tap + tap) * C : (3 * row_tap + tap) * C + C]
                for row_tap in range(3)
            ]
            fill_blocks(forward, tap, [block.T.astype(jnp.bfloat16) for block in direct], zero)
            fill_blocks(
                back, 2 - tap, [block.astype(jnp.bfloat16) for block in direct[::-1]], zero
            )
    zero = jnp.zeros((C2, C), jnp.bfloat16)
    back = {}
    for position in range(9):
        row_tap, tap = DOWN_ORDER[position]
        block = down_t[:, (3 * row_tap + tap) * C : (3 * row_tap + tap) * C + C]
        down_fwd[position * C : position * C + C, :] = block.T.astype(jnp.bfloat16)
        back[row_tap, tap] = block.astype(jnp.bfloat16)
    even = ((back[1, 1], back[2, 1]), (zero, back[0, 1]))
    odd = (
        (back[1, 2], back[2, 2]),
        (back[1, 0], back[2, 0]),
        (zero, back[0, 2]),
        (zero, back[0, 0]),
    )
    for ref, table in ((down_even, even), (down_odd, odd)):
        for position, (left, right) in enumerate(table):
            ref[position * C2 : position * C2 + C2, :C] = left
            ref[position * C2 : position * C2 + C2, C:] = right


def fill_blocks(ref, tap, blocks, zero):
    table = (
        (blocks[1], blocks[0]),
        (blocks[2], blocks[1]),
        (blocks[0], zero),
        (zero, blocks[2]),
    )
    for position, (left, right) in enumerate(table):
        base = (4 * tap + position) * C
        ref[base : base + C, :C] = left
        ref[base : base + C, C:] = right


def dot_last(lhs, rhs):
    return lax.dot_general(
        lhs,
        rhs,
        (((1,), (1,)), ((), ())),
        precision=HIGHEST,
        preferred_element_type=jnp.float32,
    )


def dot_first(lhs, rhs):
    return lax.dot_general(
        lhs,
        rhs,
        (((0,), (0,)), ((), ())),
        precision=HIGHEST,
        preferred_element_type=jnp.float32,
    )


def reduce_kernel(
    row_count,
    batch_count,
    samples,
    grad_one,
    grad_two,
    grad_down,
    sums_ref,
    scale_ref,
    gate_ref,
    hidden_ref,
    slope_ref,
    embedded_ref,
    embed_out_ref,
    owned_ref,
    small_ref,
    norm_ref,
    row_send,
    row_take,
    batch_send,
    batch_take,
    small_send,
    small_take,
    small_next,
    small_last,
    square_send,
    square_take,
    square_next,
    square_last,
    send_sem,
    recv_sem,
):
    row, batch = lax.axis_index("row"), lax.axis_index("batch")
    depth, share, wide_share = 9 * C // batch_count, C // row_count, C2 // row_count
    height = 2 * share + wide_share
    embed_share, hidden_share = EMB // batch_count, HID // batch_count
    mid_cross, mid_total = sums_ref[0], sums_ref[1]
    gain_two, shift_two = gate_ref[0:1, :], gate_ref[1:2, :]
    scale_plus = scale_ref[...]
    grad_mod = jnp.concatenate([gain_two * mid_cross + shift_two * mid_total, mid_total], axis=1)
    grad_embed_out = dot_first(grad_mod, hidden_ref[...])
    grad_hidden = (
        jnp.dot(
            grad_mod, embed_out_ref[...], precision=HIGHEST, preferred_element_type=jnp.float32
        )
        * slope_ref[...]
    )
    grad_embed_in = dot_first(grad_hidden, embedded_ref[...])

    def down_sum(value):
        return jnp.sum(value, axis=0, keepdims=True)

    small_rows = [
        down_sum(sums_ref[2]),
        down_sum(mid_cross * scale_plus),
        down_sum(sums_ref[3]),
        down_sum(mid_total * scale_plus),
    ] + [down_sum(sums_ref[place]) for place in range(4, 8)]
    hidden_total, mod_total = down_sum(grad_hidden), down_sum(grad_mod)
    small_rows += [hidden_total[:, lane : lane + C] for lane in range(0, HID, C)]
    small_rows += [mod_total[:, lane : lane + C] for lane in range(0, 2 * C, C)]
    small_rows.append(jnp.zeros((2, C), jnp.float32))
    small_send[...] = jnp.concatenate(small_rows, axis=0)
    half_rows = height // 2
    for place in range(row_count):
        low, high = place * share, place * share + share
        row_send[place, :, : 9 * C] = jnp.concatenate(
            [
                grad_one[low:high],
                grad_two[low:high],
                grad_down[place * wide_share : place * wide_share + wide_share],
            ],
            axis=0,
        ).astype(jnp.bfloat16)
        row_send[place, :, 9 * C : 10 * C] = grad_embed_in[
            place * height : place * height + height
        ].astype(jnp.bfloat16)
        piece = grad_embed_out[place * half_rows : place * half_rows + half_rows]
        row_send[place, :, 10 * C :] = jnp.concatenate(
            [piece[:, : HID // 2], piece[:, HID // 2 :]], axis=0
        ).astype(jnp.bfloat16)
    greet(row_count, batch_count)
    copies = []
    for step in range(1, row_count):
        copies.append(
            to_peer(
                "row",
                step,
                row_count,
                row_send.at[lax.rem(row + step, row_count)],
                row_take.at[step],
                send_sem.at[0, step],
                recv_sem.at[0, step],
            )
        )
        copies.append(
            to_peer(
                "row",
                step,
                row_count,
                small_send,
                small_take.at[step],
                send_sem.at[1, step],
                recv_sem.at[1, step],
            )
        )
    for copy in copies:
        copy.start()
    total = row_send[row].astype(jnp.float32)
    finish(copies)
    small_total = small_send[...]
    for step in range(1, row_count):
        total = total + row_take[step].astype(jnp.float32)
        small_total = small_total + small_take[step]
    small_next[...] = small_total
    for part in range(batch_count):
        per_half = batch_count // 2
        rows = slice(0, half_rows) if part < per_half else slice(half_rows, height)
        base = 10 * C + hidden_share * (part % per_half)
        piece = total[rows, base : base + hidden_share]
        batch_send[part] = jnp.concatenate(
            [
                total[:, part * depth : part * depth + depth],
                total[:, 9 * C + part * embed_share : 9 * C + part * embed_share + embed_share],
                jnp.concatenate([piece[:, : hidden_share // 2], piece[:, hidden_share // 2 :]], axis=0),
            ],
            axis=1,
        ).astype(jnp.bfloat16)
    copies = []
    for step in range(1, batch_count):
        copies.append(
            to_peer(
                "batch",
                step,
                batch_count,
                batch_send.at[lax.rem(batch + step, batch_count)],
                batch_take.at[step],
                send_sem.at[2, step],
                recv_sem.at[2, step],
            )
        )
        copies.append(
            to_peer(
                "batch",
                step,
                batch_count,
                small_next,
                small_last.at[step],
                send_sem.at[3, step],
                recv_sem.at[3, step],
            )
        )
    for copy in copies:
        copy.start()
    owned = batch_send[batch].astype(jnp.float32)
    finish(copies)
    small_total = small_next[...]
    for step in range(1, batch_count):
        owned = owned + batch_take[step].astype(jnp.float32)
        small_total = small_total + small_last[step]
    squares = jnp.sum(jnp.sum(owned * owned, axis=0, keepdims=True), axis=1, keepdims=True)
    square_send[...] = jnp.broadcast_to(squares, (8, C))
    copies = [
        to_peer(
            "row",
            step,
            row_count,
            square_send,
            square_take.at[step],
            send_sem.at[4, step],
            recv_sem.at[4, step],
        )
        for step in range(1, row_count)
    ]
    for copy in copies:
        copy.start()
    finish(copies)
    squares = square_send[...]
    for step in range(1, row_count):
        squares = squares + square_take[step]
    square_next[...] = squares
    copies = [
        to_peer(
            "batch",
            step,
            batch_count,
            square_next,
            square_last.at[step],
            send_sem.at[5, step],
            recv_sem.at[5, step],
        )
        for step in range(1, batch_count)
    ]
    for copy in copies:
        copy.start()
    finish(copies)
    squares = square_next[...]
    for step in range(1, batch_count):
        squares = squares + square_last[step]
    small_squares = jnp.sum(
        jnp.sum(small_total * small_total, axis=0, keepdims=True), axis=1, keepdims=True
    )
    norm = jnp.sqrt(squares + small_squares)
    clip = jnp.minimum(1.0, CLIP_NORM / (norm + 1e-06))[0:1, 0:1]
    norm_ref[...] = norm
    owned_ref[...] = owned * clip
    small_ref[...] = small_total * clip


def pack_pieces(conv, down, embed_in, embed_out):
    half = embed_out.shape[0] // 2
    tall = jnp.concatenate([embed_out[:half].T, embed_out[half:].T], axis=0)
    return jnp.concatenate(
        [jnp.concatenate([conv[0].T, conv[1].T, down.T], axis=0), embed_in.T, tall], axis=1
    )


def unpack_pieces(owned, depth, share, embed_share):
    height, half = owned.shape[0], owned.shape[0] // 2
    conv = jnp.stack([owned[:share, :depth].T, owned[share : 2 * share, :depth].T])
    down = owned[2 * share :, :depth].T
    embed_in = owned[:, depth : depth + embed_share].T
    tall = owned[:, depth + embed_share :]
    embed_out = jnp.concatenate([tall[:half].T, tall[half:].T], axis=0)
    return conv, down, embed_in, embed_out


def in_vmem(count):
    return [pl.BlockSpec(memory_space=pltpu.VMEM)] * count


def gather_weights(packed, small):
    row_count, batch_count = (lax.axis_size("row"), lax.axis_size("batch"))
    small_tile = jnp.pad(small[None, :], ((0, 7), (0, C - small.shape[0])))
    outs = (
        [jax.ShapeDtypeStruct((12 * C, 2 * C), jnp.bfloat16)] * 4
        + [
            jax.ShapeDtypeStruct((9 * C, C2), jnp.bfloat16),
            jax.ShapeDtypeStruct((2 * C2, 2 * C), jnp.bfloat16),
            jax.ShapeDtypeStruct((4 * C2, 2 * C), jnp.bfloat16),
        ]
        + [
            jax.ShapeDtypeStruct((row_count * batch_count, C), jnp.float32),
            jax.ShapeDtypeStruct((HID, EMB), jnp.float32),
            jax.ShapeDtypeStruct((2 * C, HID), jnp.float32),
        ]
    )
    slots = row_count + batch_count
    return pl.pallas_call(
        functools.partial(gather_kernel, row_count, batch_count),
        out_shape=outs,
        in_specs=in_vmem(2),
        out_specs=in_vmem(len(outs)),
        scratch_shapes=[
            pltpu.VMEM((row_count, batch_count) + packed.shape, jnp.bfloat16),
            pltpu.VMEM((row_count, batch_count, 8, C), jnp.float32),
            pltpu.VMEM((2, C, 9 * C), jnp.float32),
            pltpu.VMEM((C2, 9 * C), jnp.float32),
            pltpu.SemaphoreType.DMA((slots,)),
            pltpu.SemaphoreType.DMA((slots,)),
            pltpu.SemaphoreType.DMA((slots,)),
            pltpu.SemaphoreType.DMA((slots,)),
            pltpu.SemaphoreType.DMA((2,)),
        ],
        compiler_params=pltpu.CompilerParams(
            collective_id=0, has_side_effects=True, vmem_limit_bytes=60 << 20
        ),
        name="gather",
    )(packed, small_tile)


def reduce_grads(grads, sums, scale_plus, gates, hidden, slope, embedded, embed_out_t):
    row_count, batch_count = (lax.axis_size("row"), lax.axis_size("batch"))
    height = 4 * C // row_count
    width = 12 * C // batch_count
    samples = hidden.shape[0]
    outs = [
        jax.ShapeDtypeStruct((height, width), jnp.float32),
        jax.ShapeDtypeStruct((16, C), jnp.float32),
        jax.ShapeDtypeStruct((8, C), jnp.float32),
    ]
    tile = (16, C)
    most = max(row_count, batch_count)
    return pl.pallas_call(
        functools.partial(reduce_kernel, row_count, batch_count, samples),
        out_shape=outs,
        in_specs=in_vmem(10),
        out_specs=in_vmem(len(outs)),
        scratch_shapes=[
            pltpu.VMEM((row_count, height, 12 * C), jnp.bfloat16),
            pltpu.VMEM((row_count, height, 12 * C), jnp.bfloat16),
            pltpu.VMEM((batch_count, height, width), jnp.bfloat16),
            pltpu.VMEM((batch_count, height, width), jnp.bfloat16),
            pltpu.VMEM(tile, jnp.float32),
            pltpu.VMEM((row_count,) + tile, jnp.float32),
            pltpu.VMEM(tile, jnp.float32),
            pltpu.VMEM((batch_count,) + tile, jnp.float32),
            pltpu.VMEM((8, C), jnp.float32),
            pltpu.VMEM((row_count, 8, C), jnp.float32),
            pltpu.VMEM((8, C), jnp.float32),
            pltpu.VMEM((batch_count, 8, C), jnp.float32),
            pltpu.SemaphoreType.DMA((6, most)),
            pltpu.SemaphoreType.DMA((6, most)),
        ],
        compiler_params=pltpu.CompilerParams(
            collective_id=1, has_side_effects=True, vmem_limit_bytes=60 << 20
        ),
        name="reduce",
    )(*grads, sums, scale_plus, gates, hidden, slope, embedded, embed_out_t)


def adam_update(weight, gradient, first_old, second_old, step_rate, clip_factor):
    scaled = gradient * clip_factor
    first_new = BETA_ONE * first_old + (1.0 - BETA_ONE) * scaled
    second_new = BETA_TWO * second_old + (1.0 - BETA_TWO) * scaled * scaled
    corrected = (
        first_new
        / (1.0 - BETA_ONE**STEP_COUNT)
        / (jnp.sqrt(second_new / (1.0 - BETA_TWO**STEP_COUNT)) + ADAM_EPS)
    )
    return (weight - step_rate * (corrected + DECAY * weight), first_new, second_new)


def body(
    field_in,
    refine_step,
    cotangent,
    conv_weight,
    down_weight,
    embed_in_weight,
    embed_out_weight,
    small_params,
    conv_first,
    down_first,
    embed_in_first,
    embed_out_first,
    small_first,
    conv_second,
    down_second,
    embed_in_second,
    embed_out_second,
    small_second,
):
    packed = pack_pieces(
        conv_weight.astype(jnp.bfloat16),
        down_weight.astype(jnp.bfloat16),
        embed_in_weight.astype(jnp.bfloat16),
        embed_out_weight.astype(jnp.bfloat16),
    )
    small_rounded = small_params.astype(jnp.bfloat16).astype(jnp.float32)
    gathered = gather_weights(packed, small_rounded)
    weights, small_rows = gathered[:7], gathered[7]
    embed_in_t, embed_out_t = gathered[8], gathered[9]
    small_low = small_rows[:, : small_params.shape[0]].reshape(-1)
    owned = refine_step.shape[0] // lax.axis_size("row")
    padded = -(-owned // 8) * 8
    own_steps = lax.dynamic_slice_in_dim(refine_step, lax.axis_index("row") * owned, owned, 0)
    embedded = embed_steps(own_steps)
    lanes = small_low[: 6 * C].reshape(6, C)
    bias_down = small_low[6 * C : 6 * C + C2]
    bias_hidden = small_low[6 * C + C2 : 6 * C + C2 + HID]
    bias_mod = small_low[6 * C + C2 + HID :]
    hidden_pre = jnp.dot(embedded, embed_in_t.T, precision=HIGHEST) + bias_hidden
    hidden, pull_hidden = jax.vjp(jax.nn.gelu, hidden_pre)
    slope = pull_hidden(jnp.ones_like(hidden_pre))[0]
    modulate = jnp.dot(hidden, embed_out_t.T, precision=HIGHEST) + bias_mod
    modulation = jnp.stack([1.0 + modulate[:, :C], modulate[:, C:]], axis=1)
    vectors = jnp.concatenate(
        [
            jnp.concatenate([lanes, jnp.zeros_like(lanes)], axis=1),
            bias_down[None, :],
            jnp.zeros((1, C2), jnp.float32),
        ],
        axis=0,
    )
    block_out, grad_start, grad_w1, grad_w2, grad_wd, sums = run_samples(
        field_in, cotangent, modulation, weights, vectors
    )

    def lengthened(value):
        return jnp.pad(value, ((0, padded - owned), (0, 0)))

    gates = jnp.concatenate([lanes[1:2], lanes[3:4], jnp.zeros((6, C), jnp.float32)], axis=0)
    sums = jnp.pad(jnp.transpose(sums, (1, 0, 2)), ((0, 0), (0, padded - owned), (0, 0)))
    owned_grads, small_grads, norm_tile = reduce_grads(
        (grad_w1, grad_w2, grad_wd),
        sums,
        lengthened(modulation[:, 0]),
        gates,
        lengthened(hidden),
        lengthened(slope),
        lengthened(embedded),
        embed_out_t,
    )
    grad_norm = norm_tile[0, 0]
    small_len = small_params.shape[0]
    place = (lax.axis_index("batch") * lax.axis_size("row") + lax.axis_index("row")) * small_len
    owned_shards = unpack_pieces(
        owned_grads, conv_weight.shape[1], conv_weight.shape[2], embed_in_weight.shape[0]
    ) + (lax.dynamic_slice_in_dim(small_grads.reshape(-1), place, small_len, 0),)
    clip_factor = 1.0
    conv_new = adam_update(
        conv_weight, owned_shards[0], conv_first, conv_second, RATE_MATRIX, clip_factor
    )
    down_new = adam_update(
        down_weight, owned_shards[1], down_first, down_second, RATE_MATRIX, clip_factor
    )
    embed_in_new = adam_update(
        embed_in_weight, owned_shards[2], embed_in_first, embed_in_second, RATE_MATRIX, clip_factor
    )
    embed_out_new = adam_update(
        embed_out_weight,
        owned_shards[3],
        embed_out_first,
        embed_out_second,
        RATE_MATRIX,
        clip_factor,
    )
    small_new = adam_update(
        small_params, owned_shards[4], small_first, small_second, RATE_SMALL, clip_factor
    )
    return (
        block_out,
        grad_start,
        grad_norm,
        conv_new[0],
        down_new[0],
        embed_in_new[0],
        embed_out_new[0],
        small_new[0],
        conv_new[1],
        down_new[1],
        embed_in_new[1],
        embed_out_new[1],
        small_new[1],
        conv_new[2],
        down_new[2],
        embed_in_new[2],
        embed_out_new[2],
        small_new[2],
    )


def solution(mesh):
    placed = (
        P("batch", "row", None, None),
        P("batch"),
        P(("batch", "row"), None, None, None),
        P(None, "batch", "row"),
        P("batch", "row"),
        P("batch", "row"),
        P("batch", "row"),
        P(("batch", "row")),
        P(None, "batch", "row"),
        P("batch", "row"),
        P("batch", "row"),
        P("batch", "row"),
        P(("batch", "row")),
        P(None, "batch", "row"),
        P("batch", "row"),
        P("batch", "row"),
        P("batch", "row"),
        P(("batch", "row")),
    )
    return jax.shard_map(
        body,
        mesh=mesh,
        in_specs=placed,
        out_specs=(
            P(("batch", "row"), None, None, None),
            P("batch", "row", None, None),
            P(),
            P(None, "batch", "row"),
            P("batch", "row"),
            P("batch", "row"),
            P("batch", "row"),
            P(("batch", "row")),
            P(None, "batch", "row"),
            P("batch", "row"),
            P("batch", "row"),
            P("batch", "row"),
            P(("batch", "row")),
            P(None, "batch", "row"),
            P("batch", "row"),
            P("batch", "row"),
            P("batch", "row"),
            P(("batch", "row")),
        ),
        check_vma=False,
    )
```

```python
import functools
import math

import jax
import jax.numpy as jnp
import numpy as np
from jax import lax
from jax.experimental import pallas as pl
from jax.experimental.pallas import tpu as pltpu
from jax.sharding import PartitionSpec as P

C = 128
C2 = 256
EMB = 128
HID = 512
GROUPS = 8
REFINE = 4


NORM_EPS = 1e-05
BETA_ONE = 0.9
BETA_TWO = 0.999
ADAM_EPS = 1e-08
DECAY = 0.01
RATE_MATRIX = 0.05
RATE_SMALL = 0.5
CLIP_NORM = 1.0
STEP_COUNT = 10
HIGHEST = lax.Precision.HIGHEST


def embed_steps(refine_step):
    halfway = EMB // 2
    frequency = jnp.exp(-math.log(10000.0) * jnp.arange(halfway).astype(jnp.float32) / halfway)
    angles = (refine_step.astype(jnp.float32) * (1000.0 / REFINE))[:, None] * frequency[None, :]
    return jnp.concatenate([jnp.sin(angles), jnp.cos(angles)], axis=1)


MESH = pl.DeviceIdType.MESH


def greet(row_count, batch_count=1):
    row, batch = lax.axis_index("row"), lax.axis_index("batch")
    barrier = pltpu.get_barrier_semaphore()
    for step in range(1, row_count):
        pl.semaphore_signal(
            barrier,
            inc=1,
            device_id={"row": lax.rem(row + step, row_count), "batch": batch},
            device_id_type=MESH,
        )
    for step in range(1, batch_count):
        pl.semaphore_signal(
            barrier,
            inc=1,
            device_id={"row": row, "batch": lax.rem(batch + step, batch_count)},
            device_id_type=MESH,
        )
    pl.semaphore_wait(barrier, row_count + batch_count - 2)


def to_peer(axis, step, count, source, target, send_sem, recv_sem):
    row, batch = lax.axis_index("row"), lax.axis_index("batch")
    if axis == "row":
        device = {"row": lax.rem(row + step, count), "batch": batch}
    else:
        device = {"row": row, "batch": lax.rem(batch + step, count)}
    return pltpu.make_async_remote_copy(
        src_ref=source,
        dst_ref=target,
        send_sem=send_sem,
        recv_sem=recv_sem,
        device_id=device,
        device_id_type=MESH,
    )


def finish(copies):
    for copy in copies:
        copy.wait()


FIELD_COLS = 64
HALF_COLS = 32
ROOT = math.sqrt(2.0 / math.pi)
CUBIC = ROOT * 0.044715


def chunk_of(total, most):
    size = min(total, most)
    while total % size:
        size -= 1
    return size


def over(total, most, body, init):
    size = chunk_of(total, most)

    def several(step, carry):
        for inner in range(size):
            carry = body(step * size + inner, carry)
        return carry

    if size == total:
        return several(0, init)
    return lax.fori_loop(0, total // size, several, init)


def folded(values):
    return jnp.sum(values.reshape(values.shape[0] // 8, 8, values.shape[1]), axis=0)


def twice(row):
    return jnp.concatenate([row, row], axis=1)


def channel_sum(partial):
    both = partial[:, :C] + partial[:, C:]
    return jnp.sum(both, axis=0, keepdims=True)


def group_means(first, second, same_group, entries):
    stacked = jnp.concatenate([first, second, jnp.zeros((6, C), jnp.float32)], axis=0)
    totals = jnp.dot(stacked, same_group, precision=HIGHEST, preferred_element_type=jnp.float32)
    return totals[0:1] / entries, totals[1:2] / entries


def gelu_pair(values):
    square = values * values
    weight = 0.5 + 0.5 * jnp.tanh(values * (ROOT + CUBIC * square))
    result = values * weight
    slope = weight + (result - result * weight) * (2.0 * ROOT + (6.0 * CUBIC) * square)
    return result, slope


def put_shifted(ref, pair, values):
    for tap, shift in ((0, 1), (1, 0), (2, FIELD_COLS - 1)):
        moved = pltpu.roll(values, shift, 0) if shift else values
        ref[tap, pair + 1] = moved.astype(jnp.bfloat16)


def close_ring(ref, pairs):
    ref[:, 0, :, C:] = ref[:, pairs, :, C:]
    ref[:, pairs + 1, :, :C] = ref[:, 1, :, :C]


def windows(ref, start, count):
    rows = count * FIELD_COLS
    pieces = []
    for tap in range(3):
        pieces.append(ref[tap, pl.ds(start + 1, count)].reshape(rows, 2 * C))
        pieces.append(ref[tap, pl.ds(start, count), :, C:].reshape(rows, C))
        pieces.append(ref[tap, pl.ds(start + 2, count), :, :C].reshape(rows, C))
    return jnp.concatenate(pieces, axis=1)


def over_steps(steps, body, init=0):
    if steps == 1:
        return body(0, init)
    return lax.fori_loop(0, steps, body, init)


def add_conv_grad(out_ref, act_ref, grad_ref, pairs):
    size = chunk_of(pairs, 8)
    rows = size * FIELD_COLS

    def body(step, carry):
        start = step * size
        grad = grad_ref[1, pl.ds(start + 1, size)].reshape(rows, 2 * C)
        product = jnp.dot(
            grad.T, windows(act_ref, start, size), preferred_element_type=jnp.float32
        )
        for tap in range(3):
            base = tap * 4 * C
            middle = product[:C, base : base + C] + product[C:, base + C : base + 2 * C]
            up = product[C:, base : base + C] + product[:C, base + 2 * C : base + 3 * C]
            down = product[:C, base + C : base + 2 * C] + product[C:, base + 3 * C : base + 4 * C]
            for row_tap, value in ((0, up), (1, middle), (2, down)):
                lanes = pl.ds((3 * row_tap + tap) * C, C)
                out_ref[:, lanes] = out_ref[:, lanes] + value
        return carry

    over_steps(pairs // size, body)


class Sample:
    def __init__(self, pairs, x_ref, cot_ref, mod_ref, out_ref, sums_ref, shared, scratch):
        self.pairs, self.x_ref, self.cot_ref = pairs, x_ref, cot_ref
        self.out_ref, self.sums_ref = out_ref, sums_ref
        (
            self.fwd_one,
            self.back_one,
            self.fwd_two,
            self.back_two,
            self.down_fwd,
            self.down_even,
            self.down_odd,
            vec_ref,
            group_ref,
            self.conv_grad_one,
            self.conv_grad_two,
            self.down_grad,
            self.raw_sums,
        ) = shared
        (
            self.act_one,
            self.act_two,
            self.grad_one,
            self.grad_two,
            self.slope_one,
            self.slope_two,
            self.conv_one,
            self.grad_mid,
            self.sum_even,
            self.sum_odd,
            self.grad_even,
            self.grad_odd,
            self.down_win,
            self.cot_win,
            self.state,
            self.partial,
        ) = scratch
        self.entries = 2.0 * pairs * FIELD_COLS * (C // GROUPS)
        self.size = chunk_of(pairs, 8)
        self.steps = pairs // self.size
        self.rows = self.size * FIELD_COLS
        self.small = self.size * HALF_COLS
        self.same_group = group_ref[...]
        self.gain_one, self.gain_two = vec_ref[0:1, :C], vec_ref[1:2, :C]
        self.shift_one, self.shift_two = vec_ref[2:3, :C], vec_ref[3:4, :C]
        self.bias_one, self.bias_two = twice(vec_ref[4:5, :C]), twice(vec_ref[5:6, :C])
        self.bias_down = vec_ref[6:7, :]
        self.scale_plus, self.offset = mod_ref[0:1, :], mod_ref[1:2, :]
        self.nothing = jnp.zeros((8, 2 * C), jnp.float32)

    def keep(self, **values):
        for name, value in values.items():
            place = STATE.index(name)
            self.state[place : place + 1, :] = value

    def kept(self, name):
        place = STATE.index(name)
        return self.state[place : place + 1, :]

    def report(self, place, value):
        self.sums_ref[place : place + 1, :] = value

    def field(self, pair):
        return jnp.concatenate(
            [
                self.x_ref[pair, 0].astype(jnp.float32),
                self.x_ref[pair, 1].astype(jnp.float32),
            ],
            axis=1,
        )

    def means(self, first, second):
        return group_means(first, second, self.same_group, self.entries)

    def first_stats(self):
        def body(pair, carry):
            value = self.field(pair)
            return carry[0] + folded(value), carry[1] + folded(value * value)

        total, squares = over(self.pairs, 8, body, (self.nothing, self.nothing))
        self.partial[0], self.partial[1] = total, squares

    def partial_sums(self):
        return channel_sum(self.partial[0]), channel_sum(self.partial[1])

    def norm_of(self):
        mean, square = self.means(*self.partial_sums())
        inverse = lax.rsqrt(square - mean * mean + NORM_EPS)
        return inverse, -mean * inverse

    def first_act(self):
        inverse, center = self.norm_of()
        self.keep(inverse_one=inverse, center_one=center)
        gain = twice(inverse * self.gain_one)
        shift = twice(center * self.gain_one + self.shift_one)

        def body(pair, carry):
            value, slope = gelu_pair(self.field(pair) * gain + shift)
            put_shifted(self.act_one, pair, value)
            self.slope_one[pair] = slope
            return carry

        over(self.pairs, 8, body, 0)
        close_ring(self.act_one, self.pairs)

    def first_conv(self):
        def body(step, carry):
            start = step * self.size
            value = (
                jnp.dot(
                    windows(self.act_one, start, self.size),
                    self.fwd_one[...],
                    preferred_element_type=jnp.float32,
                )
                + self.bias_one
            )
            self.conv_one[pl.ds(start, self.size)] = value.reshape(self.size, FIELD_COLS, 2 * C)
            return carry[0] + folded(value), carry[1] + folded(value * value)

        total, squares = over_steps(self.steps, body, (self.nothing, self.nothing))
        self.partial[0], self.partial[1] = total, squares

    def second_act(self):
        inverse, center = self.norm_of()
        self.keep(inverse_two=inverse, center_two=center)
        factor = self.gain_two * self.scale_plus
        gain = twice(inverse * factor)
        shift = twice(center * factor + self.shift_two * self.scale_plus + self.offset)

        def body(pair, carry):
            value, slope = gelu_pair(self.conv_one[pair] * gain + shift)
            put_shifted(self.act_two, pair, value)
            self.slope_two[pair] = slope
            return carry

        over(self.pairs, 8, body, 0)
        close_ring(self.act_two, self.pairs)

    def second_conv(self):
        def body(step, carry):
            start = step * self.size
            value = (
                jnp.dot(
                    windows(self.act_two, start, self.size),
                    self.fwd_two[...],
                    preferred_element_type=jnp.float32,
                )
                + self.bias_two
            )
            value = value.reshape(self.size, FIELD_COLS, 2 * C)
            for half, ref in ((0, self.sum_even), (1, self.sum_odd)):
                base = self.x_ref[pl.ds(start, self.size), half].astype(jnp.float32)
                ref[pl.ds(start, self.size)] = base + value[:, :, half * C : half * C + C]
            return carry

        over_steps(self.steps, body)

    def split_columns(self):
        def body(pair, carry):
            even, odd = [], []
            for ref in (self.sum_even, self.sum_odd):
                even.append(ref[pair, pl.ds(0, HALF_COLS, stride=2), :])
                odd.append(ref[pair, pl.ds(1, HALF_COLS, stride=2), :])
            even = jnp.concatenate(even, axis=1)
            odd = jnp.concatenate(odd, axis=1)
            self.down_win[0, pair + 1] = pltpu.roll(odd, 1, 0).astype(jnp.bfloat16)
            self.down_win[1, pair + 1] = even.astype(jnp.bfloat16)
            self.down_win[2, pair + 1] = odd.astype(jnp.bfloat16)
            return carry

        over(self.pairs, 8, body, 0)
        self.down_win[:, 0, :, C:] = self.down_win[:, self.pairs, :, C:]

    def shift_cotangent(self):
        def body(pair, carry):
            value = self.cot_ref[pair]
            wide = value.astype(jnp.float32)
            self.cot_win[0, pair] = value
            self.cot_win[1, pair] = pltpu.roll(wide, HALF_COLS - 1, 0).astype(jnp.bfloat16)
            return carry + folded(wide)

        total = over(self.pairs, 8, body, self.nothing)
        self.cot_win[:, self.pairs] = self.cot_win[:, 0]
        self.raw_sums[16:24, :] = self.raw_sums[16:24, :] + total

    def down_windows(self, start):
        pieces = [
            self.down_win[tap, pl.ds(start + 1, self.size)].reshape(self.small, 2 * C)
            for tap in range(3)
        ]
        pieces += [
            self.down_win[tap, pl.ds(start, self.size), :, C:].reshape(self.small, C)
            for tap in range(3)
        ]
        return jnp.concatenate(pieces, axis=1)

    def down_output(self):
        def body(step, carry):
            start = step * self.size
            value = jnp.dot(
                self.down_windows(start), self.down_fwd[...], preferred_element_type=jnp.float32
            )
            self.out_ref[pl.ds(start, self.size)] = (
                (value + self.bias_down)
                .reshape(self.size, HALF_COLS, 2 * C)
                .astype(jnp.bfloat16)
            )
            return carry

        over_steps(self.steps, body)

    def add_down_grad(self):
        def body(step, carry):
            start = step * self.size
            here = self.cot_win[0, pl.ds(start, self.size)].reshape(self.small, 2 * C)
            product = jnp.dot(
                here.T, self.down_windows(start), preferred_element_type=jnp.float32
            )
            for position in range(9):
                row_tap, tap = DOWN_ORDER[position]
                lanes = pl.ds((3 * row_tap + tap) * C, C)
                self.down_grad[:, lanes] = (
                    self.down_grad[:, lanes] + product[:, position * C : position * C + C]
                )
            return carry

        over_steps(self.steps, body)

    def down_adjoint(self):
        def body(step, carry):
            start = step * self.size
            pieces = [
                self.cot_win[shift, pl.ds(start + below, self.size)].reshape(self.small, 2 * C)
                for below in range(2)
                for shift in range(2)
            ]
            even = jnp.dot(
                jnp.concatenate([pieces[0], pieces[2]], axis=1),
                self.down_even[...],
                preferred_element_type=jnp.float32,
            ).reshape(self.size, HALF_COLS, 2 * C)
            odd = jnp.dot(
                jnp.concatenate(pieces, axis=1),
                self.down_odd[...],
                preferred_element_type=jnp.float32,
            ).reshape(self.size, HALF_COLS, 2 * C)
            for half, ref in ((0, self.grad_even), (1, self.grad_odd)):
                lanes = slice(half * C, half * C + C)
                for inner in range(self.size):
                    ref[start + inner, pl.ds(0, HALF_COLS, stride=2), :] = even[inner, :, lanes]
                    ref[start + inner, pl.ds(1, HALF_COLS, stride=2), :] = odd[inner, :, lanes]
            return carry

        over_steps(self.steps, body)

    def second_grad(self):
        def body(pair, carry):
            value = jnp.concatenate([self.grad_even[pair], self.grad_odd[pair]], axis=1)
            put_shifted(self.grad_two, pair, value)
            return carry + folded(value)

        total = over(self.pairs, 8, body, self.nothing)
        close_ring(self.grad_two, self.pairs)
        self.raw_sums[8:16, :] = self.raw_sums[8:16, :] + total

    def second_conv_grad(self):
        add_conv_grad(self.conv_grad_two, self.act_two, self.grad_two, self.pairs)

    def second_back(self):
        def body(step, carry):
            start = step * self.size
            value = jnp.dot(
                windows(self.grad_two, start, self.size),
                self.back_two[...],
                preferred_element_type=jnp.float32,
            )
            value = value * self.slope_two[pl.ds(start, self.size)].reshape(self.rows, 2 * C)
            self.grad_mid[pl.ds(start, self.size)] = value.reshape(self.size, FIELD_COLS, 2 * C)
            conv = self.conv_one[pl.ds(start, self.size)].reshape(self.rows, 2 * C)
            return carry[0] + folded(value), carry[1] + folded(value * conv)

        total, cross = over_steps(self.steps, body, (self.nothing, self.nothing))
        self.partial[0], self.partial[1] = total, cross

    def first_grad(self):
        inverse, center = self.kept("inverse_two"), self.kept("center_two")
        total, cross = self.partial_sums()
        cross = cross * inverse + total * center
        self.report(0, cross)
        self.report(1, total)
        factor = self.scale_plus * self.gain_two
        mean_grad, mean_cross = self.means(total * factor, cross * factor)
        from_mid = twice(inverse * factor)
        from_conv = twice(inverse * inverse * mean_cross)
        from_mean = twice(inverse * (mean_grad + center * mean_cross))

        def body(pair, carry):
            value = self.grad_mid[pair] * from_mid - from_mean - self.conv_one[pair] * from_conv
            put_shifted(self.grad_one, pair, value)
            return carry + folded(value)

        total = over(self.pairs, 8, body, self.nothing)
        close_ring(self.grad_one, self.pairs)
        self.raw_sums[0:8, :] = self.raw_sums[0:8, :] + total

    def first_conv_grad(self):
        add_conv_grad(self.conv_grad_one, self.act_one, self.grad_one, self.pairs)

    def first_back(self):
        def body(step, carry):
            start = step * self.size
            value = jnp.dot(
                windows(self.grad_one, start, self.size),
                self.back_one[...],
                preferred_element_type=jnp.float32,
            )
            value = value * self.slope_one[pl.ds(start, self.size)].reshape(self.rows, 2 * C)
            self.grad_mid[pl.ds(start, self.size)] = value.reshape(self.size, FIELD_COLS, 2 * C)
            base = jnp.concatenate(
                [
                    self.x_ref[pl.ds(start, self.size), half]
                    .astype(jnp.float32)
                    .reshape(self.rows, C)
                    for half in range(2)
                ],
                axis=1,
            )
            return carry[0] + folded(value), carry[1] + folded(value * base)

        total, cross = over_steps(self.steps, body, (self.nothing, self.nothing))
        self.partial[0], self.partial[1] = total, cross

    def field_grad(self, rows_ref):
        inverse, center = self.kept("inverse_one"), self.kept("center_one")
        total, cross = self.partial_sums()
        cross = cross * inverse + total * center
        self.report(2, cross)
        self.report(3, total)
        mean_grad, mean_cross = self.means(total * self.gain_one, cross * self.gain_one)
        from_pre = twice(inverse * self.gain_one)
        from_field = twice(inverse * inverse * mean_cross)
        from_mean = twice(inverse * (mean_grad + center * mean_cross))

        def body(pair, carry):
            summed = jnp.concatenate([self.grad_even[pair], self.grad_odd[pair]], axis=1)
            change = self.grad_mid[pair] * from_pre - from_mean - self.field(pair) * from_field
            value = (summed + change).astype(jnp.bfloat16)
            rows_ref[pair, 0] = value[:, :C]
            rows_ref[pair, 1] = value[:, C:]
            return carry

        over(self.pairs, 8, body, 0)


STATE = (
    "inverse_one",
    "center_one",
    "inverse_two",
    "center_two",
)
BEFORE = -1
SLOTS = (
    (
        ("first_stats", 0),
        ("shift_cotangent", 0),
        ("add_down_grad", BEFORE),
        ("second_conv_grad", BEFORE),
    ),
    (
        ("first_act", 0),
        ("first_stats", 1),
        ("down_adjoint", 0),
        ("first_conv_grad", BEFORE),
    ),
    (
        ("first_act", 1),
        ("second_grad", 0),
        ("shift_cotangent", 1),
        ("first_conv", 0),
        ("down_adjoint", 1),
    ),
    (("second_act", 0), ("second_grad", 1), ("first_conv", 1)),
    (("second_act", 1), ("second_back", 0), ("second_conv", 0)),
    (("first_grad", 0), ("split_columns", 0), ("second_back", 1), ("second_conv_grad", 0)),
    (("first_grad", 1), ("first_back", 0), ("second_conv", 1)),
    (("field_grad", 0), ("split_columns", 1), ("first_back", 1), ("first_conv_grad", 0)),
    (("field_grad", 1), ("down_output", 0), ("add_down_grad", 0), ("down_output", 1)),
)
LATE = ("add_down_grad", "second_conv_grad", "first_conv_grad")


def sample_kernel(pairs, samples, together, row_count, field_ref, cot_ref, mod_ref, *refs):
    constants, refs = refs[:9], refs[9:]
    out_ref, grad_ref, conv_grad_one, conv_grad_two, down_grad, raw_sums, sums_ref = refs[:7]
    scratch, rest = refs[7 : 7 + 16 * together], refs[7 + 16 * together :]
    x_ref, grad_rows, field_sem, field_sent, grad_sem, grad_sent = rest
    base = pl.program_id(0) * together
    row = lax.axis_index("row")
    share = pairs // row_count

    @pl.when(base == 0)
    def _():
        greet(row_count)

        def send_field(index, carry):
            mine = x_ref.at[index, pl.ds(row * share, share)]
            for step in range(1, row_count):
                place = lax.rem(row + step, row_count) * samples + index
                to_peer(
                    "row",
                    step,
                    row_count,
                    field_ref.at[place],
                    mine,
                    field_sent,
                    field_sem.at[index],
                ).start()
            pltpu.make_async_copy(
                field_ref.at[row * samples + index], mine, field_sem.at[index]
            ).start()
            return carry

        lax.fori_loop(0, samples, send_field, 0)
        conv_grad_one[...] = jnp.zeros_like(conv_grad_one)
        conv_grad_two[...] = jnp.zeros_like(conv_grad_two)
        down_grad[...] = jnp.zeros_like(down_grad)
        raw_sums[...] = jnp.zeros_like(raw_sums)
        if together > 1:
            for ref in scratch[-16:-12] + scratch[-4:-2]:
                ref[...] = jnp.zeros_like(ref)

    def send_grad(index):
        target = grad_ref.at[row * samples + index]
        for step in range(1, row_count):
            place = lax.rem(row + step, row_count) * share
            to_peer(
                "row",
                step,
                row_count,
                grad_rows.at[index, pl.ds(place, share)],
                target,
                grad_sent,
                grad_sem,
            ).start()
        pltpu.make_async_copy(
            grad_rows.at[index, pl.ds(row * share, share)], target, grad_sem
        ).start()

    @pl.when(base > 0)
    def _():
        for place in range(together):
            send_grad(base - together + place)

    for place in range(together):
        arrived = x_ref.at[base + place]
        pltpu.make_async_copy(arrived, arrived, field_sem.at[base + place]).wait()
    shared = constants + (conv_grad_one, conv_grad_two, down_grad, raw_sums)
    stages = [
        Sample(
            pairs,
            x_ref.at[base + place],
            cot_ref.at[place],
            mod_ref.at[place],
            out_ref.at[place],
            sums_ref.at[place],
            shared,
            scratch[16 * place : 16 * place + 16],
        )
        for place in range(together)
    ]
    def run_slot(slot):
        for name, place in slot:
            if place >= together or (place == BEFORE and together == 1):
                continue
            stage = getattr(stages[place], name)
            if name == "field_grad":
                stage(grad_rows.at[base + place])
            else:
                stage()

    for slot in SLOTS:
        run_slot(slot)

    @pl.when(base == samples - together)
    def _():
        for place in range(together):
            send_grad(base + place)
        if together > 1:
            for name in LATE:
                getattr(stages[-1], name)()
        pltpu.make_async_copy(grad_ref, grad_ref, grad_sem).wait()
        others = pl.ds(0, pairs - share)
        for ref, sem in ((x_ref, field_sent), (grad_rows, grad_sent)):
            pltpu.make_async_copy(ref.at[:, others], ref.at[:, others], sem).wait()


DOWN_ORDER = ((1, 0), (2, 0), (1, 1), (2, 1), (1, 2), (2, 2), (0, 0), (0, 1), (0, 2))


def run_samples(field_in, cotangent, modulation, weights, vectors):
    row_count = lax.axis_size("row")
    samples = cotangent.shape[0]
    pairs = field_in.shape[1] // 2 * row_count
    together = chunk_of(samples, 2)
    share = pairs // row_count
    halves = field_in.reshape(field_in.shape[0], share, 2, FIELD_COLS, C)
    same_group = jnp.asarray(
        np.kron(np.eye(GROUPS), np.ones((C // GROUPS, C // GROUPS))), jnp.float32
    )

    def whole(array):
        return pl.BlockSpec(array.shape, lambda i: (0,) * array.ndim, pipeline_mode=pl.Buffered(1))

    def per_sample(array):
        rank = len(array.shape)
        return pl.BlockSpec((together,) + array.shape[1:], lambda i: (i,) + (0,) * (rank - 1))

    constants = tuple(weights) + (vectors, same_group)
    outs = (
        jax.ShapeDtypeStruct((samples, pairs, HALF_COLS, C2), jnp.bfloat16),
        jax.ShapeDtypeStruct(halves.shape, jnp.bfloat16),
        jax.ShapeDtypeStruct((C, 9 * C), jnp.float32),
        jax.ShapeDtypeStruct((C, 9 * C), jnp.float32),
        jax.ShapeDtypeStruct((C2, 9 * C), jnp.float32),
        jax.ShapeDtypeStruct((24, 2 * C), jnp.float32),
        jax.ShapeDtypeStruct((samples, 4, C), jnp.float32),
    )
    anywhere = pl.BlockSpec(memory_space=pl.ANY)
    ring = pltpu.VMEM((3, pairs + 2, FIELD_COLS, 2 * C), jnp.bfloat16)
    wide = pltpu.VMEM((pairs, FIELD_COLS, 2 * C), jnp.float32)
    half = pltpu.VMEM((pairs, FIELD_COLS, C), jnp.float32)
    result = pl.pallas_call(
        functools.partial(sample_kernel, pairs, samples, together, row_count),
        grid=(samples // together,),
        in_specs=[anywhere, per_sample(cotangent), per_sample(modulation)]
        + [whole(array) for array in constants],
        out_specs=[per_sample(outs[0]), anywhere]
        + [pl.BlockSpec(out.shape, lambda i: (0, 0)) for out in outs[2:6]]
        + [per_sample(outs[6])],
        out_shape=outs,
        scratch_shapes=(
            [ring] * 4
            + [wide] * 4
            + [half] * 4
            + [
                pltpu.VMEM((3, pairs + 1, HALF_COLS, 2 * C), jnp.bfloat16),
                pltpu.VMEM((2, pairs + 1, HALF_COLS, C2), jnp.bfloat16),
                pltpu.VMEM((8, C), jnp.float32),
                pltpu.VMEM((2, 8, 2 * C), jnp.float32),
            ]
        )
        * together
        + [
            pltpu.VMEM((samples, pairs, 2, FIELD_COLS, C), jnp.bfloat16),
            pltpu.VMEM((samples, pairs, 2, FIELD_COLS, C), jnp.bfloat16),
            pltpu.SemaphoreType.DMA((samples,)),
            pltpu.SemaphoreType.DMA,
            pltpu.SemaphoreType.DMA,
            pltpu.SemaphoreType.DMA,
        ],
        compiler_params=pltpu.CompilerParams(
            dimension_semantics=("arbitrary",),
            vmem_limit_bytes=60 << 20,
            collective_id=2,
            has_side_effects=True,
        ),
        name="samples",
    )(halves, cotangent, modulation, *constants)
    return (result[0], result[1].reshape(field_in.shape)) + tuple(result[2:])


def gather_kernel(
    row_count,
    batch_count,
    shard_ref,
    small_ref,
    fwd_one,
    back_one,
    fwd_two,
    back_two,
    down_fwd,
    down_even,
    down_odd,
    small_out,
    embed_in_t,
    embed_out_ref,
    shards,
    smalls,
    conv_t,
    down_t,
    send_main,
    recv_main,
    send_small,
    recv_small,
    local_sem,
):
    row, batch = lax.axis_index("row"), lax.axis_index("batch")
    greet(row_count, batch_count)
    own_main = pltpu.make_async_copy(shard_ref, shards.at[row, batch], local_sem.at[0])
    own_small = pltpu.make_async_copy(small_ref, smalls.at[row, batch], local_sem.at[1])
    own_main.start()
    own_small.start()
    copies = []
    for step in range(1, batch_count):
        copies.append(
            to_peer(
                "batch",
                step,
                batch_count,
                shard_ref,
                shards.at[row, batch],
                send_main.at[step],
                recv_main.at[step],
            )
        )
        copies.append(
            to_peer(
                "batch",
                step,
                batch_count,
                small_ref,
                smalls.at[row, batch],
                send_small.at[step],
                recv_small.at[step],
            )
        )
    for copy in copies:
        copy.start()
    own_main.wait()
    own_small.wait()
    finish(copies)
    copies = []
    for step in range(1, row_count):
        slot = batch_count + step
        copies.append(
            to_peer(
                "row",
                step,
                row_count,
                shards.at[row],
                shards.at[row],
                send_main.at[slot],
                recv_main.at[slot],
            )
        )
        copies.append(
            to_peer(
                "row",
                step,
                row_count,
                smalls.at[row],
                smalls.at[row],
                send_small.at[slot],
                recv_small.at[slot],
            )
        )
    for copy in copies:
        copy.start()
    finish(copies)
    depth, share, wide_share = 9 * C // batch_count, C // row_count, C2 // row_count
    height = 2 * share + wide_share
    embed_share, hidden_share = EMB // batch_count, HID // batch_count
    for place in range(row_count):
        parts = [shards[place, part].astype(jnp.float32) for part in range(batch_count)]
        main = jnp.concatenate([part[:, :depth] for part in parts], axis=1)
        for which in range(2):
            conv_t[which, place * share : place * share + share, :] = main[
                which * share : which * share + share
            ]
        down_t[place * wide_share : place * wide_share + wide_share, :] = main[2 * share :]
        embed_in_t[place * height : place * height + height, :] = jnp.concatenate(
            [part[:, depth : depth + embed_share] for part in parts], axis=1
        )
        tail = depth + embed_share
        half_rows, half_lanes = height // 2, hidden_share // 2
        lanes = []
        for part in parts:
            lanes.append(part[:half_rows, tail : tail + half_lanes])
            lanes.append(part[half_rows:, tail : tail + half_lanes])
        embed_out_ref[place * half_rows : place * half_rows + half_rows, :] = jnp.concatenate(
            lanes, axis=1
        )
        for part in range(batch_count):
            small_out[part * row_count + place : part * row_count + place + 1, :] = smalls[
                place, part, 0:1, :
            ]
    for which, forward, back in ((0, fwd_one, back_one), (1, fwd_two, back_two)):
        zero = jnp.zeros((C, C), jnp.bfloat16)
        for tap in range(3):
            direct = [
                conv_t[which, :, (3 * row_tap + tap) * C : (3 * row_tap + tap) * C + C]
                for row_tap in range(3)
            ]
            fill_blocks(forward, tap, [block.T.astype(jnp.bfloat16) for block in direct], zero)
            fill_blocks(
                back, 2 - tap, [block.astype(jnp.bfloat16) for block in direct[::-1]], zero
            )
    zero = jnp.zeros((C2, C), jnp.bfloat16)
    back = {}
    for position in range(9):
        row_tap, tap = DOWN_ORDER[position]
        block = down_t[:, (3 * row_tap + tap) * C : (3 * row_tap + tap) * C + C]
        down_fwd[position * C : position * C + C, :] = block.T.astype(jnp.bfloat16)
        back[row_tap, tap] = block.astype(jnp.bfloat16)
    even = ((back[1, 1], back[2, 1]), (zero, back[0, 1]))
    odd = (
        (back[1, 2], back[2, 2]),
        (back[1, 0], back[2, 0]),
        (zero, back[0, 2]),
        (zero, back[0, 0]),
    )
    for ref, table in ((down_even, even), (down_odd, odd)):
        for position, (left, right) in enumerate(table):
            ref[position * C2 : position * C2 + C2, :C] = left
            ref[position * C2 : position * C2 + C2, C:] = right


def fill_blocks(ref, tap, blocks, zero):
    table = (
        (blocks[1], blocks[0]),
        (blocks[2], blocks[1]),
        (blocks[0], zero),
        (zero, blocks[2]),
    )
    for position, (left, right) in enumerate(table):
        base = (4 * tap + position) * C
        ref[base : base + C, :C] = left
        ref[base : base + C, C:] = right


def dot_last(lhs, rhs):
    return lax.dot_general(
        lhs,
        rhs,
        (((1,), (1,)), ((), ())),
        precision=HIGHEST,
        preferred_element_type=jnp.float32,
    )


def dot_first(lhs, rhs):
    return lax.dot_general(
        lhs,
        rhs,
        (((0,), (0,)), ((), ())),
        precision=HIGHEST,
        preferred_element_type=jnp.float32,
    )


def reduce_kernel(
    row_count,
    batch_count,
    samples,
    grad_one,
    grad_two,
    grad_down,
    raw_ref,
    sums_ref,
    scale_ref,
    gate_ref,
    hidden_ref,
    slope_ref,
    embedded_ref,
    embed_out_ref,
    owned_ref,
    small_ref,
    norm_ref,
    row_send,
    row_take,
    batch_send,
    batch_take,
    small_send,
    small_take,
    small_next,
    small_last,
    square_send,
    square_take,
    square_next,
    square_last,
    send_sem,
    recv_sem,
):
    row, batch = lax.axis_index("row"), lax.axis_index("batch")
    depth, share, wide_share = 9 * C // batch_count, C // row_count, C2 // row_count
    height = 2 * share + wide_share
    embed_share, hidden_share = EMB // batch_count, HID // batch_count
    mid_cross, mid_total = sums_ref[0], sums_ref[1]
    gain_two, shift_two = gate_ref[0:1, :], gate_ref[1:2, :]
    scale_plus = scale_ref[...]
    grad_mod = jnp.concatenate([gain_two * mid_cross + shift_two * mid_total, mid_total], axis=1)
    grad_embed_out = dot_first(grad_mod, hidden_ref[...])
    grad_hidden = (
        jnp.dot(
            grad_mod, embed_out_ref[...], precision=HIGHEST, preferred_element_type=jnp.float32
        )
        * slope_ref[...]
    )
    grad_embed_in = dot_first(grad_hidden, embedded_ref[...])

    def down_sum(value):
        return jnp.sum(value, axis=0, keepdims=True)

    small_rows = [
        down_sum(sums_ref[2]),
        down_sum(mid_cross * scale_plus),
        down_sum(sums_ref[3]),
        down_sum(mid_total * scale_plus),
        channel_sum(raw_ref[0:8]),
        channel_sum(raw_ref[8:16]),
    ]
    cot_total = down_sum(raw_ref[16:24])
    small_rows += [cot_total[:, :C], cot_total[:, C:]]
    hidden_total, mod_total = down_sum(grad_hidden), down_sum(grad_mod)
    small_rows += [hidden_total[:, lane : lane + C] for lane in range(0, HID, C)]
    small_rows += [mod_total[:, lane : lane + C] for lane in range(0, 2 * C, C)]
    small_rows.append(jnp.zeros((2, C), jnp.float32))
    small_send[...] = jnp.concatenate(small_rows, axis=0)
    half_rows = height // 2
    for place in range(row_count):
        low, high = place * share, place * share + share
        row_send[place, :, : 9 * C] = jnp.concatenate(
            [
                grad_one[low:high],
                grad_two[low:high],
                grad_down[place * wide_share : place * wide_share + wide_share],
            ],
            axis=0,
        ).astype(jnp.bfloat16)
        row_send[place, :, 9 * C : 10 * C] = grad_embed_in[
            place * height : place * height + height
        ].astype(jnp.bfloat16)
        piece = grad_embed_out[place * half_rows : place * half_rows + half_rows]
        row_send[place, :, 10 * C :] = jnp.concatenate(
            [piece[:, : HID // 2], piece[:, HID // 2 :]], axis=0
        ).astype(jnp.bfloat16)
    greet(row_count, batch_count)
    copies = []
    for step in range(1, row_count):
        copies.append(
            to_peer(
                "row",
                step,
                row_count,
                row_send.at[lax.rem(row + step, row_count)],
                row_take.at[step],
                send_sem.at[0, step],
                recv_sem.at[0, step],
            )
        )
        copies.append(
            to_peer(
                "row",
                step,
                row_count,
                small_send,
                small_take.at[step],
                send_sem.at[1, step],
                recv_sem.at[1, step],
            )
        )
    for copy in copies:
        copy.start()
    total = row_send[row].astype(jnp.float32)
    finish(copies)
    small_total = small_send[...]
    for step in range(1, row_count):
        total = total + row_take[step].astype(jnp.float32)
        small_total = small_total + small_take[step]
    small_next[...] = small_total
    for part in range(batch_count):
        per_half = batch_count // 2
        rows = slice(0, half_rows) if part < per_half else slice(half_rows, height)
        base = 10 * C + hidden_share * (part % per_half)
        piece = total[rows, base : base + hidden_share]
        batch_send[part] = jnp.concatenate(
            [
                total[:, part * depth : part * depth + depth],
                total[:, 9 * C + part * embed_share : 9 * C + part * embed_share + embed_share],
                jnp.concatenate([piece[:, : hidden_share // 2], piece[:, hidden_share // 2 :]], axis=0),
            ],
            axis=1,
        ).astype(jnp.bfloat16)
    copies = []
    for step in range(1, batch_count):
        copies.append(
            to_peer(
                "batch",
                step,
                batch_count,
                batch_send.at[lax.rem(batch + step, batch_count)],
                batch_take.at[step],
                send_sem.at[2, step],
                recv_sem.at[2, step],
            )
        )
        copies.append(
            to_peer(
                "batch",
                step,
                batch_count,
                small_next,
                small_last.at[step],
                send_sem.at[3, step],
                recv_sem.at[3, step],
            )
        )
    for copy in copies:
        copy.start()
    owned = batch_send[batch].astype(jnp.float32)
    finish(copies)
    small_total = small_next[...]
    for step in range(1, batch_count):
        owned = owned + batch_take[step].astype(jnp.float32)
        small_total = small_total + small_last[step]
    squares = jnp.sum(jnp.sum(owned * owned, axis=0, keepdims=True), axis=1, keepdims=True)
    square_send[...] = jnp.broadcast_to(squares, (8, C))
    copies = [
        to_peer(
            "row",
            step,
            row_count,
            square_send,
            square_take.at[step],
            send_sem.at[4, step],
            recv_sem.at[4, step],
        )
        for step in range(1, row_count)
    ]
    for copy in copies:
        copy.start()
    finish(copies)
    squares = square_send[...]
    for step in range(1, row_count):
        squares = squares + square_take[step]
    square_next[...] = squares
    copies = [
        to_peer(
            "batch",
            step,
            batch_count,
            square_next,
            square_last.at[step],
            send_sem.at[5, step],
            recv_sem.at[5, step],
        )
        for step in range(1, batch_count)
    ]
    for copy in copies:
        copy.start()
    finish(copies)
    squares = square_next[...]
    for step in range(1, batch_count):
        squares = squares + square_last[step]
    small_squares = jnp.sum(
        jnp.sum(small_total * small_total, axis=0, keepdims=True), axis=1, keepdims=True
    )
    norm = jnp.sqrt(squares + small_squares)
    clip = jnp.minimum(1.0, CLIP_NORM / (norm + 1e-06))[0:1, 0:1]
    norm_ref[...] = norm
    owned_ref[...] = owned * clip
    small_ref[...] = small_total * clip


def pack_pieces(conv, down, embed_in, embed_out):
    half = embed_out.shape[0] // 2
    tall = jnp.concatenate([embed_out[:half].T, embed_out[half:].T], axis=0)
    return jnp.concatenate(
        [jnp.concatenate([conv[0].T, conv[1].T, down.T], axis=0), embed_in.T, tall], axis=1
    )


def unpack_pieces(owned, depth, share, embed_share):
    height, half = owned.shape[0], owned.shape[0] // 2
    conv = jnp.stack([owned[:share, :depth].T, owned[share : 2 * share, :depth].T])
    down = owned[2 * share :, :depth].T
    embed_in = owned[:, depth : depth + embed_share].T
    tall = owned[:, depth + embed_share :]
    embed_out = jnp.concatenate([tall[:half].T, tall[half:].T], axis=0)
    return conv, down, embed_in, embed_out


def in_vmem(count):
    return [pl.BlockSpec(memory_space=pltpu.VMEM)] * count


def gather_weights(packed, small):
    row_count, batch_count = (lax.axis_size("row"), lax.axis_size("batch"))
    small_tile = jnp.pad(small[None, :], ((0, 7), (0, C - small.shape[0])))
    outs = (
        [jax.ShapeDtypeStruct((12 * C, 2 * C), jnp.bfloat16)] * 4
        + [
            jax.ShapeDtypeStruct((9 * C, C2), jnp.bfloat16),
            jax.ShapeDtypeStruct((2 * C2, 2 * C), jnp.bfloat16),
            jax.ShapeDtypeStruct((4 * C2, 2 * C), jnp.bfloat16),
        ]
        + [
            jax.ShapeDtypeStruct((row_count * batch_count, C), jnp.float32),
            jax.ShapeDtypeStruct((HID, EMB), jnp.float32),
            jax.ShapeDtypeStruct((2 * C, HID), jnp.float32),
        ]
    )
    slots = row_count + batch_count
    return pl.pallas_call(
        functools.partial(gather_kernel, row_count, batch_count),
        out_shape=outs,
        in_specs=in_vmem(2),
        out_specs=in_vmem(len(outs)),
        scratch_shapes=[
            pltpu.VMEM((row_count, batch_count) + packed.shape, jnp.bfloat16),
            pltpu.VMEM((row_count, batch_count, 8, C), jnp.float32),
            pltpu.VMEM((2, C, 9 * C), jnp.float32),
            pltpu.VMEM((C2, 9 * C), jnp.float32),
            pltpu.SemaphoreType.DMA((slots,)),
            pltpu.SemaphoreType.DMA((slots,)),
            pltpu.SemaphoreType.DMA((slots,)),
            pltpu.SemaphoreType.DMA((slots,)),
            pltpu.SemaphoreType.DMA((2,)),
        ],
        compiler_params=pltpu.CompilerParams(
            collective_id=0, has_side_effects=True, vmem_limit_bytes=60 << 20
        ),
        name="gather",
    )(packed, small_tile)


def reduce_grads(grads, sums, scale_plus, gates, hidden, slope, embedded, embed_out_t):
    row_count, batch_count = (lax.axis_size("row"), lax.axis_size("batch"))
    height = 4 * C // row_count
    width = 12 * C // batch_count
    samples = hidden.shape[0]
    outs = [
        jax.ShapeDtypeStruct((height, width), jnp.float32),
        jax.ShapeDtypeStruct((16, C), jnp.float32),
        jax.ShapeDtypeStruct((8, C), jnp.float32),
    ]
    tile = (16, C)
    most = max(row_count, batch_count)
    return pl.pallas_call(
        functools.partial(reduce_kernel, row_count, batch_count, samples),
        out_shape=outs,
        in_specs=in_vmem(11),
        out_specs=in_vmem(len(outs)),
        scratch_shapes=[
            pltpu.VMEM((row_count, height, 12 * C), jnp.bfloat16),
            pltpu.VMEM((row_count, height, 12 * C), jnp.bfloat16),
            pltpu.VMEM((batch_count, height, width), jnp.bfloat16),
            pltpu.VMEM((batch_count, height, width), jnp.bfloat16),
            pltpu.VMEM(tile, jnp.float32),
            pltpu.VMEM((row_count,) + tile, jnp.float32),
            pltpu.VMEM(tile, jnp.float32),
            pltpu.VMEM((batch_count,) + tile, jnp.float32),
            pltpu.VMEM((8, C), jnp.float32),
            pltpu.VMEM((row_count, 8, C), jnp.float32),
            pltpu.VMEM((8, C), jnp.float32),
            pltpu.VMEM((batch_count, 8, C), jnp.float32),
            pltpu.SemaphoreType.DMA((6, most)),
            pltpu.SemaphoreType.DMA((6, most)),
        ],
        compiler_params=pltpu.CompilerParams(
            collective_id=1, has_side_effects=True, vmem_limit_bytes=60 << 20
        ),
        name="reduce",
    )(*grads, sums, scale_plus, gates, hidden, slope, embedded, embed_out_t)


def adam_update(weight, gradient, first_old, second_old, step_rate, clip_factor):
    scaled = gradient * clip_factor
    first_new = BETA_ONE * first_old + (1.0 - BETA_ONE) * scaled
    second_new = BETA_TWO * second_old + (1.0 - BETA_TWO) * scaled * scaled
    corrected = (
        first_new
        / (1.0 - BETA_ONE**STEP_COUNT)
        / (jnp.sqrt(second_new / (1.0 - BETA_TWO**STEP_COUNT)) + ADAM_EPS)
    )
    return (weight - step_rate * (corrected + DECAY * weight), first_new, second_new)


def body(
    field_in,
    refine_step,
    cotangent,
    conv_weight,
    down_weight,
    embed_in_weight,
    embed_out_weight,
    small_params,
    conv_first,
    down_first,
    embed_in_first,
    embed_out_first,
    small_first,
    conv_second,
    down_second,
    embed_in_second,
    embed_out_second,
    small_second,
):
    packed = pack_pieces(
        conv_weight.astype(jnp.bfloat16),
        down_weight.astype(jnp.bfloat16),
        embed_in_weight.astype(jnp.bfloat16),
        embed_out_weight.astype(jnp.bfloat16),
    )
    small_rounded = small_params.astype(jnp.bfloat16).astype(jnp.float32)
    gathered = gather_weights(packed, small_rounded)
    weights, small_rows = gathered[:7], gathered[7]
    embed_in_t, embed_out_t = gathered[8], gathered[9]
    small_low = small_rows[:, : small_params.shape[0]].reshape(-1)
    owned = refine_step.shape[0] // lax.axis_size("row")
    padded = -(-owned // 8) * 8
    own_steps = lax.dynamic_slice_in_dim(refine_step, lax.axis_index("row") * owned, owned, 0)
    embedded = embed_steps(own_steps)
    lanes = small_low[: 6 * C].reshape(6, C)
    bias_down = small_low[6 * C : 6 * C + C2]
    bias_hidden = small_low[6 * C + C2 : 6 * C + C2 + HID]
    bias_mod = small_low[6 * C + C2 + HID :]
    hidden_pre = jnp.dot(embedded, embed_in_t.T, precision=HIGHEST) + bias_hidden
    hidden, pull_hidden = jax.vjp(jax.nn.gelu, hidden_pre)
    slope = pull_hidden(jnp.ones_like(hidden_pre))[0]
    modulate = jnp.dot(hidden, embed_out_t.T, precision=HIGHEST) + bias_mod
    modulation = jnp.stack([1.0 + modulate[:, :C], modulate[:, C:]], axis=1)
    vectors = jnp.concatenate(
        [
            jnp.concatenate([lanes, jnp.zeros_like(lanes)], axis=1),
            bias_down[None, :],
            jnp.zeros((1, C2), jnp.float32),
        ],
        axis=0,
    )
    block_out, grad_start, grad_w1, grad_w2, grad_wd, raw_sums, sums = run_samples(
        field_in, cotangent, modulation, weights, vectors
    )

    def lengthened(value):
        return jnp.pad(value, ((0, padded - owned), (0, 0)))

    gates = jnp.concatenate([lanes[1:2], lanes[3:4], jnp.zeros((6, C), jnp.float32)], axis=0)
    sums = jnp.pad(jnp.transpose(sums, (1, 0, 2)), ((0, 0), (0, padded - owned), (0, 0)))
    owned_grads, small_grads, norm_tile = reduce_grads(
        (grad_w1, grad_w2, grad_wd, raw_sums),
        sums,
        lengthened(modulation[:, 0]),
        gates,
        lengthened(hidden),
        lengthened(slope),
        lengthened(embedded),
        embed_out_t,
    )
    grad_norm = norm_tile[0, 0]
    small_len = small_params.shape[0]
    place = (lax.axis_index("batch") * lax.axis_size("row") + lax.axis_index("row")) * small_len
    owned_shards = unpack_pieces(
        owned_grads, conv_weight.shape[1], conv_weight.shape[2], embed_in_weight.shape[0]
    ) + (lax.dynamic_slice_in_dim(small_grads.reshape(-1), place, small_len, 0),)
    clip_factor = 1.0
    conv_new = adam_update(
        conv_weight, owned_shards[0], conv_first, conv_second, RATE_MATRIX, clip_factor
    )
    down_new = adam_update(
        down_weight, owned_shards[1], down_first, down_second, RATE_MATRIX, clip_factor
    )
    embed_in_new = adam_update(
        embed_in_weight, owned_shards[2], embed_in_first, embed_in_second, RATE_MATRIX, clip_factor
    )
    embed_out_new = adam_update(
        embed_out_weight,
        owned_shards[3],
        embed_out_first,
        embed_out_second,
        RATE_MATRIX,
        clip_factor,
    )
    small_new = adam_update(
        small_params, owned_shards[4], small_first, small_second, RATE_SMALL, clip_factor
    )
    return (
        block_out,
        grad_start,
        grad_norm,
        conv_new[0],
        down_new[0],
        embed_in_new[0],
        embed_out_new[0],
        small_new[0],
        conv_new[1],
        down_new[1],
        embed_in_new[1],
        embed_out_new[1],
        small_new[1],
        conv_new[2],
        down_new[2],
        embed_in_new[2],
        embed_out_new[2],
        small_new[2],
    )


def solution(mesh):
    placed = (
        P("batch", "row", None, None),
        P("batch"),
        P(("batch", "row"), None, None, None),
        P(None, "batch", "row"),
        P("batch", "row"),
        P("batch", "row"),
        P("batch", "row"),
        P(("batch", "row")),
        P(None, "batch", "row"),
        P("batch", "row"),
        P("batch", "row"),
        P("batch", "row"),
        P(("batch", "row")),
        P(None, "batch", "row"),
        P("batch", "row"),
        P("batch", "row"),
        P("batch", "row"),
        P(("batch", "row")),
    )
    return jax.shard_map(
        body,
        mesh=mesh,
        in_specs=placed,
        out_specs=(
            P(("batch", "row"), None, None, None),
            P("batch", "row", None, None),
            P(),
            P(None, "batch", "row"),
            P("batch", "row"),
            P("batch", "row"),
            P("batch", "row"),
            P(("batch", "row")),
            P(None, "batch", "row"),
            P("batch", "row"),
            P("batch", "row"),
            P("batch", "row"),
            P(("batch", "row")),
            P(None, "batch", "row"),
            P("batch", "row"),
            P("batch", "row"),
            P("batch", "row"),
            P(("batch", "row")),
        ),
        check_vma=False,
    )
```

```python
import functools
import math
from types import SimpleNamespace

import jax
import jax.numpy as jnp
import numpy as np
from jax import lax
from jax.experimental import pallas as pl
from jax.experimental.pallas import tpu as pltpu
from jax.sharding import PartitionSpec as P

C = 128
C2 = 256
EMB = 128
HID = 512
GROUPS = 8
REFINE = 4


NORM_EPS = 1e-05
BETA_ONE = 0.9
BETA_TWO = 0.999
ADAM_EPS = 1e-08
DECAY = 0.01
RATE_MATRIX = 0.05
RATE_SMALL = 0.5
CLIP_NORM = 1.0
STEP_COUNT = 10
HIGHEST = lax.Precision.HIGHEST


def embed_steps(refine_step):
    halfway = EMB // 2
    frequency = jnp.exp(-math.log(10000.0) * jnp.arange(halfway).astype(jnp.float32) / halfway)
    angles = (refine_step.astype(jnp.float32) * (1000.0 / REFINE))[:, None] * frequency[None, :]
    return jnp.concatenate([jnp.sin(angles), jnp.cos(angles)], axis=1)


MESH = pl.DeviceIdType.MESH


def greet(row_count, batch_count=1):
    row, batch = lax.axis_index("row"), lax.axis_index("batch")
    barrier = pltpu.get_barrier_semaphore()
    for step in range(1, row_count):
        pl.semaphore_signal(
            barrier,
            inc=1,
            device_id={"row": lax.rem(row + step, row_count), "batch": batch},
            device_id_type=MESH,
        )
    for step in range(1, batch_count):
        pl.semaphore_signal(
            barrier,
            inc=1,
            device_id={"row": row, "batch": lax.rem(batch + step, batch_count)},
            device_id_type=MESH,
        )
    pl.semaphore_wait(barrier, row_count + batch_count - 2)


def to_peer(axis, step, count, source, target, send_sem, recv_sem):
    row, batch = lax.axis_index("row"), lax.axis_index("batch")
    if axis == "row":
        device = {"row": lax.rem(row + step, count), "batch": batch}
    else:
        device = {"row": row, "batch": lax.rem(batch + step, count)}
    return pltpu.make_async_remote_copy(
        src_ref=source,
        dst_ref=target,
        send_sem=send_sem,
        recv_sem=recv_sem,
        device_id=device,
        device_id_type=MESH,
    )


def finish(copies):
    for copy in copies:
        copy.wait()


FIELD_COLS = 64
HALF_COLS = 32
ROOT = math.sqrt(2.0 / math.pi)
CUBIC = ROOT * 0.044715


def chunk_of(total, most):
    size = min(total, most)
    while total % size:
        size -= 1
    return size


def over(total, most, body, init):
    size = chunk_of(total, most)

    def several(step, carry):
        for inner in range(size):
            carry = body(step * size + inner, carry)
        return carry

    if size == total:
        return several(0, init)
    return lax.fori_loop(0, total // size, several, init)


def folded(values):
    return jnp.sum(values.reshape(values.shape[0] // 8, 8, values.shape[1]), axis=0)


def twice(row):
    return jnp.concatenate([row, row], axis=1)


def channel_sum(partial):
    both = partial[:, :C] + partial[:, C:]
    return jnp.sum(both, axis=0, keepdims=True)


def group_means(first, second, same_group, entries):
    stacked = jnp.concatenate([first, second, jnp.zeros((6, C), jnp.float32)], axis=0)
    totals = jnp.dot(stacked, same_group, precision=HIGHEST, preferred_element_type=jnp.float32)
    return totals[0:1] / entries, totals[1:2] / entries


def gelu_pair(values):
    square = values * values
    weight = 0.5 + 0.5 * jnp.tanh(values * (ROOT + CUBIC * square))
    result = values * weight
    slope = weight + (result - result * weight) * (2.0 * ROOT + (6.0 * CUBIC) * square)
    return result, slope


def put_shifted(ref, pair, values):
    for tap, shift in ((0, 1), (1, 0), (2, FIELD_COLS - 1)):
        moved = pltpu.roll(values, shift, 0) if shift else values
        ref[tap, pair + 1] = moved.astype(jnp.bfloat16)


def close_ring(ref, pairs):
    ref[:, 0, :, C:] = ref[:, pairs, :, C:]
    ref[:, pairs + 1, :, :C] = ref[:, 1, :, :C]


def windows(ref, start, count):
    rows = count * FIELD_COLS
    pieces = []
    for tap in range(3):
        pieces.append(ref[tap, pl.ds(start + 1, count)].reshape(rows, 2 * C))
        pieces.append(ref[tap, pl.ds(start, count), :, C:].reshape(rows, C))
        pieces.append(ref[tap, pl.ds(start + 2, count), :, :C].reshape(rows, C))
    return jnp.concatenate(pieces, axis=1)


def over_steps(steps, body, init=0):
    if steps == 1:
        return body(0, init)
    return lax.fori_loop(0, steps, body, init)


def add_conv_grad(out_ref, act_ref, grad_ref, pairs):
    size = chunk_of(pairs, 8)
    rows = size * FIELD_COLS

    def body(step, carry):
        start = step * size
        grad = grad_ref[1, pl.ds(start + 1, size)].reshape(rows, 2 * C)
        product = jnp.dot(
            grad.T, windows(act_ref, start, size), preferred_element_type=jnp.float32
        )
        for tap in range(3):
            base = tap * 4 * C
            middle = product[:C, base : base + C] + product[C:, base + C : base + 2 * C]
            up = product[C:, base : base + C] + product[:C, base + 2 * C : base + 3 * C]
            down = product[:C, base + C : base + 2 * C] + product[C:, base + 3 * C : base + 4 * C]
            for row_tap, value in ((0, up), (1, middle), (2, down)):
                lanes = pl.ds((3 * row_tap + tap) * C, C)
                out_ref[:, lanes] = out_ref[:, lanes] + value
        return carry

    over_steps(pairs // size, body)


class Sample:
    def __init__(self, pairs, sample, x_ref, cot_ref, out_ref, refs, scratch):
        self.pairs, self.sample = pairs, sample
        self.x_ref, self.cot_ref, self.out_ref = x_ref, cot_ref, out_ref
        self.refs = refs
        (
            self.act_one,
            self.act_two,
            self.grad_one,
            self.grad_two,
            self.slope_one,
            self.slope_two,
            self.conv_one,
            self.grad_mid,
            self.sum_even,
            self.sum_odd,
            self.grad_even,
            self.grad_odd,
            self.down_win,
            self.cot_win,
            self.state,
            self.partial,
        ) = scratch
        self.entries = 2.0 * pairs * FIELD_COLS * (C // GROUPS)
        self.size = chunk_of(pairs, 8)
        self.steps = pairs // self.size
        self.rows = self.size * FIELD_COLS
        self.small = self.size * HALF_COLS
        self.same_group = refs.group[...]
        small = refs.small_all
        self.gain_one, self.gain_two = small[0:1, :], small[1:2, :]
        self.shift_one, self.shift_two = small[2:3, :], small[3:4, :]
        self.bias_one, self.bias_two = twice(small[4:5, :]), twice(small[5:6, :])
        self.bias_down = jnp.concatenate([small[6:7, :], small[7:8, :]], axis=1)
        self.scale_plus = refs.modulation[0, pl.ds(sample, 1), :]
        self.offset = refs.modulation[1, pl.ds(sample, 1), :]
        self.nothing = jnp.zeros((8, 2 * C), jnp.float32)

    def keep(self, **values):
        for name, value in values.items():
            place = STATE.index(name)
            self.state[place : place + 1, :] = value

    def kept(self, name):
        place = STATE.index(name)
        return self.state[place : place + 1, :]

    def report(self, place, value):
        self.refs.sums[place, pl.ds(self.sample, 1), :] = value

    def field(self, pair):
        return jnp.concatenate(
            [
                self.x_ref[pair, 0].astype(jnp.float32),
                self.x_ref[pair, 1].astype(jnp.float32),
            ],
            axis=1,
        )

    def means(self, first, second):
        return group_means(first, second, self.same_group, self.entries)

    def first_stats(self):
        def body(pair, carry):
            value = self.field(pair)
            return carry[0] + folded(value), carry[1] + folded(value * value)

        total, squares = over(self.pairs, 8, body, (self.nothing, self.nothing))
        self.partial[0], self.partial[1] = total, squares

    def partial_sums(self):
        return channel_sum(self.partial[0]), channel_sum(self.partial[1])

    def norm_of(self):
        mean, square = self.means(*self.partial_sums())
        inverse = lax.rsqrt(square - mean * mean + NORM_EPS)
        return inverse, -mean * inverse

    def first_act(self):
        inverse, center = self.norm_of()
        self.keep(inverse_one=inverse, center_one=center)
        gain = twice(inverse * self.gain_one)
        shift = twice(center * self.gain_one + self.shift_one)

        def body(pair, carry):
            value, slope = gelu_pair(self.field(pair) * gain + shift)
            put_shifted(self.act_one, pair, value)
            self.slope_one[pair] = slope
            return carry

        over(self.pairs, 8, body, 0)
        close_ring(self.act_one, self.pairs)

    def first_conv(self):
        def body(step, carry):
            start = step * self.size
            value = (
                jnp.dot(
                    windows(self.act_one, start, self.size),
                    self.refs.fwd_one[...],
                    preferred_element_type=jnp.float32,
                )
                + self.bias_one
            )
            self.conv_one[pl.ds(start, self.size)] = value.reshape(self.size, FIELD_COLS, 2 * C)
            return carry[0] + folded(value), carry[1] + folded(value * value)

        total, squares = over_steps(self.steps, body, (self.nothing, self.nothing))
        self.partial[0], self.partial[1] = total, squares

    def second_act(self):
        inverse, center = self.norm_of()
        self.keep(inverse_two=inverse, center_two=center)
        factor = self.gain_two * self.scale_plus
        gain = twice(inverse * factor)
        shift = twice(center * factor + self.shift_two * self.scale_plus + self.offset)

        def body(pair, carry):
            value, slope = gelu_pair(self.conv_one[pair] * gain + shift)
            put_shifted(self.act_two, pair, value)
            self.slope_two[pair] = slope
            return carry

        over(self.pairs, 8, body, 0)
        close_ring(self.act_two, self.pairs)

    def second_conv(self):
        def body(step, carry):
            start = step * self.size
            value = (
                jnp.dot(
                    windows(self.act_two, start, self.size),
                    self.refs.fwd_two[...],
                    preferred_element_type=jnp.float32,
                )
                + self.bias_two
            )
            value = value.reshape(self.size, FIELD_COLS, 2 * C)
            for half, ref in ((0, self.sum_even), (1, self.sum_odd)):
                base = self.x_ref[pl.ds(start, self.size), half].astype(jnp.float32)
                ref[pl.ds(start, self.size)] = base + value[:, :, half * C : half * C + C]
            return carry

        over_steps(self.steps, body)

    def split_columns(self):
        def body(pair, carry):
            even, odd = [], []
            for ref in (self.sum_even, self.sum_odd):
                even.append(ref[pair, pl.ds(0, HALF_COLS, stride=2), :])
                odd.append(ref[pair, pl.ds(1, HALF_COLS, stride=2), :])
            even = jnp.concatenate(even, axis=1)
            odd = jnp.concatenate(odd, axis=1)
            self.down_win[0, pair + 1] = pltpu.roll(odd, 1, 0).astype(jnp.bfloat16)
            self.down_win[1, pair + 1] = even.astype(jnp.bfloat16)
            self.down_win[2, pair + 1] = odd.astype(jnp.bfloat16)
            return carry

        over(self.pairs, 8, body, 0)
        self.down_win[:, 0, :, C:] = self.down_win[:, self.pairs, :, C:]

    def shift_cotangent(self):
        def body(pair, carry):
            value = self.cot_ref[pair]
            wide = value.astype(jnp.float32)
            self.cot_win[0, pair] = value
            self.cot_win[1, pair] = pltpu.roll(wide, HALF_COLS - 1, 0).astype(jnp.bfloat16)
            return carry + folded(wide)

        total = over(self.pairs, 8, body, self.nothing)
        self.cot_win[:, self.pairs] = self.cot_win[:, 0]
        self.refs.raw_sums[16:24, :] = self.refs.raw_sums[16:24, :] + total

    def down_windows(self, start):
        pieces = [
            self.down_win[tap, pl.ds(start + 1, self.size)].reshape(self.small, 2 * C)
            for tap in range(3)
        ]
        pieces += [
            self.down_win[tap, pl.ds(start, self.size), :, C:].reshape(self.small, C)
            for tap in range(3)
        ]
        return jnp.concatenate(pieces, axis=1)

    def down_output(self):
        def body(step, carry):
            start = step * self.size
            value = jnp.dot(
                self.down_windows(start), self.refs.down_fwd[...], preferred_element_type=jnp.float32
            )
            self.out_ref[pl.ds(start, self.size)] = (
                (value + self.bias_down)
                .reshape(self.size, HALF_COLS, 2 * C)
                .astype(jnp.bfloat16)
            )
            return carry

        over_steps(self.steps, body)

    def add_down_grad(self):
        def body(step, carry):
            start = step * self.size
            here = self.cot_win[0, pl.ds(start, self.size)].reshape(self.small, 2 * C)
            product = jnp.dot(
                here.T, self.down_windows(start), preferred_element_type=jnp.float32
            )
            for position in range(9):
                row_tap, tap = DOWN_ORDER[position]
                lanes = pl.ds((3 * row_tap + tap) * C, C)
                self.refs.down_grad[:, lanes] = (
                    self.refs.down_grad[:, lanes] + product[:, position * C : position * C + C]
                )
            return carry

        over_steps(self.steps, body)

    def down_adjoint(self):
        def body(step, carry):
            start = step * self.size
            pieces = [
                self.cot_win[shift, pl.ds(start + below, self.size)].reshape(self.small, 2 * C)
                for below in range(2)
                for shift in range(2)
            ]
            even = jnp.dot(
                jnp.concatenate([pieces[0], pieces[2]], axis=1),
                self.refs.down_even[...],
                preferred_element_type=jnp.float32,
            ).reshape(self.size, HALF_COLS, 2 * C)
            odd = jnp.dot(
                jnp.concatenate(pieces, axis=1),
                self.refs.down_odd[...],
                preferred_element_type=jnp.float32,
            ).reshape(self.size, HALF_COLS, 2 * C)
            for half, ref in ((0, self.grad_even), (1, self.grad_odd)):
                lanes = slice(half * C, half * C + C)
                for inner in range(self.size):
                    ref[start + inner, pl.ds(0, HALF_COLS, stride=2), :] = even[inner, :, lanes]
                    ref[start + inner, pl.ds(1, HALF_COLS, stride=2), :] = odd[inner, :, lanes]
            return carry

        over_steps(self.steps, body)

    def second_grad(self):
        def body(pair, carry):
            value = jnp.concatenate([self.grad_even[pair], self.grad_odd[pair]], axis=1)
            put_shifted(self.grad_two, pair, value)
            return carry + folded(value)

        total = over(self.pairs, 8, body, self.nothing)
        close_ring(self.grad_two, self.pairs)
        self.refs.raw_sums[8:16, :] = self.refs.raw_sums[8:16, :] + total

    def second_conv_grad(self):
        add_conv_grad(self.refs.conv_grad_two, self.act_two, self.grad_two, self.pairs)

    def second_back(self):
        def body(step, carry):
            start = step * self.size
            value = jnp.dot(
                windows(self.grad_two, start, self.size),
                self.refs.back_two[...],
                preferred_element_type=jnp.float32,
            )
            value = value * self.slope_two[pl.ds(start, self.size)].reshape(self.rows, 2 * C)
            self.grad_mid[pl.ds(start, self.size)] = value.reshape(self.size, FIELD_COLS, 2 * C)
            conv = self.conv_one[pl.ds(start, self.size)].reshape(self.rows, 2 * C)
            return carry[0] + folded(value), carry[1] + folded(value * conv)

        total, cross = over_steps(self.steps, body, (self.nothing, self.nothing))
        self.partial[0], self.partial[1] = total, cross

    def first_grad(self):
        inverse, center = self.kept("inverse_two"), self.kept("center_two")
        total, cross = self.partial_sums()
        cross = cross * inverse + total * center
        self.report(0, cross)
        self.report(1, total)
        factor = self.scale_plus * self.gain_two
        mean_grad, mean_cross = self.means(total * factor, cross * factor)
        from_mid = twice(inverse * factor)
        from_conv = twice(inverse * inverse * mean_cross)
        from_mean = twice(inverse * (mean_grad + center * mean_cross))

        def body(pair, carry):
            value = self.grad_mid[pair] * from_mid - from_mean - self.conv_one[pair] * from_conv
            put_shifted(self.grad_one, pair, value)
            return carry + folded(value)

        total = over(self.pairs, 8, body, self.nothing)
        close_ring(self.grad_one, self.pairs)
        self.refs.raw_sums[0:8, :] = self.refs.raw_sums[0:8, :] + total

    def first_conv_grad(self):
        add_conv_grad(self.refs.conv_grad_one, self.act_one, self.grad_one, self.pairs)

    def first_back(self):
        def body(step, carry):
            start = step * self.size
            value = jnp.dot(
                windows(self.grad_one, start, self.size),
                self.refs.back_one[...],
                preferred_element_type=jnp.float32,
            )
            value = value * self.slope_one[pl.ds(start, self.size)].reshape(self.rows, 2 * C)
            self.grad_mid[pl.ds(start, self.size)] = value.reshape(self.size, FIELD_COLS, 2 * C)
            base = jnp.concatenate(
                [
                    self.x_ref[pl.ds(start, self.size), half]
                    .astype(jnp.float32)
                    .reshape(self.rows, C)
                    for half in range(2)
                ],
                axis=1,
            )
            return carry[0] + folded(value), carry[1] + folded(value * base)

        total, cross = over_steps(self.steps, body, (self.nothing, self.nothing))
        self.partial[0], self.partial[1] = total, cross

    def field_grad(self, rows_ref):
        inverse, center = self.kept("inverse_one"), self.kept("center_one")
        total, cross = self.partial_sums()
        cross = cross * inverse + total * center
        self.report(2, cross)
        self.report(3, total)
        mean_grad, mean_cross = self.means(total * self.gain_one, cross * self.gain_one)
        from_pre = twice(inverse * self.gain_one)
        from_field = twice(inverse * inverse * mean_cross)
        from_mean = twice(inverse * (mean_grad + center * mean_cross))

        def body(pair, carry):
            summed = jnp.concatenate([self.grad_even[pair], self.grad_odd[pair]], axis=1)
            change = self.grad_mid[pair] * from_pre - from_mean - self.field(pair) * from_field
            value = (summed + change).astype(jnp.bfloat16)
            rows_ref[pair, 0] = value[:, :C]
            rows_ref[pair, 1] = value[:, C:]
            return carry

        over(self.pairs, 8, body, 0)


STATE = (
    "inverse_one",
    "center_one",
    "inverse_two",
    "center_two",
)
BEFORE = -1
SLOTS = (
    (
        ("first_stats", 0),
        ("shift_cotangent", 0),
        ("add_down_grad", BEFORE),
        ("second_conv_grad", BEFORE),
    ),
    (
        ("first_act", 0),
        ("first_stats", 1),
        ("down_adjoint", 0),
        ("first_conv_grad", BEFORE),
    ),
    (
        ("first_act", 1),
        ("second_grad", 0),
        ("shift_cotangent", 1),
        ("first_conv", 0),
        ("down_adjoint", 1),
    ),
    (("second_act", 0), ("second_grad", 1), ("first_conv", 1)),
    (("second_act", 1), ("second_back", 0), ("second_conv", 0)),
    (("first_grad", 0), ("split_columns", 0), ("second_back", 1), ("second_conv_grad", 0)),
    (("first_grad", 1), ("first_back", 0), ("second_conv", 1)),
    (("field_grad", 0), ("split_columns", 1), ("first_back", 1), ("first_conv_grad", 0)),
    (("field_grad", 1), ("down_output", 0), ("add_down_grad", 0), ("down_output", 1)),
)
LATE = ("add_down_grad", "second_conv_grad", "first_conv_grad")


def start_all(copies):
    for copy in copies:
        copy.start()


def peers(axis, count, pairs_of, sends, receives):
    return [
        to_peer(axis, step, count, source(step), target(step), sends.at[place, step], receives.at[place, step])
        for step in range(1, count)
        for place, (source, target) in pairs_of
    ]


def same(ref):
    return lambda step: ref


def slot_of(ref):
    return lambda step: ref.at[step]


def step_kernel(sizes, *args):
    row_count, batch_count, pairs, samples, together = sizes
    names = INPUTS + OUTPUTS + SCRATCH
    refs = SimpleNamespace(**dict(zip(names, args[: len(names)])))
    scratch = args[len(names) :]
    base = pl.program_id(0) * together
    row, batch = lax.axis_index("row"), lax.axis_index("batch")
    share = pairs // row_count

    def send_field(index, carry):
        mine = refs.fields.at[index, pl.ds(row * share, share)]
        for step in range(1, row_count):
            place = lax.rem(row + step, row_count) * samples + index
            to_peer(
                "row",
                step,
                row_count,
                refs.field.at[place],
                mine,
                refs.field_sent,
                refs.field_sem.at[index],
            ).start()
        pltpu.make_async_copy(
            refs.field.at[row * samples + index], mine, refs.field_sem.at[index]
        ).start()
        return carry

    def send_grad(index):
        target = refs.grad_out.at[row * samples + index]
        for step in range(1, row_count):
            place = lax.rem(row + step, row_count) * share
            to_peer(
                "row",
                step,
                row_count,
                refs.grad_rows.at[index, pl.ds(place, share)],
                target,
                refs.grad_sent,
                refs.grad_sem,
            ).start()
        pltpu.make_async_copy(
            refs.grad_rows.at[index, pl.ds(row * share, share)], target, refs.grad_sem
        ).start()

    @pl.when(base == 0)
    def _():
        greet(row_count, batch_count)
        own = pltpu.make_async_copy(refs.shard, refs.shards.at[row, batch], refs.local_sem)
        own.start()
        copies = peers(
            "batch",
            batch_count,
            [
                (0, (same(refs.shard), same(refs.shards.at[row, batch]))),
                (1, (same(refs.small), slot_of(refs.small_z))),
            ],
            refs.send_z,
            refs.recv_z,
        )
        start_all(copies)
        lax.fori_loop(0, together, send_field, 0)
        for ref in (refs.conv_grad_one, refs.conv_grad_two, refs.down_grad, refs.raw_sums, refs.sums):
            ref[...] = jnp.zeros_like(ref)
        if together > 1:
            for ref in scratch[-16:-12] + scratch[-4:-2]:
                ref[...] = jnp.zeros_like(ref)
        own.wait()
        finish(copies)
        total = refs.small[...]
        for step in range(1, batch_count):
            total = total + refs.small_z[step]
        refs.small_one[...] = total
        copies = peers(
            "row",
            row_count,
            [
                (0, (same(refs.shards.at[row]), same(refs.shards.at[row]))),
                (1, (same(refs.small_one), slot_of(refs.small_row))),
            ],
            refs.send_row,
            refs.recv_row,
        )
        start_all(copies)
        lax.fori_loop(together, samples, send_field, 0)
        finish(copies)
        total = refs.small_one[...]
        for step in range(1, row_count):
            total = total + refs.small_row[step]
        refs.small_all[...] = total
        lay_out(row_count, batch_count, refs)
        modulate(refs)

    @pl.when(base > 0)
    def _():
        for place in range(together):
            send_grad(base - together + place)

    for place in range(together):
        arrived = refs.fields.at[base + place]
        pltpu.make_async_copy(arrived, arrived, refs.field_sem.at[base + place]).wait()
    stages = [
        Sample(
            pairs,
            base + place,
            refs.fields.at[base + place],
            refs.cot.at[place],
            refs.block_out.at[place],
            refs,
            scratch[16 * place : 16 * place + 16],
        )
        for place in range(together)
    ]

    def run_slot(slot):
        for name, place in slot:
            if place >= together or (place == BEFORE and together == 1):
                continue
            stage = getattr(stages[place], name)
            if name == "field_grad":
                stage(refs.grad_rows.at[base + place])
            else:
                stage()

    for slot in SLOTS:
        run_slot(slot)

    @pl.when(base == samples - together)
    def _():
        for place in range(together):
            send_grad(base + place)
        if together > 1:
            for name in LATE:
                getattr(stages[-1], name)()
        reduce_all(row_count, batch_count, refs)
        pltpu.make_async_copy(refs.grad_out, refs.grad_out, refs.grad_sem).wait()
        others = pl.ds(0, pairs - share)
        for ref, sem in ((refs.fields, refs.field_sent), (refs.grad_rows, refs.grad_sent)):
            pltpu.make_async_copy(ref.at[:, others], ref.at[:, others], sem).wait()


INPUTS = ("field", "cot", "shard", "small", "embedded", "group")
OUTPUTS = ("block_out", "grad_out", "owned", "small_grad", "norm")
SCRATCH = (
    "fwd_one",
    "back_one",
    "fwd_two",
    "back_two",
    "down_fwd",
    "down_even",
    "down_odd",
    "small_all",
    "embed_in_t",
    "embed_out_t",
    "modulation",
    "hidden",
    "hidden_slope",
    "sums",
    "raw_sums",
    "conv_grad_one",
    "conv_grad_two",
    "down_grad",
    "shards",
    "small_z",
    "small_one",
    "small_row",
    "conv_t",
    "down_t",
    "fields",
    "grad_rows",
    "row_send",
    "row_take",
    "batch_send",
    "batch_take",
    "small_send",
    "small_take",
    "small_next",
    "small_last",
    "square_send",
    "square_take",
    "square_next",
    "square_last",
    "field_sem",
    "field_sent",
    "grad_sem",
    "grad_sent",
    "local_sem",
    "send_z",
    "recv_z",
    "send_row",
    "recv_row",
    "send_sem",
    "recv_sem",
)
DOWN_ORDER = ((1, 0), (2, 0), (1, 1), (2, 1), (1, 2), (2, 2), (0, 0), (0, 1), (0, 2))


def lay_out(row_count, batch_count, refs):
    depth, share, wide_share = 9 * C // batch_count, C // row_count, C2 // row_count
    height = 2 * share + wide_share
    embed_share, hidden_share = EMB // batch_count, HID // batch_count
    for place in range(row_count):
        parts = [refs.shards[place, part].astype(jnp.float32) for part in range(batch_count)]
        main = jnp.concatenate([part[:, :depth] for part in parts], axis=1)
        for which in range(2):
            refs.conv_t[which, place * share : place * share + share, :] = main[
                which * share : which * share + share
            ]
        refs.down_t[place * wide_share : place * wide_share + wide_share, :] = main[2 * share :]
        refs.embed_in_t[place * height : place * height + height, :] = jnp.concatenate(
            [part[:, depth : depth + embed_share] for part in parts], axis=1
        )
        tail = depth + embed_share
        half_rows, half_lanes = height // 2, hidden_share // 2
        lanes = []
        for part in parts:
            lanes.append(part[:half_rows, tail : tail + half_lanes])
            lanes.append(part[half_rows:, tail : tail + half_lanes])
        refs.embed_out_t[place * half_rows : place * half_rows + half_rows, :] = jnp.concatenate(
            lanes, axis=1
        )
    for which, forward, back in (
        (0, refs.fwd_one, refs.back_one),
        (1, refs.fwd_two, refs.back_two),
    ):
        zero = jnp.zeros((C, C), jnp.bfloat16)
        for tap in range(3):
            direct = [
                refs.conv_t[which, :, (3 * row_tap + tap) * C : (3 * row_tap + tap) * C + C]
                for row_tap in range(3)
            ]
            fill_blocks(forward, tap, [block.T.astype(jnp.bfloat16) for block in direct], zero)
            fill_blocks(
                back, 2 - tap, [block.astype(jnp.bfloat16) for block in direct[::-1]], zero
            )
    zero = jnp.zeros((C2, C), jnp.bfloat16)
    back = {}
    for position in range(9):
        row_tap, tap = DOWN_ORDER[position]
        block = refs.down_t[:, (3 * row_tap + tap) * C : (3 * row_tap + tap) * C + C]
        refs.down_fwd[position * C : position * C + C, :] = block.T.astype(jnp.bfloat16)
        back[row_tap, tap] = block.astype(jnp.bfloat16)
    even = ((back[1, 1], back[2, 1]), (zero, back[0, 1]))
    odd = (
        (back[1, 2], back[2, 2]),
        (back[1, 0], back[2, 0]),
        (zero, back[0, 2]),
        (zero, back[0, 0]),
    )
    for ref, table in ((refs.down_even, even), (refs.down_odd, odd)):
        for position, (left, right) in enumerate(table):
            ref[position * C2 : position * C2 + C2, :C] = left
            ref[position * C2 : position * C2 + C2, C:] = right


def lanes_of(ref, first, last):
    return jnp.concatenate([ref[place : place + 1, :] for place in range(first, last)], axis=1)


def modulate(refs):
    small = refs.small_all
    before = dot_last(refs.embedded[...], refs.embed_in_t[...]) + lanes_of(small, 8, 12)
    hidden, slope = gelu_pair(before)
    refs.hidden[...] = hidden
    refs.hidden_slope[...] = slope
    result = dot_last(hidden, refs.embed_out_t[...]) + lanes_of(small, 12, 14)
    refs.modulation[0] = 1.0 + result[:, :C]
    refs.modulation[1] = result[:, C:]


def fill_blocks(ref, tap, blocks, zero):
    table = (
        (blocks[1], blocks[0]),
        (blocks[2], blocks[1]),
        (blocks[0], zero),
        (zero, blocks[2]),
    )
    for position, (left, right) in enumerate(table):
        base = (4 * tap + position) * C
        ref[base : base + C, :C] = left
        ref[base : base + C, C:] = right


def dot_last(lhs, rhs):
    return lax.dot_general(
        lhs,
        rhs,
        (((1,), (1,)), ((), ())),
        precision=HIGHEST,
        preferred_element_type=jnp.float32,
    )


def dot_first(lhs, rhs):
    return lax.dot_general(
        lhs,
        rhs,
        (((0,), (0,)), ((), ())),
        precision=HIGHEST,
        preferred_element_type=jnp.float32,
    )


def reduce_all(row_count, batch_count, refs):
    row, batch = lax.axis_index("row"), lax.axis_index("batch")
    depth, share, wide_share = 9 * C // batch_count, C // row_count, C2 // row_count
    height = 2 * share + wide_share
    embed_share, hidden_share = EMB // batch_count, HID // batch_count
    mid_cross, mid_total = refs.sums[0], refs.sums[1]
    gain_two, shift_two = refs.small_all[1:2, :], refs.small_all[3:4, :]
    scale_plus = refs.modulation[0]
    grad_mod = jnp.concatenate([gain_two * mid_cross + shift_two * mid_total, mid_total], axis=1)
    grad_embed_out = dot_first(grad_mod, refs.hidden[...])
    grad_hidden = (
        jnp.dot(
            grad_mod, refs.embed_out_t[...], precision=HIGHEST, preferred_element_type=jnp.float32
        )
        * refs.hidden_slope[...]
    )
    grad_embed_in = dot_first(grad_hidden, refs.embedded[...])

    def down_sum(value):
        return jnp.sum(value, axis=0, keepdims=True)

    small_rows = [
        down_sum(refs.sums[2]),
        down_sum(mid_cross * scale_plus),
        down_sum(refs.sums[3]),
        down_sum(mid_total * scale_plus),
        channel_sum(refs.raw_sums[0:8]),
        channel_sum(refs.raw_sums[8:16]),
    ]
    cot_total = down_sum(refs.raw_sums[16:24])
    small_rows += [cot_total[:, :C], cot_total[:, C:]]
    hidden_total, mod_total = down_sum(grad_hidden), down_sum(grad_mod)
    small_rows += [hidden_total[:, lane : lane + C] for lane in range(0, HID, C)]
    small_rows += [mod_total[:, lane : lane + C] for lane in range(0, 2 * C, C)]
    small_rows.append(jnp.zeros((2, C), jnp.float32))
    refs.small_send[...] = jnp.concatenate(small_rows, axis=0)
    half_rows = height // 2
    for place in range(row_count):
        low, high = place * share, place * share + share
        refs.row_send[place, :, : 9 * C] = jnp.concatenate(
            [
                refs.conv_grad_one[low:high],
                refs.conv_grad_two[low:high],
                refs.down_grad[place * wide_share : place * wide_share + wide_share],
            ],
            axis=0,
        ).astype(jnp.bfloat16)
        refs.row_send[place, :, 9 * C : 10 * C] = grad_embed_in[
            place * height : place * height + height
        ].astype(jnp.bfloat16)
        piece = grad_embed_out[place * half_rows : place * half_rows + half_rows]
        refs.row_send[place, :, 10 * C :] = jnp.concatenate(
            [piece[:, : HID // 2], piece[:, HID // 2 :]], axis=0
        ).astype(jnp.bfloat16)
    copies = []
    for step in range(1, row_count):
        copies.append(
            to_peer(
                "row",
                step,
                row_count,
                refs.row_send.at[lax.rem(row + step, row_count)],
                refs.row_take.at[step],
                refs.send_sem.at[0, step],
                refs.recv_sem.at[0, step],
            )
        )
        copies.append(
            to_peer(
                "row",
                step,
                row_count,
                refs.small_send,
                refs.small_take.at[step],
                refs.send_sem.at[1, step],
                refs.recv_sem.at[1, step],
            )
        )
    for copy in copies:
        copy.start()
    total = refs.row_send[row].astype(jnp.float32)
    finish(copies)
    small_total = refs.small_send[...]
    for step in range(1, row_count):
        total = total + refs.row_take[step].astype(jnp.float32)
        small_total = small_total + refs.small_take[step]
    refs.small_next[...] = small_total
    for part in range(batch_count):
        per_half = batch_count // 2
        rows = slice(0, half_rows) if part < per_half else slice(half_rows, height)
        base = 10 * C + hidden_share * (part % per_half)
        piece = total[rows, base : base + hidden_share]
        refs.batch_send[part] = jnp.concatenate(
            [
                total[:, part * depth : part * depth + depth],
                total[:, 9 * C + part * embed_share : 9 * C + part * embed_share + embed_share],
                jnp.concatenate([piece[:, : hidden_share // 2], piece[:, hidden_share // 2 :]], axis=0),
            ],
            axis=1,
        ).astype(jnp.bfloat16)
    copies = []
    for step in range(1, batch_count):
        copies.append(
            to_peer(
                "batch",
                step,
                batch_count,
                refs.batch_send.at[lax.rem(batch + step, batch_count)],
                refs.batch_take.at[step],
                refs.send_sem.at[2, step],
                refs.recv_sem.at[2, step],
            )
        )
        copies.append(
            to_peer(
                "batch",
                step,
                batch_count,
                refs.small_next,
                refs.small_last.at[step],
                refs.send_sem.at[3, step],
                refs.recv_sem.at[3, step],
            )
        )
    for copy in copies:
        copy.start()
    owned = refs.batch_send[batch].astype(jnp.float32)
    finish(copies)
    small_total = refs.small_next[...]
    for step in range(1, batch_count):
        owned = owned + refs.batch_take[step].astype(jnp.float32)
        small_total = small_total + refs.small_last[step]
    squares = jnp.sum(jnp.sum(owned * owned, axis=0, keepdims=True), axis=1, keepdims=True)
    refs.square_send[...] = jnp.broadcast_to(squares, (8, C))
    copies = [
        to_peer(
            "row",
            step,
            row_count,
            refs.square_send,
            refs.square_take.at[step],
            refs.send_sem.at[4, step],
            refs.recv_sem.at[4, step],
        )
        for step in range(1, row_count)
    ]
    for copy in copies:
        copy.start()
    finish(copies)
    squares = refs.square_send[...]
    for step in range(1, row_count):
        squares = squares + refs.square_take[step]
    refs.square_next[...] = squares
    copies = [
        to_peer(
            "batch",
            step,
            batch_count,
            refs.square_next,
            refs.square_last.at[step],
            refs.send_sem.at[5, step],
            refs.recv_sem.at[5, step],
        )
        for step in range(1, batch_count)
    ]
    for copy in copies:
        copy.start()
    finish(copies)
    squares = refs.square_next[...]
    for step in range(1, batch_count):
        squares = squares + refs.square_last[step]
    small_squares = jnp.sum(
        jnp.sum(small_total * small_total, axis=0, keepdims=True), axis=1, keepdims=True
    )
    norm = jnp.sqrt(squares + small_squares)
    clip = jnp.minimum(1.0, CLIP_NORM / (norm + 1e-06))[0:1, 0:1]
    refs.norm[...] = norm
    refs.owned[...] = owned * clip
    refs.small_grad[...] = small_total * clip


def pack_pieces(conv, down, embed_in, embed_out):
    half = embed_out.shape[0] // 2
    tall = jnp.concatenate([embed_out[:half].T, embed_out[half:].T], axis=0)
    return jnp.concatenate(
        [jnp.concatenate([conv[0].T, conv[1].T, down.T], axis=0), embed_in.T, tall], axis=1
    )


def unpack_pieces(owned, depth, share, embed_share):
    height, half = owned.shape[0], owned.shape[0] // 2
    conv = jnp.stack([owned[:share, :depth].T, owned[share : 2 * share, :depth].T])
    down = owned[2 * share :, :depth].T
    embed_in = owned[:, depth : depth + embed_share].T
    tall = owned[:, depth + embed_share :]
    embed_out = jnp.concatenate([tall[:half].T, tall[half:].T], axis=0)
    return conv, down, embed_in, embed_out


def run_step(field_in, cotangent, packed, small_tile, embedded):
    row_count, batch_count = (lax.axis_size("row"), lax.axis_size("batch"))
    samples = cotangent.shape[0]
    padded = embedded.shape[0]
    pairs = field_in.shape[1] // 2 * row_count
    together = chunk_of(samples, 2)
    share = pairs // row_count
    height, width = packed.shape
    halves = field_in.reshape(field_in.shape[0], share, 2, FIELD_COLS, C)
    same_group = jnp.asarray(
        np.kron(np.eye(GROUPS), np.ones((C // GROUPS, C // GROUPS))), jnp.float32
    )
    low, full = jnp.bfloat16, jnp.float32
    anywhere = pl.BlockSpec(memory_space=pl.ANY)

    def whole(array):
        return pl.BlockSpec(array.shape, lambda i: (0,) * len(array.shape))

    def per_step(array):
        rank = len(array.shape)
        return pl.BlockSpec((together,) + array.shape[1:], lambda i: (i,) + (0,) * (rank - 1))

    outs = (
        jax.ShapeDtypeStruct(cotangent.shape, low),
        jax.ShapeDtypeStruct(halves.shape, low),
        jax.ShapeDtypeStruct((height, width), full),
        jax.ShapeDtypeStruct((16, C), full),
        jax.ShapeDtypeStruct((8, C), full),
    )
    ring = pltpu.VMEM((3, pairs + 2, FIELD_COLS, 2 * C), low)
    wide = pltpu.VMEM((pairs, FIELD_COLS, 2 * C), full)
    half = pltpu.VMEM((pairs, FIELD_COLS, C), full)
    fields = pltpu.VMEM((samples, pairs, 2, FIELD_COLS, C), low)
    dma = pltpu.SemaphoreType.DMA
    most = max(row_count, batch_count)
    tile = (16, C)
    scratch = (
        [pltpu.VMEM((12 * C, 2 * C), low)] * 4
        + [
            pltpu.VMEM((9 * C, C2), low),
            pltpu.VMEM((2 * C2, 2 * C), low),
            pltpu.VMEM((4 * C2, 2 * C), low),
            pltpu.VMEM(tile, full),
            pltpu.VMEM((HID, EMB), full),
            pltpu.VMEM((2 * C, HID), full),
            pltpu.VMEM((2, padded, C), full),
            pltpu.VMEM((padded, HID), full),
            pltpu.VMEM((padded, HID), full),
            pltpu.VMEM((4, padded, C), full),
            pltpu.VMEM((24, 2 * C), full),
            pltpu.VMEM((C, 9 * C), full),
            pltpu.VMEM((C, 9 * C), full),
            pltpu.VMEM((C2, 9 * C), full),
            pltpu.VMEM((row_count, batch_count, height, width), low),
            pltpu.VMEM((batch_count,) + tile, full),
            pltpu.VMEM(tile, full),
            pltpu.VMEM((row_count,) + tile, full),
            pltpu.VMEM((2, C, 9 * C), full),
            pltpu.VMEM((C2, 9 * C), full),
            fields,
            fields,
            pltpu.VMEM((row_count, height, 12 * C), low),
            pltpu.VMEM((row_count, height, 12 * C), low),
            pltpu.VMEM((batch_count, height, width), low),
            pltpu.VMEM((batch_count, height, width), low),
            pltpu.VMEM(tile, full),
            pltpu.VMEM((row_count,) + tile, full),
            pltpu.VMEM(tile, full),
            pltpu.VMEM((batch_count,) + tile, full),
            pltpu.VMEM((8, C), full),
            pltpu.VMEM((row_count, 8, C), full),
            pltpu.VMEM((8, C), full),
            pltpu.VMEM((batch_count, 8, C), full),
            dma((samples,)),
            dma,
            dma,
            dma,
            dma,
            dma((2, batch_count)),
            dma((2, batch_count)),
            dma((2, row_count)),
            dma((2, row_count)),
            dma((6, most)),
            dma((6, most)),
        ]
        + (
            [ring] * 4
            + [wide] * 4
            + [half] * 4
            + [
                pltpu.VMEM((3, pairs + 1, HALF_COLS, 2 * C), low),
                pltpu.VMEM((2, pairs + 1, HALF_COLS, C2), low),
                pltpu.VMEM((8, C), full),
                pltpu.VMEM((2, 8, 2 * C), full),
            ]
        )
        * together
    )
    result = pl.pallas_call(
        functools.partial(step_kernel, (row_count, batch_count, pairs, samples, together)),
        grid=(samples // together,),
        in_specs=[anywhere, per_step(cotangent)]
        + [whole(array) for array in (packed, small_tile, embedded, same_group)],
        out_specs=[per_step(outs[0]), anywhere] + [whole(out) for out in outs[2:]],
        out_shape=outs,
        scratch_shapes=scratch,
        compiler_params=pltpu.CompilerParams(
            dimension_semantics=("arbitrary",),
            vmem_limit_bytes=62 << 20,
            collective_id=0,
            has_side_effects=True,
        ),
        name="step",
    )(halves, cotangent, packed, small_tile, embedded, same_group)
    return (result[0], result[1].reshape(field_in.shape)) + tuple(result[2:])


def adam_update(weight, gradient, first_old, second_old, step_rate, clip_factor):
    scaled = gradient * clip_factor
    first_new = BETA_ONE * first_old + (1.0 - BETA_ONE) * scaled
    second_new = BETA_TWO * second_old + (1.0 - BETA_TWO) * scaled * scaled
    corrected = (
        first_new
        / (1.0 - BETA_ONE**STEP_COUNT)
        / (jnp.sqrt(second_new / (1.0 - BETA_TWO**STEP_COUNT)) + ADAM_EPS)
    )
    return (weight - step_rate * (corrected + DECAY * weight), first_new, second_new)


def body(
    field_in,
    refine_step,
    cotangent,
    conv_weight,
    down_weight,
    embed_in_weight,
    embed_out_weight,
    small_params,
    conv_first,
    down_first,
    embed_in_first,
    embed_out_first,
    small_first,
    conv_second,
    down_second,
    embed_in_second,
    embed_out_second,
    small_second,
):
    packed = pack_pieces(
        conv_weight.astype(jnp.bfloat16),
        down_weight.astype(jnp.bfloat16),
        embed_in_weight.astype(jnp.bfloat16),
        embed_out_weight.astype(jnp.bfloat16),
    )
    small_len = small_params.shape[0]
    place = (lax.axis_index("batch") * lax.axis_size("row") + lax.axis_index("row")) * small_len
    small_rounded = small_params.astype(jnp.bfloat16).astype(jnp.float32)
    small_tile = lax.dynamic_update_slice_in_dim(
        jnp.zeros((16 * C,), jnp.float32), small_rounded, place, 0
    ).reshape(16, C)
    owned = refine_step.shape[0] // lax.axis_size("row")
    padded = -(-owned // 8) * 8
    own_steps = lax.dynamic_slice_in_dim(refine_step, lax.axis_index("row") * owned, owned, 0)
    embedded = embed_steps(jnp.pad(own_steps, (0, padded - owned)))
    block_out, grad_start, owned_grads, small_grads, norm_tile = run_step(
        field_in, cotangent, packed, small_tile, embedded
    )
    grad_norm = norm_tile[0, 0]
    owned_shards = unpack_pieces(
        owned_grads, conv_weight.shape[1], conv_weight.shape[2], embed_in_weight.shape[0]
    ) + (lax.dynamic_slice_in_dim(small_grads.reshape(-1), place, small_len, 0),)
    clip_factor = 1.0
    conv_new = adam_update(
        conv_weight, owned_shards[0], conv_first, conv_second, RATE_MATRIX, clip_factor
    )
    down_new = adam_update(
        down_weight, owned_shards[1], down_first, down_second, RATE_MATRIX, clip_factor
    )
    embed_in_new = adam_update(
        embed_in_weight, owned_shards[2], embed_in_first, embed_in_second, RATE_MATRIX, clip_factor
    )
    embed_out_new = adam_update(
        embed_out_weight,
        owned_shards[3],
        embed_out_first,
        embed_out_second,
        RATE_MATRIX,
        clip_factor,
    )
    small_new = adam_update(
        small_params, owned_shards[4], small_first, small_second, RATE_SMALL, clip_factor
    )
    return (
        block_out,
        grad_start,
        grad_norm,
        conv_new[0],
        down_new[0],
        embed_in_new[0],
        embed_out_new[0],
        small_new[0],
        conv_new[1],
        down_new[1],
        embed_in_new[1],
        embed_out_new[1],
        small_new[1],
        conv_new[2],
        down_new[2],
        embed_in_new[2],
        embed_out_new[2],
        small_new[2],
    )


def solution(mesh):
    placed = (
        P("batch", "row", None, None),
        P("batch"),
        P(("batch", "row"), None, None, None),
        P(None, "batch", "row"),
        P("batch", "row"),
        P("batch", "row"),
        P("batch", "row"),
        P(("batch", "row")),
        P(None, "batch", "row"),
        P("batch", "row"),
        P("batch", "row"),
        P("batch", "row"),
        P(("batch", "row")),
        P(None, "batch", "row"),
        P("batch", "row"),
        P("batch", "row"),
        P("batch", "row"),
        P(("batch", "row")),
    )
    return jax.shard_map(
        body,
        mesh=mesh,
        in_specs=placed,
        out_specs=(
            P(("batch", "row"), None, None, None),
            P("batch", "row", None, None),
            P(),
            P(None, "batch", "row"),
            P("batch", "row"),
            P("batch", "row"),
            P("batch", "row"),
            P(("batch", "row")),
            P(None, "batch", "row"),
            P("batch", "row"),
            P("batch", "row"),
            P("batch", "row"),
            P(("batch", "row")),
            P(None, "batch", "row"),
            P("batch", "row"),
            P("batch", "row"),
            P("batch", "row"),
            P(("batch", "row")),
        ),
        check_vma=False,
    )
```

```python
import functools
import math
from types import SimpleNamespace

import jax
import jax.numpy as jnp
import numpy as np
from jax import lax
from jax.experimental import pallas as pl
from jax.experimental.pallas import tpu as pltpu
from jax.sharding import PartitionSpec as P

C = 128
C2 = 256
EMB = 128
HID = 512
GROUPS = 8
REFINE = 4


NORM_EPS = 1e-05
BETA_ONE = 0.9
BETA_TWO = 0.999
ADAM_EPS = 1e-08
DECAY = 0.01
RATE_MATRIX = 0.05
RATE_SMALL = 0.5
CLIP_NORM = 1.0
STEP_COUNT = 10
HIGHEST = lax.Precision.HIGHEST


def embed_steps(refine_step):
    halfway = EMB // 2
    frequency = jnp.exp(-math.log(10000.0) * jnp.arange(halfway).astype(jnp.float32) / halfway)
    angles = (refine_step.astype(jnp.float32) * (1000.0 / REFINE))[:, None] * frequency[None, :]
    return jnp.concatenate([jnp.sin(angles), jnp.cos(angles)], axis=1)


MESH = pl.DeviceIdType.MESH


def greet(row_count, batch_count=1):
    row, batch = lax.axis_index("row"), lax.axis_index("batch")
    barrier = pltpu.get_barrier_semaphore()
    for step in range(1, row_count):
        pl.semaphore_signal(
            barrier,
            inc=1,
            device_id={"row": lax.rem(row + step, row_count), "batch": batch},
            device_id_type=MESH,
        )
    for step in range(1, batch_count):
        pl.semaphore_signal(
            barrier,
            inc=1,
            device_id={"row": row, "batch": lax.rem(batch + step, batch_count)},
            device_id_type=MESH,
        )
    pl.semaphore_wait(barrier, row_count + batch_count - 2)


def to_peer(axis, step, count, source, target, send_sem, recv_sem):
    row, batch = lax.axis_index("row"), lax.axis_index("batch")
    if axis == "row":
        device = {"row": lax.rem(row + step, count), "batch": batch}
    else:
        device = {"row": row, "batch": lax.rem(batch + step, count)}
    return pltpu.make_async_remote_copy(
        src_ref=source,
        dst_ref=target,
        send_sem=send_sem,
        recv_sem=recv_sem,
        device_id=device,
        device_id_type=MESH,
    )


def to_row(place, source, target, send_sem, recv_sem):
    return pltpu.make_async_remote_copy(
        src_ref=source,
        dst_ref=target,
        send_sem=send_sem,
        recv_sem=recv_sem,
        device_id={"row": place, "batch": lax.axis_index("batch")},
        device_id_type=MESH,
    )


def sibling_of(row):
    return row + 1 - 2 * lax.rem(row, 2)


def finish(copies):
    for copy in copies:
        copy.wait()


FIELD_COLS = 64
HALF_COLS = 32
ROOT = math.sqrt(2.0 / math.pi)
CUBIC = ROOT * 0.044715


def chunk_of(total, most):
    size = min(total, most)
    while total % size:
        size -= 1
    return size


def over(total, most, body, init):
    size = chunk_of(total, most)

    def several(step, carry):
        for inner in range(size):
            carry = body(step * size + inner, carry)
        return carry

    if size == total:
        return several(0, init)
    return lax.fori_loop(0, total // size, several, init)


def folded(values):
    return jnp.sum(values.reshape(values.shape[0] // 8, 8, values.shape[1]), axis=0)


def twice(row):
    return jnp.concatenate([row, row], axis=1)


def channel_sum(partial):
    both = partial[:, :C] + partial[:, C:]
    return jnp.sum(both, axis=0, keepdims=True)


def group_means(first, second, same_group, entries):
    stacked = jnp.concatenate([first, second, jnp.zeros((6, C), jnp.float32)], axis=0)
    totals = jnp.dot(stacked, same_group, precision=HIGHEST, preferred_element_type=jnp.float32)
    return totals[0:1] / entries, totals[1:2] / entries


def gelu_pair(values):
    square = values * values
    weight = 0.5 + 0.5 * jnp.tanh(values * (ROOT + CUBIC * square))
    result = values * weight
    slope = weight + (result - result * weight) * (2.0 * ROOT + (6.0 * CUBIC) * square)
    return result, slope


def put_shifted(ref, pair, values):
    for tap, shift in ((0, 1), (1, 0), (2, FIELD_COLS - 1)):
        moved = pltpu.roll(values, shift, 0) if shift else values
        ref[tap, pair + 1] = moved.astype(jnp.bfloat16)


def close_ring(ref, pairs):
    ref[:, 0, :, C:] = ref[:, pairs, :, C:]
    ref[:, pairs + 1, :, :C] = ref[:, 1, :, :C]


def windows(ref, start, count):
    rows = count * FIELD_COLS
    pieces = []
    for tap in range(3):
        pieces.append(ref[tap, pl.ds(start + 1, count)].reshape(rows, 2 * C))
        pieces.append(ref[tap, pl.ds(start, count), :, C:].reshape(rows, C))
        pieces.append(ref[tap, pl.ds(start + 2, count), :, :C].reshape(rows, C))
    return jnp.concatenate(pieces, axis=1)


def over_steps(steps, body, init=0):
    if steps == 1:
        return body(0, init)
    return lax.fori_loop(0, steps, body, init)


def add_conv_grad(out_ref, act_ref, grad_ref, pairs):
    size = chunk_of(pairs, 8)
    rows = size * FIELD_COLS

    def body(step, carry):
        start = step * size
        grad = grad_ref[1, pl.ds(start + 1, size)].reshape(rows, 2 * C)
        product = jnp.dot(
            grad.T, windows(act_ref, start, size), preferred_element_type=jnp.float32
        )
        for tap in range(3):
            base = tap * 4 * C
            middle = product[:C, base : base + C] + product[C:, base + C : base + 2 * C]
            up = product[C:, base : base + C] + product[:C, base + 2 * C : base + 3 * C]
            down = product[:C, base + C : base + 2 * C] + product[C:, base + 3 * C : base + 4 * C]
            for row_tap, value in ((0, up), (1, middle), (2, down)):
                lanes = pl.ds((3 * row_tap + tap) * C, C)
                out_ref[:, lanes] = out_ref[:, lanes] + value
        return carry

    over_steps(pairs // size, body)


class Sample:
    def __init__(self, pairs, sample, x_ref, cot_ref, out_ref, refs, scratch):
        self.pairs, self.sample = pairs, sample
        self.x_ref, self.cot_ref, self.out_ref = x_ref, cot_ref, out_ref
        self.refs = refs
        (
            self.act_one,
            self.act_two,
            self.grad_one,
            self.grad_two,
            self.slope_one,
            self.slope_two,
            self.conv_one,
            self.grad_mid,
            self.sum_even,
            self.sum_odd,
            self.grad_even,
            self.grad_odd,
            self.down_win,
            self.cot_win,
            self.state,
            self.partial,
        ) = scratch
        self.entries = 2.0 * pairs * FIELD_COLS * (C // GROUPS)
        self.size = chunk_of(pairs, 8)
        self.steps = pairs // self.size
        self.rows = self.size * FIELD_COLS
        self.small = self.size * HALF_COLS
        self.same_group = refs.group[...]
        small = refs.small_all
        self.gain_one, self.gain_two = small[0:1, :], small[1:2, :]
        self.shift_one, self.shift_two = small[2:3, :], small[3:4, :]
        self.bias_one, self.bias_two = twice(small[4:5, :]), twice(small[5:6, :])
        self.bias_down = jnp.concatenate([small[6:7, :], small[7:8, :]], axis=1)
        self.scale_plus = refs.modulation[0, pl.ds(sample, 1), :]
        self.offset = refs.modulation[1, pl.ds(sample, 1), :]
        self.nothing = jnp.zeros((8, 2 * C), jnp.float32)

    def keep(self, **values):
        for name, value in values.items():
            place = STATE.index(name)
            self.state[place : place + 1, :] = value

    def kept(self, name):
        place = STATE.index(name)
        return self.state[place : place + 1, :]

    def report(self, place, value):
        self.refs.sums[place, pl.ds(self.sample, 1), :] = value

    def field(self, pair):
        return jnp.concatenate(
            [
                self.x_ref[pair, 0].astype(jnp.float32),
                self.x_ref[pair, 1].astype(jnp.float32),
            ],
            axis=1,
        )

    def means(self, first, second):
        return group_means(first, second, self.same_group, self.entries)

    def first_stats(self):
        def body(pair, carry):
            value = self.field(pair)
            return carry[0] + folded(value), carry[1] + folded(value * value)

        total, squares = over(self.pairs, 8, body, (self.nothing, self.nothing))
        self.partial[0], self.partial[1] = total, squares

    def partial_sums(self):
        return channel_sum(self.partial[0]), channel_sum(self.partial[1])

    def norm_of(self):
        mean, square = self.means(*self.partial_sums())
        inverse = lax.rsqrt(square - mean * mean + NORM_EPS)
        return inverse, -mean * inverse

    def first_act(self):
        inverse, center = self.norm_of()
        self.keep(inverse_one=inverse, center_one=center)
        gain = twice(inverse * self.gain_one)
        shift = twice(center * self.gain_one + self.shift_one)

        def body(pair, carry):
            value, slope = gelu_pair(self.field(pair) * gain + shift)
            put_shifted(self.act_one, pair, value)
            self.slope_one[pair] = slope
            return carry

        over(self.pairs, 8, body, 0)
        close_ring(self.act_one, self.pairs)

    def first_conv(self):
        def body(step, carry):
            start = step * self.size
            value = (
                jnp.dot(
                    windows(self.act_one, start, self.size),
                    self.refs.fwd_one[...],
                    preferred_element_type=jnp.float32,
                )
                + self.bias_one
            )
            self.conv_one[pl.ds(start, self.size)] = value.reshape(self.size, FIELD_COLS, 2 * C)
            return carry[0] + folded(value), carry[1] + folded(value * value)

        total, squares = over_steps(self.steps, body, (self.nothing, self.nothing))
        self.partial[0], self.partial[1] = total, squares

    def second_act(self):
        inverse, center = self.norm_of()
        self.keep(inverse_two=inverse, center_two=center)
        factor = self.gain_two * self.scale_plus
        gain = twice(inverse * factor)
        shift = twice(center * factor + self.shift_two * self.scale_plus + self.offset)

        def body(pair, carry):
            value, slope = gelu_pair(self.conv_one[pair] * gain + shift)
            put_shifted(self.act_two, pair, value)
            self.slope_two[pair] = slope
            return carry

        over(self.pairs, 8, body, 0)
        close_ring(self.act_two, self.pairs)

    def second_conv(self):
        def body(step, carry):
            start = step * self.size
            value = (
                jnp.dot(
                    windows(self.act_two, start, self.size),
                    self.refs.fwd_two[...],
                    preferred_element_type=jnp.float32,
                )
                + self.bias_two
            )
            value = value.reshape(self.size, FIELD_COLS, 2 * C)
            for half, ref in ((0, self.sum_even), (1, self.sum_odd)):
                base = self.x_ref[pl.ds(start, self.size), half].astype(jnp.float32)
                ref[pl.ds(start, self.size)] = base + value[:, :, half * C : half * C + C]
            return carry

        over_steps(self.steps, body)

    def split_columns(self):
        def body(pair, carry):
            even, odd = [], []
            for ref in (self.sum_even, self.sum_odd):
                even.append(ref[pair, pl.ds(0, HALF_COLS, stride=2), :])
                odd.append(ref[pair, pl.ds(1, HALF_COLS, stride=2), :])
            even = jnp.concatenate(even, axis=1)
            odd = jnp.concatenate(odd, axis=1)
            self.down_win[0, pair + 1] = pltpu.roll(odd, 1, 0).astype(jnp.bfloat16)
            self.down_win[1, pair + 1] = even.astype(jnp.bfloat16)
            self.down_win[2, pair + 1] = odd.astype(jnp.bfloat16)
            return carry

        over(self.pairs, 8, body, 0)
        self.down_win[:, 0, :, C:] = self.down_win[:, self.pairs, :, C:]

    def shift_cotangent(self):
        def body(pair, carry):
            value = self.cot_ref[pair]
            wide = value.astype(jnp.float32)
            self.cot_win[0, pair] = value
            self.cot_win[1, pair] = pltpu.roll(wide, HALF_COLS - 1, 0).astype(jnp.bfloat16)
            return carry + folded(wide)

        total = over(self.pairs, 8, body, self.nothing)
        self.cot_win[:, self.pairs] = self.cot_win[:, 0]
        self.refs.raw_sums[16:24, :] = self.refs.raw_sums[16:24, :] + total

    def down_windows(self, start):
        pieces = [
            self.down_win[tap, pl.ds(start + 1, self.size)].reshape(self.small, 2 * C)
            for tap in range(3)
        ]
        pieces += [
            self.down_win[tap, pl.ds(start, self.size), :, C:].reshape(self.small, C)
            for tap in range(3)
        ]
        return jnp.concatenate(pieces, axis=1)

    def down_output(self):
        def body(step, carry):
            start = step * self.size
            value = jnp.dot(
                self.down_windows(start), self.refs.down_fwd[...], preferred_element_type=jnp.float32
            )
            self.out_ref[pl.ds(start, self.size)] = (
                (value + self.bias_down)
                .reshape(self.size, HALF_COLS, 2 * C)
                .astype(jnp.bfloat16)
            )
            return carry

        over_steps(self.steps, body)

    def add_down_grad(self):
        def body(step, carry):
            start = step * self.size
            here = self.cot_win[0, pl.ds(start, self.size)].reshape(self.small, 2 * C)
            product = jnp.dot(
                here.T, self.down_windows(start), preferred_element_type=jnp.float32
            )
            for position in range(9):
                row_tap, tap = DOWN_ORDER[position]
                lanes = pl.ds((3 * row_tap + tap) * C, C)
                self.refs.down_grad[:, lanes] = (
                    self.refs.down_grad[:, lanes] + product[:, position * C : position * C + C]
                )
            return carry

        over_steps(self.steps, body)

    def down_adjoint(self):
        def body(step, carry):
            start = step * self.size
            pieces = [
                self.cot_win[shift, pl.ds(start + below, self.size)].reshape(self.small, 2 * C)
                for below in range(2)
                for shift in range(2)
            ]
            even = jnp.dot(
                jnp.concatenate([pieces[0], pieces[2]], axis=1),
                self.refs.down_even[...],
                preferred_element_type=jnp.float32,
            ).reshape(self.size, HALF_COLS, 2 * C)
            odd = jnp.dot(
                jnp.concatenate(pieces, axis=1),
                self.refs.down_odd[...],
                preferred_element_type=jnp.float32,
            ).reshape(self.size, HALF_COLS, 2 * C)
            for half, ref in ((0, self.grad_even), (1, self.grad_odd)):
                lanes = slice(half * C, half * C + C)
                for inner in range(self.size):
                    ref[start + inner, pl.ds(0, HALF_COLS, stride=2), :] = even[inner, :, lanes]
                    ref[start + inner, pl.ds(1, HALF_COLS, stride=2), :] = odd[inner, :, lanes]
            return carry

        over_steps(self.steps, body)

    def second_grad(self):
        def body(pair, carry):
            value = jnp.concatenate([self.grad_even[pair], self.grad_odd[pair]], axis=1)
            put_shifted(self.grad_two, pair, value)
            return carry + folded(value)

        total = over(self.pairs, 8, body, self.nothing)
        close_ring(self.grad_two, self.pairs)
        self.refs.raw_sums[8:16, :] = self.refs.raw_sums[8:16, :] + total

    def second_conv_grad(self):
        add_conv_grad(self.refs.conv_grad_two, self.act_two, self.grad_two, self.pairs)

    def second_back(self):
        def body(step, carry):
            start = step * self.size
            value = jnp.dot(
                windows(self.grad_two, start, self.size),
                self.refs.back_two[...],
                preferred_element_type=jnp.float32,
            )
            value = value * self.slope_two[pl.ds(start, self.size)].reshape(self.rows, 2 * C)
            self.grad_mid[pl.ds(start, self.size)] = value.reshape(self.size, FIELD_COLS, 2 * C)
            conv = self.conv_one[pl.ds(start, self.size)].reshape(self.rows, 2 * C)
            return carry[0] + folded(value), carry[1] + folded(value * conv)

        total, cross = over_steps(self.steps, body, (self.nothing, self.nothing))
        self.partial[0], self.partial[1] = total, cross

    def first_grad(self):
        inverse, center = self.kept("inverse_two"), self.kept("center_two")
        total, cross = self.partial_sums()
        cross = cross * inverse + total * center
        self.report(0, cross)
        self.report(1, total)
        factor = self.scale_plus * self.gain_two
        mean_grad, mean_cross = self.means(total * factor, cross * factor)
        from_mid = twice(inverse * factor)
        from_conv = twice(inverse * inverse * mean_cross)
        from_mean = twice(inverse * (mean_grad + center * mean_cross))

        def body(pair, carry):
            value = self.grad_mid[pair] * from_mid - from_mean - self.conv_one[pair] * from_conv
            put_shifted(self.grad_one, pair, value)
            return carry + folded(value)

        total = over(self.pairs, 8, body, self.nothing)
        close_ring(self.grad_one, self.pairs)
        self.refs.raw_sums[0:8, :] = self.refs.raw_sums[0:8, :] + total

    def first_conv_grad(self):
        add_conv_grad(self.refs.conv_grad_one, self.act_one, self.grad_one, self.pairs)

    def first_back(self):
        def body(step, carry):
            start = step * self.size
            value = jnp.dot(
                windows(self.grad_one, start, self.size),
                self.refs.back_one[...],
                preferred_element_type=jnp.float32,
            )
            value = value * self.slope_one[pl.ds(start, self.size)].reshape(self.rows, 2 * C)
            self.grad_mid[pl.ds(start, self.size)] = value.reshape(self.size, FIELD_COLS, 2 * C)
            base = jnp.concatenate(
                [
                    self.x_ref[pl.ds(start, self.size), half]
                    .astype(jnp.float32)
                    .reshape(self.rows, C)
                    for half in range(2)
                ],
                axis=1,
            )
            return carry[0] + folded(value), carry[1] + folded(value * base)

        total, cross = over_steps(self.steps, body, (self.nothing, self.nothing))
        self.partial[0], self.partial[1] = total, cross

    def field_grad(self, rows_ref):
        inverse, center = self.kept("inverse_one"), self.kept("center_one")
        total, cross = self.partial_sums()
        cross = cross * inverse + total * center
        self.report(2, cross)
        self.report(3, total)
        mean_grad, mean_cross = self.means(total * self.gain_one, cross * self.gain_one)
        from_pre = twice(inverse * self.gain_one)
        from_field = twice(inverse * inverse * mean_cross)
        from_mean = twice(inverse * (mean_grad + center * mean_cross))

        def body(pair, carry):
            summed = jnp.concatenate([self.grad_even[pair], self.grad_odd[pair]], axis=1)
            change = self.grad_mid[pair] * from_pre - from_mean - self.field(pair) * from_field
            value = (summed + change).astype(jnp.bfloat16)
            rows_ref[pair, 0] = value[:, :C]
            rows_ref[pair, 1] = value[:, C:]
            return carry

        over(self.pairs, 8, body, 0)


STATE = (
    "inverse_one",
    "center_one",
    "inverse_two",
    "center_two",
)
BEFORE = -1
SLOTS = (
    (
        ("first_stats", 0),
        ("shift_cotangent", 0),
        ("add_down_grad", BEFORE),
        ("second_conv_grad", BEFORE),
    ),
    (
        ("first_act", 0),
        ("first_stats", 1),
        ("down_adjoint", 0),
        ("first_conv_grad", BEFORE),
    ),
    (
        ("first_act", 1),
        ("second_grad", 0),
        ("shift_cotangent", 1),
        ("first_conv", 0),
        ("down_adjoint", 1),
    ),
    (("second_act", 0), ("second_grad", 1), ("first_conv", 1)),
    (("second_act", 1), ("second_back", 0), ("second_conv", 0)),
    (("first_grad", 0), ("split_columns", 0), ("second_back", 1), ("second_conv_grad", 0)),
    (("first_grad", 1), ("first_back", 0), ("second_conv", 1)),
    (("field_grad", 0), ("split_columns", 1), ("first_back", 1), ("first_conv_grad", 0)),
    (("field_grad", 1), ("down_output", 0), ("add_down_grad", 0), ("down_output", 1)),
)
LATE = ("add_down_grad", "second_conv_grad", "first_conv_grad")


def start_all(copies):
    for copy in copies:
        copy.start()


def peers(axis, count, pairs_of, sends, receives):
    return [
        to_peer(axis, step, count, source(step), target(step), sends.at[place, step], receives.at[place, step])
        for step in range(1, count)
        for place, (source, target) in pairs_of
    ]


def same(ref):
    return lambda step: ref


def slot_of(ref):
    return lambda step: ref.at[step]


def step_kernel(sizes, *args):
    row_count, batch_count, pairs, samples, together = sizes
    names = INPUTS + OUTPUTS + SCRATCH
    refs = SimpleNamespace(**dict(zip(names, args[: len(names)])))
    scratch = args[len(names) :]
    base = pl.program_id(0) * together
    row, batch = lax.axis_index("row"), lax.axis_index("batch")
    share = pairs // row_count

    def send_field(index, carry):
        mine = refs.fields.at[index, pl.ds(row * share, share)]
        for step in range(1, row_count):
            place = lax.rem(row + step, row_count) * samples + index
            to_peer(
                "row",
                step,
                row_count,
                refs.field.at[place],
                mine,
                refs.field_sent,
                refs.field_sem.at[index],
            ).start()
        pltpu.make_async_copy(
            refs.field.at[row * samples + index], mine, refs.field_sem.at[index]
        ).start()
        return carry

    def send_grad(index):
        target = refs.grad_out.at[row * samples + index]
        for step in range(1, row_count):
            place = lax.rem(row + step, row_count) * share
            to_peer(
                "row",
                step,
                row_count,
                refs.grad_rows.at[index, pl.ds(place, share)],
                target,
                refs.grad_sent,
                refs.grad_sem,
            ).start()
        pltpu.make_async_copy(
            refs.grad_rows.at[index, pl.ds(row * share, share)], target, refs.grad_sem
        ).start()

    @pl.when(base == 0)
    def _():
        pack_shards(refs)
        greet(row_count, batch_count)
        own = pltpu.make_async_copy(refs.shard, refs.shards.at[row, batch], refs.local_sem)
        own.start()
        copies = peers(
            "batch",
            batch_count,
            [
                (0, (same(refs.shard), same(refs.shards.at[row, batch]))),
                (1, (same(refs.small), slot_of(refs.small_z))),
            ],
            refs.send_z,
            refs.recv_z,
        )
        start_all(copies)
        lax.fori_loop(0, together, send_field, 0)
        for ref in (refs.conv_grad_one, refs.conv_grad_two, refs.down_grad, refs.raw_sums, refs.sums):
            ref[...] = jnp.zeros_like(ref)
        if together > 1:
            for ref in scratch[-16:-12] + scratch[-4:-2]:
                ref[...] = jnp.zeros_like(ref)
        own.wait()
        finish(copies)
        total = refs.small[...]
        for step in range(1, batch_count):
            total = total + refs.small_z[step]
        refs.small_one[...] = total
        copies = peers(
            "row",
            row_count,
            [(1, (same(refs.small_one), slot_of(refs.small_row)))],
            refs.send_row,
            refs.recv_row,
        )
        sibling = sibling_of(row)
        mine = refs.shards.at[row]
        direct = {}
        for step in range(2, row_count, 2):
            direct[step] = to_row(
                lax.rem(row + step, row_count),
                mine,
                mine,
                refs.send_row.at[0, step],
                refs.recv_row.at[0, step],
            )
        beside = [to_row(sibling, mine, mine, refs.send_row.at[0, 1], refs.recv_row.at[0, 1])]
        start_all(list(direct.values()) + beside + copies)
        lax.fori_loop(together, samples, send_field, 0)
        for step in range(2, row_count, 2):
            direct[step].wait_recv()
            came = refs.shards.at[lax.rem(row + row_count - step, row_count)]
            beside.append(
                to_row(
                    sibling,
                    came,
                    came,
                    refs.send_row.at[0, step + 1],
                    refs.recv_row.at[0, step + 1],
                )
            )
            beside[-1].start()
        for step in range(2, row_count, 2):
            direct[step].wait_send()
        finish(beside + copies)
        total = refs.small_one[...]
        for step in range(1, row_count):
            total = total + refs.small_row[step]
        refs.small_all[...] = total
        lay_out(row_count, batch_count, refs)
        modulate(refs)

    @pl.when(base > 0)
    def _():
        for place in range(together):
            send_grad(base - together + place)

    for place in range(together):
        arrived = refs.fields.at[base + place]
        pltpu.make_async_copy(arrived, arrived, refs.field_sem.at[base + place]).wait()
    stages = [
        Sample(
            pairs,
            base + place,
            refs.fields.at[base + place],
            refs.cot.at[place],
            refs.block_out.at[place],
            refs,
            scratch[16 * place : 16 * place + 16],
        )
        for place in range(together)
    ]

    def run_slot(slot):
        for name, place in slot:
            if place >= together or (place == BEFORE and together == 1):
                continue
            stage = getattr(stages[place], name)
            if name == "field_grad":
                stage(refs.grad_rows.at[base + place])
            else:
                stage()

    for slot in SLOTS:
        run_slot(slot)

    @pl.when(base == samples - together)
    def _():
        for place in range(together):
            send_grad(base + place)
        if together > 1:
            for name in LATE:
                getattr(stages[-1], name)()
        reduce_all(row_count, batch_count, refs)
        pltpu.make_async_copy(refs.grad_out, refs.grad_out, refs.grad_sem).wait()
        others = pl.ds(0, pairs - share)
        for ref, sem in ((refs.fields, refs.field_sent), (refs.grad_rows, refs.grad_sent)):
            pltpu.make_async_copy(ref.at[:, others], ref.at[:, others], sem).wait()


INPUTS = ("field", "cot", "conv", "down", "embed_in", "embed_out", "small", "embedded", "group")
OUTPUTS = (
    "block_out",
    "grad_out",
    "conv_grad",
    "down_share",
    "embed_in_grad",
    "embed_out_grad",
    "small_grad",
    "norm",
)
SCRATCH = (
    "fwd_one",
    "back_one",
    "fwd_two",
    "back_two",
    "down_fwd",
    "down_even",
    "down_odd",
    "small_all",
    "embed_in_t",
    "embed_out_t",
    "modulation",
    "hidden",
    "hidden_slope",
    "sums",
    "raw_sums",
    "conv_grad_one",
    "conv_grad_two",
    "down_grad",
    "shard",
    "shards",
    "small_z",
    "small_one",
    "small_row",
    "conv_t",
    "down_t",
    "fields",
    "grad_rows",
    "row_send",
    "pair_take",
    "chip_send",
    "row_take",
    "batch_send",
    "batch_take",
    "small_send",
    "small_take",
    "small_next",
    "small_last",
    "square_send",
    "square_take",
    "square_next",
    "square_last",
    "field_sem",
    "field_sent",
    "grad_sem",
    "grad_sent",
    "local_sem",
    "send_z",
    "recv_z",
    "send_row",
    "recv_row",
    "send_sem",
    "recv_sem",
)
DOWN_ORDER = ((1, 0), (2, 0), (1, 1), (2, 1), (1, 2), (2, 2), (0, 0), (0, 1), (0, 2))


def lay_out(row_count, batch_count, refs):
    depth, share, wide_share = 9 * C // batch_count, C // row_count, C2 // row_count
    height = 2 * share + wide_share
    embed_share, hidden_share = EMB // batch_count, HID // batch_count
    for place in range(row_count):
        parts = [refs.shards[place, part].astype(jnp.float32) for part in range(batch_count)]
        main = jnp.concatenate([part[:, :depth] for part in parts], axis=1)
        for which in range(2):
            refs.conv_t[which, place * share : place * share + share, :] = main[
                which * share : which * share + share
            ]
        refs.down_t[place * wide_share : place * wide_share + wide_share, :] = main[2 * share :]
        refs.embed_in_t[place * height : place * height + height, :] = jnp.concatenate(
            [part[:, depth : depth + embed_share] for part in parts], axis=1
        )
        tail = depth + embed_share
        half_rows, half_lanes = height // 2, hidden_share // 2
        lanes = []
        for part in parts:
            lanes.append(part[:half_rows, tail : tail + half_lanes])
            lanes.append(part[half_rows:, tail : tail + half_lanes])
        refs.embed_out_t[place * half_rows : place * half_rows + half_rows, :] = jnp.concatenate(
            lanes, axis=1
        )
    for which, forward, back in (
        (0, refs.fwd_one, refs.back_one),
        (1, refs.fwd_two, refs.back_two),
    ):
        zero = jnp.zeros((C, C), jnp.bfloat16)
        for tap in range(3):
            direct = [
                refs.conv_t[which, :, (3 * row_tap + tap) * C : (3 * row_tap + tap) * C + C]
                for row_tap in range(3)
            ]
            fill_blocks(forward, tap, [block.T.astype(jnp.bfloat16) for block in direct], zero)
            fill_blocks(
                back, 2 - tap, [block.astype(jnp.bfloat16) for block in direct[::-1]], zero
            )
    zero = jnp.zeros((C2, C), jnp.bfloat16)
    back = {}
    for position in range(9):
        row_tap, tap = DOWN_ORDER[position]
        block = refs.down_t[:, (3 * row_tap + tap) * C : (3 * row_tap + tap) * C + C]
        refs.down_fwd[position * C : position * C + C, :] = block.T.astype(jnp.bfloat16)
        back[row_tap, tap] = block.astype(jnp.bfloat16)
    even = ((back[1, 1], back[2, 1]), (zero, back[0, 1]))
    odd = (
        (back[1, 2], back[2, 2]),
        (back[1, 0], back[2, 0]),
        (zero, back[0, 2]),
        (zero, back[0, 0]),
    )
    for ref, table in ((refs.down_even, even), (refs.down_odd, odd)):
        for position, (left, right) in enumerate(table):
            ref[position * C2 : position * C2 + C2, :C] = left
            ref[position * C2 : position * C2 + C2, C:] = right


def lanes_of(ref, first, last):
    return jnp.concatenate([ref[place : place + 1, :] for place in range(first, last)], axis=1)


def modulate(refs):
    small = refs.small_all
    before = dot_full(refs.embedded[...], refs.embed_in_t[...].T) + lanes_of(small, 8, 12)
    hidden, slope = gelu_pair(before)
    refs.hidden[...] = hidden
    refs.hidden_slope[...] = slope
    result = dot_full(hidden, refs.embed_out_t[...].T) + lanes_of(small, 12, 14)
    refs.modulation[0] = 1.0 + result[:, :C]
    refs.modulation[1] = result[:, C:]


def fill_blocks(ref, tap, blocks, zero):
    table = (
        (blocks[1], blocks[0]),
        (blocks[2], blocks[1]),
        (blocks[0], zero),
        (zero, blocks[2]),
    )
    for position, (left, right) in enumerate(table):
        base = (4 * tap + position) * C
        ref[base : base + C, :C] = left
        ref[base : base + C, C:] = right


def dot_full(lhs, rhs):
    return jnp.dot(lhs, rhs, precision=HIGHEST, preferred_element_type=jnp.float32)


def dot_first(lhs, rhs):
    return lax.dot_general(
        lhs,
        rhs,
        (((0,), (0,)), ((), ())),
        precision=HIGHEST,
        preferred_element_type=jnp.float32,
    )


def reduce_all(row_count, batch_count, refs):
    row, batch = lax.axis_index("row"), lax.axis_index("batch")
    depth, share, wide_share = 9 * C // batch_count, C // row_count, C2 // row_count
    height = 2 * share + wide_share
    embed_share, hidden_share = EMB // batch_count, HID // batch_count
    mid_cross, mid_total = refs.sums[0], refs.sums[1]
    gain_two, shift_two = refs.small_all[1:2, :], refs.small_all[3:4, :]
    scale_plus = refs.modulation[0]
    grad_mod = jnp.concatenate([gain_two * mid_cross + shift_two * mid_total, mid_total], axis=1)
    grad_embed_out = dot_first(grad_mod, refs.hidden[...])
    grad_hidden = (
        dot_full(grad_mod, refs.embed_out_t[...])
        * refs.hidden_slope[...]
    )
    grad_embed_in = dot_first(grad_hidden, refs.embedded[...])

    def down_sum(value):
        return jnp.sum(value, axis=0, keepdims=True)

    small_rows = [
        down_sum(refs.sums[2]),
        down_sum(mid_cross * scale_plus),
        down_sum(refs.sums[3]),
        down_sum(mid_total * scale_plus),
        channel_sum(refs.raw_sums[0:8]),
        channel_sum(refs.raw_sums[8:16]),
    ]
    cot_total = down_sum(refs.raw_sums[16:24])
    small_rows += [cot_total[:, :C], cot_total[:, C:]]
    hidden_total, mod_total = down_sum(grad_hidden), down_sum(grad_mod)
    small_rows += [hidden_total[:, lane : lane + C] for lane in range(0, HID, C)]
    small_rows += [mod_total[:, lane : lane + C] for lane in range(0, 2 * C, C)]
    small_rows.append(jnp.zeros((2, C), jnp.float32))
    refs.small_send[...] = jnp.concatenate(small_rows, axis=0)
    half_rows = height // 2
    for place in range(row_count):
        low, high = place * share, place * share + share
        refs.row_send[place, :, : 9 * C] = jnp.concatenate(
            [
                refs.conv_grad_one[low:high],
                refs.conv_grad_two[low:high],
                refs.down_grad[place * wide_share : place * wide_share + wide_share],
            ],
            axis=0,
        ).astype(jnp.bfloat16)
        refs.row_send[place, :, 9 * C : 10 * C] = grad_embed_in[
            place * height : place * height + height
        ].astype(jnp.bfloat16)
        piece = grad_embed_out[place * half_rows : place * half_rows + half_rows]
        refs.row_send[place, :, 10 * C :] = jnp.concatenate(
            [piece[:, : HID // 2], piece[:, HID // 2 :]], axis=0
        ).astype(jnp.bfloat16)
    sibling = sibling_of(row)
    beside = [
        to_row(
            sibling,
            refs.row_send.at[lax.rem(sibling + 2 * step, row_count)],
            refs.pair_take.at[step],
            refs.send_sem.at[0, step],
            refs.recv_sem.at[0, step],
        )
        for step in range(row_count // 2)
    ]
    smalls = [
        to_peer(
            "row",
            step,
            row_count,
            refs.small_send,
            refs.small_take.at[step],
            refs.send_sem.at[1, step],
            refs.recv_sem.at[1, step],
        )
        for step in range(1, row_count)
    ]
    order = list(range(1, row_count // 2)) + [0]
    start_all([beside[step] for step in order] + smalls)
    copies = []
    for step in order:
        beside[step].wait_recv()
        place = lax.rem(row + 2 * step, row_count)
        total = refs.row_send[place].astype(jnp.float32) + refs.pair_take[step].astype(jnp.float32)
        if step:
            refs.chip_send[step] = total.astype(jnp.bfloat16)
            copies.append(
                to_row(
                    place,
                    refs.chip_send.at[step],
                    refs.row_take.at[step],
                    refs.send_sem.at[6, step],
                    refs.recv_sem.at[6, step],
                )
            )
            copies[-1].start()
    for copy in beside:
        copy.wait_send()
    finish(copies + smalls)
    small_total = refs.small_send[...]
    for step in range(1, row_count // 2):
        total = total + refs.row_take[step].astype(jnp.float32)
    for step in range(1, row_count):
        small_total = small_total + refs.small_take[step]
    refs.small_next[...] = small_total
    for part in range(batch_count):
        per_half = batch_count // 2
        rows = slice(0, half_rows) if part < per_half else slice(half_rows, height)
        base = 10 * C + hidden_share * (part % per_half)
        piece = total[rows, base : base + hidden_share]
        refs.batch_send[part] = jnp.concatenate(
            [
                total[:, part * depth : part * depth + depth],
                total[:, 9 * C + part * embed_share : 9 * C + part * embed_share + embed_share],
                jnp.concatenate([piece[:, : hidden_share // 2], piece[:, hidden_share // 2 :]], axis=0),
            ],
            axis=1,
        ).astype(jnp.bfloat16)
    copies = []
    for step in range(1, batch_count):
        copies.append(
            to_peer(
                "batch",
                step,
                batch_count,
                refs.batch_send.at[lax.rem(batch + step, batch_count)],
                refs.batch_take.at[step],
                refs.send_sem.at[2, step],
                refs.recv_sem.at[2, step],
            )
        )
        copies.append(
            to_peer(
                "batch",
                step,
                batch_count,
                refs.small_next,
                refs.small_last.at[step],
                refs.send_sem.at[3, step],
                refs.recv_sem.at[3, step],
            )
        )
    for copy in copies:
        copy.start()
    owned = refs.batch_send[batch].astype(jnp.float32)
    finish(copies)
    small_total = refs.small_next[...]
    for step in range(1, batch_count):
        owned = owned + refs.batch_take[step].astype(jnp.float32)
        small_total = small_total + refs.small_last[step]
    squares = jnp.sum(jnp.sum(owned * owned, axis=0, keepdims=True), axis=1, keepdims=True)
    refs.square_send[...] = jnp.broadcast_to(squares, (8, C))
    copies = [
        to_peer(
            "row",
            step,
            row_count,
            refs.square_send,
            refs.square_take.at[step],
            refs.send_sem.at[4, step],
            refs.recv_sem.at[4, step],
        )
        for step in range(1, row_count)
    ]
    for copy in copies:
        copy.start()
    finish(copies)
    squares = refs.square_send[...]
    for step in range(1, row_count):
        squares = squares + refs.square_take[step]
    refs.square_next[...] = squares
    copies = [
        to_peer(
            "batch",
            step,
            batch_count,
            refs.square_next,
            refs.square_last.at[step],
            refs.send_sem.at[5, step],
            refs.recv_sem.at[5, step],
        )
        for step in range(1, batch_count)
    ]
    for copy in copies:
        copy.start()
    finish(copies)
    squares = refs.square_next[...]
    for step in range(1, batch_count):
        squares = squares + refs.square_last[step]
    small_squares = jnp.sum(
        jnp.sum(small_total * small_total, axis=0, keepdims=True), axis=1, keepdims=True
    )
    norm = jnp.sqrt(squares + small_squares)
    clip = jnp.minimum(1.0, CLIP_NORM / (norm + 1e-06))[0:1, 0:1]
    refs.norm[...] = norm
    flipped = (owned * clip).T
    refs.conv_grad[0] = flipped[:depth, :share]
    refs.conv_grad[1] = flipped[:depth, share : 2 * share]
    refs.down_share[...] = flipped[:depth, 2 * share :]
    refs.embed_in_grad[...] = flipped[depth : depth + embed_share]
    tall = flipped[depth + embed_share :]
    half_hidden = hidden_share // 2
    refs.embed_out_grad[:half_hidden, :] = tall[:, :half_rows]
    refs.embed_out_grad[half_hidden:, :] = tall[:, half_rows:]
    refs.small_grad[...] = small_total * clip


def pack_shards(refs):
    half = refs.embed_out.shape[0] // 2
    stacked = jnp.concatenate(
        [
            jnp.concatenate([refs.conv[0], refs.conv[1], refs.down[...]], axis=1),
            refs.embed_in[...],
            jnp.concatenate([refs.embed_out[:half, :], refs.embed_out[half:, :]], axis=1),
        ],
        axis=0,
    )
    refs.shard[...] = stacked.T.astype(jnp.bfloat16)


def run_step(field_in, cotangent, shards, small_tile, embedded):
    row_count, batch_count = (lax.axis_size("row"), lax.axis_size("batch"))
    samples = cotangent.shape[0]
    padded = embedded.shape[0]
    pairs = field_in.shape[1] // 2 * row_count
    together = chunk_of(samples, 2)
    share = pairs // row_count
    height, width = 4 * C // row_count, 12 * C // batch_count
    halves = field_in.reshape(field_in.shape[0], share, 2, FIELD_COLS, C)
    same_group = jnp.asarray(
        np.kron(np.eye(GROUPS), np.ones((C // GROUPS, C // GROUPS))), jnp.float32
    )
    low, full = jnp.bfloat16, jnp.float32
    anywhere = pl.BlockSpec(memory_space=pl.ANY)

    def whole(array):
        return pl.BlockSpec(array.shape, lambda i: (0,) * len(array.shape))

    def per_step(array):
        rank = len(array.shape)
        return pl.BlockSpec((together,) + array.shape[1:], lambda i: (i,) + (0,) * (rank - 1))

    outs = (
        jax.ShapeDtypeStruct(cotangent.shape, low),
        jax.ShapeDtypeStruct(halves.shape, low),
        *[jax.ShapeDtypeStruct(shard.shape, full) for shard in shards],
        jax.ShapeDtypeStruct((16, C), full),
        jax.ShapeDtypeStruct((8, C), full),
    )
    ring = pltpu.VMEM((3, pairs + 2, FIELD_COLS, 2 * C), low)
    wide = pltpu.VMEM((pairs, FIELD_COLS, 2 * C), full)
    half = pltpu.VMEM((pairs, FIELD_COLS, C), full)
    fields = pltpu.VMEM((samples, pairs, 2, FIELD_COLS, C), low)
    dma = pltpu.SemaphoreType.DMA
    most = max(row_count, batch_count)
    tile = (16, C)
    scratch = (
        [pltpu.VMEM((12 * C, 2 * C), low)] * 4
        + [
            pltpu.VMEM((9 * C, C2), low),
            pltpu.VMEM((2 * C2, 2 * C), low),
            pltpu.VMEM((4 * C2, 2 * C), low),
            pltpu.VMEM(tile, full),
            pltpu.VMEM((HID, EMB), full),
            pltpu.VMEM((2 * C, HID), full),
            pltpu.VMEM((2, padded, C), full),
            pltpu.VMEM((padded, HID), full),
            pltpu.VMEM((padded, HID), full),
            pltpu.VMEM((4, padded, C), full),
            pltpu.VMEM((24, 2 * C), full),
            pltpu.VMEM((C, 9 * C), full),
            pltpu.VMEM((C, 9 * C), full),
            pltpu.VMEM((C2, 9 * C), full),
            pltpu.VMEM((height, width), low),
            pltpu.VMEM((row_count, batch_count, height, width), low),
            pltpu.VMEM((batch_count,) + tile, full),
            pltpu.VMEM(tile, full),
            pltpu.VMEM((row_count,) + tile, full),
            pltpu.VMEM((2, C, 9 * C), full),
            pltpu.VMEM((C2, 9 * C), full),
            fields,
            fields,
            pltpu.VMEM((row_count, height, 12 * C), low),
            pltpu.VMEM((row_count // 2, height, 12 * C), low),
            pltpu.VMEM((row_count // 2, height, 12 * C), low),
            pltpu.VMEM((row_count // 2, height, 12 * C), low),
            pltpu.VMEM((batch_count, height, width), low),
            pltpu.VMEM((batch_count, height, width), low),
            pltpu.VMEM(tile, full),
            pltpu.VMEM((row_count,) + tile, full),
            pltpu.VMEM(tile, full),
            pltpu.VMEM((batch_count,) + tile, full),
            pltpu.VMEM((8, C), full),
            pltpu.VMEM((row_count, 8, C), full),
            pltpu.VMEM((8, C), full),
            pltpu.VMEM((batch_count, 8, C), full),
            dma((samples,)),
            dma,
            dma,
            dma,
            dma,
            dma((2, batch_count)),
            dma((2, batch_count)),
            dma((2, row_count)),
            dma((2, row_count)),
            dma((7, most)),
            dma((7, most)),
        ]
        + (
            [ring] * 4
            + [wide] * 4
            + [half] * 4
            + [
                pltpu.VMEM((3, pairs + 1, HALF_COLS, 2 * C), low),
                pltpu.VMEM((2, pairs + 1, HALF_COLS, C2), low),
                pltpu.VMEM((8, C), full),
                pltpu.VMEM((2, 8, 2 * C), full),
            ]
        )
        * together
    )
    result = pl.pallas_call(
        functools.partial(step_kernel, (row_count, batch_count, pairs, samples, together)),
        grid=(samples // together,),
        in_specs=[anywhere, per_step(cotangent)]
        + [whole(array) for array in shards + (small_tile, embedded, same_group)],
        out_specs=[per_step(outs[0]), anywhere] + [whole(out) for out in outs[2:]],
        out_shape=outs,
        scratch_shapes=scratch,
        compiler_params=pltpu.CompilerParams(
            dimension_semantics=("arbitrary",),
            vmem_limit_bytes=62 << 20,
            collective_id=0,
            has_side_effects=True,
        ),
        name="step",
    )(halves, cotangent, *shards, small_tile, embedded, same_group)
    return (result[0], result[1].reshape(field_in.shape)) + tuple(result[2:])


def adam_update(weight, gradient, first_old, second_old, step_rate, clip_factor):
    scaled = gradient * clip_factor
    first_new = BETA_ONE * first_old + (1.0 - BETA_ONE) * scaled
    second_new = BETA_TWO * second_old + (1.0 - BETA_TWO) * scaled * scaled
    corrected = (
        first_new
        / (1.0 - BETA_ONE**STEP_COUNT)
        / (jnp.sqrt(second_new / (1.0 - BETA_TWO**STEP_COUNT)) + ADAM_EPS)
    )
    return (weight - step_rate * (corrected + DECAY * weight), first_new, second_new)


def body(
    field_in,
    refine_step,
    cotangent,
    conv_weight,
    down_weight,
    embed_in_weight,
    embed_out_weight,
    small_params,
    conv_first,
    down_first,
    embed_in_first,
    embed_out_first,
    small_first,
    conv_second,
    down_second,
    embed_in_second,
    embed_out_second,
    small_second,
):
    small_len = small_params.shape[0]
    place = (lax.axis_index("batch") * lax.axis_size("row") + lax.axis_index("row")) * small_len
    small_rounded = small_params.astype(jnp.bfloat16).astype(jnp.float32)
    small_tile = lax.dynamic_update_slice_in_dim(
        jnp.zeros((16 * C,), jnp.float32), small_rounded, place, 0
    ).reshape(16, C)
    owned = refine_step.shape[0] // lax.axis_size("row")
    padded = -(-owned // 8) * 8
    own_steps = lax.dynamic_slice_in_dim(refine_step, lax.axis_index("row") * owned, owned, 0)
    embedded = embed_steps(jnp.pad(own_steps, (0, padded - owned)))
    block_out, grad_start, *owned_shards, small_grads, norm_tile = run_step(
        field_in,
        cotangent,
        (conv_weight, down_weight, embed_in_weight, embed_out_weight),
        small_tile,
        embedded,
    )
    grad_norm = norm_tile[0, 0]
    owned_shards.append(lax.dynamic_slice_in_dim(small_grads.reshape(-1), place, small_len, 0))
    clip_factor = 1.0
    conv_new = adam_update(
        conv_weight, owned_shards[0], conv_first, conv_second, RATE_MATRIX, clip_factor
    )
    down_new = adam_update(
        down_weight, owned_shards[1], down_first, down_second, RATE_MATRIX, clip_factor
    )
    embed_in_new = adam_update(
        embed_in_weight, owned_shards[2], embed_in_first, embed_in_second, RATE_MATRIX, clip_factor
    )
    embed_out_new = adam_update(
        embed_out_weight,
        owned_shards[3],
        embed_out_first,
        embed_out_second,
        RATE_MATRIX,
        clip_factor,
    )
    small_new = adam_update(
        small_params, owned_shards[4], small_first, small_second, RATE_SMALL, clip_factor
    )
    return (
        block_out,
        grad_start,
        grad_norm,
        conv_new[0],
        down_new[0],
        embed_in_new[0],
        embed_out_new[0],
        small_new[0],
        conv_new[1],
        down_new[1],
        embed_in_new[1],
        embed_out_new[1],
        small_new[1],
        conv_new[2],
        down_new[2],
        embed_in_new[2],
        embed_out_new[2],
        small_new[2],
    )


def solution(mesh):
    placed = (
        P("batch", "row", None, None),
        P("batch"),
        P(("batch", "row"), None, None, None),
        P(None, "batch", "row"),
        P("batch", "row"),
        P("batch", "row"),
        P("batch", "row"),
        P(("batch", "row")),
        P(None, "batch", "row"),
        P("batch", "row"),
        P("batch", "row"),
        P("batch", "row"),
        P(("batch", "row")),
        P(None, "batch", "row"),
        P("batch", "row"),
        P("batch", "row"),
        P("batch", "row"),
        P(("batch", "row")),
    )
    return jax.shard_map(
        body,
        mesh=mesh,
        in_specs=placed,
        out_specs=(
            P(("batch", "row"), None, None, None),
            P("batch", "row", None, None),
            P(),
            P(None, "batch", "row"),
            P("batch", "row"),
            P("batch", "row"),
            P("batch", "row"),
            P(("batch", "row")),
            P(None, "batch", "row"),
            P("batch", "row"),
            P("batch", "row"),
            P("batch", "row"),
            P(("batch", "row")),
            P(None, "batch", "row"),
            P("batch", "row"),
            P("batch", "row"),
            P("batch", "row"),
            P(("batch", "row")),
        ),
        check_vma=False,
    )
```

```python
import functools
import math
from types import SimpleNamespace

import jax
import jax.numpy as jnp
import numpy as np
from jax import lax
from jax.experimental import pallas as pl
from jax.experimental.pallas import tpu as pltpu
from jax.sharding import PartitionSpec as P

C = 128
C2 = 256
EMB = 128
HID = 512
GROUPS = 8
REFINE = 4


NORM_EPS = 1e-05
BETA_ONE = 0.9
BETA_TWO = 0.999
ADAM_EPS = 1e-08
DECAY = 0.01
RATE_MATRIX = 0.05
RATE_SMALL = 0.5
CLIP_NORM = 1.0
STEP_COUNT = 10
HIGHEST = lax.Precision.HIGHEST


def embed_steps(refine_step):
    halfway = EMB // 2
    frequency = jnp.exp(-math.log(10000.0) * jnp.arange(halfway).astype(jnp.float32) / halfway)
    angles = (refine_step.astype(jnp.float32) * (1000.0 / REFINE))[:, None] * frequency[None, :]
    return jnp.concatenate([jnp.sin(angles), jnp.cos(angles)], axis=1)


MESH = pl.DeviceIdType.MESH


def greet(row_count, batch_count=1):
    row, batch = lax.axis_index("row"), lax.axis_index("batch")
    barrier = pltpu.get_barrier_semaphore()
    for step in range(1, row_count):
        pl.semaphore_signal(
            barrier,
            inc=1,
            device_id={"row": lax.rem(row + step, row_count), "batch": batch},
            device_id_type=MESH,
        )
    for step in range(1, batch_count):
        pl.semaphore_signal(
            barrier,
            inc=1,
            device_id={"row": row, "batch": lax.rem(batch + step, batch_count)},
            device_id_type=MESH,
        )
    pl.semaphore_wait(barrier, row_count + batch_count - 2)


def to_peer(axis, step, count, source, target, send_sem, recv_sem):
    row, batch = lax.axis_index("row"), lax.axis_index("batch")
    if axis == "row":
        device = {"row": lax.rem(row + step, count), "batch": batch}
    else:
        device = {"row": row, "batch": lax.rem(batch + step, count)}
    return pltpu.make_async_remote_copy(
        src_ref=source,
        dst_ref=target,
        send_sem=send_sem,
        recv_sem=recv_sem,
        device_id=device,
        device_id_type=MESH,
    )


def to_row(place, source, target, send_sem, recv_sem):
    return pltpu.make_async_remote_copy(
        src_ref=source,
        dst_ref=target,
        send_sem=send_sem,
        recv_sem=recv_sem,
        device_id={"row": place, "batch": lax.axis_index("batch")},
        device_id_type=MESH,
    )


def sibling_of(row):
    return row + 1 - 2 * lax.rem(row, 2)


def finish(copies):
    for copy in copies:
        copy.wait()


FIELD_COLS = 64
HALF_COLS = 32
ROOT = math.sqrt(2.0 / math.pi)
CUBIC = ROOT * 0.044715


def chunk_of(total, most):
    size = min(total, most)
    while total % size:
        size -= 1
    return size


def over(total, most, body, init):
    size = chunk_of(total, most)

    def several(step, carry):
        for inner in range(size):
            carry = body(step * size + inner, carry)
        return carry

    if size == total:
        return several(0, init)
    return lax.fori_loop(0, total // size, several, init)


def folded(values):
    return jnp.sum(values.reshape(values.shape[0] // 8, 8, values.shape[1]), axis=0)


def twice(row):
    return jnp.concatenate([row, row], axis=1)


def channel_sum(partial):
    both = partial[:, :C] + partial[:, C:]
    return jnp.sum(both, axis=0, keepdims=True)


def group_means(first, second, same_group, entries):
    stacked = jnp.concatenate([first, second, jnp.zeros((6, C), jnp.float32)], axis=0)
    totals = jnp.dot(stacked, same_group, precision=HIGHEST, preferred_element_type=jnp.float32)
    return totals[0:1] / entries, totals[1:2] / entries


def gelu_pair(values):
    square = values * values
    weight = 0.5 + 0.5 * jnp.tanh(values * (ROOT + CUBIC * square))
    result = values * weight
    slope = weight + (result - result * weight) * (2.0 * ROOT + (6.0 * CUBIC) * square)
    return result, slope


def put_shifted(ref, pair, values):
    for tap, shift in ((0, 1), (1, 0), (2, FIELD_COLS - 1)):
        moved = pltpu.roll(values, shift, 0) if shift else values
        ref[tap, pair + 1] = moved.astype(jnp.bfloat16)


def close_ring(ref, pairs):
    ref[:, 0, :, C:] = ref[:, pairs, :, C:]
    ref[:, pairs + 1, :, :C] = ref[:, 1, :, :C]


def windows(ref, start, count):
    rows = count * FIELD_COLS
    pieces = []
    for tap in range(3):
        pieces.append(ref[tap, pl.ds(start + 1, count)].reshape(rows, 2 * C))
        pieces.append(ref[tap, pl.ds(start, count), :, C:].reshape(rows, C))
        pieces.append(ref[tap, pl.ds(start + 2, count), :, :C].reshape(rows, C))
    return jnp.concatenate(pieces, axis=1)


def over_steps(steps, body, init=0):
    if steps == 1:
        return body(0, init)
    return lax.fori_loop(0, steps, body, init)


def add_conv_grad(out_ref, act_ref, grad_ref, pairs):
    size = chunk_of(pairs, 8)
    rows = size * FIELD_COLS

    def body(step, carry):
        start = step * size
        grad = grad_ref[1, pl.ds(start + 1, size)].reshape(rows, 2 * C)
        product = jnp.dot(
            grad.T, windows(act_ref, start, size), preferred_element_type=jnp.float32
        )
        for tap in range(3):
            base = tap * 4 * C
            middle = product[:C, base : base + C] + product[C:, base + C : base + 2 * C]
            up = product[C:, base : base + C] + product[:C, base + 2 * C : base + 3 * C]
            down = product[:C, base + C : base + 2 * C] + product[C:, base + 3 * C : base + 4 * C]
            for row_tap, value in ((0, up), (1, middle), (2, down)):
                lanes = pl.ds((3 * row_tap + tap) * C, C)
                out_ref[:, lanes] = out_ref[:, lanes] + value
        return carry

    over_steps(pairs // size, body)


class Sample:
    def __init__(self, pairs, sample, x_ref, cot_ref, out_ref, refs, scratch):
        self.pairs, self.sample = pairs, sample
        self.x_ref, self.cot_ref, self.out_ref = x_ref, cot_ref, out_ref
        self.refs = refs
        (
            self.act_one,
            self.act_two,
            self.grad_one,
            self.grad_two,
            self.slope_one,
            self.slope_two,
            self.conv_one,
            self.grad_mid,
            self.sum_even,
            self.sum_odd,
            self.grad_even,
            self.grad_odd,
            self.down_win,
            self.cot_win,
            self.state,
            self.partial,
        ) = scratch
        self.entries = 2.0 * pairs * FIELD_COLS * (C // GROUPS)
        self.size = chunk_of(pairs, 8)
        self.steps = pairs // self.size
        self.rows = self.size * FIELD_COLS
        self.small = self.size * HALF_COLS
        self.same_group = refs.group[...]
        small = refs.small_all
        self.gain_one, self.gain_two = small[0:1, :], small[1:2, :]
        self.shift_one, self.shift_two = small[2:3, :], small[3:4, :]
        self.bias_one, self.bias_two = twice(small[4:5, :]), twice(small[5:6, :])
        self.bias_down = jnp.concatenate([small[6:7, :], small[7:8, :]], axis=1)
        self.scale_plus = refs.modulation[0, pl.ds(sample, 1), :]
        self.offset = refs.modulation[1, pl.ds(sample, 1), :]
        self.nothing = jnp.zeros((8, 2 * C), jnp.float32)

    def keep(self, **values):
        for name, value in values.items():
            place = STATE.index(name)
            self.state[place : place + 1, :] = value

    def kept(self, name):
        place = STATE.index(name)
        return self.state[place : place + 1, :]

    def report(self, place, value):
        self.refs.sums[place, pl.ds(self.sample, 1), :] = value

    def field(self, pair):
        return jnp.concatenate(
            [
                self.x_ref[pair, 0].astype(jnp.float32),
                self.x_ref[pair, 1].astype(jnp.float32),
            ],
            axis=1,
        )

    def means(self, first, second):
        return group_means(first, second, self.same_group, self.entries)

    def first_stats(self):
        def body(pair, carry):
            value = self.field(pair)
            return carry[0] + folded(value), carry[1] + folded(value * value)

        total, squares = over(self.pairs, 8, body, (self.nothing, self.nothing))
        self.partial[0], self.partial[1] = total, squares

    def partial_sums(self):
        return channel_sum(self.partial[0]), channel_sum(self.partial[1])

    def norm_of(self):
        mean, square = self.means(*self.partial_sums())
        inverse = lax.rsqrt(square - mean * mean + NORM_EPS)
        return inverse, -mean * inverse

    def first_act(self):
        inverse, center = self.norm_of()
        self.keep(inverse_one=inverse, center_one=center)
        gain = twice(inverse * self.gain_one)
        shift = twice(center * self.gain_one + self.shift_one)

        def body(pair, carry):
            value, slope = gelu_pair(self.field(pair) * gain + shift)
            put_shifted(self.act_one, pair, value)
            self.slope_one[pair] = slope
            return carry

        over(self.pairs, 8, body, 0)
        close_ring(self.act_one, self.pairs)

    def first_conv(self):
        def body(step, carry):
            start = step * self.size
            value = (
                jnp.dot(
                    windows(self.act_one, start, self.size),
                    self.refs.fwd_one[...],
                    preferred_element_type=jnp.float32,
                )
                + self.bias_one
            )
            self.conv_one[pl.ds(start, self.size)] = value.reshape(self.size, FIELD_COLS, 2 * C)
            return carry[0] + folded(value), carry[1] + folded(value * value)

        total, squares = over_steps(self.steps, body, (self.nothing, self.nothing))
        self.partial[0], self.partial[1] = total, squares

    def second_act(self):
        inverse, center = self.norm_of()
        self.keep(inverse_two=inverse, center_two=center)
        factor = self.gain_two * self.scale_plus
        gain = twice(inverse * factor)
        shift = twice(center * factor + self.shift_two * self.scale_plus + self.offset)

        def body(pair, carry):
            value, slope = gelu_pair(self.conv_one[pair] * gain + shift)
            put_shifted(self.act_two, pair, value)
            self.slope_two[pair] = slope
            return carry

        over(self.pairs, 8, body, 0)
        close_ring(self.act_two, self.pairs)

    def second_conv(self):
        def body(step, carry):
            start = step * self.size
            value = (
                jnp.dot(
                    windows(self.act_two, start, self.size),
                    self.refs.fwd_two[...],
                    preferred_element_type=jnp.float32,
                )
                + self.bias_two
            )
            value = value.reshape(self.size, FIELD_COLS, 2 * C)
            for half, ref in ((0, self.sum_even), (1, self.sum_odd)):
                base = self.x_ref[pl.ds(start, self.size), half].astype(jnp.float32)
                ref[pl.ds(start, self.size)] = base + value[:, :, half * C : half * C + C]
            return carry

        over_steps(self.steps, body)

    def split_columns(self):
        def body(pair, carry):
            even, odd = [], []
            for ref in (self.sum_even, self.sum_odd):
                even.append(ref[pair, pl.ds(0, HALF_COLS, stride=2), :])
                odd.append(ref[pair, pl.ds(1, HALF_COLS, stride=2), :])
            even = jnp.concatenate(even, axis=1)
            odd = jnp.concatenate(odd, axis=1)
            self.down_win[0, pair + 1] = pltpu.roll(odd, 1, 0).astype(jnp.bfloat16)
            self.down_win[1, pair + 1] = even.astype(jnp.bfloat16)
            self.down_win[2, pair + 1] = odd.astype(jnp.bfloat16)
            return carry

        over(self.pairs, 8, body, 0)
        self.down_win[:, 0, :, C:] = self.down_win[:, self.pairs, :, C:]

    def shift_cotangent(self):
        def body(pair, carry):
            value = self.cot_ref[pair]
            wide = value.astype(jnp.float32)
            self.cot_win[0, pair] = value
            self.cot_win[1, pair] = pltpu.roll(wide, HALF_COLS - 1, 0).astype(jnp.bfloat16)
            return carry + folded(wide)

        total = over(self.pairs, 8, body, self.nothing)
        self.cot_win[:, self.pairs] = self.cot_win[:, 0]
        self.refs.raw_sums[16:24, :] = self.refs.raw_sums[16:24, :] + total

    def down_windows(self, start):
        pieces = [
            self.down_win[tap, pl.ds(start + 1, self.size)].reshape(self.small, 2 * C)
            for tap in range(3)
        ]
        pieces += [
            self.down_win[tap, pl.ds(start, self.size), :, C:].reshape(self.small, C)
            for tap in range(3)
        ]
        return jnp.concatenate(pieces, axis=1)

    def down_output(self):
        def body(step, carry):
            start = step * self.size
            value = jnp.dot(
                self.down_windows(start), self.refs.down_fwd[...], preferred_element_type=jnp.float32
            )
            self.out_ref[pl.ds(start, self.size)] = (
                (value + self.bias_down)
                .reshape(self.size, HALF_COLS, 2 * C)
                .astype(jnp.bfloat16)
            )
            return carry

        over_steps(self.steps, body)

    def add_down_grad(self):
        def body(step, carry):
            start = step * self.size
            here = self.cot_win[0, pl.ds(start, self.size)].reshape(self.small, 2 * C)
            product = jnp.dot(
                here.T, self.down_windows(start), preferred_element_type=jnp.float32
            )
            for position in range(9):
                row_tap, tap = DOWN_ORDER[position]
                lanes = pl.ds((3 * row_tap + tap) * C, C)
                self.refs.down_grad[:, lanes] = (
                    self.refs.down_grad[:, lanes] + product[:, position * C : position * C + C]
                )
            return carry

        over_steps(self.steps, body)

    def down_adjoint(self):
        def body(step, carry):
            start = step * self.size
            pieces = [
                self.cot_win[shift, pl.ds(start + below, self.size)].reshape(self.small, 2 * C)
                for below in range(2)
                for shift in range(2)
            ]
            even = jnp.dot(
                jnp.concatenate([pieces[0], pieces[2]], axis=1),
                self.refs.down_even[...],
                preferred_element_type=jnp.float32,
            ).reshape(self.size, HALF_COLS, 2 * C)
            odd = jnp.dot(
                jnp.concatenate(pieces, axis=1),
                self.refs.down_odd[...],
                preferred_element_type=jnp.float32,
            ).reshape(self.size, HALF_COLS, 2 * C)
            for half, ref in ((0, self.grad_even), (1, self.grad_odd)):
                lanes = slice(half * C, half * C + C)
                for inner in range(self.size):
                    ref[start + inner, pl.ds(0, HALF_COLS, stride=2), :] = even[inner, :, lanes]
                    ref[start + inner, pl.ds(1, HALF_COLS, stride=2), :] = odd[inner, :, lanes]
            return carry

        over_steps(self.steps, body)

    def second_grad(self):
        def body(pair, carry):
            value = jnp.concatenate([self.grad_even[pair], self.grad_odd[pair]], axis=1)
            put_shifted(self.grad_two, pair, value)
            return carry + folded(value)

        total = over(self.pairs, 8, body, self.nothing)
        close_ring(self.grad_two, self.pairs)
        self.refs.raw_sums[8:16, :] = self.refs.raw_sums[8:16, :] + total

    def second_conv_grad(self):
        add_conv_grad(self.refs.conv_grad_two, self.act_two, self.grad_two, self.pairs)

    def second_back(self):
        def body(step, carry):
            start = step * self.size
            value = jnp.dot(
                windows(self.grad_two, start, self.size),
                self.refs.back_two[...],
                preferred_element_type=jnp.float32,
            )
            value = value * self.slope_two[pl.ds(start, self.size)].reshape(self.rows, 2 * C)
            self.grad_mid[pl.ds(start, self.size)] = value.reshape(self.size, FIELD_COLS, 2 * C)
            conv = self.conv_one[pl.ds(start, self.size)].reshape(self.rows, 2 * C)
            return carry[0] + folded(value), carry[1] + folded(value * conv)

        total, cross = over_steps(self.steps, body, (self.nothing, self.nothing))
        self.partial[0], self.partial[1] = total, cross

    def first_grad(self):
        inverse, center = self.kept("inverse_two"), self.kept("center_two")
        total, cross = self.partial_sums()
        cross = cross * inverse + total * center
        self.report(0, cross)
        self.report(1, total)
        factor = self.scale_plus * self.gain_two
        mean_grad, mean_cross = self.means(total * factor, cross * factor)
        from_mid = twice(inverse * factor)
        from_conv = twice(inverse * inverse * mean_cross)
        from_mean = twice(inverse * (mean_grad + center * mean_cross))

        def body(pair, carry):
            value = self.grad_mid[pair] * from_mid - from_mean - self.conv_one[pair] * from_conv
            put_shifted(self.grad_one, pair, value)
            return carry + folded(value)

        total = over(self.pairs, 8, body, self.nothing)
        close_ring(self.grad_one, self.pairs)
        self.refs.raw_sums[0:8, :] = self.refs.raw_sums[0:8, :] + total

    def first_conv_grad(self):
        add_conv_grad(self.refs.conv_grad_one, self.act_one, self.grad_one, self.pairs)

    def first_back(self):
        def body(step, carry):
            start = step * self.size
            value = jnp.dot(
                windows(self.grad_one, start, self.size),
                self.refs.back_one[...],
                preferred_element_type=jnp.float32,
            )
            value = value * self.slope_one[pl.ds(start, self.size)].reshape(self.rows, 2 * C)
            self.grad_mid[pl.ds(start, self.size)] = value.reshape(self.size, FIELD_COLS, 2 * C)
            base = jnp.concatenate(
                [
                    self.x_ref[pl.ds(start, self.size), half]
                    .astype(jnp.float32)
                    .reshape(self.rows, C)
                    for half in range(2)
                ],
                axis=1,
            )
            return carry[0] + folded(value), carry[1] + folded(value * base)

        total, cross = over_steps(self.steps, body, (self.nothing, self.nothing))
        self.partial[0], self.partial[1] = total, cross

    def field_grad(self, rows_ref):
        inverse, center = self.kept("inverse_one"), self.kept("center_one")
        total, cross = self.partial_sums()
        cross = cross * inverse + total * center
        self.report(2, cross)
        self.report(3, total)
        mean_grad, mean_cross = self.means(total * self.gain_one, cross * self.gain_one)
        from_pre = twice(inverse * self.gain_one)
        from_field = twice(inverse * inverse * mean_cross)
        from_mean = twice(inverse * (mean_grad + center * mean_cross))

        def body(pair, carry):
            summed = jnp.concatenate([self.grad_even[pair], self.grad_odd[pair]], axis=1)
            change = self.grad_mid[pair] * from_pre - from_mean - self.field(pair) * from_field
            value = (summed + change).astype(jnp.bfloat16)
            rows_ref[pair, 0] = value[:, :C]
            rows_ref[pair, 1] = value[:, C:]
            return carry

        over(self.pairs, 8, body, 0)


STATE = (
    "inverse_one",
    "center_one",
    "inverse_two",
    "center_two",
)
BEFORE = -1
SLOTS = (
    (
        ("first_stats", 0),
        ("shift_cotangent", 0),
        ("add_down_grad", BEFORE),
        ("second_conv_grad", BEFORE),
    ),
    (
        ("first_act", 0),
        ("first_stats", 1),
        ("down_adjoint", 0),
        ("first_conv_grad", BEFORE),
    ),
    (
        ("first_act", 1),
        ("second_grad", 0),
        ("shift_cotangent", 1),
        ("first_conv", 0),
        ("down_adjoint", 1),
    ),
    (("second_act", 0), ("second_grad", 1), ("first_conv", 1)),
    (("second_act", 1), ("second_back", 0), ("second_conv", 0)),
    (("first_grad", 0), ("split_columns", 0), ("second_back", 1), ("second_conv_grad", 0)),
    (("first_grad", 1), ("first_back", 0), ("second_conv", 1)),
    (("field_grad", 0), ("split_columns", 1), ("first_back", 1), ("first_conv_grad", 0)),
    (("field_grad", 1), ("down_output", 0), ("add_down_grad", 0), ("down_output", 1)),
)
LATE = ("add_down_grad", "second_conv_grad", "first_conv_grad")


def start_all(copies):
    for copy in copies:
        copy.start()


def peers(axis, count, pairs_of, sends, receives):
    return [
        to_peer(axis, step, count, source(step), target(step), sends.at[place, step], receives.at[place, step])
        for step in range(1, count)
        for place, (source, target) in pairs_of
    ]


def same(ref):
    return lambda step: ref


def slot_of(ref):
    return lambda step: ref.at[step]


def step_kernel(sizes, *args):
    row_count, batch_count, pairs, samples, together = sizes
    names = INPUTS + OUTPUTS + SCRATCH
    refs = SimpleNamespace(**dict(zip(names, args[: len(names)])))
    scratch = args[len(names) :]
    base = pl.program_id(0) * together
    row, batch = lax.axis_index("row"), lax.axis_index("batch")
    share = pairs // row_count

    def send_field(index, carry):
        mine = refs.fields.at[index, pl.ds(row * share, share)]
        for step in range(1, row_count):
            place = lax.rem(row + step, row_count) * samples + index
            to_peer(
                "row",
                step,
                row_count,
                refs.field.at[place],
                mine,
                refs.field_sent,
                refs.field_sem.at[index],
            ).start()
        pltpu.make_async_copy(
            refs.field.at[row * samples + index], mine, refs.field_sem.at[index]
        ).start()
        return carry

    def send_grad(index):
        target = refs.grad_out.at[row * samples + index]
        for step in range(1, row_count):
            place = lax.rem(row + step, row_count) * share
            to_peer(
                "row",
                step,
                row_count,
                refs.grad_rows.at[index, pl.ds(place, share)],
                target,
                refs.grad_sent,
                refs.grad_sem,
            ).start()
        pltpu.make_async_copy(
            refs.grad_rows.at[index, pl.ds(row * share, share)], target, refs.grad_sem
        ).start()

    @pl.when(base == 0)
    def _():
        pack_shards(refs)
        greet(row_count, batch_count)
        own = pltpu.make_async_copy(refs.shard, refs.shards.at[row, batch], refs.local_sem)
        own.start()
        copies = peers(
            "batch",
            batch_count,
            [
                (0, (same(refs.shard), same(refs.shards.at[row, batch]))),
                (1, (same(refs.small), slot_of(refs.small_z))),
            ],
            refs.send_z,
            refs.recv_z,
        )
        start_all(copies)
        lax.fori_loop(0, together, send_field, 0)
        for ref in (refs.conv_grad_one, refs.conv_grad_two, refs.down_grad, refs.raw_sums, refs.sums):
            ref[...] = jnp.zeros_like(ref)
        if together > 1:
            for ref in scratch[-16:-12] + scratch[-4:-2]:
                ref[...] = jnp.zeros_like(ref)
        own.wait()
        finish(copies)
        total = refs.small[...]
        for step in range(1, batch_count):
            total = total + refs.small_z[step]
        refs.small_one[...] = total
        copies = peers(
            "row",
            row_count,
            [(1, (same(refs.small_one), slot_of(refs.small_row)))],
            refs.send_row,
            refs.recv_row,
        )
        sibling = sibling_of(row)
        mine = refs.shards.at[row]
        direct = {}
        for step in range(2, row_count, 2):
            direct[step] = to_row(
                lax.rem(row + step, row_count),
                mine,
                mine,
                refs.send_row.at[0, step],
                refs.recv_row.at[0, step],
            )
        beside = [to_row(sibling, mine, mine, refs.send_row.at[0, 1], refs.recv_row.at[0, 1])]
        start_all(list(direct.values()) + beside + copies)
        lax.fori_loop(together, samples, send_field, 0)
        for step in range(2, row_count, 2):
            direct[step].wait_recv()
            came = refs.shards.at[lax.rem(row + row_count - step, row_count)]
            beside.append(
                to_row(
                    sibling,
                    came,
                    came,
                    refs.send_row.at[0, step + 1],
                    refs.recv_row.at[0, step + 1],
                )
            )
            beside[-1].start()
        for step in range(2, row_count, 2):
            direct[step].wait_send()
        finish(beside + copies)
        total = refs.small_one[...]
        for step in range(1, row_count):
            total = total + refs.small_row[step]
        refs.small_all[...] = total
        lay_out(row_count, batch_count, refs)
        modulate(refs)

    @pl.when(base > 0)
    def _():
        for place in range(together):
            send_grad(base - together + place)

    for place in range(together):
        arrived = refs.fields.at[base + place]
        pltpu.make_async_copy(arrived, arrived, refs.field_sem.at[base + place]).wait()
    stages = [
        Sample(
            pairs,
            base + place,
            refs.fields.at[base + place],
            refs.cot.at[place],
            refs.block_out.at[place],
            refs,
            scratch[16 * place : 16 * place + 16],
        )
        for place in range(together)
    ]

    def run_slot(slot):
        for name, place in slot:
            if place >= together or (place == BEFORE and together == 1):
                continue
            stage = getattr(stages[place], name)
            if name == "field_grad":
                stage(refs.grad_rows.at[base + place])
            else:
                stage()

    for slot in SLOTS:
        run_slot(slot)

    @pl.when(base == samples - together)
    def _():
        for place in range(together):
            send_grad(base + place)
        if together > 1:
            for name in LATE:
                getattr(stages[-1], name)()
        reduce_all(row_count, batch_count, refs)
        pltpu.make_async_copy(refs.grad_out, refs.grad_out, refs.grad_sem).wait()
        others = pl.ds(0, pairs - share)
        for ref, sem in ((refs.fields, refs.field_sent), (refs.grad_rows, refs.grad_sent)):
            pltpu.make_async_copy(ref.at[:, others], ref.at[:, others], sem).wait()


INPUTS = ("field", "cot", "conv", "down", "embed_in", "embed_out", "small", "embedded", "group")
OUTPUTS = (
    "block_out",
    "grad_out",
    "conv_grad",
    "down_share",
    "embed_in_grad",
    "embed_out_grad",
    "small_grad",
    "norm",
)
SCRATCH = (
    "fwd_one",
    "back_one",
    "fwd_two",
    "back_two",
    "down_fwd",
    "down_even",
    "down_odd",
    "small_all",
    "embed_in_t",
    "embed_out_t",
    "modulation",
    "hidden",
    "hidden_slope",
    "sums",
    "raw_sums",
    "conv_grad_one",
    "conv_grad_two",
    "down_grad",
    "shard",
    "shards",
    "small_z",
    "small_one",
    "small_row",
    "conv_t",
    "down_t",
    "fields",
    "grad_rows",
    "row_send",
    "pair_take",
    "chip_send",
    "row_take",
    "batch_send",
    "batch_take",
    "small_send",
    "small_take",
    "small_next",
    "small_last",
    "square_send",
    "square_take",
    "square_next",
    "square_last",
    "field_sem",
    "field_sent",
    "grad_sem",
    "grad_sent",
    "local_sem",
    "send_z",
    "recv_z",
    "send_row",
    "recv_row",
    "send_sem",
    "recv_sem",
)
DOWN_ORDER = ((1, 0), (2, 0), (1, 1), (2, 1), (1, 2), (2, 2), (0, 0), (0, 1), (0, 2))


def lay_out(row_count, batch_count, refs):
    depth, share, wide_share = 9 * C // batch_count, C // row_count, C2 // row_count
    height = 2 * share + wide_share
    embed_share, hidden_share = EMB // batch_count, HID // batch_count
    for place in range(row_count):
        parts = [refs.shards[place, part].astype(jnp.float32) for part in range(batch_count)]
        main = jnp.concatenate([part[:, :depth] for part in parts], axis=1)
        for which in range(2):
            refs.conv_t[which, place * share : place * share + share, :] = main[
                which * share : which * share + share
            ]
        refs.down_t[place * wide_share : place * wide_share + wide_share, :] = main[2 * share :]
        refs.embed_in_t[place * height : place * height + height, :] = jnp.concatenate(
            [part[:, depth : depth + embed_share] for part in parts], axis=1
        )
        tail = depth + embed_share
        half_rows, half_lanes = height // 2, hidden_share // 2
        lanes = []
        for part in parts:
            lanes.append(part[:half_rows, tail : tail + half_lanes])
            lanes.append(part[half_rows:, tail : tail + half_lanes])
        refs.embed_out_t[place * half_rows : place * half_rows + half_rows, :] = jnp.concatenate(
            lanes, axis=1
        )
    for which, forward, back in (
        (0, refs.fwd_one, refs.back_one),
        (1, refs.fwd_two, refs.back_two),
    ):
        zero = jnp.zeros((C, C), jnp.bfloat16)
        for tap in range(3):
            direct = [
                refs.conv_t[which, :, (3 * row_tap + tap) * C : (3 * row_tap + tap) * C + C]
                for row_tap in range(3)
            ]
            fill_blocks(forward, tap, [block.T.astype(jnp.bfloat16) for block in direct], zero)
            fill_blocks(
                back, 2 - tap, [block.astype(jnp.bfloat16) for block in direct[::-1]], zero
            )
    zero = jnp.zeros((C2, C), jnp.bfloat16)
    back = {}
    for position in range(9):
        row_tap, tap = DOWN_ORDER[position]
        block = refs.down_t[:, (3 * row_tap + tap) * C : (3 * row_tap + tap) * C + C]
        refs.down_fwd[position * C : position * C + C, :] = block.T.astype(jnp.bfloat16)
        back[row_tap, tap] = block.astype(jnp.bfloat16)
    even = ((back[1, 1], back[2, 1]), (zero, back[0, 1]))
    odd = (
        (back[1, 2], back[2, 2]),
        (back[1, 0], back[2, 0]),
        (zero, back[0, 2]),
        (zero, back[0, 0]),
    )
    for ref, table in ((refs.down_even, even), (refs.down_odd, odd)):
        for position, (left, right) in enumerate(table):
            ref[position * C2 : position * C2 + C2, :C] = left
            ref[position * C2 : position * C2 + C2, C:] = right


def lanes_of(ref, first, last):
    return jnp.concatenate([ref[place : place + 1, :] for place in range(first, last)], axis=1)


def modulate(refs):
    small = refs.small_all
    before = dot_full(refs.embedded[...], refs.embed_in_t[...].T) + lanes_of(small, 8, 12)
    hidden, slope = gelu_pair(before)
    refs.hidden[...] = hidden
    refs.hidden_slope[...] = slope
    result = dot_full(hidden, refs.embed_out_t[...].T) + lanes_of(small, 12, 14)
    refs.modulation[0] = 1.0 + result[:, :C]
    refs.modulation[1] = result[:, C:]


def fill_blocks(ref, tap, blocks, zero):
    table = (
        (blocks[1], blocks[0]),
        (blocks[2], blocks[1]),
        (blocks[0], zero),
        (zero, blocks[2]),
    )
    for position, (left, right) in enumerate(table):
        base = (4 * tap + position) * C
        ref[base : base + C, :C] = left
        ref[base : base + C, C:] = right


def dot_full(lhs, rhs):
    return jnp.dot(lhs, rhs, precision=HIGHEST, preferred_element_type=jnp.float32)


def dot_first(lhs, rhs):
    return lax.dot_general(
        lhs,
        rhs,
        (((0,), (0,)), ((), ())),
        precision=HIGHEST,
        preferred_element_type=jnp.float32,
    )


def reduce_all(row_count, batch_count, refs):
    row, batch = lax.axis_index("row"), lax.axis_index("batch")
    depth, share, wide_share = 9 * C // batch_count, C // row_count, C2 // row_count
    height = 2 * share + wide_share
    embed_share, hidden_share = EMB // batch_count, HID // batch_count
    mid_cross, mid_total = refs.sums[0], refs.sums[1]
    gain_two, shift_two = refs.small_all[1:2, :], refs.small_all[3:4, :]
    scale_plus = refs.modulation[0]
    grad_mod = jnp.concatenate([gain_two * mid_cross + shift_two * mid_total, mid_total], axis=1)
    grad_embed_out = dot_first(grad_mod, refs.hidden[...])
    grad_hidden = (
        dot_full(grad_mod, refs.embed_out_t[...])
        * refs.hidden_slope[...]
    )
    grad_embed_in = dot_first(grad_hidden, refs.embedded[...])

    def down_sum(value):
        return jnp.sum(value, axis=0, keepdims=True)

    small_rows = [
        down_sum(refs.sums[2]),
        down_sum(mid_cross * scale_plus),
        down_sum(refs.sums[3]),
        down_sum(mid_total * scale_plus),
        channel_sum(refs.raw_sums[0:8]),
        channel_sum(refs.raw_sums[8:16]),
    ]
    cot_total = down_sum(refs.raw_sums[16:24])
    small_rows += [cot_total[:, :C], cot_total[:, C:]]
    hidden_total, mod_total = down_sum(grad_hidden), down_sum(grad_mod)
    small_rows += [hidden_total[:, lane : lane + C] for lane in range(0, HID, C)]
    small_rows += [mod_total[:, lane : lane + C] for lane in range(0, 2 * C, C)]
    small_rows.append(jnp.zeros((2, C), jnp.float32))
    refs.small_send[...] = jnp.concatenate(small_rows, axis=0)
    half_rows = height // 2
    for place in range(row_count):
        low, high = place * share, place * share + share
        refs.row_send[place, :, : 9 * C] = jnp.concatenate(
            [
                refs.conv_grad_one[low:high],
                refs.conv_grad_two[low:high],
                refs.down_grad[place * wide_share : place * wide_share + wide_share],
            ],
            axis=0,
        ).astype(jnp.bfloat16)
        refs.row_send[place, :, 9 * C : 10 * C] = grad_embed_in[
            place * height : place * height + height
        ].astype(jnp.bfloat16)
        piece = grad_embed_out[place * half_rows : place * half_rows + half_rows]
        refs.row_send[place, :, 10 * C :] = jnp.concatenate(
            [piece[:, : HID // 2], piece[:, HID // 2 :]], axis=0
        ).astype(jnp.bfloat16)
    sibling = sibling_of(row)
    beside = [
        to_row(
            sibling,
            refs.row_send.at[lax.rem(sibling + 2 * step, row_count)],
            refs.pair_take.at[step],
            refs.send_sem.at[0, step],
            refs.recv_sem.at[0, step],
        )
        for step in range(row_count // 2)
    ]
    smalls = [
        to_peer(
            "row",
            step,
            row_count,
            refs.small_send,
            refs.small_take.at[step],
            refs.send_sem.at[1, step],
            refs.recv_sem.at[1, step],
        )
        for step in range(1, row_count)
    ]
    order = list(range(1, row_count // 2)) + [0]
    start_all([beside[step] for step in order] + smalls)
    copies = []
    for step in order:
        beside[step].wait_recv()
        place = lax.rem(row + 2 * step, row_count)
        total = refs.row_send[place].astype(jnp.float32) + refs.pair_take[step].astype(jnp.float32)
        if step:
            refs.chip_send[step] = total.astype(jnp.bfloat16)
            copies.append(
                to_row(
                    place,
                    refs.chip_send.at[step],
                    refs.row_take.at[step],
                    refs.send_sem.at[6, step],
                    refs.recv_sem.at[6, step],
                )
            )
            copies[-1].start()
    for copy in beside:
        copy.wait_send()
    finish(copies + smalls)
    small_total = refs.small_send[...]
    for step in range(1, row_count // 2):
        total = total + refs.row_take[step].astype(jnp.float32)
    for step in range(1, row_count):
        small_total = small_total + refs.small_take[step]
    refs.small_next[...] = small_total
    for part in range(batch_count):
        per_half = batch_count // 2
        rows = slice(0, half_rows) if part < per_half else slice(half_rows, height)
        base = 10 * C + hidden_share * (part % per_half)
        piece = total[rows, base : base + hidden_share]
        refs.batch_send[part] = jnp.concatenate(
            [
                total[:, part * depth : part * depth + depth],
                total[:, 9 * C + part * embed_share : 9 * C + part * embed_share + embed_share],
                jnp.concatenate([piece[:, : hidden_share // 2], piece[:, hidden_share // 2 :]], axis=0),
            ],
            axis=1,
        ).astype(jnp.bfloat16)
    copies = []
    for step in range(1, batch_count):
        copies.append(
            to_peer(
                "batch",
                step,
                batch_count,
                refs.batch_send.at[lax.rem(batch + step, batch_count)],
                refs.batch_take.at[step],
                refs.send_sem.at[2, step],
                refs.recv_sem.at[2, step],
            )
        )
        copies.append(
            to_peer(
                "batch",
                step,
                batch_count,
                refs.small_next,
                refs.small_last.at[step],
                refs.send_sem.at[3, step],
                refs.recv_sem.at[3, step],
            )
        )
    for copy in copies:
        copy.start()
    owned = refs.batch_send[batch].astype(jnp.float32)
    finish(copies)
    small_total = refs.small_next[...]
    for step in range(1, batch_count):
        owned = owned + refs.batch_take[step].astype(jnp.float32)
        small_total = small_total + refs.small_last[step]
    squares = jnp.sum(jnp.sum(owned * owned, axis=0, keepdims=True), axis=1, keepdims=True)
    refs.square_send[...] = jnp.broadcast_to(squares, (8, C))
    copies = [
        to_peer(
            "row",
            step,
            row_count,
            refs.square_send,
            refs.square_take.at[step],
            refs.send_sem.at[4, step],
            refs.recv_sem.at[4, step],
        )
        for step in range(1, row_count)
    ]
    for copy in copies:
        copy.start()
    finish(copies)
    squares = refs.square_send[...]
    for step in range(1, row_count):
        squares = squares + refs.square_take[step]
    refs.square_next[...] = squares
    copies = [
        to_peer(
            "batch",
            step,
            batch_count,
            refs.square_next,
            refs.square_last.at[step],
            refs.send_sem.at[5, step],
            refs.recv_sem.at[5, step],
        )
        for step in range(1, batch_count)
    ]
    for copy in copies:
        copy.start()
    finish(copies)
    squares = refs.square_next[...]
    for step in range(1, batch_count):
        squares = squares + refs.square_last[step]
    small_squares = jnp.sum(
        jnp.sum(small_total * small_total, axis=0, keepdims=True), axis=1, keepdims=True
    )
    norm = jnp.sqrt(squares + small_squares)
    clip = jnp.minimum(1.0, CLIP_NORM / (norm + 1e-06))[0:1, 0:1]
    refs.norm[...] = norm
    owned = owned * clip
    refs.conv_grad[0] = owned[:share, :depth]
    refs.conv_grad[1] = owned[share : 2 * share, :depth]
    refs.down_share[...] = owned[2 * share :, :depth]
    refs.embed_in_grad[...] = owned[:, depth : depth + embed_share].T
    tail = depth + embed_share
    refs.embed_out_grad[...] = jnp.concatenate(
        [owned[:half_rows, tail:], owned[half_rows:, tail:]], axis=1
    )
    refs.small_grad[...] = small_total * clip


def pack_shards(refs):
    half = refs.embed_out.shape[1] // 2
    refs.shard[...] = jnp.concatenate(
        [
            jnp.concatenate([refs.conv[0], refs.conv[1], refs.down[...]], axis=0),
            refs.embed_in[...].T,
            jnp.concatenate([refs.embed_out[:, :half], refs.embed_out[:, half:]], axis=0),
        ],
        axis=1,
    ).astype(jnp.bfloat16)


def run_step(field_in, cotangent, shards, small_tile, embedded):
    row_count, batch_count = (lax.axis_size("row"), lax.axis_size("batch"))
    samples = cotangent.shape[0]
    padded = embedded.shape[0]
    pairs = field_in.shape[1] // 2 * row_count
    together = chunk_of(samples, 2)
    share = pairs // row_count
    height, width = 4 * C // row_count, 12 * C // batch_count
    halves = field_in.reshape(field_in.shape[0], share, 2, FIELD_COLS, C)
    same_group = jnp.asarray(
        np.kron(np.eye(GROUPS), np.ones((C // GROUPS, C // GROUPS))), jnp.float32
    )
    low, full = jnp.bfloat16, jnp.float32
    anywhere = pl.BlockSpec(memory_space=pl.ANY)

    def whole(array):
        return pl.BlockSpec(array.shape, lambda i: (0,) * len(array.shape))

    def per_step(array):
        rank = len(array.shape)
        return pl.BlockSpec((together,) + array.shape[1:], lambda i: (i,) + (0,) * (rank - 1))

    outs = (
        jax.ShapeDtypeStruct(cotangent.shape, low),
        jax.ShapeDtypeStruct(halves.shape, low),
        *[jax.ShapeDtypeStruct(shard.shape, full) for shard in shards],
        jax.ShapeDtypeStruct((16, C), full),
        jax.ShapeDtypeStruct((8, C), full),
    )
    ring = pltpu.VMEM((3, pairs + 2, FIELD_COLS, 2 * C), low)
    wide = pltpu.VMEM((pairs, FIELD_COLS, 2 * C), full)
    half = pltpu.VMEM((pairs, FIELD_COLS, C), full)
    fields = pltpu.VMEM((samples, pairs, 2, FIELD_COLS, C), low)
    dma = pltpu.SemaphoreType.DMA
    most = max(row_count, batch_count)
    tile = (16, C)
    scratch = (
        [pltpu.VMEM((12 * C, 2 * C), low)] * 4
        + [
            pltpu.VMEM((9 * C, C2), low),
            pltpu.VMEM((2 * C2, 2 * C), low),
            pltpu.VMEM((4 * C2, 2 * C), low),
            pltpu.VMEM(tile, full),
            pltpu.VMEM((HID, EMB), full),
            pltpu.VMEM((2 * C, HID), full),
            pltpu.VMEM((2, padded, C), full),
            pltpu.VMEM((padded, HID), full),
            pltpu.VMEM((padded, HID), full),
            pltpu.VMEM((4, padded, C), full),
            pltpu.VMEM((24, 2 * C), full),
            pltpu.VMEM((C, 9 * C), full),
            pltpu.VMEM((C, 9 * C), full),
            pltpu.VMEM((C2, 9 * C), full),
            pltpu.VMEM((height, width), low),
            pltpu.VMEM((row_count, batch_count, height, width), low),
            pltpu.VMEM((batch_count,) + tile, full),
            pltpu.VMEM(tile, full),
            pltpu.VMEM((row_count,) + tile, full),
            pltpu.VMEM((2, C, 9 * C), full),
            pltpu.VMEM((C2, 9 * C), full),
            fields,
            fields,
            pltpu.VMEM((row_count, height, 12 * C), low),
            pltpu.VMEM((row_count // 2, height, 12 * C), low),
            pltpu.VMEM((row_count // 2, height, 12 * C), low),
            pltpu.VMEM((row_count // 2, height, 12 * C), low),
            pltpu.VMEM((batch_count, height, width), low),
            pltpu.VMEM((batch_count, height, width), low),
            pltpu.VMEM(tile, full),
            pltpu.VMEM((row_count,) + tile, full),
            pltpu.VMEM(tile, full),
            pltpu.VMEM((batch_count,) + tile, full),
            pltpu.VMEM((8, C), full),
            pltpu.VMEM((row_count, 8, C), full),
            pltpu.VMEM((8, C), full),
            pltpu.VMEM((batch_count, 8, C), full),
            dma((samples,)),
            dma,
            dma,
            dma,
            dma,
            dma((2, batch_count)),
            dma((2, batch_count)),
            dma((2, row_count)),
            dma((2, row_count)),
            dma((7, most)),
            dma((7, most)),
        ]
        + (
            [ring] * 4
            + [wide] * 4
            + [half] * 4
            + [
                pltpu.VMEM((3, pairs + 1, HALF_COLS, 2 * C), low),
                pltpu.VMEM((2, pairs + 1, HALF_COLS, C2), low),
                pltpu.VMEM((8, C), full),
                pltpu.VMEM((2, 8, 2 * C), full),
            ]
        )
        * together
    )
    result = pl.pallas_call(
        functools.partial(step_kernel, (row_count, batch_count, pairs, samples, together)),
        grid=(samples // together,),
        in_specs=[anywhere, per_step(cotangent)]
        + [whole(array) for array in shards + (small_tile, embedded, same_group)],
        out_specs=[per_step(outs[0]), anywhere] + [whole(out) for out in outs[2:]],
        out_shape=outs,
        scratch_shapes=scratch,
        compiler_params=pltpu.CompilerParams(
            dimension_semantics=("arbitrary",),
            vmem_limit_bytes=62 << 20,
            collective_id=0,
            has_side_effects=True,
        ),
        name="step",
    )(halves, cotangent, *shards, small_tile, embedded, same_group)
    return (result[0], result[1].reshape(field_in.shape)) + tuple(result[2:])


def adam_update(weight, gradient, first_old, second_old, step_rate, clip_factor):
    scaled = gradient * clip_factor
    first_new = BETA_ONE * first_old + (1.0 - BETA_ONE) * scaled
    second_new = BETA_TWO * second_old + (1.0 - BETA_TWO) * scaled * scaled
    corrected = (
        first_new
        / (1.0 - BETA_ONE**STEP_COUNT)
        / (jnp.sqrt(second_new / (1.0 - BETA_TWO**STEP_COUNT)) + ADAM_EPS)
    )
    return (weight - step_rate * (corrected + DECAY * weight), first_new, second_new)


def body(
    field_in,
    refine_step,
    cotangent,
    conv_weight,
    down_weight,
    embed_in_weight,
    embed_out_weight,
    small_params,
    conv_first,
    down_first,
    embed_in_first,
    embed_out_first,
    small_first,
    conv_second,
    down_second,
    embed_in_second,
    embed_out_second,
    small_second,
):
    small_len = small_params.shape[0]
    place = (lax.axis_index("batch") * lax.axis_size("row") + lax.axis_index("row")) * small_len
    small_rounded = lax.reduce_precision(small_params, exponent_bits=8, mantissa_bits=7)
    small_tile = lax.dynamic_update_slice_in_dim(
        jnp.zeros((16 * C,), jnp.float32), small_rounded, place, 0
    ).reshape(16, C)
    owned = refine_step.shape[0] // lax.axis_size("row")
    padded = -(-owned // 8) * 8
    own_steps = lax.dynamic_slice_in_dim(refine_step, lax.axis_index("row") * owned, owned, 0)
    embedded = embed_steps(jnp.pad(own_steps, (0, padded - owned)))
    block_out, grad_start, *owned_shards, small_grads, norm_tile = run_step(
        field_in,
        cotangent,
        (
            jnp.transpose(conv_weight, (0, 2, 1)),
            down_weight.T,
            embed_in_weight,
            embed_out_weight.T,
        ),
        small_tile,
        embedded,
    )
    grad_norm = norm_tile[0, 0]
    owned_shards = [
        jnp.transpose(owned_shards[0], (0, 2, 1)),
        owned_shards[1].T,
        owned_shards[2],
        owned_shards[3].T,
    ]
    owned_shards.append(lax.dynamic_slice_in_dim(small_grads.reshape(-1), place, small_len, 0))
    clip_factor = 1.0
    conv_new = adam_update(
        conv_weight, owned_shards[0], conv_first, conv_second, RATE_MATRIX, clip_factor
    )
    down_new = adam_update(
        down_weight, owned_shards[1], down_first, down_second, RATE_MATRIX, clip_factor
    )
    embed_in_new = adam_update(
        embed_in_weight, owned_shards[2], embed_in_first, embed_in_second, RATE_MATRIX, clip_factor
    )
    embed_out_new = adam_update(
        embed_out_weight,
        owned_shards[3],
        embed_out_first,
        embed_out_second,
        RATE_MATRIX,
        clip_factor,
    )
    small_new = adam_update(
        small_params, owned_shards[4], small_first, small_second, RATE_SMALL, clip_factor
    )
    return (
        block_out,
        grad_start,
        grad_norm,
        conv_new[0],
        down_new[0],
        embed_in_new[0],
        embed_out_new[0],
        small_new[0],
        conv_new[1],
        down_new[1],
        embed_in_new[1],
        embed_out_new[1],
        small_new[1],
        conv_new[2],
        down_new[2],
        embed_in_new[2],
        embed_out_new[2],
        small_new[2],
    )


def solution(mesh):
    placed = (
        P("batch", "row", None, None),
        P("batch"),
        P(("batch", "row"), None, None, None),
        P(None, "batch", "row"),
        P("batch", "row"),
        P("batch", "row"),
        P("batch", "row"),
        P(("batch", "row")),
        P(None, "batch", "row"),
        P("batch", "row"),
        P("batch", "row"),
        P("batch", "row"),
        P(("batch", "row")),
        P(None, "batch", "row"),
        P("batch", "row"),
        P("batch", "row"),
        P("batch", "row"),
        P(("batch", "row")),
    )
    return jax.shard_map(
        body,
        mesh=mesh,
        in_specs=placed,
        out_specs=(
            P(("batch", "row"), None, None, None),
            P("batch", "row", None, None),
            P(),
            P(None, "batch", "row"),
            P("batch", "row"),
            P("batch", "row"),
            P("batch", "row"),
            P(("batch", "row")),
            P(None, "batch", "row"),
            P("batch", "row"),
            P("batch", "row"),
            P("batch", "row"),
            P(("batch", "row")),
            P(None, "batch", "row"),
            P("batch", "row"),
            P("batch", "row"),
            P("batch", "row"),
            P(("batch", "row")),
        ),
        check_vma=False,
    )
```

```python
import functools
import math
from types import SimpleNamespace

import jax
import jax.numpy as jnp
import numpy as np
from jax import lax
from jax.experimental import pallas as pl
from jax.experimental.pallas import tpu as pltpu
from jax.sharding import PartitionSpec as P

C = 128
C2 = 256
EMB = 128
HID = 512
GROUPS = 8
REFINE = 4


NORM_EPS = 1e-05
BETA_ONE = 0.9
BETA_TWO = 0.999
ADAM_EPS = 1e-08
DECAY = 0.01
RATE_MATRIX = 0.05
RATE_SMALL = 0.5
CLIP_NORM = 1.0
STEP_COUNT = 10
HIGHEST = lax.Precision.HIGHEST


def embed_steps(refine_step):
    halfway = EMB // 2
    frequency = jnp.exp(-math.log(10000.0) * jnp.arange(halfway).astype(jnp.float32) / halfway)
    angles = (refine_step.astype(jnp.float32) * (1000.0 / REFINE))[:, None] * frequency[None, :]
    return jnp.concatenate([jnp.sin(angles), jnp.cos(angles)], axis=1)


MESH = pl.DeviceIdType.MESH


def greet(row_count, batch_count=1):
    row, batch = lax.axis_index("row"), lax.axis_index("batch")
    barrier = pltpu.get_barrier_semaphore()
    for step in range(1, row_count):
        pl.semaphore_signal(
            barrier,
            inc=1,
            device_id={"row": lax.rem(row + step, row_count), "batch": batch},
            device_id_type=MESH,
        )
    for step in range(1, batch_count):
        pl.semaphore_signal(
            barrier,
            inc=1,
            device_id={"row": row, "batch": lax.rem(batch + step, batch_count)},
            device_id_type=MESH,
        )
    pl.semaphore_wait(barrier, row_count + batch_count - 2)


def to_peer(axis, step, count, source, target, send_sem, recv_sem):
    row, batch = lax.axis_index("row"), lax.axis_index("batch")
    if axis == "row":
        device = {"row": lax.rem(row + step, count), "batch": batch}
    else:
        device = {"row": row, "batch": lax.rem(batch + step, count)}
    return pltpu.make_async_remote_copy(
        src_ref=source,
        dst_ref=target,
        send_sem=send_sem,
        recv_sem=recv_sem,
        device_id=device,
        device_id_type=MESH,
    )


def to_row(place, source, target, send_sem, recv_sem):
    return pltpu.make_async_remote_copy(
        src_ref=source,
        dst_ref=target,
        send_sem=send_sem,
        recv_sem=recv_sem,
        device_id={"row": place, "batch": lax.axis_index("batch")},
        device_id_type=MESH,
    )


def sibling_of(row):
    return row + 1 - 2 * lax.rem(row, 2)


def finish(copies):
    for copy in copies:
        copy.wait()


FIELD_COLS = 64
HALF_COLS = 32
ROOT = math.sqrt(2.0 / math.pi)
CUBIC = ROOT * 0.044715


def chunk_of(total, most):
    size = min(total, most)
    while total % size:
        size -= 1
    return size


def over(total, most, body, init):
    size = chunk_of(total, most)

    def several(step, carry):
        for inner in range(size):
            carry = body(step * size + inner, carry)
        return carry

    if size == total:
        return several(0, init)
    return lax.fori_loop(0, total // size, several, init)


def folded(values):
    return jnp.sum(values.reshape(values.shape[0] // 8, 8, values.shape[1]), axis=0)


def twice(row):
    return jnp.concatenate([row, row], axis=1)


def channel_sum(partial):
    both = partial[:, :C] + partial[:, C:]
    return jnp.sum(both, axis=0, keepdims=True)


def group_means(first, second, same_group, entries):
    stacked = jnp.concatenate([first, second, jnp.zeros((6, C), jnp.float32)], axis=0)
    totals = jnp.dot(stacked, same_group, precision=HIGHEST, preferred_element_type=jnp.float32)
    return totals[0:1] / entries, totals[1:2] / entries


def gelu_pair(values):
    square = values * values
    weight = 0.5 + 0.5 * jnp.tanh(values * (ROOT + CUBIC * square))
    result = values * weight
    slope = weight + (result - result * weight) * (2.0 * ROOT + (6.0 * CUBIC) * square)
    return result, slope


def put_shifted(ref, pair, values):
    for tap, shift in ((0, 1), (1, 0), (2, FIELD_COLS - 1)):
        moved = pltpu.roll(values, shift, 0) if shift else values
        ref[tap, pair + 1] = moved.astype(jnp.bfloat16)


def close_ring(ref, pairs):
    ref[:, 0, :, C:] = ref[:, pairs, :, C:]
    ref[:, pairs + 1, :, :C] = ref[:, 1, :, :C]


def windows(ref, start, count):
    rows = count * FIELD_COLS
    pieces = []
    for tap in range(3):
        pieces.append(ref[tap, pl.ds(start + 1, count)].reshape(rows, 2 * C))
        pieces.append(ref[tap, pl.ds(start, count), :, C:].reshape(rows, C))
        pieces.append(ref[tap, pl.ds(start + 2, count), :, :C].reshape(rows, C))
    return jnp.concatenate(pieces, axis=1)


def over_steps(steps, body, init=0):
    if steps == 1:
        return body(0, init)
    return lax.fori_loop(0, steps, body, init)


def add_conv_grad(out_ref, act_ref, grad_ref, pairs):
    size = chunk_of(pairs, 8)
    rows = size * FIELD_COLS

    def body(step, carry):
        start = step * size
        grad = grad_ref[1, pl.ds(start + 1, size)].reshape(rows, 2 * C)
        product = jnp.dot(
            grad.T, windows(act_ref, start, size), preferred_element_type=jnp.float32
        )
        for tap in range(3):
            base = tap * 4 * C
            middle = product[:C, base : base + C] + product[C:, base + C : base + 2 * C]
            up = product[C:, base : base + C] + product[:C, base + 2 * C : base + 3 * C]
            down = product[:C, base + C : base + 2 * C] + product[C:, base + 3 * C : base + 4 * C]
            for row_tap, value in ((0, up), (1, middle), (2, down)):
                lanes = pl.ds((3 * row_tap + tap) * C, C)
                out_ref[:, lanes] = out_ref[:, lanes] + value
        return carry

    over_steps(pairs // size, body)


class Sample:
    def __init__(self, pairs, sample, x_ref, cot_ref, out_ref, refs, scratch):
        self.pairs, self.sample = pairs, sample
        self.x_ref, self.cot_ref, self.out_ref = x_ref, cot_ref, out_ref
        self.refs = refs
        (
            self.act_one,
            self.act_two,
            self.grad_one,
            self.grad_two,
            self.slope_one,
            self.slope_two,
            self.conv_one,
            self.grad_mid,
            self.sum_even,
            self.sum_odd,
            self.grad_even,
            self.grad_odd,
            self.down_win,
            self.cot_win,
            self.state,
            self.partial,
        ) = scratch
        self.entries = 2.0 * pairs * FIELD_COLS * (C // GROUPS)
        self.size = chunk_of(pairs, 8)
        self.steps = pairs // self.size
        self.rows = self.size * FIELD_COLS
        self.small = self.size * HALF_COLS
        self.same_group = refs.group[...]
        small = refs.small_all
        self.gain_one, self.gain_two = small[0:1, :], small[1:2, :]
        self.shift_one, self.shift_two = small[2:3, :], small[3:4, :]
        self.bias_one, self.bias_two = twice(small[4:5, :]), twice(small[5:6, :])
        self.bias_down = jnp.concatenate([small[6:7, :], small[7:8, :]], axis=1)
        self.scale_plus = refs.modulation[0, pl.ds(sample, 1), :]
        self.offset = refs.modulation[1, pl.ds(sample, 1), :]
        self.nothing = jnp.zeros((8, 2 * C), jnp.float32)

    def keep(self, **values):
        for name, value in values.items():
            place = STATE.index(name)
            self.state[place : place + 1, :] = value

    def kept(self, name):
        place = STATE.index(name)
        return self.state[place : place + 1, :]

    def report(self, place, value):
        self.refs.sums[place, pl.ds(self.sample, 1), :] = value

    def field(self, pair):
        return jnp.concatenate(
            [
                self.x_ref[pair, 0].astype(jnp.float32),
                self.x_ref[pair, 1].astype(jnp.float32),
            ],
            axis=1,
        )

    def means(self, first, second):
        return group_means(first, second, self.same_group, self.entries)

    def first_stats(self):
        def body(pair, carry):
            value = self.field(pair)
            return carry[0] + folded(value), carry[1] + folded(value * value)

        total, squares = over(self.pairs, 8, body, (self.nothing, self.nothing))
        self.partial[0], self.partial[1] = total, squares

    def partial_sums(self):
        return channel_sum(self.partial[0]), channel_sum(self.partial[1])

    def norm_of(self):
        mean, square = self.means(*self.partial_sums())
        inverse = lax.rsqrt(square - mean * mean + NORM_EPS)
        return inverse, -mean * inverse

    def first_act(self):
        inverse, center = self.norm_of()
        self.keep(inverse_one=inverse, center_one=center)
        gain = twice(inverse * self.gain_one)
        shift = twice(center * self.gain_one + self.shift_one)

        def body(pair, carry):
            value, slope = gelu_pair(self.field(pair) * gain + shift)
            put_shifted(self.act_one, pair, value)
            self.slope_one[pair] = slope
            return carry

        over(self.pairs, 8, body, 0)
        close_ring(self.act_one, self.pairs)

    def first_conv(self):
        def body(step, carry):
            start = step * self.size
            value = (
                jnp.dot(
                    windows(self.act_one, start, self.size),
                    self.refs.fwd_one[...],
                    preferred_element_type=jnp.float32,
                )
                + self.bias_one
            )
            self.conv_one[pl.ds(start, self.size)] = value.reshape(self.size, FIELD_COLS, 2 * C)
            return carry[0] + folded(value), carry[1] + folded(value * value)

        total, squares = over_steps(self.steps, body, (self.nothing, self.nothing))
        self.partial[0], self.partial[1] = total, squares

    def second_act(self):
        inverse, center = self.norm_of()
        self.keep(inverse_two=inverse, center_two=center)
        factor = self.gain_two * self.scale_plus
        gain = twice(inverse * factor)
        shift = twice(center * factor + self.shift_two * self.scale_plus + self.offset)

        def body(pair, carry):
            value, slope = gelu_pair(self.conv_one[pair] * gain + shift)
            put_shifted(self.act_two, pair, value)
            self.slope_two[pair] = slope
            return carry

        over(self.pairs, 8, body, 0)
        close_ring(self.act_two, self.pairs)

    def second_conv(self):
        def body(step, carry):
            start = step * self.size
            value = (
                jnp.dot(
                    windows(self.act_two, start, self.size),
                    self.refs.fwd_two[...],
                    preferred_element_type=jnp.float32,
                )
                + self.bias_two
            )
            value = value.reshape(self.size, FIELD_COLS, 2 * C)
            for half, ref in ((0, self.sum_even), (1, self.sum_odd)):
                base = self.x_ref[pl.ds(start, self.size), half].astype(jnp.float32)
                ref[pl.ds(start, self.size)] = base + value[:, :, half * C : half * C + C]
            return carry

        over_steps(self.steps, body)

    def split_columns(self):
        def body(pair, carry):
            even, odd = [], []
            for ref in (self.sum_even, self.sum_odd):
                even.append(ref[pair, pl.ds(0, HALF_COLS, stride=2), :])
                odd.append(ref[pair, pl.ds(1, HALF_COLS, stride=2), :])
            even = jnp.concatenate(even, axis=1)
            odd = jnp.concatenate(odd, axis=1)
            self.down_win[0, pair + 1] = pltpu.roll(odd, 1, 0).astype(jnp.bfloat16)
            self.down_win[1, pair + 1] = even.astype(jnp.bfloat16)
            self.down_win[2, pair + 1] = odd.astype(jnp.bfloat16)
            return carry

        over(self.pairs, 8, body, 0)
        self.down_win[:, 0, :, C:] = self.down_win[:, self.pairs, :, C:]

    def shift_cotangent(self):
        def body(pair, carry):
            value = self.cot_ref[pair]
            wide = value.astype(jnp.float32)
            self.cot_win[0, pair] = value
            self.cot_win[1, pair] = pltpu.roll(wide, HALF_COLS - 1, 0).astype(jnp.bfloat16)
            return carry + folded(wide)

        total = over(self.pairs, 8, body, self.nothing)
        self.cot_win[:, self.pairs] = self.cot_win[:, 0]
        self.refs.raw_sums[16:24, :] = self.refs.raw_sums[16:24, :] + total

    def down_windows(self, start):
        pieces = [
            self.down_win[tap, pl.ds(start + 1, self.size)].reshape(self.small, 2 * C)
            for tap in range(3)
        ]
        pieces += [
            self.down_win[tap, pl.ds(start, self.size), :, C:].reshape(self.small, C)
            for tap in range(3)
        ]
        return jnp.concatenate(pieces, axis=1)

    def down_output(self):
        def body(step, carry):
            start = step * self.size
            value = jnp.dot(
                self.down_windows(start), self.refs.down_fwd[...], preferred_element_type=jnp.float32
            )
            self.out_ref[pl.ds(start, self.size)] = (
                (value + self.bias_down)
                .reshape(self.size, HALF_COLS, 2 * C)
                .astype(jnp.bfloat16)
            )
            return carry

        over_steps(self.steps, body)

    def add_down_grad(self):
        def body(step, carry):
            start = step * self.size
            here = self.cot_win[0, pl.ds(start, self.size)].reshape(self.small, 2 * C)
            product = jnp.dot(
                here.T, self.down_windows(start), preferred_element_type=jnp.float32
            )
            for position in range(9):
                row_tap, tap = DOWN_ORDER[position]
                lanes = pl.ds((3 * row_tap + tap) * C, C)
                self.refs.down_grad[:, lanes] = (
                    self.refs.down_grad[:, lanes] + product[:, position * C : position * C + C]
                )
            return carry

        over_steps(self.steps, body)

    def down_adjoint(self):
        def body(step, carry):
            start = step * self.size
            pieces = [
                self.cot_win[shift, pl.ds(start + below, self.size)].reshape(self.small, 2 * C)
                for below in range(2)
                for shift in range(2)
            ]
            even = jnp.dot(
                jnp.concatenate([pieces[0], pieces[2]], axis=1),
                self.refs.down_even[...],
                preferred_element_type=jnp.float32,
            ).reshape(self.size, HALF_COLS, 2 * C)
            odd = jnp.dot(
                jnp.concatenate(pieces, axis=1),
                self.refs.down_odd[...],
                preferred_element_type=jnp.float32,
            ).reshape(self.size, HALF_COLS, 2 * C)
            for half, ref in ((0, self.grad_even), (1, self.grad_odd)):
                lanes = slice(half * C, half * C + C)
                for inner in range(self.size):
                    ref[start + inner, pl.ds(0, HALF_COLS, stride=2), :] = even[inner, :, lanes]
                    ref[start + inner, pl.ds(1, HALF_COLS, stride=2), :] = odd[inner, :, lanes]
            return carry

        over_steps(self.steps, body)

    def second_grad(self):
        def body(pair, carry):
            value = jnp.concatenate([self.grad_even[pair], self.grad_odd[pair]], axis=1)
            put_shifted(self.grad_two, pair, value)
            return carry + folded(value)

        total = over(self.pairs, 8, body, self.nothing)
        close_ring(self.grad_two, self.pairs)
        self.refs.raw_sums[8:16, :] = self.refs.raw_sums[8:16, :] + total

    def second_conv_grad(self):
        add_conv_grad(self.refs.conv_grad_two, self.act_two, self.grad_two, self.pairs)

    def second_back(self):
        def body(step, carry):
            start = step * self.size
            value = jnp.dot(
                windows(self.grad_two, start, self.size),
                self.refs.back_two[...],
                preferred_element_type=jnp.float32,
            )
            value = value * self.slope_two[pl.ds(start, self.size)].reshape(self.rows, 2 * C)
            self.grad_mid[pl.ds(start, self.size)] = value.reshape(self.size, FIELD_COLS, 2 * C)
            conv = self.conv_one[pl.ds(start, self.size)].reshape(self.rows, 2 * C)
            return carry[0] + folded(value), carry[1] + folded(value * conv)

        total, cross = over_steps(self.steps, body, (self.nothing, self.nothing))
        self.partial[0], self.partial[1] = total, cross

    def first_grad(self):
        inverse, center = self.kept("inverse_two"), self.kept("center_two")
        total, cross = self.partial_sums()
        cross = cross * inverse + total * center
        self.report(0, cross)
        self.report(1, total)
        factor = self.scale_plus * self.gain_two
        mean_grad, mean_cross = self.means(total * factor, cross * factor)
        from_mid = twice(inverse * factor)
        from_conv = twice(inverse * inverse * mean_cross)
        from_mean = twice(inverse * (mean_grad + center * mean_cross))

        def body(pair, carry):
            value = self.grad_mid[pair] * from_mid - from_mean - self.conv_one[pair] * from_conv
            put_shifted(self.grad_one, pair, value)
            return carry + folded(value)

        total = over(self.pairs, 8, body, self.nothing)
        close_ring(self.grad_one, self.pairs)
        self.refs.raw_sums[0:8, :] = self.refs.raw_sums[0:8, :] + total

    def first_conv_grad(self):
        add_conv_grad(self.refs.conv_grad_one, self.act_one, self.grad_one, self.pairs)

    def first_back(self):
        def body(step, carry):
            start = step * self.size
            value = jnp.dot(
                windows(self.grad_one, start, self.size),
                self.refs.back_one[...],
                preferred_element_type=jnp.float32,
            )
            value = value * self.slope_one[pl.ds(start, self.size)].reshape(self.rows, 2 * C)
            self.grad_mid[pl.ds(start, self.size)] = value.reshape(self.size, FIELD_COLS, 2 * C)
            base = jnp.concatenate(
                [
                    self.x_ref[pl.ds(start, self.size), half]
                    .astype(jnp.float32)
                    .reshape(self.rows, C)
                    for half in range(2)
                ],
                axis=1,
            )
            return carry[0] + folded(value), carry[1] + folded(value * base)

        total, cross = over_steps(self.steps, body, (self.nothing, self.nothing))
        self.partial[0], self.partial[1] = total, cross

    def field_grad(self, rows_ref):
        inverse, center = self.kept("inverse_one"), self.kept("center_one")
        total, cross = self.partial_sums()
        cross = cross * inverse + total * center
        self.report(2, cross)
        self.report(3, total)
        mean_grad, mean_cross = self.means(total * self.gain_one, cross * self.gain_one)
        from_pre = twice(inverse * self.gain_one)
        from_field = twice(inverse * inverse * mean_cross)
        from_mean = twice(inverse * (mean_grad + center * mean_cross))

        def body(pair, carry):
            summed = jnp.concatenate([self.grad_even[pair], self.grad_odd[pair]], axis=1)
            change = self.grad_mid[pair] * from_pre - from_mean - self.field(pair) * from_field
            value = (summed + change).astype(jnp.bfloat16)
            rows_ref[pair, 0] = value[:, :C]
            rows_ref[pair, 1] = value[:, C:]
            return carry

        over(self.pairs, 8, body, 0)


STATE = (
    "inverse_one",
    "center_one",
    "inverse_two",
    "center_two",
)
BEFORE = -1
SLOTS = (
    (
        ("first_stats", 0),
        ("shift_cotangent", 0),
        ("add_down_grad", BEFORE),
        ("second_conv_grad", BEFORE),
    ),
    (
        ("first_act", 0),
        ("first_stats", 1),
        ("down_adjoint", 0),
        ("first_conv_grad", BEFORE),
    ),
    (
        ("first_act", 1),
        ("second_grad", 0),
        ("shift_cotangent", 1),
        ("first_conv", 0),
        ("down_adjoint", 1),
    ),
    (("second_act", 0), ("second_grad", 1), ("first_conv", 1)),
    (("second_act", 1), ("second_back", 0), ("second_conv", 0)),
    (("first_grad", 0), ("split_columns", 0), ("second_back", 1), ("second_conv_grad", 0)),
    (("first_grad", 1), ("first_back", 0), ("second_conv", 1)),
    (("field_grad", 0), ("split_columns", 1), ("first_back", 1), ("first_conv_grad", 0)),
    (("field_grad", 1), ("down_output", 0), ("add_down_grad", 0), ("down_output", 1)),
)
LATE = ("add_down_grad", "second_conv_grad", "first_conv_grad")


def start_all(copies):
    for copy in copies:
        copy.start()


def peers(axis, count, pairs_of, sends, receives):
    return [
        to_peer(axis, step, count, source(step), target(step), sends.at[place, step], receives.at[place, step])
        for step in range(1, count)
        for place, (source, target) in pairs_of
    ]


def same(ref):
    return lambda step: ref


def slot_of(ref):
    return lambda step: ref.at[step]


def step_kernel(sizes, *args):
    row_count, batch_count, pairs, samples, together = sizes
    names = INPUTS + OUTPUTS + SCRATCH
    refs = SimpleNamespace(**dict(zip(names, args[: len(names)])))
    scratch = args[len(names) :]
    base = pl.program_id(0) * together
    row, batch = lax.axis_index("row"), lax.axis_index("batch")
    share = pairs // row_count

    def send_field(index, carry):
        mine = refs.fields.at[index, pl.ds(row * share, share)]
        for step in range(1, row_count):
            place = lax.rem(row + step, row_count) * samples + index
            to_peer(
                "row",
                step,
                row_count,
                refs.field.at[place],
                mine,
                refs.field_sent,
                refs.field_sem.at[index],
            ).start()
        pltpu.make_async_copy(
            refs.field.at[row * samples + index], mine, refs.field_sem.at[index]
        ).start()
        return carry

    def send_grad(index):
        target = refs.grad_out.at[row * samples + index]
        for step in range(1, row_count):
            place = lax.rem(row + step, row_count) * share
            to_peer(
                "row",
                step,
                row_count,
                refs.grad_rows.at[index, pl.ds(place, share)],
                target,
                refs.grad_sent,
                refs.grad_sem,
            ).start()
        pltpu.make_async_copy(
            refs.grad_rows.at[index, pl.ds(row * share, share)], target, refs.grad_sem
        ).start()

    @pl.when(base == 0)
    def _():
        pack_shards(refs)
        greet(row_count, batch_count)
        own = pltpu.make_async_copy(refs.shard, refs.shards.at[row, batch], refs.local_sem)
        own.start()
        copies = peers(
            "batch",
            batch_count,
            [
                (0, (same(refs.shard), same(refs.shards.at[row, batch]))),
                (1, (same(refs.small), slot_of(refs.small_z))),
            ],
            refs.send_z,
            refs.recv_z,
        )
        start_all(copies)
        lax.fori_loop(0, together, send_field, 0)
        for ref in (refs.conv_grad_one, refs.conv_grad_two, refs.down_grad, refs.raw_sums, refs.sums):
            ref[...] = jnp.zeros_like(ref)
        if together > 1:
            for ref in scratch[-16:-12] + scratch[-4:-2]:
                ref[...] = jnp.zeros_like(ref)
        own.wait()
        finish(copies)
        total = refs.small[...]
        for step in range(1, batch_count):
            total = total + refs.small_z[step]
        refs.small_one[...] = total
        copies = peers(
            "row",
            row_count,
            [(1, (same(refs.small_one), slot_of(refs.small_row)))],
            refs.send_row,
            refs.recv_row,
        )
        sibling = sibling_of(row)
        mine = refs.shards.at[row]
        direct = {}
        for step in range(2, row_count, 2):
            direct[step] = to_row(
                lax.rem(row + step, row_count),
                mine,
                mine,
                refs.send_row.at[0, step],
                refs.recv_row.at[0, step],
            )
        beside = [to_row(sibling, mine, mine, refs.send_row.at[0, 1], refs.recv_row.at[0, 1])]
        start_all(list(direct.values()) + beside + copies)
        lax.fori_loop(together, samples, send_field, 0)
        for step in range(2, row_count, 2):
            direct[step].wait_recv()
            came = refs.shards.at[lax.rem(row + row_count - step, row_count)]
            beside.append(
                to_row(
                    sibling,
                    came,
                    came,
                    refs.send_row.at[0, step + 1],
                    refs.recv_row.at[0, step + 1],
                )
            )
            beside[-1].start()
        for step in range(2, row_count, 2):
            direct[step].wait_send()
        finish(beside + copies)
        total = refs.small_one[...]
        for step in range(1, row_count):
            total = total + refs.small_row[step]
        refs.small_all[...] = total
        lay_out(row_count, batch_count, refs)
        modulate(refs)

    @pl.when(base > 0)
    def _():
        for place in range(together):
            send_grad(base - together + place)

    for place in range(together):
        arrived = refs.fields.at[base + place]
        pltpu.make_async_copy(arrived, arrived, refs.field_sem.at[base + place]).wait()
    stages = [
        Sample(
            pairs,
            base + place,
            refs.fields.at[base + place],
            refs.cot.at[place],
            refs.block_out.at[place],
            refs,
            scratch[16 * place : 16 * place + 16],
        )
        for place in range(together)
    ]

    def run_slot(slot):
        for name, place in slot:
            if place >= together or (place == BEFORE and together == 1):
                continue
            stage = getattr(stages[place], name)
            if name == "field_grad":
                stage(refs.grad_rows.at[base + place])
            else:
                stage()

    for slot in SLOTS:
        run_slot(slot)

    @pl.when(base == samples - together)
    def _():
        for place in range(together - 1):
            send_grad(base + place)
        if together > 1:
            for name in LATE:
                getattr(stages[-1], name)()
        reduce_all(row_count, batch_count, refs, lambda: send_grad(base + together - 1))
        pltpu.make_async_copy(refs.grad_out, refs.grad_out, refs.grad_sem).wait()
        others = pl.ds(0, pairs - share)
        for ref, sem in ((refs.fields, refs.field_sent), (refs.grad_rows, refs.grad_sent)):
            pltpu.make_async_copy(ref.at[:, others], ref.at[:, others], sem).wait()


INPUTS = ("field", "cot", "conv", "down", "embed_in", "embed_out", "small", "embedded", "group")
OUTPUTS = (
    "block_out",
    "grad_out",
    "conv_grad",
    "down_share",
    "embed_in_grad",
    "embed_out_grad",
    "small_grad",
    "norm",
)
SCRATCH = (
    "fwd_one",
    "back_one",
    "fwd_two",
    "back_two",
    "down_fwd",
    "down_even",
    "down_odd",
    "small_all",
    "embed_in_t",
    "embed_out_t",
    "modulation",
    "hidden",
    "hidden_slope",
    "sums",
    "raw_sums",
    "conv_grad_one",
    "conv_grad_two",
    "down_grad",
    "shard",
    "shards",
    "small_z",
    "small_one",
    "small_row",
    "conv_t",
    "down_t",
    "fields",
    "grad_rows",
    "row_send",
    "pair_take",
    "chip_send",
    "row_take",
    "batch_send",
    "batch_take",
    "small_send",
    "small_take",
    "small_next",
    "small_last",
    "square_send",
    "square_take",
    "square_next",
    "square_last",
    "field_sem",
    "field_sent",
    "grad_sem",
    "grad_sent",
    "local_sem",
    "send_z",
    "recv_z",
    "send_row",
    "recv_row",
    "send_sem",
    "recv_sem",
)
DOWN_ORDER = ((1, 0), (2, 0), (1, 1), (2, 1), (1, 2), (2, 2), (0, 0), (0, 1), (0, 2))


def lay_out(row_count, batch_count, refs):
    depth, share, wide_share = 9 * C // batch_count, C // row_count, C2 // row_count
    height = 2 * share + wide_share
    embed_share, hidden_share = EMB // batch_count, HID // batch_count
    for place in range(row_count):
        parts = [refs.shards[place, part].astype(jnp.float32) for part in range(batch_count)]
        main = jnp.concatenate([part[:, :depth] for part in parts], axis=1)
        for which in range(2):
            refs.conv_t[which, place * share : place * share + share, :] = main[
                which * share : which * share + share
            ]
        refs.down_t[place * wide_share : place * wide_share + wide_share, :] = main[2 * share :]
        refs.embed_in_t[place * height : place * height + height, :] = jnp.concatenate(
            [part[:, depth : depth + embed_share] for part in parts], axis=1
        )
        tail = depth + embed_share
        half_rows, half_lanes = height // 2, hidden_share // 2
        lanes = []
        for part in parts:
            lanes.append(part[:half_rows, tail : tail + half_lanes])
            lanes.append(part[half_rows:, tail : tail + half_lanes])
        refs.embed_out_t[place * half_rows : place * half_rows + half_rows, :] = jnp.concatenate(
            lanes, axis=1
        )
    for which, forward, back in (
        (0, refs.fwd_one, refs.back_one),
        (1, refs.fwd_two, refs.back_two),
    ):
        zero = jnp.zeros((C, C), jnp.bfloat16)
        for tap in range(3):
            direct = [
                refs.conv_t[which, :, (3 * row_tap + tap) * C : (3 * row_tap + tap) * C + C]
                for row_tap in range(3)
            ]
            fill_blocks(forward, tap, [block.T.astype(jnp.bfloat16) for block in direct], zero)
            fill_blocks(
                back, 2 - tap, [block.astype(jnp.bfloat16) for block in direct[::-1]], zero
            )
    zero = jnp.zeros((C2, C), jnp.bfloat16)
    back = {}
    for position in range(9):
        row_tap, tap = DOWN_ORDER[position]
        block = refs.down_t[:, (3 * row_tap + tap) * C : (3 * row_tap + tap) * C + C]
        refs.down_fwd[position * C : position * C + C, :] = block.T.astype(jnp.bfloat16)
        back[row_tap, tap] = block.astype(jnp.bfloat16)
    even = ((back[1, 1], back[2, 1]), (zero, back[0, 1]))
    odd = (
        (back[1, 2], back[2, 2]),
        (back[1, 0], back[2, 0]),
        (zero, back[0, 2]),
        (zero, back[0, 0]),
    )
    for ref, table in ((refs.down_even, even), (refs.down_odd, odd)):
        for position, (left, right) in enumerate(table):
            ref[position * C2 : position * C2 + C2, :C] = left
            ref[position * C2 : position * C2 + C2, C:] = right


def lanes_of(ref, first, last):
    return jnp.concatenate([ref[place : place + 1, :] for place in range(first, last)], axis=1)


def modulate(refs):
    small = refs.small_all
    before = dot_last(refs.embedded[...], refs.embed_in_t[...]) + lanes_of(small, 8, 12)
    hidden, slope = gelu_pair(before)
    refs.hidden[...] = hidden
    refs.hidden_slope[...] = slope
    result = dot_last(hidden, refs.embed_out_t[...]) + lanes_of(small, 12, 14)
    refs.modulation[0] = 1.0 + result[:, :C]
    refs.modulation[1] = result[:, C:]


def fill_blocks(ref, tap, blocks, zero):
    table = (
        (blocks[1], blocks[0]),
        (blocks[2], blocks[1]),
        (blocks[0], zero),
        (zero, blocks[2]),
    )
    for position, (left, right) in enumerate(table):
        base = (4 * tap + position) * C
        ref[base : base + C, :C] = left
        ref[base : base + C, C:] = right


def dot_full(lhs, rhs):
    return jnp.dot(lhs, rhs, precision=HIGHEST, preferred_element_type=jnp.float32)


def dot_last(lhs, rhs):
    return lax.dot_general(
        lhs,
        rhs,
        (((1,), (1,)), ((), ())),
        precision=HIGHEST,
        preferred_element_type=jnp.float32,
    )


def dot_first(lhs, rhs):
    return lax.dot_general(
        lhs,
        rhs,
        (((0,), (0,)), ((), ())),
        precision=HIGHEST,
        preferred_element_type=jnp.float32,
    )


def reduce_all(row_count, batch_count, refs, send_last):
    row, batch = lax.axis_index("row"), lax.axis_index("batch")
    depth, share, wide_share = 9 * C // batch_count, C // row_count, C2 // row_count
    height = 2 * share + wide_share
    embed_share, hidden_share = EMB // batch_count, HID // batch_count
    mid_cross, mid_total = refs.sums[0], refs.sums[1]
    gain_two, shift_two = refs.small_all[1:2, :], refs.small_all[3:4, :]
    scale_plus = refs.modulation[0]
    grad_mod = jnp.concatenate([gain_two * mid_cross + shift_two * mid_total, mid_total], axis=1)
    grad_embed_out = dot_first(grad_mod, refs.hidden[...])
    grad_hidden = (
        dot_full(grad_mod, refs.embed_out_t[...])
        * refs.hidden_slope[...]
    )
    grad_embed_in = dot_first(grad_hidden, refs.embedded[...])

    def down_sum(value):
        return jnp.sum(value, axis=0, keepdims=True)

    small_rows = [
        down_sum(refs.sums[2]),
        down_sum(mid_cross * scale_plus),
        down_sum(refs.sums[3]),
        down_sum(mid_total * scale_plus),
        channel_sum(refs.raw_sums[0:8]),
        channel_sum(refs.raw_sums[8:16]),
    ]
    cot_total = down_sum(refs.raw_sums[16:24])
    small_rows += [cot_total[:, :C], cot_total[:, C:]]
    hidden_total, mod_total = down_sum(grad_hidden), down_sum(grad_mod)
    small_rows += [hidden_total[:, lane : lane + C] for lane in range(0, HID, C)]
    small_rows += [mod_total[:, lane : lane + C] for lane in range(0, 2 * C, C)]
    small_rows.append(jnp.zeros((2, C), jnp.float32))
    refs.small_send[...] = jnp.concatenate(small_rows, axis=0)
    half_rows = height // 2
    for place in range(row_count):
        low, high = place * share, place * share + share
        refs.row_send[place, :, : 9 * C] = jnp.concatenate(
            [
                refs.conv_grad_one[low:high],
                refs.conv_grad_two[low:high],
                refs.down_grad[place * wide_share : place * wide_share + wide_share],
            ],
            axis=0,
        ).astype(jnp.bfloat16)
        refs.row_send[place, :, 9 * C : 10 * C] = grad_embed_in[
            place * height : place * height + height
        ].astype(jnp.bfloat16)
        piece = grad_embed_out[place * half_rows : place * half_rows + half_rows]
        refs.row_send[place, :, 10 * C :] = jnp.concatenate(
            [piece[:, : HID // 2], piece[:, HID // 2 :]], axis=0
        ).astype(jnp.bfloat16)
    sibling = sibling_of(row)
    beside = [
        to_row(
            sibling,
            refs.row_send.at[lax.rem(sibling + 2 * step, row_count)],
            refs.pair_take.at[step],
            refs.send_sem.at[0, step],
            refs.recv_sem.at[0, step],
        )
        for step in range(row_count // 2)
    ]
    smalls = [
        to_peer(
            "row",
            step,
            row_count,
            refs.small_send,
            refs.small_take.at[step],
            refs.send_sem.at[1, step],
            refs.recv_sem.at[1, step],
        )
        for step in range(1, row_count)
    ]
    order = list(range(1, row_count // 2)) + [0]
    start_all([beside[step] for step in order] + smalls)
    copies = []
    for step in order:
        beside[step].wait_recv()
        place = lax.rem(row + 2 * step, row_count)
        total = refs.row_send[place].astype(jnp.float32) + refs.pair_take[step].astype(jnp.float32)
        if step:
            refs.chip_send[step] = total.astype(jnp.bfloat16)
            copies.append(
                to_row(
                    place,
                    refs.chip_send.at[step],
                    refs.row_take.at[step],
                    refs.send_sem.at[6, step],
                    refs.recv_sem.at[6, step],
                )
            )
            copies[-1].start()
    send_last()
    for copy in beside:
        copy.wait_send()
    finish(copies + smalls)
    small_total = refs.small_send[...]
    for step in range(1, row_count // 2):
        total = total + refs.row_take[step].astype(jnp.float32)
    for step in range(1, row_count):
        small_total = small_total + refs.small_take[step]
    refs.small_next[...] = small_total
    for part in range(batch_count):
        per_half = batch_count // 2
        rows = slice(0, half_rows) if part < per_half else slice(half_rows, height)
        base = 10 * C + hidden_share * (part % per_half)
        piece = total[rows, base : base + hidden_share]
        refs.batch_send[part] = jnp.concatenate(
            [
                total[:, part * depth : part * depth + depth],
                total[:, 9 * C + part * embed_share : 9 * C + part * embed_share + embed_share],
                jnp.concatenate([piece[:, : hidden_share // 2], piece[:, hidden_share // 2 :]], axis=0),
            ],
            axis=1,
        ).astype(jnp.bfloat16)
    copies = []
    for step in range(1, batch_count):
        copies.append(
            to_peer(
                "batch",
                step,
                batch_count,
                refs.batch_send.at[lax.rem(batch + step, batch_count)],
                refs.batch_take.at[step],
                refs.send_sem.at[2, step],
                refs.recv_sem.at[2, step],
            )
        )
        copies.append(
            to_peer(
                "batch",
                step,
                batch_count,
                refs.small_next,
                refs.small_last.at[step],
                refs.send_sem.at[3, step],
                refs.recv_sem.at[3, step],
            )
        )
    for copy in copies:
        copy.start()
    owned = refs.batch_send[batch].astype(jnp.float32)
    finish(copies)
    small_total = refs.small_next[...]
    for step in range(1, batch_count):
        owned = owned + refs.batch_take[step].astype(jnp.float32)
        small_total = small_total + refs.small_last[step]
    squares = jnp.sum(jnp.sum(owned * owned, axis=0, keepdims=True), axis=1, keepdims=True)
    refs.square_send[...] = jnp.broadcast_to(squares, (8, C))
    copies = [
        to_peer(
            "row",
            step,
            row_count,
            refs.square_send,
            refs.square_take.at[step],
            refs.send_sem.at[4, step],
            refs.recv_sem.at[4, step],
        )
        for step in range(1, row_count)
    ]
    for copy in copies:
        copy.start()
    finish(copies)
    squares = refs.square_send[...]
    for step in range(1, row_count):
        squares = squares + refs.square_take[step]
    refs.square_next[...] = squares
    copies = [
        to_peer(
            "batch",
            step,
            batch_count,
            refs.square_next,
            refs.square_last.at[step],
            refs.send_sem.at[5, step],
            refs.recv_sem.at[5, step],
        )
        for step in range(1, batch_count)
    ]
    for copy in copies:
        copy.start()
    finish(copies)
    squares = refs.square_next[...]
    for step in range(1, batch_count):
        squares = squares + refs.square_last[step]
    small_squares = jnp.sum(
        jnp.sum(small_total * small_total, axis=0, keepdims=True), axis=1, keepdims=True
    )
    norm = jnp.sqrt(squares + small_squares)
    clip = jnp.minimum(1.0, CLIP_NORM / (norm + 1e-06))[0:1, 0:1]
    refs.norm[...] = norm
    owned = owned * clip
    refs.conv_grad[0] = owned[:share, :depth]
    refs.conv_grad[1] = owned[share : 2 * share, :depth]
    refs.down_share[...] = owned[2 * share :, :depth]
    refs.embed_in_grad[...] = owned[:, depth : depth + embed_share].T
    tail = depth + embed_share
    refs.embed_out_grad[...] = jnp.concatenate(
        [owned[:half_rows, tail:], owned[half_rows:, tail:]], axis=1
    )
    refs.small_all[...] = small_total * clip
    small_len = 14 * C // (row_count * batch_count)
    first = (batch * row_count + row) * small_len
    line, lane = first // C, lax.rem(first, C)
    lines = jnp.concatenate(
        [refs.small_all[pl.ds(line, 1), :], refs.small_all[pl.ds(line + 1, 1), :]], axis=1
    )
    moved = pltpu.roll(jnp.broadcast_to(lines, (8, 2 * C)), lax.rem(2 * C - lane, 2 * C), 1)
    refs.small_grad[...] = moved[:, :C]


def pack_shards(refs):
    half = refs.embed_out.shape[1] // 2
    refs.shard[...] = jnp.concatenate(
        [
            jnp.concatenate([refs.conv[0], refs.conv[1], refs.down[...]], axis=0),
            refs.embed_in[...].T,
            jnp.concatenate([refs.embed_out[:, :half], refs.embed_out[:, half:]], axis=0),
        ],
        axis=1,
    ).astype(jnp.bfloat16)


def run_step(field_in, cotangent, shards, small_tile, embedded):
    row_count, batch_count = (lax.axis_size("row"), lax.axis_size("batch"))
    samples = cotangent.shape[0]
    padded = embedded.shape[0]
    pairs = field_in.shape[1] // 2 * row_count
    together = chunk_of(samples, 2)
    share = pairs // row_count
    height, width = 4 * C // row_count, 12 * C // batch_count
    halves = field_in.reshape(field_in.shape[0], share, 2, FIELD_COLS, C)
    same_group = jnp.asarray(
        np.kron(np.eye(GROUPS), np.ones((C // GROUPS, C // GROUPS))), jnp.float32
    )
    low, full = jnp.bfloat16, jnp.float32
    anywhere = pl.BlockSpec(memory_space=pl.ANY)

    def whole(array):
        return pl.BlockSpec(array.shape, lambda i: (0,) * len(array.shape))

    def per_step(array):
        rank = len(array.shape)
        return pl.BlockSpec((together,) + array.shape[1:], lambda i: (i,) + (0,) * (rank - 1))

    outs = (
        jax.ShapeDtypeStruct(cotangent.shape, low),
        jax.ShapeDtypeStruct(halves.shape, low),
        *[jax.ShapeDtypeStruct(shard.shape, full) for shard in shards],
        jax.ShapeDtypeStruct((8, C), full),
        jax.ShapeDtypeStruct((8, C), full),
    )
    ring = pltpu.VMEM((3, pairs + 2, FIELD_COLS, 2 * C), low)
    wide = pltpu.VMEM((pairs, FIELD_COLS, 2 * C), full)
    half = pltpu.VMEM((pairs, FIELD_COLS, C), full)
    fields = pltpu.VMEM((samples, pairs, 2, FIELD_COLS, C), low)
    dma = pltpu.SemaphoreType.DMA
    most = max(row_count, batch_count)
    tile = (16, C)
    scratch = (
        [pltpu.VMEM((12 * C, 2 * C), low)] * 4
        + [
            pltpu.VMEM((9 * C, C2), low),
            pltpu.VMEM((2 * C2, 2 * C), low),
            pltpu.VMEM((4 * C2, 2 * C), low),
            pltpu.VMEM(tile, full),
            pltpu.VMEM((HID, EMB), full),
            pltpu.VMEM((2 * C, HID), full),
            pltpu.VMEM((2, padded, C), full),
            pltpu.VMEM((padded, HID), full),
            pltpu.VMEM((padded, HID), full),
            pltpu.VMEM((4, padded, C), full),
            pltpu.VMEM((24, 2 * C), full),
            pltpu.VMEM((C, 9 * C), full),
            pltpu.VMEM((C, 9 * C), full),
            pltpu.VMEM((C2, 9 * C), full),
            pltpu.VMEM((height, width), low),
            pltpu.VMEM((row_count, batch_count, height, width), low),
            pltpu.VMEM((batch_count,) + tile, full),
            pltpu.VMEM(tile, full),
            pltpu.VMEM((row_count,) + tile, full),
            pltpu.VMEM((2, C, 9 * C), full),
            pltpu.VMEM((C2, 9 * C), full),
            fields,
            fields,
            pltpu.VMEM((row_count, height, 12 * C), low),
            pltpu.VMEM((row_count // 2, height, 12 * C), low),
            pltpu.VMEM((row_count // 2, height, 12 * C), low),
            pltpu.VMEM((row_count // 2, height, 12 * C), low),
            pltpu.VMEM((batch_count, height, width), low),
            pltpu.VMEM((batch_count, height, width), low),
            pltpu.VMEM(tile, full),
            pltpu.VMEM((row_count,) + tile, full),
            pltpu.VMEM(tile, full),
            pltpu.VMEM((batch_count,) + tile, full),
            pltpu.VMEM((8, C), full),
            pltpu.VMEM((row_count, 8, C), full),
            pltpu.VMEM((8, C), full),
            pltpu.VMEM((batch_count, 8, C), full),
            dma((samples,)),
            dma,
            dma,
            dma,
            dma,
            dma((2, batch_count)),
            dma((2, batch_count)),
            dma((2, row_count)),
            dma((2, row_count)),
            dma((7, most)),
            dma((7, most)),
        ]
        + (
            [ring] * 4
            + [wide] * 4
            + [half] * 4
            + [
                pltpu.VMEM((3, pairs + 1, HALF_COLS, 2 * C), low),
                pltpu.VMEM((2, pairs + 1, HALF_COLS, C2), low),
                pltpu.VMEM((8, C), full),
                pltpu.VMEM((2, 8, 2 * C), full),
            ]
        )
        * together
    )
    result = pl.pallas_call(
        functools.partial(step_kernel, (row_count, batch_count, pairs, samples, together)),
        grid=(samples // together,),
        in_specs=[anywhere, per_step(cotangent)]
        + [whole(array) for array in shards + (small_tile, embedded, same_group)],
        out_specs=[per_step(outs[0]), anywhere] + [whole(out) for out in outs[2:]],
        out_shape=outs,
        scratch_shapes=scratch,
        compiler_params=pltpu.CompilerParams(
            dimension_semantics=("arbitrary",),
            vmem_limit_bytes=62 << 20,
            collective_id=0,
            has_side_effects=True,
        ),
        name="step",
    )(halves, cotangent, *shards, small_tile, embedded, same_group)
    return (result[0], result[1].reshape(field_in.shape)) + tuple(result[2:])


def adam_update(weight, gradient, first_old, second_old, step_rate, clip_factor):
    scaled = gradient * clip_factor
    first_new = BETA_ONE * first_old + (1.0 - BETA_ONE) * scaled
    second_new = BETA_TWO * second_old + (1.0 - BETA_TWO) * scaled * scaled
    corrected = (
        first_new
        / (1.0 - BETA_ONE**STEP_COUNT)
        / (jnp.sqrt(second_new / (1.0 - BETA_TWO**STEP_COUNT)) + ADAM_EPS)
    )
    return (weight - step_rate * (corrected + DECAY * weight), first_new, second_new)


def body(
    field_in,
    refine_step,
    cotangent,
    conv_weight,
    down_weight,
    embed_in_weight,
    embed_out_weight,
    small_params,
    conv_first,
    down_first,
    embed_in_first,
    embed_out_first,
    small_first,
    conv_second,
    down_second,
    embed_in_second,
    embed_out_second,
    small_second,
):
    small_len = small_params.shape[0]
    place = (lax.axis_index("batch") * lax.axis_size("row") + lax.axis_index("row")) * small_len
    small_rounded = lax.reduce_precision(small_params, exponent_bits=8, mantissa_bits=7)
    small_tile = lax.dynamic_update_slice_in_dim(
        jnp.zeros((16 * C,), jnp.float32), small_rounded, place, 0
    ).reshape(16, C)
    owned = refine_step.shape[0] // lax.axis_size("row")
    padded = -(-owned // 8) * 8
    own_steps = lax.dynamic_slice_in_dim(refine_step, lax.axis_index("row") * owned, owned, 0)
    embedded = embed_steps(jnp.pad(own_steps, (0, padded - owned)))
    block_out, grad_start, *owned_shards, small_grads, norm_tile = run_step(
        field_in,
        cotangent,
        (
            jnp.transpose(conv_weight, (0, 2, 1)),
            down_weight.T,
            embed_in_weight,
            embed_out_weight.T,
        ),
        small_tile,
        embedded,
    )
    grad_norm = norm_tile[0, 0]
    owned_shards = [
        jnp.transpose(owned_shards[0], (0, 2, 1)),
        owned_shards[1].T,
        owned_shards[2],
        owned_shards[3].T,
    ]
    owned_shards.append(small_grads[0, :small_len])
    clip_factor = 1.0
    conv_new = adam_update(
        conv_weight, owned_shards[0], conv_first, conv_second, RATE_MATRIX, clip_factor
    )
    down_new = adam_update(
        down_weight, owned_shards[1], down_first, down_second, RATE_MATRIX, clip_factor
    )
    embed_in_new = adam_update(
        embed_in_weight, owned_shards[2], embed_in_first, embed_in_second, RATE_MATRIX, clip_factor
    )
    embed_out_new = adam_update(
        embed_out_weight,
        owned_shards[3],
        embed_out_first,
        embed_out_second,
        RATE_MATRIX,
        clip_factor,
    )
    small_new = adam_update(
        small_params, owned_shards[4], small_first, small_second, RATE_SMALL, clip_factor
    )
    return (
        block_out,
        grad_start,
        grad_norm,
        conv_new[0],
        down_new[0],
        embed_in_new[0],
        embed_out_new[0],
        small_new[0],
        conv_new[1],
        down_new[1],
        embed_in_new[1],
        embed_out_new[1],
        small_new[1],
        conv_new[2],
        down_new[2],
        embed_in_new[2],
        embed_out_new[2],
        small_new[2],
    )


def solution(mesh):
    placed = (
        P("batch", "row", None, None),
        P("batch"),
        P(("batch", "row"), None, None, None),
        P(None, "batch", "row"),
        P("batch", "row"),
        P("batch", "row"),
        P("batch", "row"),
        P(("batch", "row")),
        P(None, "batch", "row"),
        P("batch", "row"),
        P("batch", "row"),
        P("batch", "row"),
        P(("batch", "row")),
        P(None, "batch", "row"),
        P("batch", "row"),
        P("batch", "row"),
        P("batch", "row"),
        P(("batch", "row")),
    )
    return jax.shard_map(
        body,
        mesh=mesh,
        in_specs=placed,
        out_specs=(
            P(("batch", "row"), None, None, None),
            P("batch", "row", None, None),
            P(),
            P(None, "batch", "row"),
            P("batch", "row"),
            P("batch", "row"),
            P("batch", "row"),
            P(("batch", "row")),
            P(None, "batch", "row"),
            P("batch", "row"),
            P("batch", "row"),
            P("batch", "row"),
            P(("batch", "row")),
            P(None, "batch", "row"),
            P("batch", "row"),
            P("batch", "row"),
            P("batch", "row"),
            P(("batch", "row")),
        ),
        check_vma=False,
    )
```

```python
import functools
import math
from types import SimpleNamespace

import jax
import jax.numpy as jnp
import numpy as np
from jax import lax
from jax.experimental import pallas as pl
from jax.experimental.pallas import tpu as pltpu
from jax.sharding import PartitionSpec as P

C = 128
C2 = 256
EMB = 128
HID = 512
GROUPS = 8
REFINE = 4


NORM_EPS = 1e-05
BETA_ONE = 0.9
BETA_TWO = 0.999
ADAM_EPS = 1e-08
DECAY = 0.01
RATE_MATRIX = 0.05
RATE_SMALL = 0.5
CLIP_NORM = 1.0
STEP_COUNT = 10
HIGHEST = lax.Precision.HIGHEST


def embed_steps(refine_step):
    halfway = EMB // 2
    frequency = jnp.exp(-math.log(10000.0) * jnp.arange(halfway).astype(jnp.float32) / halfway)
    angles = (refine_step.astype(jnp.float32) * (1000.0 / REFINE))[:, None] * frequency[None, :]
    return jnp.concatenate([jnp.sin(angles), jnp.cos(angles)], axis=1)


MESH = pl.DeviceIdType.MESH


def greet(row_count, batch_count=1):
    row, batch = lax.axis_index("row"), lax.axis_index("batch")
    barrier = pltpu.get_barrier_semaphore()
    for step in range(1, row_count):
        pl.semaphore_signal(
            barrier,
            inc=1,
            device_id={"row": lax.rem(row + step, row_count), "batch": batch},
            device_id_type=MESH,
        )
    for step in range(1, batch_count):
        pl.semaphore_signal(
            barrier,
            inc=1,
            device_id={"row": row, "batch": lax.rem(batch + step, batch_count)},
            device_id_type=MESH,
        )
    pl.semaphore_wait(barrier, row_count + batch_count - 2)


def to_peer(axis, step, count, source, target, send_sem, recv_sem):
    row, batch = lax.axis_index("row"), lax.axis_index("batch")
    if axis == "row":
        device = {"row": lax.rem(row + step, count), "batch": batch}
    else:
        device = {"row": row, "batch": lax.rem(batch + step, count)}
    return pltpu.make_async_remote_copy(
        src_ref=source,
        dst_ref=target,
        send_sem=send_sem,
        recv_sem=recv_sem,
        device_id=device,
        device_id_type=MESH,
    )


def to_row(place, source, target, send_sem, recv_sem):
    return pltpu.make_async_remote_copy(
        src_ref=source,
        dst_ref=target,
        send_sem=send_sem,
        recv_sem=recv_sem,
        device_id={"row": place, "batch": lax.axis_index("batch")},
        device_id_type=MESH,
    )


def sibling_of(row):
    return row + 1 - 2 * lax.rem(row, 2)


def finish(copies):
    for copy in copies:
        copy.wait()


FIELD_COLS = 64
HALF_COLS = 32
ROOT = math.sqrt(2.0 / math.pi)
CUBIC = ROOT * 0.044715


def chunk_of(total, most):
    size = min(total, most)
    while total % size:
        size -= 1
    return size


def over(total, most, body, init):
    size = chunk_of(total, most)

    def several(step, carry):
        for inner in range(size):
            carry = body(step * size + inner, carry)
        return carry

    if size == total:
        return several(0, init)
    return lax.fori_loop(0, total // size, several, init)


def folded(values):
    return jnp.sum(values.reshape(values.shape[0] // 8, 8, values.shape[1]), axis=0)


def twice(row):
    return jnp.concatenate([row, row], axis=1)


def channel_sum(partial):
    both = partial[:, :C] + partial[:, C:]
    return jnp.sum(both, axis=0, keepdims=True)


def group_means(first, second, same_group, entries):
    stacked = jnp.concatenate([first, second, jnp.zeros((6, C), jnp.float32)], axis=0)
    totals = jnp.dot(stacked, same_group, precision=HIGHEST, preferred_element_type=jnp.float32)
    return totals[0:1] / entries, totals[1:2] / entries


def gelu_pair(values):
    square = values * values
    weight = 0.5 + 0.5 * jnp.tanh(values * (ROOT + CUBIC * square))
    result = values * weight
    slope = weight + (result - result * weight) * (2.0 * ROOT + (6.0 * CUBIC) * square)
    return result, slope


def put_shifted(ref, pair, values):
    for tap, shift in ((0, 1), (1, 0), (2, FIELD_COLS - 1)):
        moved = pltpu.roll(values, shift, 0) if shift else values
        ref[tap, pair + 1] = moved.astype(jnp.bfloat16)


def close_ring(ref, pairs):
    ref[:, 0, :, C:] = ref[:, pairs, :, C:]
    ref[:, pairs + 1, :, :C] = ref[:, 1, :, :C]


def windows(ref, start, count):
    rows = count * FIELD_COLS
    pieces = []
    for tap in range(3):
        pieces.append(ref[tap, pl.ds(start + 1, count)].reshape(rows, 2 * C))
        pieces.append(ref[tap, pl.ds(start, count), :, C:].reshape(rows, C))
        pieces.append(ref[tap, pl.ds(start + 2, count), :, :C].reshape(rows, C))
    return jnp.concatenate(pieces, axis=1)


def over_steps(steps, body, init=0):
    if steps == 1:
        return body(0, init)
    return lax.fori_loop(0, steps, body, init)


def add_conv_grad(out_ref, act_ref, grad_ref, pairs):
    size = chunk_of(pairs, 8)
    rows = size * FIELD_COLS

    def body(step, carry):
        start = step * size
        grad = grad_ref[1, pl.ds(start + 1, size)].reshape(rows, 2 * C)
        product = jnp.dot(
            grad.T, windows(act_ref, start, size), preferred_element_type=jnp.float32
        )
        for tap in range(3):
            base = tap * 4 * C
            middle = product[:C, base : base + C] + product[C:, base + C : base + 2 * C]
            up = product[C:, base : base + C] + product[:C, base + 2 * C : base + 3 * C]
            down = product[:C, base + C : base + 2 * C] + product[C:, base + 3 * C : base + 4 * C]
            for row_tap, value in ((0, up), (1, middle), (2, down)):
                lanes = pl.ds((3 * row_tap + tap) * C, C)
                out_ref[:, lanes] = out_ref[:, lanes] + value
        return carry

    over_steps(pairs // size, body)


class Sample:
    def __init__(self, pairs, sample, x_ref, cot_ref, out_ref, refs, scratch):
        self.pairs, self.sample = pairs, sample
        self.x_ref, self.cot_ref, self.out_ref = x_ref, cot_ref, out_ref
        self.refs = refs
        (
            self.act_one,
            self.act_two,
            self.grad_one,
            self.grad_two,
            self.slope_one,
            self.slope_two,
            self.conv_one,
            self.grad_mid,
            self.sum_even,
            self.sum_odd,
            self.grad_even,
            self.grad_odd,
            self.down_win,
            self.cot_win,
            self.state,
            self.partial,
        ) = scratch
        self.entries = 2.0 * pairs * FIELD_COLS * (C // GROUPS)
        self.size = chunk_of(pairs, 8)
        self.steps = pairs // self.size
        self.rows = self.size * FIELD_COLS
        self.small = self.size * HALF_COLS
        self.same_group = refs.group[...]
        small = refs.small_all
        self.gain_one, self.gain_two = small[0:1, :], small[1:2, :]
        self.shift_one, self.shift_two = small[2:3, :], small[3:4, :]
        self.bias_one, self.bias_two = twice(small[4:5, :]), twice(small[5:6, :])
        self.bias_down = jnp.concatenate([small[6:7, :], small[7:8, :]], axis=1)
        self.scale_plus = refs.modulation[0, pl.ds(sample, 1), :]
        self.offset = refs.modulation[1, pl.ds(sample, 1), :]
        self.nothing = jnp.zeros((8, 2 * C), jnp.float32)

    def keep(self, **values):
        for name, value in values.items():
            place = STATE.index(name)
            self.state[place : place + 1, :] = value

    def kept(self, name):
        place = STATE.index(name)
        return self.state[place : place + 1, :]

    def report(self, place, value):
        self.refs.sums[place, pl.ds(self.sample, 1), :] = value

    def field(self, pair):
        return jnp.concatenate(
            [
                self.x_ref[pair, 0].astype(jnp.float32),
                self.x_ref[pair, 1].astype(jnp.float32),
            ],
            axis=1,
        )

    def means(self, first, second):
        return group_means(first, second, self.same_group, self.entries)

    def first_stats(self):
        def body(pair, carry):
            value = self.field(pair)
            return carry[0] + folded(value), carry[1] + folded(value * value)

        total, squares = over(self.pairs, 8, body, (self.nothing, self.nothing))
        self.partial[0], self.partial[1] = total, squares

    def partial_sums(self):
        return channel_sum(self.partial[0]), channel_sum(self.partial[1])

    def norm_of(self):
        mean, square = self.means(*self.partial_sums())
        inverse = lax.rsqrt(square - mean * mean + NORM_EPS)
        return inverse, -mean * inverse

    def first_act(self):
        inverse, center = self.norm_of()
        self.keep(inverse_one=inverse, center_one=center)
        gain = twice(inverse * self.gain_one)
        shift = twice(center * self.gain_one + self.shift_one)

        def body(pair, carry):
            value, slope = gelu_pair(self.field(pair) * gain + shift)
            put_shifted(self.act_one, pair, value)
            self.slope_one[pair] = slope
            return carry

        over(self.pairs, 8, body, 0)
        close_ring(self.act_one, self.pairs)

    def first_conv(self):
        def body(step, carry):
            start = step * self.size
            value = (
                jnp.dot(
                    windows(self.act_one, start, self.size),
                    self.refs.fwd_one[...],
                    preferred_element_type=jnp.float32,
                )
                + self.bias_one
            )
            self.conv_one[pl.ds(start, self.size)] = value.reshape(self.size, FIELD_COLS, 2 * C)
            return carry[0] + folded(value), carry[1] + folded(value * value)

        total, squares = over_steps(self.steps, body, (self.nothing, self.nothing))
        self.partial[0], self.partial[1] = total, squares

    def second_act(self):
        inverse, center = self.norm_of()
        self.keep(inverse_two=inverse, center_two=center)
        factor = self.gain_two * self.scale_plus
        gain = twice(inverse * factor)
        shift = twice(center * factor + self.shift_two * self.scale_plus + self.offset)

        def body(pair, carry):
            value, slope = gelu_pair(self.conv_one[pair] * gain + shift)
            put_shifted(self.act_two, pair, value)
            self.slope_two[pair] = slope
            return carry

        over(self.pairs, 8, body, 0)
        close_ring(self.act_two, self.pairs)

    def second_conv(self):
        def body(step, carry):
            start = step * self.size
            value = (
                jnp.dot(
                    windows(self.act_two, start, self.size),
                    self.refs.fwd_two[...],
                    preferred_element_type=jnp.float32,
                )
                + self.bias_two
            )
            value = value.reshape(self.size, FIELD_COLS, 2 * C)
            for half, ref in ((0, self.sum_even), (1, self.sum_odd)):
                base = self.x_ref[pl.ds(start, self.size), half].astype(jnp.float32)
                ref[pl.ds(start, self.size)] = base + value[:, :, half * C : half * C + C]
            return carry

        over_steps(self.steps, body)

    def split_columns(self):
        def body(pair, carry):
            even, odd = [], []
            for ref in (self.sum_even, self.sum_odd):
                even.append(ref[pair, pl.ds(0, HALF_COLS, stride=2), :])
                odd.append(ref[pair, pl.ds(1, HALF_COLS, stride=2), :])
            even = jnp.concatenate(even, axis=1)
            odd = jnp.concatenate(odd, axis=1)
            self.down_win[0, pair + 1] = pltpu.roll(odd, 1, 0).astype(jnp.bfloat16)
            self.down_win[1, pair + 1] = even.astype(jnp.bfloat16)
            self.down_win[2, pair + 1] = odd.astype(jnp.bfloat16)
            return carry

        over(self.pairs, 8, body, 0)
        self.down_win[:, 0, :, C:] = self.down_win[:, self.pairs, :, C:]

    def shift_cotangent(self):
        def body(pair, carry):
            value = self.cot_ref[pair]
            wide = value.astype(jnp.float32)
            self.cot_win[0, pair] = value
            self.cot_win[1, pair] = pltpu.roll(wide, HALF_COLS - 1, 0).astype(jnp.bfloat16)
            return carry + folded(wide)

        total = over(self.pairs, 8, body, self.nothing)
        self.cot_win[:, self.pairs] = self.cot_win[:, 0]
        self.refs.raw_sums[16:24, :] = self.refs.raw_sums[16:24, :] + total

    def down_windows(self, start):
        pieces = [
            self.down_win[tap, pl.ds(start + 1, self.size)].reshape(self.small, 2 * C)
            for tap in range(3)
        ]
        pieces += [
            self.down_win[tap, pl.ds(start, self.size), :, C:].reshape(self.small, C)
            for tap in range(3)
        ]
        return jnp.concatenate(pieces, axis=1)

    def down_output(self):
        def body(step, carry):
            start = step * self.size
            value = jnp.dot(
                self.down_windows(start), self.refs.down_fwd[...], preferred_element_type=jnp.float32
            )
            self.out_ref[pl.ds(start, self.size)] = (
                (value + self.bias_down)
                .reshape(self.size, HALF_COLS, 2 * C)
                .astype(jnp.bfloat16)
            )
            return carry

        over_steps(self.steps, body)

    def add_down_grad(self):
        def body(step, carry):
            start = step * self.size
            here = self.cot_win[0, pl.ds(start, self.size)].reshape(self.small, 2 * C)
            product = jnp.dot(
                here.T, self.down_windows(start), preferred_element_type=jnp.float32
            )
            for position in range(9):
                row_tap, tap = DOWN_ORDER[position]
                lanes = pl.ds((3 * row_tap + tap) * C, C)
                self.refs.down_grad[:, lanes] = (
                    self.refs.down_grad[:, lanes] + product[:, position * C : position * C + C]
                )
            return carry

        over_steps(self.steps, body)

    def down_adjoint(self):
        def body(step, carry):
            start = step * self.size
            pieces = [
                self.cot_win[shift, pl.ds(start + below, self.size)].reshape(self.small, 2 * C)
                for below in range(2)
                for shift in range(2)
            ]
            even = jnp.dot(
                jnp.concatenate([pieces[0], pieces[2]], axis=1),
                self.refs.down_even[...],
                preferred_element_type=jnp.float32,
            ).reshape(self.size, HALF_COLS, 2 * C)
            odd = jnp.dot(
                jnp.concatenate(pieces, axis=1),
                self.refs.down_odd[...],
                preferred_element_type=jnp.float32,
            ).reshape(self.size, HALF_COLS, 2 * C)
            for half, ref in ((0, self.grad_even), (1, self.grad_odd)):
                lanes = slice(half * C, half * C + C)
                for inner in range(self.size):
                    ref[start + inner, pl.ds(0, HALF_COLS, stride=2), :] = even[inner, :, lanes]
                    ref[start + inner, pl.ds(1, HALF_COLS, stride=2), :] = odd[inner, :, lanes]
            return carry

        over_steps(self.steps, body)

    def second_grad(self):
        def body(pair, carry):
            value = jnp.concatenate([self.grad_even[pair], self.grad_odd[pair]], axis=1)
            put_shifted(self.grad_two, pair, value)
            return carry + folded(value)

        total = over(self.pairs, 8, body, self.nothing)
        close_ring(self.grad_two, self.pairs)
        self.refs.raw_sums[8:16, :] = self.refs.raw_sums[8:16, :] + total

    def second_conv_grad(self):
        add_conv_grad(self.refs.conv_grad_two, self.act_two, self.grad_two, self.pairs)

    def second_back(self):
        def body(step, carry):
            start = step * self.size
            value = jnp.dot(
                windows(self.grad_two, start, self.size),
                self.refs.back_two[...],
                preferred_element_type=jnp.float32,
            )
            value = value * self.slope_two[pl.ds(start, self.size)].reshape(self.rows, 2 * C)
            self.grad_mid[pl.ds(start, self.size)] = value.reshape(self.size, FIELD_COLS, 2 * C)
            conv = self.conv_one[pl.ds(start, self.size)].reshape(self.rows, 2 * C)
            return carry[0] + folded(value), carry[1] + folded(value * conv)

        total, cross = over_steps(self.steps, body, (self.nothing, self.nothing))
        self.partial[0], self.partial[1] = total, cross

    def first_grad(self):
        inverse, center = self.kept("inverse_two"), self.kept("center_two")
        total, cross = self.partial_sums()
        cross = cross * inverse + total * center
        self.report(0, cross)
        self.report(1, total)
        factor = self.scale_plus * self.gain_two
        mean_grad, mean_cross = self.means(total * factor, cross * factor)
        from_mid = twice(inverse * factor)
        from_conv = twice(inverse * inverse * mean_cross)
        from_mean = twice(inverse * (mean_grad + center * mean_cross))

        def body(pair, carry):
            value = self.grad_mid[pair] * from_mid - from_mean - self.conv_one[pair] * from_conv
            put_shifted(self.grad_one, pair, value)
            return carry + folded(value)

        total = over(self.pairs, 8, body, self.nothing)
        close_ring(self.grad_one, self.pairs)
        self.refs.raw_sums[0:8, :] = self.refs.raw_sums[0:8, :] + total

    def first_conv_grad(self):
        add_conv_grad(self.refs.conv_grad_one, self.act_one, self.grad_one, self.pairs)

    def first_back(self):
        def body(step, carry):
            start = step * self.size
            value = jnp.dot(
                windows(self.grad_one, start, self.size),
                self.refs.back_one[...],
                preferred_element_type=jnp.float32,
            )
            value = value * self.slope_one[pl.ds(start, self.size)].reshape(self.rows, 2 * C)
            self.grad_mid[pl.ds(start, self.size)] = value.reshape(self.size, FIELD_COLS, 2 * C)
            base = jnp.concatenate(
                [
                    self.x_ref[pl.ds(start, self.size), half]
                    .astype(jnp.float32)
                    .reshape(self.rows, C)
                    for half in range(2)
                ],
                axis=1,
            )
            return carry[0] + folded(value), carry[1] + folded(value * base)

        total, cross = over_steps(self.steps, body, (self.nothing, self.nothing))
        self.partial[0], self.partial[1] = total, cross

    def field_grad(self, rows_ref):
        inverse, center = self.kept("inverse_one"), self.kept("center_one")
        total, cross = self.partial_sums()
        cross = cross * inverse + total * center
        self.report(2, cross)
        self.report(3, total)
        mean_grad, mean_cross = self.means(total * self.gain_one, cross * self.gain_one)
        from_pre = twice(inverse * self.gain_one)
        from_field = twice(inverse * inverse * mean_cross)
        from_mean = twice(inverse * (mean_grad + center * mean_cross))

        def body(pair, carry):
            summed = jnp.concatenate([self.grad_even[pair], self.grad_odd[pair]], axis=1)
            change = self.grad_mid[pair] * from_pre - from_mean - self.field(pair) * from_field
            value = (summed + change).astype(jnp.bfloat16)
            rows_ref[pair, 0] = value[:, :C]
            rows_ref[pair, 1] = value[:, C:]
            return carry

        over(self.pairs, 8, body, 0)


STATE = (
    "inverse_one",
    "center_one",
    "inverse_two",
    "center_two",
)
BEFORE = -1
STAGES = (
    ("first_stats", 0),
    ("shift_cotangent", 0),
    ("first_stats", 1),
    ("second_conv_grad", BEFORE),
    ("add_down_grad", BEFORE),
    ("shift_cotangent", 1),
    ("first_act", 0),
    ("down_adjoint", 0),
    ("first_conv_grad", BEFORE),
    ("first_act", 1),
    ("second_grad", 0),
    ("first_conv", 0),
    ("down_adjoint", 1),
    ("second_grad", 1),
    ("first_conv", 1),
    ("second_act", 0),
    ("second_back", 0),
    ("second_act", 1),
    ("second_conv", 0),
    ("first_grad", 0),
    ("second_back", 1),
    ("second_conv_grad", 0),
    ("split_columns", 0),
    ("first_back", 0),
    ("first_grad", 1),
    ("second_conv", 1),
    ("field_grad", 0),
    ("first_conv_grad", 0),
    ("first_back", 1),
    ("split_columns", 1),
    ("down_output", 0),
    ("add_down_grad", 0),
    ("field_grad", 1),
    ("down_output", 1),
)
LATE = ("add_down_grad", "second_conv_grad", "first_conv_grad")


def start_all(copies):
    for copy in copies:
        copy.start()


def peers(axis, count, pairs_of, sends, receives):
    return [
        to_peer(axis, step, count, source(step), target(step), sends.at[place, step], receives.at[place, step])
        for step in range(1, count)
        for place, (source, target) in pairs_of
    ]


def same(ref):
    return lambda step: ref


def slot_of(ref):
    return lambda step: ref.at[step]


def step_kernel(sizes, *args):
    row_count, batch_count, pairs, samples, together = sizes
    names = INPUTS + OUTPUTS + SCRATCH
    refs = SimpleNamespace(**dict(zip(names, args[: len(names)])))
    scratch = args[len(names) :]
    base = pl.program_id(0) * together
    row, batch = lax.axis_index("row"), lax.axis_index("batch")
    share = pairs // row_count

    def send_field(index, carry):
        mine = refs.fields.at[index, pl.ds(row * share, share)]
        for step in range(1, row_count):
            place = lax.rem(row + step, row_count) * samples + index
            to_peer(
                "row",
                step,
                row_count,
                refs.field.at[place],
                mine,
                refs.field_sent,
                refs.field_sem.at[index],
            ).start()
        pltpu.make_async_copy(
            refs.field.at[row * samples + index], mine, refs.field_sem.at[index]
        ).start()
        return carry

    def send_grad(index):
        target = refs.grad_out.at[row * samples + index]
        for step in range(1, row_count):
            place = lax.rem(row + step, row_count) * share
            to_peer(
                "row",
                step,
                row_count,
                refs.grad_rows.at[index, pl.ds(place, share)],
                target,
                refs.grad_sent,
                refs.grad_sem,
            ).start()
        pltpu.make_async_copy(
            refs.grad_rows.at[index, pl.ds(row * share, share)], target, refs.grad_sem
        ).start()

    @pl.when(base == 0)
    def _():
        pack_shards(refs)
        greet(row_count, batch_count)
        own = pltpu.make_async_copy(refs.shard, refs.shards.at[row, batch], refs.local_sem)
        own.start()
        copies = peers(
            "batch",
            batch_count,
            [
                (0, (same(refs.shard), same(refs.shards.at[row, batch]))),
                (1, (same(refs.small), slot_of(refs.small_z))),
            ],
            refs.send_z,
            refs.recv_z,
        )
        start_all(copies)
        lax.fori_loop(0, together, send_field, 0)
        for ref in (refs.conv_grad_one, refs.conv_grad_two, refs.down_grad, refs.raw_sums, refs.sums):
            ref[...] = jnp.zeros_like(ref)
        if together > 1:
            for ref in scratch[-16:-12] + scratch[-4:-2]:
                ref[...] = jnp.zeros_like(ref)
        own.wait()
        finish(copies)
        total = refs.small[...]
        for step in range(1, batch_count):
            total = total + refs.small_z[step]
        refs.small_one[...] = total
        copies = peers(
            "row",
            row_count,
            [(1, (same(refs.small_one), slot_of(refs.small_row)))],
            refs.send_row,
            refs.recv_row,
        )
        sibling = sibling_of(row)
        mine = refs.shards.at[row]
        direct = {}
        for step in range(2, row_count, 2):
            direct[step] = to_row(
                lax.rem(row + step, row_count),
                mine,
                mine,
                refs.send_row.at[0, step],
                refs.recv_row.at[0, step],
            )
        beside = [to_row(sibling, mine, mine, refs.send_row.at[0, 1], refs.recv_row.at[0, 1])]
        start_all(list(direct.values()) + beside + copies)
        lax.fori_loop(together, samples, send_field, 0)
        for step in range(2, row_count, 2):
            direct[step].wait_recv()
            came = refs.shards.at[lax.rem(row + row_count - step, row_count)]
            beside.append(
                to_row(
                    sibling,
                    came,
                    came,
                    refs.send_row.at[0, step + 1],
                    refs.recv_row.at[0, step + 1],
                )
            )
            beside[-1].start()
        for step in range(2, row_count, 2):
            direct[step].wait_send()
        finish(beside + copies)
        total = refs.small_one[...]
        for step in range(1, row_count):
            total = total + refs.small_row[step]
        refs.small_all[...] = total
        lay_out(row_count, batch_count, refs)
        modulate(refs)

    @pl.when(base > 0)
    def _():
        for place in range(together):
            send_grad(base - together + place)

    for place in range(together):
        arrived = refs.fields.at[base + place]
        pltpu.make_async_copy(arrived, arrived, refs.field_sem.at[base + place]).wait()
    stages = [
        Sample(
            pairs,
            base + place,
            refs.fields.at[base + place],
            refs.cot.at[place],
            refs.block_out.at[place],
            refs,
            scratch[16 * place : 16 * place + 16],
        )
        for place in range(together)
    ]

    for name, place in STAGES:
        if place >= together or (place == BEFORE and together == 1):
            continue
        stage = getattr(stages[place], name)
        if name == "field_grad":
            stage(refs.grad_rows.at[base + place])
        else:
            stage()

    @pl.when(base == samples - together)
    def _():
        for place in range(together - 1):
            send_grad(base + place)
        if together > 1:
            for name in LATE:
                getattr(stages[-1], name)()
        reduce_all(row_count, batch_count, refs, lambda: send_grad(base + together - 1))
        pltpu.make_async_copy(refs.grad_out, refs.grad_out, refs.grad_sem).wait()
        others = pl.ds(0, pairs - share)
        for ref, sem in ((refs.fields, refs.field_sent), (refs.grad_rows, refs.grad_sent)):
            pltpu.make_async_copy(ref.at[:, others], ref.at[:, others], sem).wait()


INPUTS = ("field", "cot", "conv", "down", "embed_in", "embed_out", "small", "embedded", "group")
OUTPUTS = (
    "block_out",
    "grad_out",
    "conv_grad",
    "down_share",
    "embed_in_grad",
    "embed_out_grad",
    "small_grad",
    "norm",
)
SCRATCH = (
    "fwd_one",
    "back_one",
    "fwd_two",
    "back_two",
    "down_fwd",
    "down_even",
    "down_odd",
    "small_all",
    "embed_in_t",
    "embed_out_t",
    "modulation",
    "hidden",
    "hidden_slope",
    "sums",
    "raw_sums",
    "conv_grad_one",
    "conv_grad_two",
    "down_grad",
    "shard",
    "shards",
    "small_z",
    "small_one",
    "small_row",
    "conv_t",
    "down_t",
    "fields",
    "grad_rows",
    "row_send",
    "pair_take",
    "chip_send",
    "row_take",
    "batch_send",
    "batch_take",
    "small_send",
    "small_take",
    "small_next",
    "small_last",
    "square_send",
    "square_take",
    "square_next",
    "square_last",
    "field_sem",
    "field_sent",
    "grad_sem",
    "grad_sent",
    "local_sem",
    "send_z",
    "recv_z",
    "send_row",
    "recv_row",
    "send_sem",
    "recv_sem",
)
DOWN_ORDER = ((1, 0), (2, 0), (1, 1), (2, 1), (1, 2), (2, 2), (0, 0), (0, 1), (0, 2))


def lay_out(row_count, batch_count, refs):
    depth, share, wide_share = 9 * C // batch_count, C // row_count, C2 // row_count
    height = 2 * share + wide_share
    embed_share, hidden_share = EMB // batch_count, HID // batch_count
    for place in range(row_count):
        parts = [refs.shards[place, part].astype(jnp.float32) for part in range(batch_count)]
        main = jnp.concatenate([part[:, :depth] for part in parts], axis=1)
        for which in range(2):
            refs.conv_t[which, place * share : place * share + share, :] = main[
                which * share : which * share + share
            ]
        refs.down_t[place * wide_share : place * wide_share + wide_share, :] = main[2 * share :]
        refs.embed_in_t[place * height : place * height + height, :] = jnp.concatenate(
            [part[:, depth : depth + embed_share] for part in parts], axis=1
        )
        tail = depth + embed_share
        half_rows, half_lanes = height // 2, hidden_share // 2
        lanes = []
        for part in parts:
            lanes.append(part[:half_rows, tail : tail + half_lanes])
            lanes.append(part[half_rows:, tail : tail + half_lanes])
        refs.embed_out_t[place * half_rows : place * half_rows + half_rows, :] = jnp.concatenate(
            lanes, axis=1
        )
    for which, forward, back in (
        (0, refs.fwd_one, refs.back_one),
        (1, refs.fwd_two, refs.back_two),
    ):
        zero = jnp.zeros((C, C), jnp.bfloat16)
        for tap in range(3):
            direct = [
                refs.conv_t[which, :, (3 * row_tap + tap) * C : (3 * row_tap + tap) * C + C]
                for row_tap in range(3)
            ]
            fill_blocks(forward, tap, [block.T.astype(jnp.bfloat16) for block in direct], zero)
            fill_blocks(
                back, 2 - tap, [block.astype(jnp.bfloat16) for block in direct[::-1]], zero
            )
    zero = jnp.zeros((C2, C), jnp.bfloat16)
    back = {}
    for position in range(9):
        row_tap, tap = DOWN_ORDER[position]
        block = refs.down_t[:, (3 * row_tap + tap) * C : (3 * row_tap + tap) * C + C]
        refs.down_fwd[position * C : position * C + C, :] = block.T.astype(jnp.bfloat16)
        back[row_tap, tap] = block.astype(jnp.bfloat16)
    even = ((back[1, 1], back[2, 1]), (zero, back[0, 1]))
    odd = (
        (back[1, 2], back[2, 2]),
        (back[1, 0], back[2, 0]),
        (zero, back[0, 2]),
        (zero, back[0, 0]),
    )
    for ref, table in ((refs.down_even, even), (refs.down_odd, odd)):
        for position, (left, right) in enumerate(table):
            ref[position * C2 : position * C2 + C2, :C] = left
            ref[position * C2 : position * C2 + C2, C:] = right


def lanes_of(ref, first, last):
    return jnp.concatenate([ref[place : place + 1, :] for place in range(first, last)], axis=1)


def modulate(refs):
    small = refs.small_all
    before = dot_last(refs.embedded[...], refs.embed_in_t[...]) + lanes_of(small, 8, 12)
    hidden, slope = gelu_pair(before)
    refs.hidden[...] = hidden
    refs.hidden_slope[...] = slope
    result = dot_last(hidden, refs.embed_out_t[...]) + lanes_of(small, 12, 14)
    refs.modulation[0] = 1.0 + result[:, :C]
    refs.modulation[1] = result[:, C:]


def fill_blocks(ref, tap, blocks, zero):
    table = (
        (blocks[1], blocks[0]),
        (blocks[2], blocks[1]),
        (blocks[0], zero),
        (zero, blocks[2]),
    )
    for position, (left, right) in enumerate(table):
        base = (4 * tap + position) * C
        ref[base : base + C, :C] = left
        ref[base : base + C, C:] = right


def dot_full(lhs, rhs):
    return jnp.dot(lhs, rhs, precision=HIGHEST, preferred_element_type=jnp.float32)


def dot_last(lhs, rhs):
    return lax.dot_general(
        lhs,
        rhs,
        (((1,), (1,)), ((), ())),
        precision=HIGHEST,
        preferred_element_type=jnp.float32,
    )


def dot_first(lhs, rhs):
    return lax.dot_general(
        lhs,
        rhs,
        (((0,), (0,)), ((), ())),
        precision=HIGHEST,
        preferred_element_type=jnp.float32,
    )


def reduce_all(row_count, batch_count, refs, send_last):
    row, batch = lax.axis_index("row"), lax.axis_index("batch")
    depth, share, wide_share = 9 * C // batch_count, C // row_count, C2 // row_count
    height = 2 * share + wide_share
    embed_share, hidden_share = EMB // batch_count, HID // batch_count
    mid_cross, mid_total = refs.sums[0], refs.sums[1]
    gain_two, shift_two = refs.small_all[1:2, :], refs.small_all[3:4, :]
    scale_plus = refs.modulation[0]
    grad_mod = jnp.concatenate([gain_two * mid_cross + shift_two * mid_total, mid_total], axis=1)
    grad_embed_out = dot_first(grad_mod, refs.hidden[...])
    grad_hidden = (
        dot_full(grad_mod, refs.embed_out_t[...])
        * refs.hidden_slope[...]
    )
    grad_embed_in = dot_first(grad_hidden, refs.embedded[...])

    def down_sum(value):
        return jnp.sum(value, axis=0, keepdims=True)

    small_rows = [
        down_sum(refs.sums[2]),
        down_sum(mid_cross * scale_plus),
        down_sum(refs.sums[3]),
        down_sum(mid_total * scale_plus),
        channel_sum(refs.raw_sums[0:8]),
        channel_sum(refs.raw_sums[8:16]),
    ]
    cot_total = down_sum(refs.raw_sums[16:24])
    small_rows += [cot_total[:, :C], cot_total[:, C:]]
    hidden_total, mod_total = down_sum(grad_hidden), down_sum(grad_mod)
    small_rows += [hidden_total[:, lane : lane + C] for lane in range(0, HID, C)]
    small_rows += [mod_total[:, lane : lane + C] for lane in range(0, 2 * C, C)]
    small_rows.append(jnp.zeros((2, C), jnp.float32))
    refs.small_send[...] = jnp.concatenate(small_rows, axis=0)
    half_rows = height // 2
    for place in range(row_count):
        low, high = place * share, place * share + share
        refs.row_send[place, :, : 9 * C] = jnp.concatenate(
            [
                refs.conv_grad_one[low:high],
                refs.conv_grad_two[low:high],
                refs.down_grad[place * wide_share : place * wide_share + wide_share],
            ],
            axis=0,
        ).astype(jnp.bfloat16)
        refs.row_send[place, :, 9 * C : 10 * C] = grad_embed_in[
            place * height : place * height + height
        ].astype(jnp.bfloat16)
        piece = grad_embed_out[place * half_rows : place * half_rows + half_rows]
        refs.row_send[place, :, 10 * C :] = jnp.concatenate(
            [piece[:, : HID // 2], piece[:, HID // 2 :]], axis=0
        ).astype(jnp.bfloat16)
    sibling = sibling_of(row)
    beside = [
        to_row(
            sibling,
            refs.row_send.at[lax.rem(sibling + 2 * step, row_count)],
            refs.pair_take.at[step],
            refs.send_sem.at[0, step],
            refs.recv_sem.at[0, step],
        )
        for step in range(row_count // 2)
    ]
    smalls = [
        to_peer(
            "row",
            step,
            row_count,
            refs.small_send,
            refs.small_take.at[step],
            refs.send_sem.at[1, step],
            refs.recv_sem.at[1, step],
        )
        for step in range(1, row_count)
    ]
    order = list(range(1, row_count // 2)) + [0]
    start_all([beside[step] for step in order] + smalls)
    copies = []
    for step in order:
        beside[step].wait_recv()
        place = lax.rem(row + 2 * step, row_count)
        total = refs.row_send[place].astype(jnp.float32) + refs.pair_take[step].astype(jnp.float32)
        if step:
            refs.chip_send[step] = total.astype(jnp.bfloat16)
            copies.append(
                to_row(
                    place,
                    refs.chip_send.at[step],
                    refs.row_take.at[step],
                    refs.send_sem.at[6, step],
                    refs.recv_sem.at[6, step],
                )
            )
            copies[-1].start()
    send_last()
    for copy in beside:
        copy.wait_send()
    finish(copies + smalls)
    small_total = refs.small_send[...]
    for step in range(1, row_count // 2):
        total = total + refs.row_take[step].astype(jnp.float32)
    for step in range(1, row_count):
        small_total = small_total + refs.small_take[step]
    refs.small_next[...] = small_total
    for part in range(batch_count):
        per_half = batch_count // 2
        rows = slice(0, half_rows) if part < per_half else slice(half_rows, height)
        base = 10 * C + hidden_share * (part % per_half)
        piece = total[rows, base : base + hidden_share]
        refs.batch_send[part] = jnp.concatenate(
            [
                total[:, part * depth : part * depth + depth],
                total[:, 9 * C + part * embed_share : 9 * C + part * embed_share + embed_share],
                jnp.concatenate([piece[:, : hidden_share // 2], piece[:, hidden_share // 2 :]], axis=0),
            ],
            axis=1,
        ).astype(jnp.bfloat16)
    copies = []
    for step in range(1, batch_count):
        copies.append(
            to_peer(
                "batch",
                step,
                batch_count,
                refs.batch_send.at[lax.rem(batch + step, batch_count)],
                refs.batch_take.at[step],
                refs.send_sem.at[2, step],
                refs.recv_sem.at[2, step],
            )
        )
        copies.append(
            to_peer(
                "batch",
                step,
                batch_count,
                refs.small_next,
                refs.small_last.at[step],
                refs.send_sem.at[3, step],
                refs.recv_sem.at[3, step],
            )
        )
    for copy in copies:
        copy.start()
    owned = refs.batch_send[batch].astype(jnp.float32)
    finish(copies)
    small_total = refs.small_next[...]
    for step in range(1, batch_count):
        owned = owned + refs.batch_take[step].astype(jnp.float32)
        small_total = small_total + refs.small_last[step]
    squares = jnp.sum(jnp.sum(owned * owned, axis=0, keepdims=True), axis=1, keepdims=True)
    refs.square_send[...] = jnp.broadcast_to(squares, (8, C))
    copies = [
        to_peer(
            "row",
            step,
            row_count,
            refs.square_send,
            refs.square_take.at[step],
            refs.send_sem.at[4, step],
            refs.recv_sem.at[4, step],
        )
        for step in range(1, row_count)
    ]
    for copy in copies:
        copy.start()
    finish(copies)
    squares = refs.square_send[...]
    for step in range(1, row_count):
        squares = squares + refs.square_take[step]
    refs.square_next[...] = squares
    copies = [
        to_peer(
            "batch",
            step,
            batch_count,
            refs.square_next,
            refs.square_last.at[step],
            refs.send_sem.at[5, step],
            refs.recv_sem.at[5, step],
        )
        for step in range(1, batch_count)
    ]
    for copy in copies:
        copy.start()
    finish(copies)
    squares = refs.square_next[...]
    for step in range(1, batch_count):
        squares = squares + refs.square_last[step]
    small_squares = jnp.sum(
        jnp.sum(small_total * small_total, axis=0, keepdims=True), axis=1, keepdims=True
    )
    norm = jnp.sqrt(squares + small_squares)
    clip = jnp.minimum(1.0, CLIP_NORM / (norm + 1e-06))[0:1, 0:1]
    refs.norm[...] = norm[0:1, 0:1]
    owned = owned * clip
    refs.conv_grad[0] = owned[:share, :depth]
    refs.conv_grad[1] = owned[share : 2 * share, :depth]
    refs.down_share[...] = owned[2 * share :, :depth]
    refs.embed_in_grad[...] = owned[:, depth : depth + embed_share].T
    tail = depth + embed_share
    refs.embed_out_grad[...] = jnp.concatenate(
        [owned[:half_rows, tail:], owned[half_rows:, tail:]], axis=1
    )
    refs.small_all[...] = small_total * clip
    small_len = 14 * C // (row_count * batch_count)
    first = (batch * row_count + row) * small_len
    line, lane = first // C, lax.rem(first, C)
    lines = jnp.concatenate(
        [refs.small_all[pl.ds(line, 1), :], refs.small_all[pl.ds(line + 1, 1), :]], axis=1
    )
    moved = pltpu.roll(jnp.broadcast_to(lines, (8, 2 * C)), lax.rem(2 * C - lane, 2 * C), 1)
    refs.small_grad[...] = moved[0:1, :small_len]


def pack_shards(refs):
    half = refs.embed_out.shape[1] // 2
    refs.shard[...] = jnp.concatenate(
        [
            jnp.concatenate([refs.conv[0], refs.conv[1], refs.down[...]], axis=0),
            refs.embed_in[...].T,
            jnp.concatenate([refs.embed_out[:, :half], refs.embed_out[:, half:]], axis=0),
        ],
        axis=1,
    ).astype(jnp.bfloat16)


def run_step(field_in, cotangent, shards, small_tile, embedded):
    row_count, batch_count = (lax.axis_size("row"), lax.axis_size("batch"))
    samples = cotangent.shape[0]
    padded = embedded.shape[0]
    pairs = field_in.shape[1] // 2 * row_count
    together = chunk_of(samples, 2)
    share = pairs // row_count
    height, width = 4 * C // row_count, 12 * C // batch_count
    halves = field_in.reshape(field_in.shape[0], share, 2, FIELD_COLS, C)
    same_group = jnp.asarray(
        np.kron(np.eye(GROUPS), np.ones((C // GROUPS, C // GROUPS))), jnp.float32
    )
    low, full = jnp.bfloat16, jnp.float32
    anywhere = pl.BlockSpec(memory_space=pl.ANY)

    def whole(array):
        return pl.BlockSpec(array.shape, lambda i: (0,) * len(array.shape))

    def per_step(array):
        rank = len(array.shape)
        return pl.BlockSpec((together,) + array.shape[1:], lambda i: (i,) + (0,) * (rank - 1))

    outs = (
        jax.ShapeDtypeStruct(cotangent.shape, low),
        jax.ShapeDtypeStruct(halves.shape, low),
        *[jax.ShapeDtypeStruct(shard.shape, full) for shard in shards],
        jax.ShapeDtypeStruct((1, 14 * C // (row_count * batch_count)), full),
        jax.ShapeDtypeStruct((1, 1), full),
    )
    ring = pltpu.VMEM((3, pairs + 2, FIELD_COLS, 2 * C), low)
    wide = pltpu.VMEM((pairs, FIELD_COLS, 2 * C), full)
    half = pltpu.VMEM((pairs, FIELD_COLS, C), full)
    fields = pltpu.VMEM((samples, pairs, 2, FIELD_COLS, C), low)
    dma = pltpu.SemaphoreType.DMA
    most = max(row_count, batch_count)
    tile = (16, C)
    scratch = (
        [pltpu.VMEM((12 * C, 2 * C), low)] * 4
        + [
            pltpu.VMEM((9 * C, C2), low),
            pltpu.VMEM((2 * C2, 2 * C), low),
            pltpu.VMEM((4 * C2, 2 * C), low),
            pltpu.VMEM(tile, full),
            pltpu.VMEM((HID, EMB), full),
            pltpu.VMEM((2 * C, HID), full),
            pltpu.VMEM((2, padded, C), full),
            pltpu.VMEM((padded, HID), full),
            pltpu.VMEM((padded, HID), full),
            pltpu.VMEM((4, padded, C), full),
            pltpu.VMEM((24, 2 * C), full),
            pltpu.VMEM((C, 9 * C), full),
            pltpu.VMEM((C, 9 * C), full),
            pltpu.VMEM((C2, 9 * C), full),
            pltpu.VMEM((height, width), low),
            pltpu.VMEM((row_count, batch_count, height, width), low),
            pltpu.VMEM((batch_count,) + tile, full),
            pltpu.VMEM(tile, full),
            pltpu.VMEM((row_count,) + tile, full),
            pltpu.VMEM((2, C, 9 * C), full),
            pltpu.VMEM((C2, 9 * C), full),
            fields,
            fields,
            pltpu.VMEM((row_count, height, 12 * C), low),
            pltpu.VMEM((row_count // 2, height, 12 * C), low),
            pltpu.VMEM((row_count // 2, height, 12 * C), low),
            pltpu.VMEM((row_count // 2, height, 12 * C), low),
            pltpu.VMEM((batch_count, height, width), low),
            pltpu.VMEM((batch_count, height, width), low),
            pltpu.VMEM(tile, full),
            pltpu.VMEM((row_count,) + tile, full),
            pltpu.VMEM(tile, full),
            pltpu.VMEM((batch_count,) + tile, full),
            pltpu.VMEM((8, C), full),
            pltpu.VMEM((row_count, 8, C), full),
            pltpu.VMEM((8, C), full),
            pltpu.VMEM((batch_count, 8, C), full),
            dma((samples,)),
            dma,
            dma,
            dma,
            dma,
            dma((2, batch_count)),
            dma((2, batch_count)),
            dma((2, row_count)),
            dma((2, row_count)),
            dma((7, most)),
            dma((7, most)),
        ]
        + (
            [ring] * 4
            + [wide] * 4
            + [half] * 4
            + [
                pltpu.VMEM((3, pairs + 1, HALF_COLS, 2 * C), low),
                pltpu.VMEM((2, pairs + 1, HALF_COLS, C2), low),
                pltpu.VMEM((8, C), full),
                pltpu.VMEM((2, 8, 2 * C), full),
            ]
        )
        * together
    )
    result = pl.pallas_call(
        functools.partial(step_kernel, (row_count, batch_count, pairs, samples, together)),
        grid=(samples // together,),
        in_specs=[anywhere, per_step(cotangent)]
        + [whole(array) for array in shards + (small_tile, embedded, same_group)],
        out_specs=[per_step(outs[0]), anywhere] + [whole(out) for out in outs[2:]],
        out_shape=outs,
        scratch_shapes=scratch,
        compiler_params=pltpu.CompilerParams(
            dimension_semantics=("arbitrary",),
            vmem_limit_bytes=62 << 20,
            collective_id=0,
            has_side_effects=True,
        ),
        name="step",
    )(halves, cotangent, *shards, small_tile, embedded, same_group)
    return (result[0], result[1].reshape(field_in.shape)) + tuple(result[2:])


def adam_update(weight, gradient, first_old, second_old, step_rate, clip_factor):
    scaled = gradient * clip_factor
    first_new = BETA_ONE * first_old + (1.0 - BETA_ONE) * scaled
    second_new = BETA_TWO * second_old + (1.0 - BETA_TWO) * scaled * scaled
    corrected = (
        first_new
        / (1.0 - BETA_ONE**STEP_COUNT)
        / (jnp.sqrt(second_new / (1.0 - BETA_TWO**STEP_COUNT)) + ADAM_EPS)
    )
    return (weight - step_rate * (corrected + DECAY * weight), first_new, second_new)


def body(
    field_in,
    refine_step,
    cotangent,
    conv_weight,
    down_weight,
    embed_in_weight,
    embed_out_weight,
    small_params,
    conv_first,
    down_first,
    embed_in_first,
    embed_out_first,
    small_first,
    conv_second,
    down_second,
    embed_in_second,
    embed_out_second,
    small_second,
):
    small_len = small_params.shape[0]
    place = (lax.axis_index("batch") * lax.axis_size("row") + lax.axis_index("row")) * small_len
    small_rounded = lax.reduce_precision(small_params, exponent_bits=8, mantissa_bits=7)
    small_tile = lax.dynamic_update_slice_in_dim(
        jnp.zeros((16 * C,), jnp.float32), small_rounded, place, 0
    ).reshape(16, C)
    owned = refine_step.shape[0] // lax.axis_size("row")
    padded = -(-owned // 8) * 8
    own_steps = lax.dynamic_slice_in_dim(refine_step, lax.axis_index("row") * owned, owned, 0)
    embedded = embed_steps(jnp.pad(own_steps, (0, padded - owned)))
    block_out, grad_start, *owned_shards, small_grads, norm_tile = run_step(
        field_in,
        cotangent,
        (
            jnp.transpose(conv_weight, (0, 2, 1)),
            down_weight.T,
            embed_in_weight,
            embed_out_weight.T,
        ),
        small_tile,
        embedded,
    )
    grad_norm = norm_tile.reshape(())
    owned_shards = [
        jnp.transpose(owned_shards[0], (0, 2, 1)),
        owned_shards[1].T,
        owned_shards[2],
        owned_shards[3].T,
    ]
    owned_shards.append(small_grads.reshape(small_len))
    clip_factor = 1.0
    conv_new = adam_update(
        conv_weight, owned_shards[0], conv_first, conv_second, RATE_MATRIX, clip_factor
    )
    down_new = adam_update(
        down_weight, owned_shards[1], down_first, down_second, RATE_MATRIX, clip_factor
    )
    embed_in_new = adam_update(
        embed_in_weight, owned_shards[2], embed_in_first, embed_in_second, RATE_MATRIX, clip_factor
    )
    embed_out_new = adam_update(
        embed_out_weight,
        owned_shards[3],
        embed_out_first,
        embed_out_second,
        RATE_MATRIX,
        clip_factor,
    )
    small_new = adam_update(
        small_params, owned_shards[4], small_first, small_second, RATE_SMALL, clip_factor
    )
    return (
        block_out,
        grad_start,
        grad_norm,
        conv_new[0],
        down_new[0],
        embed_in_new[0],
        embed_out_new[0],
        small_new[0],
        conv_new[1],
        down_new[1],
        embed_in_new[1],
        embed_out_new[1],
        small_new[1],
        conv_new[2],
        down_new[2],
        embed_in_new[2],
        embed_out_new[2],
        small_new[2],
    )


def solution(mesh):
    placed = (
        P("batch", "row", None, None),
        P("batch"),
        P(("batch", "row"), None, None, None),
        P(None, "batch", "row"),
        P("batch", "row"),
        P("batch", "row"),
        P("batch", "row"),
        P(("batch", "row")),
        P(None, "batch", "row"),
        P("batch", "row"),
        P("batch", "row"),
        P("batch", "row"),
        P(("batch", "row")),
        P(None, "batch", "row"),
        P("batch", "row"),
        P("batch", "row"),
        P("batch", "row"),
        P(("batch", "row")),
    )
    return jax.shard_map(
        body,
        mesh=mesh,
        in_specs=placed,
        out_specs=(
            P(("batch", "row"), None, None, None),
            P("batch", "row", None, None),
            P(),
            P(None, "batch", "row"),
            P("batch", "row"),
            P("batch", "row"),
            P("batch", "row"),
            P(("batch", "row")),
            P(None, "batch", "row"),
            P("batch", "row"),
            P("batch", "row"),
            P("batch", "row"),
            P(("batch", "row")),
            P(None, "batch", "row"),
            P("batch", "row"),
            P("batch", "row"),
            P("batch", "row"),
            P(("batch", "row")),
        ),
        check_vma=False,
    )
```

```python
import functools
import math
from types import SimpleNamespace

import jax
import jax.numpy as jnp
import numpy as np
from jax import lax
from jax.experimental import pallas as pl
from jax.experimental.pallas import tpu as pltpu
from jax.sharding import PartitionSpec as P

C = 128
C2 = 256
EMB = 128
HID = 512
GROUPS = 8
REFINE = 4


NORM_EPS = 1e-05
BETA_ONE = 0.9
BETA_TWO = 0.999
ADAM_EPS = 1e-08
DECAY = 0.01
RATE_MATRIX = 0.05
RATE_SMALL = 0.5
CLIP_NORM = 1.0
STEP_COUNT = 10
HIGHEST = lax.Precision.HIGHEST


def embed_steps(refine_step):
    halfway = EMB // 2
    frequency = jnp.exp(-math.log(10000.0) * jnp.arange(halfway).astype(jnp.float32) / halfway)
    angles = (refine_step.astype(jnp.float32) * (1000.0 / REFINE))[:, None] * frequency[None, :]
    return jnp.concatenate([jnp.sin(angles), jnp.cos(angles)], axis=1)


MESH = pl.DeviceIdType.MESH


def greet(row_count, batch_count=1):
    row, batch = lax.axis_index("row"), lax.axis_index("batch")
    barrier = pltpu.get_barrier_semaphore()
    for step in range(1, row_count):
        pl.semaphore_signal(
            barrier,
            inc=1,
            device_id={"row": lax.rem(row + step, row_count), "batch": batch},
            device_id_type=MESH,
        )
    for step in range(1, batch_count):
        pl.semaphore_signal(
            barrier,
            inc=1,
            device_id={"row": row, "batch": lax.rem(batch + step, batch_count)},
            device_id_type=MESH,
        )
    pl.semaphore_wait(barrier, row_count + batch_count - 2)


def to_peer(axis, step, count, source, target, send_sem, recv_sem):
    row, batch = lax.axis_index("row"), lax.axis_index("batch")
    if axis == "row":
        device = {"row": lax.rem(row + step, count), "batch": batch}
    else:
        device = {"row": row, "batch": lax.rem(batch + step, count)}
    return pltpu.make_async_remote_copy(
        src_ref=source,
        dst_ref=target,
        send_sem=send_sem,
        recv_sem=recv_sem,
        device_id=device,
        device_id_type=MESH,
    )


def to_row(place, source, target, send_sem, recv_sem):
    return pltpu.make_async_remote_copy(
        src_ref=source,
        dst_ref=target,
        send_sem=send_sem,
        recv_sem=recv_sem,
        device_id={"row": place, "batch": lax.axis_index("batch")},
        device_id_type=MESH,
    )


def sibling_of(row):
    return row + 1 - 2 * lax.rem(row, 2)


def finish(copies):
    for copy in copies:
        copy.wait()


FIELD_COLS = 64
HALF_COLS = 32
ROOT = math.sqrt(2.0 / math.pi)
CUBIC = ROOT * 0.044715


def chunk_of(total, most):
    size = min(total, most)
    while total % size:
        size -= 1
    return size


def over(total, most, body, init):
    size = chunk_of(total, most)

    def several(step, carry):
        for inner in range(size):
            carry = body(step * size + inner, carry)
        return carry

    if size == total:
        return several(0, init)
    return lax.fori_loop(0, total // size, several, init)


def folded(values):
    return jnp.sum(values.reshape(values.shape[0] // 8, 8, values.shape[1]), axis=0)


def twice(row):
    return jnp.concatenate([row, row], axis=1)


def channel_sum(partial):
    both = partial[:, :C] + partial[:, C:]
    return jnp.sum(both, axis=0, keepdims=True)


def group_means(first, second, same_group, entries):
    stacked = jnp.concatenate([first, second, jnp.zeros((6, C), jnp.float32)], axis=0)
    totals = jnp.dot(stacked, same_group, precision=HIGHEST, preferred_element_type=jnp.float32)
    return totals[0:1] / entries, totals[1:2] / entries


def gelu_pair(values):
    square = values * values
    weight = 0.5 + 0.5 * jnp.tanh(values * (ROOT + CUBIC * square))
    result = values * weight
    slope = weight + (result - result * weight) * (2.0 * ROOT + (6.0 * CUBIC) * square)
    return result, slope


def put_shifted(ref, pair, values):
    for tap, shift in ((0, 1), (1, 0), (2, FIELD_COLS - 1)):
        moved = pltpu.roll(values, shift, 0) if shift else values
        ref[tap, pair + 1] = moved.astype(jnp.bfloat16)


def close_ring(ref, pairs):
    ref[:, 0, :, C:] = ref[:, pairs, :, C:]
    ref[:, pairs + 1, :, :C] = ref[:, 1, :, :C]


def windows(ref, start, count):
    rows = count * FIELD_COLS
    pieces = []
    for tap in range(3):
        pieces.append(ref[tap, pl.ds(start + 1, count)].reshape(rows, 2 * C))
        pieces.append(ref[tap, pl.ds(start, count), :, C:].reshape(rows, C))
        pieces.append(ref[tap, pl.ds(start + 2, count), :, :C].reshape(rows, C))
    return jnp.concatenate(pieces, axis=1)


def over_steps(steps, body, init=0):
    if steps == 1:
        return body(0, init)
    return lax.fori_loop(0, steps, body, init)


def add_conv_grad(out_ref, act_ref, grad_ref, pairs):
    size = chunk_of(pairs, 8)
    rows = size * FIELD_COLS

    def body(step, carry):
        start = step * size
        grad = grad_ref[1, pl.ds(start + 1, size)].reshape(rows, 2 * C)
        product = jnp.dot(
            grad.T, windows(act_ref, start, size), preferred_element_type=jnp.float32
        )
        for tap in range(3):
            base = tap * 4 * C
            middle = product[:C, base : base + C] + product[C:, base + C : base + 2 * C]
            up = product[C:, base : base + C] + product[:C, base + 2 * C : base + 3 * C]
            down = product[:C, base + C : base + 2 * C] + product[C:, base + 3 * C : base + 4 * C]
            for row_tap, value in ((0, up), (1, middle), (2, down)):
                lanes = pl.ds((3 * row_tap + tap) * C, C)
                out_ref[:, lanes] = out_ref[:, lanes] + value
        return carry

    over_steps(pairs // size, body)


class Sample:
    def __init__(self, pairs, sample, x_ref, cot_ref, out_ref, refs, scratch):
        self.pairs, self.sample = pairs, sample
        self.x_ref, self.cot_ref, self.out_ref = x_ref, cot_ref, out_ref
        self.refs = refs
        (
            self.act_one,
            self.act_two,
            self.grad_one,
            self.grad_two,
            self.slope_one,
            self.slope_two,
            self.conv_one,
            self.grad_mid,
            self.sum_even,
            self.sum_odd,
            self.grad_even,
            self.grad_odd,
            self.down_win,
            self.cot_win,
            self.state,
            self.partial,
        ) = scratch
        self.entries = 2.0 * pairs * FIELD_COLS * (C // GROUPS)
        self.size = chunk_of(pairs, 8)
        self.steps = pairs // self.size
        self.rows = self.size * FIELD_COLS
        self.small = self.size * HALF_COLS
        self.same_group = refs.group[...]
        small = refs.small_all
        self.gain_one, self.gain_two = small[0:1, :], small[1:2, :]
        self.shift_one, self.shift_two = small[2:3, :], small[3:4, :]
        self.bias_one, self.bias_two = twice(small[4:5, :]), twice(small[5:6, :])
        self.bias_down = jnp.concatenate([small[6:7, :], small[7:8, :]], axis=1)
        self.scale_plus = refs.modulation[0, pl.ds(sample, 1), :]
        self.offset = refs.modulation[1, pl.ds(sample, 1), :]
        self.nothing = jnp.zeros((8, 2 * C), jnp.float32)

    def keep(self, **values):
        for name, value in values.items():
            place = STATE.index(name)
            self.state[place : place + 1, :] = value

    def kept(self, name):
        place = STATE.index(name)
        return self.state[place : place + 1, :]

    def report(self, place, value):
        self.refs.sums[place, pl.ds(self.sample, 1), :] = value

    def field(self, pair):
        return jnp.concatenate(
            [
                self.x_ref[pair, 0].astype(jnp.float32),
                self.x_ref[pair, 1].astype(jnp.float32),
            ],
            axis=1,
        )

    def means(self, first, second):
        return group_means(first, second, self.same_group, self.entries)

    def first_stats(self):
        def body(pair, carry):
            value = self.field(pair)
            return carry[0] + folded(value), carry[1] + folded(value * value)

        total, squares = over(self.pairs, 8, body, (self.nothing, self.nothing))
        self.partial[0], self.partial[1] = total, squares

    def partial_sums(self):
        return channel_sum(self.partial[0]), channel_sum(self.partial[1])

    def norm_of(self):
        mean, square = self.means(*self.partial_sums())
        inverse = lax.rsqrt(square - mean * mean + NORM_EPS)
        return inverse, -mean * inverse

    def first_act(self):
        inverse, center = self.norm_of()
        self.keep(inverse_one=inverse, center_one=center)
        gain = twice(inverse * self.gain_one)
        shift = twice(center * self.gain_one + self.shift_one)

        def body(pair, carry):
            value, slope = gelu_pair(self.field(pair) * gain + shift)
            put_shifted(self.act_one, pair, value)
            self.slope_one[pair] = slope
            return carry

        over(self.pairs, 8, body, 0)
        close_ring(self.act_one, self.pairs)

    def first_conv(self):
        def body(step, carry):
            start = step * self.size
            value = (
                jnp.dot(
                    windows(self.act_one, start, self.size),
                    self.refs.fwd_one[...],
                    preferred_element_type=jnp.float32,
                )
                + self.bias_one
            )
            self.conv_one[pl.ds(start, self.size)] = value.reshape(self.size, FIELD_COLS, 2 * C)
            return carry[0] + folded(value), carry[1] + folded(value * value)

        total, squares = over_steps(self.steps, body, (self.nothing, self.nothing))
        self.partial[0], self.partial[1] = total, squares

    def second_act(self):
        inverse, center = self.norm_of()
        self.keep(inverse_two=inverse, center_two=center)
        factor = self.gain_two * self.scale_plus
        gain = twice(inverse * factor)
        shift = twice(center * factor + self.shift_two * self.scale_plus + self.offset)

        def body(pair, carry):
            value, slope = gelu_pair(self.conv_one[pair] * gain + shift)
            put_shifted(self.act_two, pair, value)
            self.slope_two[pair] = slope
            return carry

        over(self.pairs, 8, body, 0)
        close_ring(self.act_two, self.pairs)

    def second_conv(self):
        def body(step, carry):
            start = step * self.size
            value = (
                jnp.dot(
                    windows(self.act_two, start, self.size),
                    self.refs.fwd_two[...],
                    preferred_element_type=jnp.float32,
                )
                + self.bias_two
            )
            value = value.reshape(self.size, FIELD_COLS, 2 * C)
            for half, ref in ((0, self.sum_even), (1, self.sum_odd)):
                base = self.x_ref[pl.ds(start, self.size), half].astype(jnp.float32)
                ref[pl.ds(start, self.size)] = base + value[:, :, half * C : half * C + C]
            return carry

        over_steps(self.steps, body)

    def split_columns(self):
        def body(pair, carry):
            even, odd = [], []
            for ref in (self.sum_even, self.sum_odd):
                even.append(ref[pair, pl.ds(0, HALF_COLS, stride=2), :])
                odd.append(ref[pair, pl.ds(1, HALF_COLS, stride=2), :])
            even = jnp.concatenate(even, axis=1)
            odd = jnp.concatenate(odd, axis=1)
            self.down_win[0, pair + 1] = pltpu.roll(odd, 1, 0).astype(jnp.bfloat16)
            self.down_win[1, pair + 1] = even.astype(jnp.bfloat16)
            self.down_win[2, pair + 1] = odd.astype(jnp.bfloat16)
            return carry

        over(self.pairs, 8, body, 0)
        self.down_win[:, 0, :, C:] = self.down_win[:, self.pairs, :, C:]

    def shift_cotangent(self):
        def body(pair, carry):
            value = self.cot_ref[pair]
            wide = value.astype(jnp.float32)
            self.cot_win[0, pair] = value
            self.cot_win[1, pair] = pltpu.roll(wide, HALF_COLS - 1, 0).astype(jnp.bfloat16)
            return carry + folded(wide)

        total = over(self.pairs, 8, body, self.nothing)
        self.cot_win[:, self.pairs] = self.cot_win[:, 0]
        self.refs.raw_sums[16:24, :] = self.refs.raw_sums[16:24, :] + total

    def down_windows(self, start):
        pieces = [
            self.down_win[tap, pl.ds(start + 1, self.size)].reshape(self.small, 2 * C)
            for tap in range(3)
        ]
        pieces += [
            self.down_win[tap, pl.ds(start, self.size), :, C:].reshape(self.small, C)
            for tap in range(3)
        ]
        return jnp.concatenate(pieces, axis=1)

    def down_output(self):
        def body(step, carry):
            start = step * self.size
            value = jnp.dot(
                self.down_windows(start), self.refs.down_fwd[...], preferred_element_type=jnp.float32
            )
            self.out_ref[pl.ds(start, self.size)] = (
                (value + self.bias_down)
                .reshape(self.size, HALF_COLS, 2 * C)
                .astype(jnp.bfloat16)
            )
            return carry

        over_steps(self.steps, body)

    def add_down_grad(self):
        def body(step, carry):
            start = step * self.size
            here = self.cot_win[0, pl.ds(start, self.size)].reshape(self.small, 2 * C)
            product = jnp.dot(
                here.T, self.down_windows(start), preferred_element_type=jnp.float32
            )
            for position in range(9):
                row_tap, tap = DOWN_ORDER[position]
                lanes = pl.ds((3 * row_tap + tap) * C, C)
                self.refs.down_grad[:, lanes] = (
                    self.refs.down_grad[:, lanes] + product[:, position * C : position * C + C]
                )
            return carry

        over_steps(self.steps, body)

    def down_adjoint(self):
        def body(step, carry):
            start = step * self.size
            pieces = [
                self.cot_win[shift, pl.ds(start + below, self.size)].reshape(self.small, 2 * C)
                for below in range(2)
                for shift in range(2)
            ]
            even = jnp.dot(
                jnp.concatenate([pieces[0], pieces[2]], axis=1),
                self.refs.down_even[...],
                preferred_element_type=jnp.float32,
            ).reshape(self.size, HALF_COLS, 2 * C)
            odd = jnp.dot(
                jnp.concatenate(pieces, axis=1),
                self.refs.down_odd[...],
                preferred_element_type=jnp.float32,
            ).reshape(self.size, HALF_COLS, 2 * C)
            for half, ref in ((0, self.grad_even), (1, self.grad_odd)):
                lanes = slice(half * C, half * C + C)
                for inner in range(self.size):
                    ref[start + inner, pl.ds(0, HALF_COLS, stride=2), :] = even[inner, :, lanes]
                    ref[start + inner, pl.ds(1, HALF_COLS, stride=2), :] = odd[inner, :, lanes]
            return carry

        over_steps(self.steps, body)

    def second_grad(self):
        def body(pair, carry):
            value = jnp.concatenate([self.grad_even[pair], self.grad_odd[pair]], axis=1)
            put_shifted(self.grad_two, pair, value)
            return carry + folded(value)

        total = over(self.pairs, 8, body, self.nothing)
        close_ring(self.grad_two, self.pairs)
        self.refs.raw_sums[8:16, :] = self.refs.raw_sums[8:16, :] + total

    def second_conv_grad(self):
        add_conv_grad(self.refs.conv_grad_two, self.act_two, self.grad_two, self.pairs)

    def second_back(self):
        def body(step, carry):
            start = step * self.size
            value = jnp.dot(
                windows(self.grad_two, start, self.size),
                self.refs.back_two[...],
                preferred_element_type=jnp.float32,
            )
            value = value * self.slope_two[pl.ds(start, self.size)].reshape(self.rows, 2 * C)
            self.grad_mid[pl.ds(start, self.size)] = value.reshape(self.size, FIELD_COLS, 2 * C)
            conv = self.conv_one[pl.ds(start, self.size)].reshape(self.rows, 2 * C)
            return carry[0] + folded(value), carry[1] + folded(value * conv)

        total, cross = over_steps(self.steps, body, (self.nothing, self.nothing))
        self.partial[0], self.partial[1] = total, cross

    def first_grad(self):
        inverse, center = self.kept("inverse_two"), self.kept("center_two")
        total, cross = self.partial_sums()
        cross = cross * inverse + total * center
        self.report(0, cross)
        self.report(1, total)
        factor = self.scale_plus * self.gain_two
        mean_grad, mean_cross = self.means(total * factor, cross * factor)
        from_mid = twice(inverse * factor)
        from_conv = twice(inverse * inverse * mean_cross)
        from_mean = twice(inverse * (mean_grad + center * mean_cross))

        def body(pair, carry):
            value = self.grad_mid[pair] * from_mid - from_mean - self.conv_one[pair] * from_conv
            put_shifted(self.grad_one, pair, value)
            return carry + folded(value)

        total = over(self.pairs, 8, body, self.nothing)
        close_ring(self.grad_one, self.pairs)
        self.refs.raw_sums[0:8, :] = self.refs.raw_sums[0:8, :] + total

    def first_conv_grad(self):
        add_conv_grad(self.refs.conv_grad_one, self.act_one, self.grad_one, self.pairs)

    def first_back(self):
        def body(step, carry):
            start = step * self.size
            value = jnp.dot(
                windows(self.grad_one, start, self.size),
                self.refs.back_one[...],
                preferred_element_type=jnp.float32,
            )
            value = value * self.slope_one[pl.ds(start, self.size)].reshape(self.rows, 2 * C)
            self.grad_mid[pl.ds(start, self.size)] = value.reshape(self.size, FIELD_COLS, 2 * C)
            base = jnp.concatenate(
                [
                    self.x_ref[pl.ds(start, self.size), half]
                    .astype(jnp.float32)
                    .reshape(self.rows, C)
                    for half in range(2)
                ],
                axis=1,
            )
            return carry[0] + folded(value), carry[1] + folded(value * base)

        total, cross = over_steps(self.steps, body, (self.nothing, self.nothing))
        self.partial[0], self.partial[1] = total, cross

    def field_grad(self, rows_ref):
        inverse, center = self.kept("inverse_one"), self.kept("center_one")
        total, cross = self.partial_sums()
        cross = cross * inverse + total * center
        self.report(2, cross)
        self.report(3, total)
        mean_grad, mean_cross = self.means(total * self.gain_one, cross * self.gain_one)
        from_pre = twice(inverse * self.gain_one)
        from_field = twice(inverse * inverse * mean_cross)
        from_mean = twice(inverse * (mean_grad + center * mean_cross))

        def body(pair, carry):
            summed = jnp.concatenate([self.grad_even[pair], self.grad_odd[pair]], axis=1)
            change = self.grad_mid[pair] * from_pre - from_mean - self.field(pair) * from_field
            value = (summed + change).astype(jnp.bfloat16)
            rows_ref[pair, 0] = value[:, :C]
            rows_ref[pair, 1] = value[:, C:]
            return carry

        over(self.pairs, 8, body, 0)


STATE = (
    "inverse_one",
    "center_one",
    "inverse_two",
    "center_two",
)
BEFORE = -1
STAGES = (
    ("first_stats", 0),
    ("shift_cotangent", 0),
    ("first_stats", 1),
    ("second_conv_grad", BEFORE),
    ("add_down_grad", BEFORE),
    ("shift_cotangent", 1),
    ("first_act", 0),
    ("down_adjoint", 0),
    ("first_conv_grad", BEFORE),
    ("first_act", 1),
    ("second_grad", 0),
    ("first_conv", 0),
    ("down_adjoint", 1),
    ("second_grad", 1),
    ("first_conv", 1),
    ("second_act", 0),
    ("second_back", 0),
    ("second_act", 1),
    ("second_conv", 0),
    ("first_grad", 0),
    ("second_back", 1),
    ("second_conv_grad", 0),
    ("split_columns", 0),
    ("first_back", 0),
    ("first_grad", 1),
    ("second_conv", 1),
    ("field_grad", 0),
    ("first_conv_grad", 0),
    ("first_back", 1),
    ("split_columns", 1),
    ("down_output", 0),
    ("add_down_grad", 0),
    ("field_grad", 1),
    ("down_output", 1),
)
LATE = ("add_down_grad", "second_conv_grad", "first_conv_grad")


def start_all(copies):
    for copy in copies:
        copy.start()


def peers(axis, count, pairs_of, sends, receives):
    return [
        to_peer(axis, step, count, source(step), target(step), sends.at[place, step], receives.at[place, step])
        for step in range(1, count)
        for place, (source, target) in pairs_of
    ]


def same(ref):
    return lambda step: ref


def slot_of(ref):
    return lambda step: ref.at[step]


def step_kernel(sizes, *args):
    row_count, batch_count, pairs, samples, together = sizes
    names = INPUTS + OUTPUTS + SCRATCH
    refs = SimpleNamespace(**dict(zip(names, args[: len(names)])))
    scratch = args[len(names) :]
    base = pl.program_id(0) * together
    row, batch = lax.axis_index("row"), lax.axis_index("batch")
    share = pairs // row_count

    def send_field(index, carry):
        mine = refs.fields.at[index, pl.ds(row * share, share)]
        for step in range(1, row_count):
            place = lax.rem(row + step, row_count) * samples + index
            to_peer(
                "row",
                step,
                row_count,
                refs.field.at[place],
                mine,
                refs.field_sent,
                refs.field_sem.at[index],
            ).start()
        pltpu.make_async_copy(
            refs.field.at[row * samples + index], mine, refs.field_sem.at[index]
        ).start()
        return carry

    def send_grad(index):
        target = refs.grad_out.at[row * samples + index]
        for step in range(1, row_count):
            place = lax.rem(row + step, row_count) * share
            to_peer(
                "row",
                step,
                row_count,
                refs.grad_rows.at[index, pl.ds(place, share)],
                target,
                refs.grad_sent,
                refs.grad_sem,
            ).start()
        pltpu.make_async_copy(
            refs.grad_rows.at[index, pl.ds(row * share, share)], target, refs.grad_sem
        ).start()

    @pl.when(base == 0)
    def _():
        pack_shards(refs)
        greet(row_count, batch_count)
        own = pltpu.make_async_copy(refs.shard, refs.shards.at[row, batch], refs.local_sem)
        own.start()
        copies = peers(
            "batch",
            batch_count,
            [
                (0, (same(refs.shard), same(refs.shards.at[row, batch]))),
                (1, (same(refs.small), slot_of(refs.small_z))),
            ],
            refs.send_z,
            refs.recv_z,
        )
        start_all(copies)
        lax.fori_loop(0, together, send_field, 0)
        for ref in (refs.conv_grad_one, refs.conv_grad_two, refs.down_grad, refs.raw_sums, refs.sums):
            ref[...] = jnp.zeros_like(ref)
        if together > 1:
            for ref in scratch[-16:-12] + scratch[-4:-2]:
                ref[...] = jnp.zeros_like(ref)
        own.wait()
        finish(copies)
        total = refs.small[...]
        for step in range(1, batch_count):
            total = total + refs.small_z[step]
        refs.small_one[...] = total
        copies = peers(
            "row",
            row_count,
            [(1, (same(refs.small_one), slot_of(refs.small_row)))],
            refs.send_row,
            refs.recv_row,
        )
        sibling = sibling_of(row)
        mine = refs.shards.at[row]
        direct = {}
        for step in range(2, row_count, 2):
            direct[step] = to_row(
                lax.rem(row + step, row_count),
                mine,
                mine,
                refs.send_row.at[0, step],
                refs.recv_row.at[0, step],
            )
        beside = [to_row(sibling, mine, mine, refs.send_row.at[0, 1], refs.recv_row.at[0, 1])]
        start_all(list(direct.values()) + beside + copies)
        lax.fori_loop(together, samples, send_field, 0)
        for step in range(2, row_count, 2):
            direct[step].wait_recv()
            came = refs.shards.at[lax.rem(row + row_count - step, row_count)]
            beside.append(
                to_row(
                    sibling,
                    came,
                    came,
                    refs.send_row.at[0, step + 1],
                    refs.recv_row.at[0, step + 1],
                )
            )
            beside[-1].start()
        for step in range(2, row_count, 2):
            direct[step].wait_send()
        finish(beside + copies)
        total = refs.small_one[...]
        for step in range(1, row_count):
            total = total + refs.small_row[step]
        refs.small_all[...] = total
        lay_out(row_count, batch_count, refs)
        modulate(refs)

    @pl.when(base > 0)
    def _():
        for place in range(together):
            send_grad(base - together + place)

    for place in range(together):
        arrived = refs.fields.at[base + place]
        pltpu.make_async_copy(arrived, arrived, refs.field_sem.at[base + place]).wait()
    stages = [
        Sample(
            pairs,
            base + place,
            refs.fields.at[base + place],
            refs.cot.at[place],
            refs.block_out.at[place],
            refs,
            scratch[16 * place : 16 * place + 16],
        )
        for place in range(together)
    ]

    for name, place in STAGES:
        if place >= together or (place == BEFORE and together == 1):
            continue
        stage = getattr(stages[place], name)
        if name == "field_grad":
            stage(refs.grad_rows.at[base + place])
        else:
            stage()

    @pl.when(base == samples - together)
    def _():
        for place in range(together - 1):
            send_grad(base + place)
        if together > 1:
            for name in LATE:
                getattr(stages[-1], name)()
        reduce_all(row_count, batch_count, refs, lambda: send_grad(base + together - 1))
        pltpu.make_async_copy(refs.grad_out, refs.grad_out, refs.grad_sem).wait()
        others = pl.ds(0, pairs - share)
        for ref, sem in ((refs.fields, refs.field_sent), (refs.grad_rows, refs.grad_sent)):
            pltpu.make_async_copy(ref.at[:, others], ref.at[:, others], sem).wait()


INPUTS = ("field", "cot", "conv", "down", "embed_in", "embed_out", "small", "embedded", "group")
OUTPUTS = (
    "block_out",
    "grad_out",
    "conv_grad",
    "down_share",
    "embed_in_grad",
    "embed_out_grad",
    "small_grad",
    "norm",
)
SCRATCH = (
    "fwd_one",
    "back_one",
    "fwd_two",
    "back_two",
    "down_fwd",
    "down_even",
    "down_odd",
    "small_all",
    "embed_in_t",
    "embed_out_t",
    "modulation",
    "hidden",
    "hidden_slope",
    "sums",
    "raw_sums",
    "conv_grad_one",
    "conv_grad_two",
    "down_grad",
    "shard",
    "shards",
    "small_z",
    "small_one",
    "small_row",
    "conv_t",
    "down_t",
    "fields",
    "grad_rows",
    "row_send",
    "pair_take",
    "chip_send",
    "row_take",
    "batch_send",
    "batch_take",
    "small_send",
    "small_take",
    "small_next",
    "small_last",
    "square_send",
    "square_take",
    "square_next",
    "square_last",
    "field_sem",
    "field_sent",
    "grad_sem",
    "grad_sent",
    "local_sem",
    "send_z",
    "recv_z",
    "send_row",
    "recv_row",
    "send_sem",
    "recv_sem",
)
DOWN_ORDER = ((1, 0), (2, 0), (1, 1), (2, 1), (1, 2), (2, 2), (0, 0), (0, 1), (0, 2))


def lay_out(row_count, batch_count, refs):
    depth, share, wide_share = 9 * C // batch_count, C // row_count, C2 // row_count
    height = 2 * share + wide_share
    embed_share, hidden_share = EMB // batch_count, HID // batch_count
    for place in range(row_count):
        parts = [refs.shards[place, part].astype(jnp.float32) for part in range(batch_count)]
        main = jnp.concatenate([part[:, :depth] for part in parts], axis=1)
        for which in range(2):
            refs.conv_t[which, place * share : place * share + share, :] = main[
                which * share : which * share + share
            ]
        refs.down_t[place * wide_share : place * wide_share + wide_share, :] = main[2 * share :]
        refs.embed_in_t[place * height : place * height + height, :] = jnp.concatenate(
            [part[:, depth : depth + embed_share] for part in parts], axis=1
        )
        tail = depth + embed_share
        half_rows, half_lanes = height // 2, hidden_share // 2
        lanes = []
        for part in parts:
            lanes.append(part[:half_rows, tail : tail + half_lanes])
            lanes.append(part[half_rows:, tail : tail + half_lanes])
        refs.embed_out_t[place * half_rows : place * half_rows + half_rows, :] = jnp.concatenate(
            lanes, axis=1
        )
    for which, forward, back in (
        (0, refs.fwd_one, refs.back_one),
        (1, refs.fwd_two, refs.back_two),
    ):
        zero = jnp.zeros((C, C), jnp.bfloat16)
        for tap in range(3):
            direct = [
                refs.conv_t[which, :, (3 * row_tap + tap) * C : (3 * row_tap + tap) * C + C]
                for row_tap in range(3)
            ]
            fill_blocks(forward, tap, [block.T.astype(jnp.bfloat16) for block in direct], zero)
            fill_blocks(
                back, 2 - tap, [block.astype(jnp.bfloat16) for block in direct[::-1]], zero
            )
    zero = jnp.zeros((C2, C), jnp.bfloat16)
    back = {}
    for position in range(9):
        row_tap, tap = DOWN_ORDER[position]
        block = refs.down_t[:, (3 * row_tap + tap) * C : (3 * row_tap + tap) * C + C]
        refs.down_fwd[position * C : position * C + C, :] = block.T.astype(jnp.bfloat16)
        back[row_tap, tap] = block.astype(jnp.bfloat16)
    even = ((back[1, 1], back[2, 1]), (zero, back[0, 1]))
    odd = (
        (back[1, 2], back[2, 2]),
        (back[1, 0], back[2, 0]),
        (zero, back[0, 2]),
        (zero, back[0, 0]),
    )
    for ref, table in ((refs.down_even, even), (refs.down_odd, odd)):
        for position, (left, right) in enumerate(table):
            ref[position * C2 : position * C2 + C2, :C] = left
            ref[position * C2 : position * C2 + C2, C:] = right


def lanes_of(ref, first, last):
    return jnp.concatenate([ref[place : place + 1, :] for place in range(first, last)], axis=1)


def modulate(refs):
    small = refs.small_all
    before = dot_last(refs.embedded[...], refs.embed_in_t[...]) + lanes_of(small, 8, 12)
    hidden, slope = gelu_pair(before)
    refs.hidden[...] = hidden
    refs.hidden_slope[...] = slope
    result = dot_last(hidden, refs.embed_out_t[...]) + lanes_of(small, 12, 14)
    refs.modulation[0] = 1.0 + result[:, :C]
    refs.modulation[1] = result[:, C:]


def fill_blocks(ref, tap, blocks, zero):
    table = (
        (blocks[1], blocks[0]),
        (blocks[2], blocks[1]),
        (blocks[0], zero),
        (zero, blocks[2]),
    )
    for position, (left, right) in enumerate(table):
        base = (4 * tap + position) * C
        ref[base : base + C, :C] = left
        ref[base : base + C, C:] = right


def dot_full(lhs, rhs):
    return jnp.dot(lhs, rhs, precision=HIGHEST, preferred_element_type=jnp.float32)


def dot_last(lhs, rhs):
    return lax.dot_general(
        lhs,
        rhs,
        (((1,), (1,)), ((), ())),
        precision=HIGHEST,
        preferred_element_type=jnp.float32,
    )


def dot_first(lhs, rhs):
    return lax.dot_general(
        lhs,
        rhs,
        (((0,), (0,)), ((), ())),
        precision=HIGHEST,
        preferred_element_type=jnp.float32,
    )


def reduce_all(row_count, batch_count, refs, send_last):
    row, batch = lax.axis_index("row"), lax.axis_index("batch")
    depth, share, wide_share = 9 * C // batch_count, C // row_count, C2 // row_count
    height = 2 * share + wide_share
    embed_share, hidden_share = EMB // batch_count, HID // batch_count
    half_rows = height // 2
    sibling = sibling_of(row)
    main, rest = pl.ds(0, 9 * C), pl.ds(9 * C, 3 * C)
    order = list(range(1, row_count // 2)) + [0]

    def to_sibling(step, lanes, place):
        return to_row(
            sibling,
            refs.row_send.at[lax.rem(sibling + 2 * step, row_count), :, lanes],
            refs.pair_take.at[step, :, lanes],
            refs.send_sem.at[place, step],
            refs.recv_sem.at[place, step],
        )

    for place in range(row_count):
        low, high = place * share, place * share + share
        refs.row_send[place, :, : 9 * C] = jnp.concatenate(
            [
                refs.conv_grad_one[low:high],
                refs.conv_grad_two[low:high],
                refs.down_grad[place * wide_share : place * wide_share + wide_share],
            ],
            axis=0,
        ).astype(jnp.bfloat16)
    beside = {step: to_sibling(step, main, 0) for step in order}
    start_all(list(beside.values()))
    mid_cross, mid_total = refs.sums[0], refs.sums[1]
    gain_two, shift_two = refs.small_all[1:2, :], refs.small_all[3:4, :]
    scale_plus = refs.modulation[0]
    grad_mod = jnp.concatenate([gain_two * mid_cross + shift_two * mid_total, mid_total], axis=1)
    grad_embed_out = dot_first(grad_mod, refs.hidden[...])
    grad_hidden = (
        dot_full(grad_mod, refs.embed_out_t[...])
        * refs.hidden_slope[...]
    )
    grad_embed_in = dot_first(grad_hidden, refs.embedded[...])

    def down_sum(value):
        return jnp.sum(value, axis=0, keepdims=True)

    small_rows = [
        down_sum(refs.sums[2]),
        down_sum(mid_cross * scale_plus),
        down_sum(refs.sums[3]),
        down_sum(mid_total * scale_plus),
        channel_sum(refs.raw_sums[0:8]),
        channel_sum(refs.raw_sums[8:16]),
    ]
    cot_total = down_sum(refs.raw_sums[16:24])
    small_rows += [cot_total[:, :C], cot_total[:, C:]]
    hidden_total, mod_total = down_sum(grad_hidden), down_sum(grad_mod)
    small_rows += [hidden_total[:, lane : lane + C] for lane in range(0, HID, C)]
    small_rows += [mod_total[:, lane : lane + C] for lane in range(0, 2 * C, C)]
    small_rows.append(jnp.zeros((2, C), jnp.float32))
    refs.small_send[...] = jnp.concatenate(small_rows, axis=0)
    for place in range(row_count):
        refs.row_send[place, :, 9 * C : 10 * C] = grad_embed_in[
            place * height : place * height + height
        ].astype(jnp.bfloat16)
        piece = grad_embed_out[place * half_rows : place * half_rows + half_rows]
        refs.row_send[place, :, 10 * C :] = jnp.concatenate(
            [piece[:, : HID // 2], piece[:, HID // 2 :]], axis=0
        ).astype(jnp.bfloat16)
    beyond = {step: to_sibling(step, rest, 7) for step in order}
    smalls = [
        to_peer(
            "row",
            step,
            row_count,
            refs.small_send,
            refs.small_take.at[step],
            refs.send_sem.at[1, step],
            refs.recv_sem.at[1, step],
        )
        for step in range(1, row_count)
    ]
    start_all(list(beyond.values()) + smalls)
    copies = []
    for step in order:
        beside[step].wait_recv()
        beyond[step].wait_recv()
        place = lax.rem(row + 2 * step, row_count)
        total = refs.row_send[place].astype(jnp.float32) + refs.pair_take[step].astype(jnp.float32)
        if step:
            refs.chip_send[step] = total.astype(jnp.bfloat16)
            copies.append(
                to_row(
                    place,
                    refs.chip_send.at[step],
                    refs.row_take.at[step],
                    refs.send_sem.at[6, step],
                    refs.recv_sem.at[6, step],
                )
            )
            copies[-1].start()
    send_last()
    for copy in list(beside.values()) + list(beyond.values()):
        copy.wait_send()
    finish(copies + smalls)
    small_total = refs.small_send[...]
    for step in range(1, row_count // 2):
        total = total + refs.row_take[step].astype(jnp.float32)
    for step in range(1, row_count):
        small_total = small_total + refs.small_take[step]
    refs.small_next[...] = small_total
    for part in range(batch_count):
        per_half = batch_count // 2
        rows = slice(0, half_rows) if part < per_half else slice(half_rows, height)
        base = 10 * C + hidden_share * (part % per_half)
        piece = total[rows, base : base + hidden_share]
        refs.batch_send[part] = jnp.concatenate(
            [
                total[:, part * depth : part * depth + depth],
                total[:, 9 * C + part * embed_share : 9 * C + part * embed_share + embed_share],
                jnp.concatenate([piece[:, : hidden_share // 2], piece[:, hidden_share // 2 :]], axis=0),
            ],
            axis=1,
        ).astype(jnp.bfloat16)
    copies = []
    for step in range(1, batch_count):
        copies.append(
            to_peer(
                "batch",
                step,
                batch_count,
                refs.batch_send.at[lax.rem(batch + step, batch_count)],
                refs.batch_take.at[step],
                refs.send_sem.at[2, step],
                refs.recv_sem.at[2, step],
            )
        )
        copies.append(
            to_peer(
                "batch",
                step,
                batch_count,
                refs.small_next,
                refs.small_last.at[step],
                refs.send_sem.at[3, step],
                refs.recv_sem.at[3, step],
            )
        )
    for copy in copies:
        copy.start()
    owned = refs.batch_send[batch].astype(jnp.float32)
    finish(copies)
    small_total = refs.small_next[...]
    for step in range(1, batch_count):
        owned = owned + refs.batch_take[step].astype(jnp.float32)
        small_total = small_total + refs.small_last[step]
    squares = jnp.sum(jnp.sum(owned * owned, axis=0, keepdims=True), axis=1, keepdims=True)
    refs.square_send[...] = jnp.broadcast_to(squares, (8, C))
    copies = [
        to_peer(
            "row",
            step,
            row_count,
            refs.square_send,
            refs.square_take.at[step],
            refs.send_sem.at[4, step],
            refs.recv_sem.at[4, step],
        )
        for step in range(1, row_count)
    ]
    for copy in copies:
        copy.start()
    finish(copies)
    squares = refs.square_send[...]
    for step in range(1, row_count):
        squares = squares + refs.square_take[step]
    refs.square_next[...] = squares
    copies = [
        to_peer(
            "batch",
            step,
            batch_count,
            refs.square_next,
            refs.square_last.at[step],
            refs.send_sem.at[5, step],
            refs.recv_sem.at[5, step],
        )
        for step in range(1, batch_count)
    ]
    for copy in copies:
        copy.start()
    finish(copies)
    squares = refs.square_next[...]
    for step in range(1, batch_count):
        squares = squares + refs.square_last[step]
    small_squares = jnp.sum(
        jnp.sum(small_total * small_total, axis=0, keepdims=True), axis=1, keepdims=True
    )
    norm = jnp.sqrt(squares + small_squares)
    clip = jnp.minimum(1.0, CLIP_NORM / (norm + 1e-06))[0:1, 0:1]
    refs.norm[...] = norm[0:1, 0:1]
    owned = owned * clip
    refs.conv_grad[0] = owned[:share, :depth]
    refs.conv_grad[1] = owned[share : 2 * share, :depth]
    refs.down_share[...] = owned[2 * share :, :depth]
    refs.embed_in_grad[...] = owned[:, depth : depth + embed_share].T
    tail = depth + embed_share
    refs.embed_out_grad[...] = jnp.concatenate(
        [owned[:half_rows, tail:], owned[half_rows:, tail:]], axis=1
    )
    refs.small_all[...] = small_total * clip
    small_len = 14 * C // (row_count * batch_count)
    first = (batch * row_count + row) * small_len
    line, lane = first // C, lax.rem(first, C)
    lines = jnp.concatenate(
        [refs.small_all[pl.ds(line, 1), :], refs.small_all[pl.ds(line + 1, 1), :]], axis=1
    )
    moved = pltpu.roll(jnp.broadcast_to(lines, (8, 2 * C)), lax.rem(2 * C - lane, 2 * C), 1)
    refs.small_grad[...] = moved[0:1, :small_len]


def pack_shards(refs):
    half = refs.embed_out.shape[1] // 2
    refs.shard[...] = jnp.concatenate(
        [
            jnp.concatenate([refs.conv[0], refs.conv[1], refs.down[...]], axis=0),
            refs.embed_in[...].T,
            jnp.concatenate([refs.embed_out[:, :half], refs.embed_out[:, half:]], axis=0),
        ],
        axis=1,
    ).astype(jnp.bfloat16)


def run_step(field_in, cotangent, shards, small_tile, embedded):
    row_count, batch_count = (lax.axis_size("row"), lax.axis_size("batch"))
    samples = cotangent.shape[0]
    padded = embedded.shape[0]
    pairs = field_in.shape[1] // 2 * row_count
    together = chunk_of(samples, 2)
    share = pairs // row_count
    height, width = 4 * C // row_count, 12 * C // batch_count
    halves = field_in.reshape(field_in.shape[0], share, 2, FIELD_COLS, C)
    same_group = jnp.asarray(
        np.kron(np.eye(GROUPS), np.ones((C // GROUPS, C // GROUPS))), jnp.float32
    )
    low, full = jnp.bfloat16, jnp.float32
    anywhere = pl.BlockSpec(memory_space=pl.ANY)

    def whole(array):
        return pl.BlockSpec(array.shape, lambda i: (0,) * len(array.shape))

    def per_step(array):
        rank = len(array.shape)
        return pl.BlockSpec((together,) + array.shape[1:], lambda i: (i,) + (0,) * (rank - 1))

    outs = (
        jax.ShapeDtypeStruct(cotangent.shape, low),
        jax.ShapeDtypeStruct(halves.shape, low),
        *[jax.ShapeDtypeStruct(shard.shape, full) for shard in shards],
        jax.ShapeDtypeStruct((1, 14 * C // (row_count * batch_count)), full),
        jax.ShapeDtypeStruct((1, 1), full),
    )
    ring = pltpu.VMEM((3, pairs + 2, FIELD_COLS, 2 * C), low)
    wide = pltpu.VMEM((pairs, FIELD_COLS, 2 * C), full)
    half = pltpu.VMEM((pairs, FIELD_COLS, C), full)
    fields = pltpu.VMEM((samples, pairs, 2, FIELD_COLS, C), low)
    dma = pltpu.SemaphoreType.DMA
    most = max(row_count, batch_count)
    tile = (16, C)
    scratch = (
        [pltpu.VMEM((12 * C, 2 * C), low)] * 4
        + [
            pltpu.VMEM((9 * C, C2), low),
            pltpu.VMEM((2 * C2, 2 * C), low),
            pltpu.VMEM((4 * C2, 2 * C), low),
            pltpu.VMEM(tile, full),
            pltpu.VMEM((HID, EMB), full),
            pltpu.VMEM((2 * C, HID), full),
            pltpu.VMEM((2, padded, C), full),
            pltpu.VMEM((padded, HID), full),
            pltpu.VMEM((padded, HID), full),
            pltpu.VMEM((4, padded, C), full),
            pltpu.VMEM((24, 2 * C), full),
            pltpu.VMEM((C, 9 * C), full),
            pltpu.VMEM((C, 9 * C), full),
            pltpu.VMEM((C2, 9 * C), full),
            pltpu.VMEM((height, width), low),
            pltpu.VMEM((row_count, batch_count, height, width), low),
            pltpu.VMEM((batch_count,) + tile, full),
            pltpu.VMEM(tile, full),
            pltpu.VMEM((row_count,) + tile, full),
            pltpu.VMEM((2, C, 9 * C), full),
            pltpu.VMEM((C2, 9 * C), full),
            fields,
            fields,
            pltpu.VMEM((row_count, height, 12 * C), low),
            pltpu.VMEM((row_count // 2, height, 12 * C), low),
            pltpu.VMEM((row_count // 2, height, 12 * C), low),
            pltpu.VMEM((row_count // 2, height, 12 * C), low),
            pltpu.VMEM((batch_count, height, width), low),
            pltpu.VMEM((batch_count, height, width), low),
            pltpu.VMEM(tile, full),
            pltpu.VMEM((row_count,) + tile, full),
            pltpu.VMEM(tile, full),
            pltpu.VMEM((batch_count,) + tile, full),
            pltpu.VMEM((8, C), full),
            pltpu.VMEM((row_count, 8, C), full),
            pltpu.VMEM((8, C), full),
            pltpu.VMEM((batch_count, 8, C), full),
            dma((samples,)),
            dma,
            dma,
            dma,
            dma,
            dma((2, batch_count)),
            dma((2, batch_count)),
            dma((2, row_count)),
            dma((2, row_count)),
            dma((8, most)),
            dma((8, most)),
        ]
        + (
            [ring] * 4
            + [wide] * 4
            + [half] * 4
            + [
                pltpu.VMEM((3, pairs + 1, HALF_COLS, 2 * C), low),
                pltpu.VMEM((2, pairs + 1, HALF_COLS, C2), low),
                pltpu.VMEM((8, C), full),
                pltpu.VMEM((2, 8, 2 * C), full),
            ]
        )
        * together
    )
    result = pl.pallas_call(
        functools.partial(step_kernel, (row_count, batch_count, pairs, samples, together)),
        grid=(samples // together,),
        in_specs=[anywhere, per_step(cotangent)]
        + [whole(array) for array in shards + (small_tile, embedded, same_group)],
        out_specs=[per_step(outs[0]), anywhere] + [whole(out) for out in outs[2:]],
        out_shape=outs,
        scratch_shapes=scratch,
        compiler_params=pltpu.CompilerParams(
            dimension_semantics=("arbitrary",),
            vmem_limit_bytes=62 << 20,
            collective_id=0,
            has_side_effects=True,
        ),
        name="step",
    )(halves, cotangent, *shards, small_tile, embedded, same_group)
    return (result[0], result[1].reshape(field_in.shape)) + tuple(result[2:])


def adam_update(weight, gradient, first_old, second_old, step_rate, clip_factor):
    scaled = gradient * clip_factor
    first_new = BETA_ONE * first_old + (1.0 - BETA_ONE) * scaled
    second_new = BETA_TWO * second_old + (1.0 - BETA_TWO) * scaled * scaled
    corrected = (
        first_new
        / (1.0 - BETA_ONE**STEP_COUNT)
        / (jnp.sqrt(second_new / (1.0 - BETA_TWO**STEP_COUNT)) + ADAM_EPS)
    )
    return (weight - step_rate * (corrected + DECAY * weight), first_new, second_new)


def body(
    field_in,
    refine_step,
    cotangent,
    conv_weight,
    down_weight,
    embed_in_weight,
    embed_out_weight,
    small_params,
    conv_first,
    down_first,
    embed_in_first,
    embed_out_first,
    small_first,
    conv_second,
    down_second,
    embed_in_second,
    embed_out_second,
    small_second,
):
    small_len = small_params.shape[0]
    place = (lax.axis_index("batch") * lax.axis_size("row") + lax.axis_index("row")) * small_len
    small_rounded = lax.reduce_precision(small_params, exponent_bits=8, mantissa_bits=7)
    small_tile = lax.dynamic_update_slice_in_dim(
        jnp.zeros((16 * C,), jnp.float32), small_rounded, place, 0
    ).reshape(16, C)
    owned = refine_step.shape[0] // lax.axis_size("row")
    padded = -(-owned // 8) * 8
    own_steps = lax.dynamic_slice_in_dim(refine_step, lax.axis_index("row") * owned, owned, 0)
    embedded = embed_steps(jnp.pad(own_steps, (0, padded - owned)))
    block_out, grad_start, *owned_shards, small_grads, norm_tile = run_step(
        field_in,
        cotangent,
        (
            jnp.transpose(conv_weight, (0, 2, 1)),
            down_weight.T,
            embed_in_weight,
            embed_out_weight.T,
        ),
        small_tile,
        embedded,
    )
    grad_norm = norm_tile.reshape(())
    owned_shards = [
        jnp.transpose(owned_shards[0], (0, 2, 1)),
        owned_shards[1].T,
        owned_shards[2],
        owned_shards[3].T,
    ]
    owned_shards.append(small_grads.reshape(small_len))
    clip_factor = 1.0
    conv_new = adam_update(
        conv_weight, owned_shards[0], conv_first, conv_second, RATE_MATRIX, clip_factor
    )
    down_new = adam_update(
        down_weight, owned_shards[1], down_first, down_second, RATE_MATRIX, clip_factor
    )
    embed_in_new = adam_update(
        embed_in_weight, owned_shards[2], embed_in_first, embed_in_second, RATE_MATRIX, clip_factor
    )
    embed_out_new = adam_update(
        embed_out_weight,
        owned_shards[3],
        embed_out_first,
        embed_out_second,
        RATE_MATRIX,
        clip_factor,
    )
    small_new = adam_update(
        small_params, owned_shards[4], small_first, small_second, RATE_SMALL, clip_factor
    )
    return (
        block_out,
        grad_start,
        grad_norm,
        conv_new[0],
        down_new[0],
        embed_in_new[0],
        embed_out_new[0],
        small_new[0],
        conv_new[1],
        down_new[1],
        embed_in_new[1],
        embed_out_new[1],
        small_new[1],
        conv_new[2],
        down_new[2],
        embed_in_new[2],
        embed_out_new[2],
        small_new[2],
    )


def solution(mesh):
    placed = (
        P("batch", "row", None, None),
        P("batch"),
        P(("batch", "row"), None, None, None),
        P(None, "batch", "row"),
        P("batch", "row"),
        P("batch", "row"),
        P("batch", "row"),
        P(("batch", "row")),
        P(None, "batch", "row"),
        P("batch", "row"),
        P("batch", "row"),
        P("batch", "row"),
        P(("batch", "row")),
        P(None, "batch", "row"),
        P("batch", "row"),
        P("batch", "row"),
        P("batch", "row"),
        P(("batch", "row")),
    )
    return jax.shard_map(
        body,
        mesh=mesh,
        in_specs=placed,
        out_specs=(
            P(("batch", "row"), None, None, None),
            P("batch", "row", None, None),
            P(),
            P(None, "batch", "row"),
            P("batch", "row"),
            P("batch", "row"),
            P("batch", "row"),
            P(("batch", "row")),
            P(None, "batch", "row"),
            P("batch", "row"),
            P("batch", "row"),
            P("batch", "row"),
            P(("batch", "row")),
            P(None, "batch", "row"),
            P("batch", "row"),
            P("batch", "row"),
            P("batch", "row"),
            P(("batch", "row")),
        ),
        check_vma=False,
    )
```
